32 devices in a mesh: row: 8 (over z, core), col: 4 (over y, x).
Axes of the slice: x: 2, y: 2, z: 4, core: 2. Of those that a mesh axis runs over, the one named last changes fastest.
Arguments:
- layer_input: bfloat16 [1024, 8192], P('col', 'row'), may hold values from -6 to 6
- clip_lengths: int32 [8], P('row'), may hold values from 768 to 1024, as said below
- first_gain: float32 [1024], P('col'), may hold values from 0.5 to 1.5
- first_up: bfloat16 [1024, 4096], P('row', 'col'), may hold values from -0.1875 to 0.1875
- first_down: bfloat16 [4096, 1024], P('col', 'row'), may hold values from -0.09375 to 0.09375
- attend_gain: float32 [1024], P('col'), may hold values from 0.5 to 1.5
- query_weight: bfloat16 [1024, 1024], P('row', 'col'), may hold values from -0.1875 to 0.1875
- key_weight: bfloat16 [1024, 1024], P('row', 'col'), may hold values from -0.1875 to 0.1875
- value_weight: bfloat16 [1024, 1024], P('row', 'col'), may hold values from -0.1875 to 0.1875
- output_weight: bfloat16 [1024, 1024], P('col', 'row'), may hold values from -0.75 to 0.75
- distance_table: bfloat16 [73, 64], replicated, may hold values from -6 to 6
- conv_gain: float32 [1024], P('col'), may hold values from 0.5 to 1.5
- pointwise_value: bfloat16 [1024, 1024], P('row', 'col'), may hold values from -0.1875 to 0.1875
- pointwise_gate: bfloat16 [1024, 1024], P('row', 'col'), may hold values from -0.1875 to 0.1875
- depthwise_kernel: bfloat16 [31, 1024], P(None, 'col'), may hold values from -1 to 1
- depthwise_gain: float32 [1024], P('col'), may hold values from 0.5 to 1.5
- pointwise_out: bfloat16 [1024, 1024], P('col', 'row'), may hold values from -0.1875 to 0.1875
- second_gain: float32 [1024], P('col'), may hold values from 0.5 to 1.5
- second_up: bfloat16 [1024, 4096], P('row', 'col'), may hold values from -0.1875 to 0.1875
- second_down: bfloat16 [4096, 1024], P('col', 'row'), may hold values from -0.09375 to 0.09375
- final_gain: float32 [1024], P('col'), may hold values from 0.5 to 1.5
- output_cotangent: bfloat16 [1024, 8192], P('col', 'row'), may hold values from -6 to 6
Outputs:
- layer_output: bfloat16 [1024, 8192], P('col', 'row')
- input_grad: float32 [1024, 8192], P('col', 'row')
- first_gain_grad: float32 [1024], P('col')
- first_up_grad: float32 [1024, 4096], P('row', 'col')
- first_down_grad: float32 [4096, 1024], P('col', 'row')
- attend_gain_grad: float32 [1024], P('col')
- query_weight_grad: float32 [1024, 1024], P('row', 'col')
- key_weight_grad: float32 [1024, 1024], P('row', 'col')
- value_weight_grad: float32 [1024, 1024], P('row', 'col')
- output_weight_grad: float32 [1024, 1024], P('col', 'row')
- distance_table_grad: float32 [73, 64], replicated
- conv_gain_grad: float32 [1024], P('col')
- pointwise_value_grad: float32 [1024, 1024], P('row', 'col')
- pointwise_gate_grad: float32 [1024, 1024], P('row', 'col')
- depthwise_kernel_grad: float32 [31, 1024], P(None, 'col')
- depthwise_gain_grad: float32 [1024], P('col')
- pointwise_out_grad: float32 [1024, 1024], P('col', 'row')
- second_gain_grad: float32 [1024], P('col')
- second_up_grad: float32 [1024, 4096], P('row', 'col')
- second_down_grad: float32 [4096, 1024], P('col', 'row')
- final_gain_grad: float32 [1024], P('col')
- masked_rms: float32 [8], replicated
The draws below stay inside these ranges and needn't reach their ends.
Inputs may be any that keep to these rules, and one draw needn't show every extreme that they name: Each clip's valid tokens are its first clip_lengths slots; the rest of its 1024 slots are padding. Some clip is full in every draw.
All inputs are finite; a program needn't handle non-finite values.
Results may differ from the reference program's by a relative error of at most 0.015.
Values may be sent and summed in bfloat16 or wider, within the bound.
A program may use at most 192 MiB of HBM per device.

```python
import jax
import jax.numpy as jnp
from jax import lax

D = 1024
HEADS = 16
HEAD_DIM = 64
FF = 4096
KERNEL = 31
LEFT = 64
RIGHT = 8
CLIP_TOKEN_SLOTS = 1024
CLIPS = 8
TOKENS = 8192
TABLE = 73


def draw_clip_lengths(key, part):
    first_key = jax.random.fold_in(key, 11)
    second_key = jax.random.fold_in(key, 23)
    drawn = jax.random.randint(first_key, (CLIPS,), CLIP_TOKEN_SLOTS - CLIP_TOKEN_SLOTS // 4, CLIP_TOKEN_SLOTS + 1)
    chosen = jax.random.randint(second_key, (), 0, CLIPS)
    return jnp.where(jnp.arange(CLIPS) == chosen, CLIP_TOKEN_SLOTS, drawn).astype(jnp.int32)


def level_of(rng, extent, shards, least, high):
    def one(axis_at, parts):
        draws = jax.random.uniform(jax.random.fold_in(jax.random.fold_in(rng, 6), axis_at), (parts,), jnp.float32, least / len(shards), high / len(shards))
        return jnp.repeat(jnp.exp(draws), extent[axis_at] // parts).reshape((-1,) + (1,) * (len(extent) - axis_at - 1))

    loudness = one(*shards[0])
    for cut in shards[1:]:
        loudness = loudness * one(*cut)
    return loudness


def noise(rng, extent, spread, reach, pieces=(), held_as=jnp.bfloat16):
    values = spread * jax.random.normal(rng, extent, jnp.float32)
    if pieces:
        values = values * level_of(rng, extent, pieces, -0.22, 0.18)
    return jnp.clip(values, -reach, reach).astype(held_as)


def setup_inputs(seed: int = 0) -> dict:
    key_list = jax.random.split(jax.random.key(seed), 23)
    layer_input = noise(key_list[0], (D, TOKENS), 1.0, 6.0, ((0, 4), (1, 8)))
    clip_lengths = draw_clip_lengths(jax.random.fold_in(key_list[22], 71), 0)
    first_gain = jnp.clip(1.0 + 0.1 * jax.random.normal(key_list[2], (D,), jnp.float32), 0.5, 1.5)
    first_up = noise(key_list[3], (D, FF), D ** -0.5, 0.1875, ((0, 8), (1, 4)))
    first_down = noise(key_list[4], (FF, D), FF ** -0.5, 0.09375, ((0, 4), (1, 8)))
    attend_gain = jnp.clip(1.0 + 0.1 * jax.random.normal(key_list[5], (D,), jnp.float32), 0.5, 1.5)
    query_weight = noise(key_list[6], (D, D), D ** -0.5, 0.1875, ((0, 8), (1, 4)))
    key_weight = noise(key_list[7], (D, D), D ** -0.5, 0.1875, ((0, 8), (1, 4)))
    value_weight = noise(key_list[8], (D, D), D ** -0.5, 0.1875, ((0, 8), (1, 4)))
    output_weight = noise(key_list[9], (D, D), (D // 16) ** -0.5, 0.75, ((0, 4), (1, 8)))
    distance_table = noise(key_list[10], (TABLE, HEAD_DIM), 1.0, 6.0)
    conv_gain = jnp.clip(1.0 + 0.1 * jax.random.normal(key_list[11], (D,), jnp.float32), 0.5, 1.5)
    pointwise_value = noise(key_list[12], (D, D), D ** -0.5, 0.1875, ((0, 8), (1, 4)))
    pointwise_gate = noise(key_list[13], (D, D), D ** -0.5, 0.1875, ((0, 8), (1, 4)))
    depthwise_kernel = noise(key_list[14], (KERNEL, D), KERNEL ** -0.5, 1.0, ((1, 4),))
    depthwise_gain = jnp.clip(1.0 + 0.1 * jax.random.normal(key_list[15], (D,), jnp.float32), 0.5, 1.5)
    pointwise_out = noise(key_list[16], (D, D), D ** -0.5, 0.1875, ((0, 4), (1, 8)))
    second_gain = jnp.clip(1.0 + 0.1 * jax.random.normal(key_list[17], (D,), jnp.float32), 0.5, 1.5)
    second_up = noise(key_list[18], (D, FF), D ** -0.5, 0.1875, ((0, 8), (1, 4)))
    second_down = noise(key_list[19], (FF, D), FF ** -0.5, 0.09375, ((0, 4), (1, 8)))
    final_gain = jnp.clip(1.0 + 0.1 * jax.random.normal(key_list[20], (D,), jnp.float32), 0.5, 1.5)
    output_cotangent = noise(key_list[21], (D, TOKENS), 1.0, 6.0, ((0, 4), (1, 8)))
    return dict(layer_input=layer_input, clip_lengths=clip_lengths, first_gain=first_gain, first_up=first_up, first_down=first_down, attend_gain=attend_gain, query_weight=query_weight, key_weight=key_weight, value_weight=value_weight, output_weight=output_weight, distance_table=distance_table, conv_gain=conv_gain, pointwise_value=pointwise_value, pointwise_gate=pointwise_gate, depthwise_kernel=depthwise_kernel, depthwise_gain=depthwise_gain, pointwise_out=pointwise_out, second_gain=second_gain, second_up=second_up, second_down=second_down, final_gain=final_gain, output_cotangent=output_cotangent)


@jax.custom_vjp
def low(v):
    return lax.optimization_barrier(v.astype(jnp.bfloat16)).astype(jnp.float32)

@jax.custom_vjp
def low_back(v):
    return v

def low_keep(v):
    return (low(v), None)

def low_pass(kept, grad):
    return (grad,)

def back_keep(v):
    return (v, None)

def back_low(kept, grad):
    return (low(grad),)
low.defvjp(low_keep, low_pass)
low_back.defvjp(back_keep, back_low)
HIGH_ACCURACY = lax.Precision.HIGHEST
EPSILON = 1e-05

def product(left, right):
    return jnp.dot(left, right, precision=HIGH_ACCURACY)

def layer_norm(hidden, gains):
    average = lax.optimization_barrier(jnp.mean(hidden, axis=-1, keepdims=True))
    centered = hidden - average
    return centered * lax.rsqrt(lax.optimization_barrier(jnp.mean(centered * centered, axis=-1, keepdims=True)) + EPSILON) * gains

def depthwise(signal, kernel, clip_count):
    tap_count = kernel.shape[0]
    framed = signal.reshape(clip_count, -1, signal.shape[1])
    length = framed.shape[1]
    padded = jnp.pad(framed, ((0, 0), (tap_count - 1, 0), (0, 0)))
    result = padded[:, 0:length] * kernel[0]
    for tap_index in range(1, tap_count):
        result = result + padded[:, tap_index:tap_index + length] * kernel[tap_index]
    return result.reshape(signal.shape)

def relative_index(length, left, right):
    rows_iota = lax.broadcasted_iota(jnp.int32, (length, length), 0)
    cols_iota = lax.broadcasted_iota(jnp.int32, (length, length), 1)
    return (jnp.clip(cols_iota - rows_iota, -left, right) + left).astype(jnp.int32)

def attend_clip(query_rows, incoming_keys, value_rows, table, keep_keys):
    rel_terms = jnp.einsum('lhd,rd->hlr', query_rows, table, precision=HIGH_ACCURACY)
    index_map = jnp.broadcast_to(relative_index(CLIP_TOKEN_SLOTS, LEFT, RIGHT)[None], (HEADS, CLIP_TOKEN_SLOTS, CLIP_TOKEN_SLOTS))
    positional = jnp.take_along_axis(rel_terms, index_map, axis=2)
    direct_result = jnp.einsum('ick,fck->cif', query_rows, incoming_keys, precision=HIGH_ACCURACY)
    scores = low_back((direct_result + positional) * HEAD_DIM ** (-0.5))
    scores = jnp.where(keep_keys[None, None, :], scores, -1e+30)
    attention_probability = low(jax.nn.softmax(scores, axis=-1))
    return jnp.einsum('eir,rev->iev', attention_probability, value_rows, precision=HIGH_ACCURACY)

def feed_branch(hidden, gains, up_matrix, down_matrix):
    rows_in = low(layer_norm(hidden, gains))
    pre_act = low_back(product(rows_in, up_matrix))
    return low_back(product(low(jax.nn.silu(pre_act)), down_matrix))

def layer_group(params, inputs, lengths):
    first_gain, first_up, first_down, attend_gain, query_weight, key_weight, value_weight, output_weight, distance_table, conv_gain, pointwise_value, pointwise_gate, depthwise_kernel, depthwise_gain, pointwise_out, second_gain, second_up, second_down, final_gain = params
    clip_count = lengths.shape[0]
    positions = lax.broadcasted_iota(jnp.int32, (clip_count, CLIP_TOKEN_SLOTS), 1)
    keep_keys = positions < lengths[:, None]
    keep_rows = keep_keys.reshape(-1).astype(jnp.float32)[:, None]
    branch_first = feed_branch(inputs, first_gain, first_up, first_down)
    after_first = inputs + 0.5 * branch_first
    rows_attend = low(layer_norm(after_first, attend_gain))

    def split(weight):
        return low_back(low(product(rows_attend, weight))).reshape(clip_count, CLIP_TOKEN_SLOTS, HEADS, HEAD_DIM)
    query_rows = split(query_weight)
    incoming_keys = split(key_weight)
    value_rows = split(value_weight)
    clip_step = jax.checkpoint(lambda items: attend_clip(items[0], items[1], items[2], distance_table, items[3]))
    context = lax.map(clip_step, (query_rows, incoming_keys, value_rows, keep_keys))
    context = low_back(low(context.reshape(clip_count * CLIP_TOKEN_SLOTS, HEADS * HEAD_DIM)))
    branch_attend = low_back(product(context, output_weight))
    after_attend = after_first + branch_attend
    rows_conv = low(layer_norm(after_attend, conv_gain))
    value_pre = low_back(product(rows_conv, pointwise_value))
    gate_pre = low_back(product(rows_conv, pointwise_gate))
    gated = value_pre * jax.nn.sigmoid(gate_pre) * keep_rows
    mixed = depthwise(gated, depthwise_kernel, clip_count)
    act_conv = low(jax.nn.silu(layer_norm(mixed, depthwise_gain)))
    branch_conv = low_back(product(act_conv, pointwise_out))
    after_conv = after_attend + branch_conv
    branch_second = feed_branch(after_conv, second_gain, second_up, second_down)
    after_second = after_conv + 0.5 * branch_second
    final_norm = layer_norm(after_second, final_gain)
    streams = (branch_first, branch_attend, branch_conv, branch_second, after_first, after_attend, after_conv, after_second)
    squares = jnp.stack([jnp.sum(jnp.square(stream) * keep_rows) for stream in streams])
    return (final_norm, squares)

def reference(layer_input, clip_lengths, first_gain, first_up, first_down, attend_gain, query_weight, key_weight, value_weight, output_weight, distance_table, conv_gain, pointwise_value, pointwise_gate, depthwise_kernel, depthwise_gain, pointwise_out, second_gain, second_up, second_down, final_gain, output_cotangent):
    params = tuple((param.astype(jnp.float32) for param in (first_gain, first_up, first_down, attend_gain, query_weight, key_weight, value_weight, output_weight, distance_table, conv_gain, pointwise_value, pointwise_gate, depthwise_kernel, depthwise_gain, pointwise_out, second_gain, second_up, second_down, final_gain)))
    group = max((count for count in (1, 2, 3, 4) if CLIPS % count == 0))
    inputs = layer_input.astype(jnp.float32).T.reshape(CLIPS // group, group * CLIP_TOKEN_SLOTS, D)
    lengths = clip_lengths.astype(jnp.int32).reshape(CLIPS // group, group)
    step = jax.checkpoint(layer_group)

    def whole(params_in, inputs_in):
        outputs, squares = lax.map(lambda items: step(params_in, items[0], items[1]), (inputs_in, lengths))
        return (outputs, lax.optimization_barrier(jnp.sum(squares, axis=0)))
    layer_result, vjp_fn, squares = jax.vjp(whole, params, inputs, has_aux=True)
    cotangent = output_cotangent.astype(jnp.float32).T.reshape(inputs.shape)
    param_grads, inputs_grad = vjp_fn(cotangent)
    total_count = jnp.sum(clip_lengths).astype(jnp.float32)
    masked_rms = jnp.sqrt(squares / (total_count * D))
    return (layer_result.reshape(TOKENS, D).T.astype(jnp.bfloat16), inputs_grad.reshape(TOKENS, D).T, param_grads[0], param_grads[1], param_grads[2], param_grads[3], param_grads[4], param_grads[5], param_grads[6], param_grads[7], param_grads[8], param_grads[9], param_grads[10], param_grads[11], param_grads[12], param_grads[13], param_grads[14], param_grads[15], param_grads[16], param_grads[17], param_grads[18], masked_rms)
```

```python
import functools
import math

import jax
import jax.numpy as jnp
from jax import lax
from jax.experimental import pallas as pl
from jax.experimental.pallas import tpu as pltpu
from jax.sharding import PartitionSpec as P

HEAD_DIM = 64
LEFT = 64
RIGHT = 8
EPSILON = 1e-05
NEG_FILL = -1e30
BF16 = jnp.bfloat16
F32 = jnp.float32
MESH = pl.DeviceIdType.MESH
BLOCK = 128
WINDOW = 384
SPAN = 512
VMEM_LIMIT = 60 * 1024 * 1024


def matmul(left, right):
    return jnp.dot(left, right, preferred_element_type=F32)


def matmul_nt(left, right):
    return lax.dot_general(left, right, (((1,), (1,)), ((), ())), preferred_element_type=F32)


def matmul_tn(left, right):
    return lax.dot_general(left, right, (((0,), (0,)), ((), ())), preferred_element_type=F32)


def vmem():
    return pl.BlockSpec(memory_space=pltpu.VMEM)


def anywhere():
    return pl.BlockSpec(memory_space=pl.ANY)


def comm_params(collective_id):
    return pltpu.CompilerParams(
        collective_id=collective_id, has_side_effects=True, vmem_limit_bytes=VMEM_LIMIT
    )


def tile(index, size):
    return pl.ds(pl.multiple_of(index * size, size), size)


class Wire:
    def __init__(self, sizes, send_sem, recv_sem, local_sem, side, col_on=True, row_on=False):
        self.n, self.m = sizes
        self.me = lax.axis_index("col")
        self.row = lax.axis_index("row")
        self.send_sem, self.recv_sem, self.local_sem = send_sem, recv_sem, local_sem
        self.used = 0
        self.used_local = 0
        self.core = lax.rem(self.row, 2)
        self.layer = self.row // 2
        self.partner = self.row + 1 - 2 * self.core
        self.layers = self.m // 2
        self.col_on = col_on
        self.row_on = row_on or bool(side)
        self.side = [job(self) for job in side]

    def layer_peer(self, step):
        return lax.rem(self.layer + step, self.layers) * 2 + self.core

    def greet(self):
        barrier = pltpu.get_barrier_semaphore()
        waits = 0
        if self.col_on:
            for step in range(1, self.n):
                pl.semaphore_signal(
                    barrier, inc=1, device_id={"col": lax.rem(self.me + step, self.n)},
                    device_id_type=MESH,
                )
            waits += self.n - 1
        if self.row_on:
            for step in range(1, self.layers):
                pl.semaphore_signal(
                    barrier, inc=1, device_id={"row": self.layer_peer(step)}, device_id_type=MESH
                )
            pl.semaphore_signal(
                barrier, inc=1, device_id={"row": self.partner}, device_id_type=MESH
            )
            waits += self.layers
        pl.semaphore_wait(barrier, waits)

    def remote(self, source, target, axis, peer):
        slot = self.used
        self.used += 1
        return pltpu.make_async_remote_copy(
            src_ref=source, dst_ref=target, send_sem=self.send_sem.at[slot],
            recv_sem=self.recv_sem.at[slot], device_id={axis: peer}, device_id_type=MESH,
        )

    def local(self, source, target):
        slot = self.used_local
        self.used_local += 1
        return pltpu.make_async_copy(source, target, self.local_sem.at[slot])

    def to_all(self, source_of, target):
        copies = [
            self.remote(source_of(lax.rem(self.me + step, self.n)), target, "col",
                        lax.rem(self.me + step, self.n))
            for step in range(1, self.n)
        ]
        for copy in copies:
            copy.start()
        return copies

    def begin(self):
        for job in self.side:
            job.begin()

    def early(self):
        for job in self.side:
            job.early()

    def middle(self):
        for job in self.side:
            job.middle()

    def end(self):
        for job in self.side:
            job.end()

    def peers(self):
        if self.n == 4:
            across = self.me + 1 - 2 * lax.rem(self.me, 2)
            along = lax.rem(self.me + 2, 4)
            return [(across, 0), (along, 1), (3 - self.me, 2)]
        return [
            (lax.rem(self.me + self.n - step, self.n), self.n - step - 1)
            for step in range(1, self.n)
        ]


class Spread:
    def __init__(self, wire, ref, count):
        self.wire, self.ref, self.count = wire, ref, count
        me = wire.me
        if wire.n != 4:
            self.copies = [
                wire.remote(self.part(me), self.part(me), "col", lax.rem(me + step, wire.n))
                for step in range(1, wire.n)
            ]
            return
        (across, _), (along, _), (far, _) = wire.peers()
        self.across = [wire.remote(self.part(me, q), self.part(me, q), "col", across) for q in range(4)]
        self.along = [wire.remote(self.part(me, q), self.part(me, q), "col", along) for q in range(4)]
        self.onward = [
            wire.remote(self.part(across, q), self.part(across, q), "col", along) for q in (0, 1)
        ] + [wire.remote(self.part(along, q), self.part(along, q), "col", across) for q in (2, 3)]

    def part(self, chunk, quarter=None):
        if quarter is None:
            return self.ref.at[tile(chunk, self.count)]
        size = self.count // 4
        return self.ref.at[tile(chunk * 4 + quarter, size)]

    def start(self):
        if self.wire.n != 4:
            for copy in self.copies:
                copy.start()
            return
        for first, second in ((0, 2), (1, 3), (2, 0), (3, 1)):
            self.across[first].start()
            self.along[second].start()

    def relay(self):
        if self.wire.n != 4:
            return
        for turn in range(2):
            self.across[turn].wait_recv()
            self.onward[turn].start()
            self.along[2 + turn].wait_recv()
            self.onward[2 + turn].start()

    def arrivals(self, relay=True):
        wire = self.wire
        yield wire.me, None
        if wire.n != 4:
            for step, (peer, slot) in zip(range(1, wire.n), wire.peers()):
                self.copies[step - 1].wait_recv()
                yield peer, slot
            return
        if relay:
            self.relay()
        for (peer, slot), copies in zip(
            wire.peers(), (self.across[2:], self.along[:2], self.onward)
        ):
            for copy in copies:
                copy.wait_recv()
            yield peer, slot

    def finish(self):
        copies = self.copies if self.wire.n != 4 else self.across + self.along + self.onward
        for copy in copies:
            copy.wait_send()


class Collect:
    def __init__(self, wire, got):
        self.wire, self.got = wire, got
        self.copies = {}
        self.slots = {slot: wire.used + slot for slot in range(wire.n - 1)}
        wire.used += wire.n - 1

    def send(self, source, owner, slot):
        wire = self.wire
        copy = pltpu.make_async_remote_copy(
            src_ref=source, dst_ref=self.got.at[slot], send_sem=wire.send_sem.at[self.slots[slot]],
            recv_sem=wire.recv_sem.at[self.slots[slot]], device_id={"col": owner},
            device_id_type=MESH,
        )
        copy.start()
        self.copies[slot] = copy

    def wait(self):
        for slot in range(self.wire.n - 1):
            self.copies[slot].wait()


class RowGather:
    def __init__(self, shard, full, wire):
        self.wire = wire
        count = shard.shape[0]
        mine = full.at[tile(wire.row, count)]
        self.first = [wire.local(shard, mine), wire.remote(shard, mine, "row", wire.partner)]
        self.along = [
            wire.remote(shard, mine, "row", wire.layer_peer(step))
            for step in range(1, wire.layers)
        ]
        self.onward = []
        for step in range(1, wire.layers):
            block = full.at[tile(wire.layer_peer(wire.layers - step), count)]
            self.onward.append(wire.remote(block, block, "row", wire.partner))

    def begin(self):
        for copy in self.along + self.first:
            copy.start()

    def early(self):
        pass

    def middle(self):
        for copy, onward in zip(self.along, self.onward):
            copy.wait_recv()
            onward.start()

    def end(self):
        for copy in self.along:
            copy.wait_send()
        for copy in self.first:
            copy.wait()
        for copy in self.onward:
            copy.wait()


class RowReduce:
    def __init__(self, grads, out, held, pair, got, wire, load=True):
        self.wire, self.out, self.grads = wire, out, grads
        self.held, self.pair, self.got = held, pair, got
        self.count = held.shape[1]
        other = 1 - wire.core
        self.load = []
        if load:
            self.load = [
                wire.local(grads.at[tile(layer * 2 + wire.core, self.count)], held.at[layer])
                for layer in range(wire.layers)
            ]
        self.swap = [
            wire.remote(grads.at[tile(layer * 2 + other, self.count)], pair.at[layer], "row",
                        wire.partner)
            for layer in range(wire.layers)
        ]
        self.along = []
        for step in range(1, wire.layers):
            layer = lax.rem(wire.layer + step, wire.layers)
            self.along.append(
                wire.remote(held.at[layer], got.at[step - 1], "row", wire.layer_peer(step))
            )

    def begin(self):
        for copy in self.swap + self.load:
            copy.start()

    def early(self):
        for copy in self.load + self.swap:
            copy.wait()
        size = min(32, self.count)
        for layer in range(self.wire.layers):
            def add(rows, index, layer=layer):
                if self.load:
                    mine = self.held[layer, rows]
                else:
                    at = (layer * 2 + self.wire.core) * self.count + index * size
                    mine = self.grads[pl.ds(pl.multiple_of(at, size), size)]
                self.held[layer, rows] = (
                    mine.astype(F32) + self.pair[layer, rows].astype(F32)
                ).astype(BF16)

            row_loop(self.count, add)
        for copy in self.along:
            copy.start()

    def middle(self):
        pass

    def end(self):
        for copy in self.along:
            copy.wait()

        def add(rows, index):
            total = self.held[self.wire.layer, rows].astype(F32)
            for step in range(self.wire.layers - 1):
                total = total + self.got[step, rows].astype(F32)
            self.out[rows] = total

        row_loop(self.count, add)


def reduce_scratch(layers, count, width):
    return [
        pltpu.VMEM((layers, count, width), BF16),
        pltpu.VMEM((layers, count, width), BF16),
        pltpu.VMEM((max(1, layers - 1), count, width), BF16),
    ]


class SumAll:
    def __init__(self, pieces, shared, kept, out, got, got_shared, packed, got_row, wire):
        self.wire, self.out = wire, out
        self.pieces, self.shared, self.kept = pieces, shared, kept
        self.got, self.got_shared, self.packed, self.got_row = got, got_shared, packed, got_row
        self.col = []
        for step in range(1, wire.n):
            peer = lax.rem(wire.me + step, wire.n)
            self.col.append(wire.remote(pieces.at[peer], got.at[step - 1], "col", peer))
            if shared is not None:
                self.col.append(wire.remote(shared, got_shared.at[step - 1], "col", peer))
        self.swap = wire.remote(packed.at[0], got_row.at[0], "row", wire.partner)
        self.along = [
            wire.remote(packed.at[1], got_row.at[step], "row", wire.layer_peer(step))
            for step in range(1, wire.layers)
        ]

    def begin(self):
        for copy in self.col:
            copy.start()

    def early(self):
        for copy in self.col:
            copy.wait()
        packed = self.packed.at[0]
        first = self.pieces.shape[1]
        total = self.pieces[self.wire.me]
        for step in range(self.wire.n - 1):
            total = total + self.got[step]
        packed[0:first] = total
        if self.shared is not None:
            second = first + self.shared.shape[0]
            total = self.shared[...]
            for step in range(self.wire.n - 1):
                total = total + self.got_shared[step]
            packed[first:second] = total
            packed[second:] = self.kept[...]
        self.swap.start()

    def middle(self):
        self.swap.wait()
        self.packed[1] = self.packed[0] + self.got_row[0]
        for copy in self.along:
            copy.start()

    def end(self):
        for copy in self.along:
            copy.wait()
        total = self.packed[1]
        for step in range(1, self.wire.layers):
            total = total + self.got_row[step]
        self.out[...] = total


def sum_scratch(n, layers, first, second, third, width):
    return [
        pltpu.VMEM((n - 1, first, width), F32),
        pltpu.VMEM((n - 1, max(8, second), width), F32),
        pltpu.VMEM((2, first + second + third, width), F32),
        pltpu.VMEM((layers, first + second + third, width), F32),
    ]


def row_loop(count, body):
    size = min(32, count)

    def step(index, carry):
        body(tile(index, size), index)
        return carry

    lax.fori_loop(0, count // size, step, 0)


def block_loop(extent, body):
    size = min(256, extent)

    def step(index, carry):
        body(tile(index, size), index)
        return carry

    lax.fori_loop(0, extent // size, step, 0)


def fold8(values):
    return jnp.sum(values.reshape(values.shape[0] // 8, 8, values.shape[1]), axis=0)


def normalize(values):
    average = jnp.mean(values, axis=1, keepdims=True)
    centered = values - average
    inverse = lax.rsqrt(jnp.mean(centered * centered, axis=1, keepdims=True) + EPSILON)
    return centered * inverse, inverse


def norm_back(grad_in, normed, inverse, gains):
    scaled = grad_in * gains
    first = jnp.mean(scaled, axis=1, keepdims=True)
    second = jnp.mean(scaled * normed, axis=1, keepdims=True)
    return inverse * (scaled - first - normed * second)


def comm_call(name, collective_id, sizes, main, ins, outs, scratch, gathers=(), reduces=(), cost=10**9,
              col_on=True, more_slots=0, row_on=False):
    n, m = sizes
    layers = m // 2
    in_arrays = [item[0] for item in ins] + list(gathers) + list(reduces)
    in_specs = [item[1] for item in ins] + [vmem()] * len(gathers) + [anywhere()] * len(reduces)
    out_shapes = [jax.ShapeDtypeStruct(item[0], item[1]) for item in outs]
    out_specs = [item[2] for item in outs]
    for shard in gathers:
        out_shapes.append(jax.ShapeDtypeStruct((m * shard.shape[0], shard.shape[1]), shard.dtype))
        out_specs.append(anywhere())
    side_scratch = []
    for grads in reduces:
        count, width = grads.shape[0] // m, grads.shape[1]
        out_shapes.append(jax.ShapeDtypeStruct((count, width), F32))
        out_specs.append(vmem())
        side_scratch += reduce_scratch(layers, count, width)
    remote_slots = 8 * n + 16 + len(gathers) * 2 * layers + len(reduces) * 2 * layers + more_slots
    local_slots = 8 + len(gathers) + len(reduces) * layers + more_slots

    def kernel(*refs):
        at = 0

        def take(count):
            nonlocal at
            at += count
            return refs[at - count:at]

        main_ins = take(len(ins))
        gather_ins = take(len(gathers))
        reduce_ins = take(len(reduces))
        main_outs = take(len(outs))
        gather_outs = take(len(gathers))
        reduce_outs = take(len(reduces))
        main_scratch = take(len(scratch))
        side = [
            functools.partial(RowGather, shard, full)
            for shard, full in zip(gather_ins, gather_outs)
        ]
        for grads, out in zip(reduce_ins, reduce_outs):
            side.append(functools.partial(RowReduce, grads, out, *take(3)))
        send_sem, recv_sem, local_sem = take(3)
        wire = Wire(sizes, send_sem, recv_sem, local_sem, side, col_on, row_on)
        main(wire, main_ins, main_outs, main_scratch)

    return pl.pallas_call(
        kernel,
        name=name,
        out_shape=tuple(out_shapes),
        in_specs=in_specs,
        out_specs=tuple(out_specs),
        scratch_shapes=list(scratch) + side_scratch + [
            pltpu.SemaphoreType.DMA((remote_slots,)),
            pltpu.SemaphoreType.DMA((remote_slots,)),
            pltpu.SemaphoreType.DMA((local_slots,)),
        ],
        compiler_params=comm_params(collective_id),
        cost_estimate=pl.CostEstimate(flops=cost, bytes_accessed=10**8, transcendentals=0),
    )(*in_arrays)


def norm_rows(wire, count, source, gains, rows_ref):
    base = wire.me * count

    def work(rows, index):
        normed, _ = normalize(source[rows])
        size = min(32, count)
        rows_ref[pl.ds(pl.multiple_of(base + index * size, size), size)] = (normed * gains).astype(BF16)

    row_loop(count, work)


def cast_rows(wire, count, source, factor, rows_ref):
    base = wire.me * count

    def work(rows, index):
        size = min(32, count)
        rows_ref[pl.ds(pl.multiple_of(base + index * size, size), size)] = (
            factor * source[rows]
        ).astype(BF16)

    row_loop(count, work)


def owner_sum(wire, rows, part, got):
    total = part[rows].astype(F32)
    for slot in range(wire.n - 1):
        total = total + got[slot, rows].astype(F32)
    return total


def residual(wire, count, factor, part, got, resid, keep_ref, after_ref, squares_ref):
    squares_ref[...] = jnp.zeros_like(squares_ref)

    def work(rows, index):
        branch = owner_sum(wire, rows, part, got)
        after = resid[rows] + factor * branch
        after_ref[rows] = after
        keep = keep_ref[rows]
        squares_ref[0:8] += fold8(branch * branch * keep)
        squares_ref[8:16] += fold8(after * after * keep)

    row_loop(count, work)


def residual_back(wire, count, part, got, grad_ref, resid, gains, new_grad_ref, gain_grad_ref):
    gain_grad_ref[...] = jnp.zeros_like(gain_grad_ref)

    def work(rows, index):
        rows_grad = owner_sum(wire, rows, part, got)
        normed, inverse = normalize(resid[rows])
        new_grad_ref[rows] = grad_ref[rows] + norm_back(rows_grad, normed, inverse, gains)
        gain_grad_ref[...] += fold8(rows_grad * normed)

    row_loop(count, work)


def send_pieces(wire, count, source, pieces, out_ref):
    width = pieces.shape[2]

    def split(rows, index):
        result = source[rows].astype(BF16)
        for part in range(wire.n):
            pieces[part, rows] = result[:, part * width:(part + 1) * width]

    row_loop(count, split)
    mine = out_ref.at[tile(wire.me, count)]
    copies = wire.to_all(lambda peer: pieces.at[peer], mine)
    here = wire.local(pieces.at[wire.me], mine)
    here.start()
    return copies + [here]


def feed_forward_first(count, chunk, rows_ref, up, pre_ref, act):
    rows = tile(chunk, count)
    left = rows_ref[rows]

    def first(cols, index):
        pre = matmul(left, up[:, cols])
        pre_ref[rows, cols] = pre.astype(BF16)
        act[:, cols] = (pre * jax.nn.sigmoid(pre)).astype(BF16)

    block_loop(up.shape[1], first)


def feed_forward_second(act, down_t, target):
    hidden = act[...]

    def second(cols, index):
        target[:, cols] = matmul_nt(hidden, down_t[cols]).astype(BF16)

    block_loop(down_t.shape[0], second)


def feed_forward_main(count, gain_row, factor, enter, turn, wire, ins, outs, scratch):
    ins, outs, scratch = list(ins), list(outs), list(scratch)
    if enter:
        tokens_ref, cot_in, gain_in, keep_ref = ins[:4]
        ins = ins[4:]
        resid, cot_out, gains_ref = outs[:3]
        outs = outs[3:]
        arrived, arrived_cot, arrived_gain = scratch[:3]
        scratch = scratch[3:]
    else:
        resid, keep_ref, gains_ref = ins[:3]
        ins = ins[3:]
    if enter:
        up_shard, down_shard, next_shard = ins[:3]
        ins = ins[3:]
        up_full, down_full, next_full = outs[:3]
        outs = outs[3:]
        up, down_t = scratch[:2]
        scratch = scratch[2:]
    else:
        up, down_t = ins[:2]
        ins = ins[2:]
    if turn:
        (cot_ref,) = ins
        grad_ref, gain_grad_ref, out_ref = outs[:3]
        outs = outs[3:]
        (pieces,) = scratch[:1]
        scratch = scratch[1:]
    after_ref, squares_ref, rows_ref, pre_ref = outs
    act, part, got = scratch
    wire.greet()
    wire.begin()
    if enter:
        up_job = RowGather(up_shard, up_full, wire)
        down_job = RowGather(down_shard, down_full, wire)
        next_job = RowGather(next_shard, next_full, wire)
        up_job.begin()
        width = arrived.shape[2]
        mine = [
            wire.local(tokens_ref.at[tile(wire.me, count)], arrived.at[wire.me]),
            wire.local(gain_in, arrived_gain.at[wire.me]),
            wire.local(cot_in.at[tile(wire.me, count)], arrived_cot.at[wire.me]),
        ]
        copies = wire.to_all(lambda peer: tokens_ref.at[tile(peer, count)], arrived.at[wire.me])
        copies += wire.to_all(lambda peer: gain_in, arrived_gain.at[wire.me])
        for copy in mine:
            copy.start()
        for copy in mine + copies:
            copy.wait()
        for piece in range(wire.n):
            gains_ref[:, piece * width:(piece + 1) * width] = arrived_gain[piece]

        def place(rows, index):
            for piece in range(wire.n):
                resid[rows, piece * width:(piece + 1) * width] = arrived[piece, rows].astype(F32)

        row_loop(count, place)
    gains = gains_ref[gain_row:gain_row + 1]
    norm_rows(wire, count, resid, gains, rows_ref)
    spread = Spread(wire, rows_ref, count)
    spread.start()
    collect = Collect(wire, got)
    cot_copies = []
    if enter:
        cot_copies = wire.to_all(
            lambda peer: cot_in.at[tile(peer, count)], arrived_cot.at[wire.me]
        )
    wire.early()
    if enter:
        spread.relay()
        up_job.middle()
        down_job.begin()
        up_job.end()
        load = wire.local(up_full, up)
        load.start()
        load.wait()
        chunks = []
        for chunk, slot in spread.arrivals(relay=False):
            chunks.append((chunk, slot))
            feed_forward_first(count, chunk, rows_ref, up, pre_ref, act.at[len(chunks) - 1])
        for copy in cot_copies:
            copy.wait()

        def place_cot(rows, index):
            for piece in range(wire.n):
                cot_out[rows, piece * width:(piece + 1) * width] = arrived_cot[piece, rows].astype(F32)

        row_loop(count, place_cot)
        down_job.middle()
        next_job.begin()
        down_job.end()
        load = wire.local(down_full, down_t)
        load.start()
        load.wait()
        for place, (chunk, slot) in reversed(list(enumerate(chunks))):
            target = part.at[wire.n - 1 if slot is None else slot]
            feed_forward_second(act.at[place], down_t, target)
            if slot is not None:
                collect.send(target, chunk, slot)
        next_job.middle()
    else:
        for chunk, slot in spread.arrivals():
            target = part.at[wire.n - 1 if slot is None else slot]
            feed_forward_first(count, chunk, rows_ref, up, pre_ref, act.at[0])
            feed_forward_second(act.at[0], down_t, target)
            if slot is not None:
                collect.send(target, chunk, slot)
    wire.middle()
    collect.wait()
    own = part.at[wire.n - 1]
    residual(wire, count, factor, own, got, resid, keep_ref, after_ref, squares_ref)
    late = []
    if turn:
        final_gains = gains_ref[gain_row + 1:gain_row + 2]
        gain_grad_ref[...] = jnp.zeros_like(gain_grad_ref)

        def final(rows, index):
            normed, inverse = normalize(after_ref[rows])
            cot = cot_ref[rows]
            grad_ref[rows] = norm_back(cot, normed, inverse, final_gains)
            gain_grad_ref[...] += fold8(cot * normed)
            after_ref[rows] = normed * final_gains

        row_loop(count, final)
        late = send_pieces(wire, count, after_ref, pieces, out_ref)
    spread.finish()
    for copy in late:
        copy.wait()
    if enter:
        next_job.end()
    wire.end()


def feed_forward(sizes, name, collective_id, gain_row, up, down_t, keep, resid=None, gains=None,
                 enter=None, turn=None, **side):
    n, m = sizes
    hidden = up.shape[1]
    full = up.shape[0] * (m if enter else 1)
    if enter:
        tokens, cotangent, gain_stack, next_shard = enter
        width = tokens.shape[1]
        count = tokens.shape[0] // n
        ins = [(tokens, vmem()), (cotangent, vmem()), (gain_stack, vmem()), (keep, vmem())]
        outs = [((count, full), F32, vmem()), ((count, full), F32, vmem()), ((8, full), F32, vmem())]
        scratch = [
            pltpu.VMEM((n, count, width), BF16),
            pltpu.VMEM((n, count, width), BF16),
            pltpu.VMEM((n, 8, width), F32),
            pltpu.VMEM((full, hidden), BF16),
            pltpu.VMEM((full, hidden), BF16),
        ]
        ins += [(up, vmem()), (down_t, vmem()), (next_shard, vmem())]
        for shard in (up, down_t, next_shard):
            outs.append(((m * shard.shape[0], shard.shape[1]), BF16, anywhere()))
        side = dict(side, more_slots=6 * m, row_on=True)
    else:
        count = resid.shape[0]
        ins = [(resid, vmem()), (keep, vmem()), (gains, vmem())]
        outs, scratch = [], []
        ins += [(up, vmem()), (down_t, vmem())]
    if turn is not None:
        ins.append((turn, vmem()))
        outs += [
            ((count, full), F32, vmem()),
            ((8, full), F32, vmem()),
            ((n * count, full // n), BF16, anywhere()),
        ]
        scratch.append(pltpu.VMEM((n, count, full // n), BF16))
    outs += [
        ((count, full), F32, vmem()),
        ((16, full), F32, vmem()),
        ((n * count, full), BF16, vmem()),
        ((n * count, hidden), BF16, vmem()),
    ]
    scratch += [
        pltpu.VMEM((n if enter else 1, count, hidden), BF16),
        pltpu.VMEM((n, count, full), BF16),
        pltpu.VMEM((n - 1, count, full), BF16),
    ]
    return comm_call(
        name, collective_id, sizes,
        functools.partial(feed_forward_main, count, gain_row, 0.5, bool(enter), turn is not None),
        ins, outs, scratch, **side,
    )


def feed_forward_back_main(count, gain_row, leave, wire, ins, outs, scratch):
    grad_ref, resid, gains_ref, up, down_t, rows_ref, pre_ref = ins[:7]
    grads, pre_grad, act, part, got = scratch[:5]
    scratch = scratch[5:]
    if leave:
        gain_sum_ref, up_out, down_out, last_ref, sum_out = outs
        gain_grad_ref, up_grad_ref, down_grad_ref = scratch[:3]
        up_job = RowReduce(up_grad_ref, up_out, *scratch[3:6], wire, load=False)
        down_job = RowReduce(down_grad_ref, down_out, *scratch[6:9], wire, load=False)
        sums = SumAll(*ins[7:10], sum_out, *scratch[9:13], wire)
        gain_pieces = scratch[13]
        gain_sums = SumAll(gain_pieces, None, None, gain_sum_ref, *scratch[14:18], wire)
        new_grad_ref, pieces = scratch[18:]
    else:
        gain_grad_ref, up_grad_ref, down_grad_ref, last_ref = outs
        new_grad_ref = last_ref
    gains = gains_ref[gain_row:gain_row + 1]
    wire.greet()
    wire.begin()
    cast_rows(wire, count, grad_ref, 0.5, grads)
    spread = Spread(wire, grads, count)
    spread.start()
    collect = Collect(wire, got)
    if leave:
        sums.begin()
    hidden = up.shape[1]

    def activate(rows, cols):
        pre = pre_ref[rows, cols].astype(F32)
        act[rows, cols] = (pre * jax.nn.sigmoid(pre)).astype(BF16)

    for chunk, slot in spread.arrivals():
        rows = tile(chunk, count)
        target = part.at[wire.n - 1 if slot is None else slot]
        left = grads[rows]

        def first(cols, index):
            act_grad = matmul(left, down_t[:, cols])
            pre = pre_ref[rows, cols].astype(F32)
            sig = jax.nn.sigmoid(pre)
            act[rows, cols] = (pre * sig).astype(BF16)
            pre_grad[rows, cols] = (act_grad * (sig + pre * sig * (1.0 - sig))).astype(BF16)

        block_loop(hidden, first)
        through = pre_grad[rows]

        def second(cols, index):
            target[:, cols] = matmul_nt(through, up[cols]).astype(BF16)

        block_loop(up.shape[0], second)
        if slot is not None:
            collect.send(target, chunk, slot)
        if slot is None:
            wire.early()
            if leave:
                sums.early()
    wire.middle()
    if leave:
        sums.middle()
    size = min(256, hidden)

    def weight_grad(left_ref, right_ref, out):
        for start in range(0, hidden, size):
            cols = slice(start, start + size)

            def block(rows, index):
                out[rows, cols] = matmul_tn(left_ref[:, rows], right_ref[:, cols]).astype(BF16)

            block_loop(up.shape[0], block)

    weight_grad(grads, act, down_grad_ref)
    if leave:
        down_job.begin()
    weight_grad(rows_ref, pre_grad, up_grad_ref)
    if leave:
        up_job.begin()
        down_job.early()
    collect.wait()
    own = part.at[wire.n - 1]
    residual_back(wire, count, own, got, grad_ref, resid, gains, new_grad_ref, gain_grad_ref)
    if leave:
        late = send_pieces(wire, count, new_grad_ref, pieces, last_ref)
        width = gain_pieces.shape[2]
        for piece in range(wire.n):
            gain_pieces[piece] = gain_grad_ref[:, piece * width:(piece + 1) * width]
        gain_sums.begin()
        up_job.early()
        gain_sums.early()
        for copy in late:
            copy.wait()
        gain_sums.middle()
        sums.end()
        down_job.end()
        gain_sums.end()
        up_job.end()
    spread.finish()
    wire.end()


def feed_forward_back(sizes, name, collective_id, gain_row, grad, resid, gains, up, down_t, rows, pre,
                      leave=None, **side):
    n, m = sizes
    full, hidden = up.shape
    count = resid.shape[0]
    ins = [(item, vmem()) for item in (grad, resid, gains, up, down_t, rows, pre)]
    scratch = [
        pltpu.VMEM((n * count, full), BF16),
        pltpu.VMEM((n * count, hidden), BF16),
        pltpu.VMEM((n * count, hidden), BF16),
        pltpu.VMEM((n, count, full), BF16),
        pltpu.VMEM((n - 1, count, full), BF16),
    ]
    if leave:
        width, layers = full // n, m // 2
        heights = [leave[0].shape[1], leave[1].shape[0], leave[2].shape[0]]
        ins += [(item, vmem()) for item in leave]
        outs = [
            ((8, width), F32, vmem()),
            ((full // m, hidden), F32, vmem()),
            ((full // m, hidden), F32, vmem()),
            ((n * count, width), BF16, anywhere()),
            ((sum(heights), width), F32, vmem()),
        ]
        scratch += [
            pltpu.VMEM((8, full), F32),
            pltpu.VMEM((full, hidden), BF16),
            pltpu.VMEM((full, hidden), BF16),
        ]
        scratch += 2 * reduce_scratch(layers, full // m, hidden)
        scratch += sum_scratch(n, layers, *heights, width)
        scratch += [pltpu.VMEM((n, 8, width), F32)]
        scratch += sum_scratch(n, layers, 8, 0, 0, width)
        scratch += [pltpu.VMEM((count, full), F32), pltpu.VMEM((n, count, width), BF16)]
        side = dict(side, more_slots=8 * m + 8 * n, row_on=True)
    else:
        outs = [
            ((8, full), F32, vmem()),
            ((full, hidden), BF16, vmem()),
            ((full, hidden), BF16, vmem()),
            ((count, full), F32, vmem()),
        ]
    return comm_call(
        name, collective_id, sizes,
        functools.partial(feed_forward_back_main, count, gain_row, bool(leave)),
        ins, outs, scratch, **side,
    )


def extend_table(table):
    slots = jnp.arange(SPAN)
    signed = jnp.where(slots < SPAN - BLOCK + 1, slots, slots - SPAN)
    row_of = jnp.clip(signed - (BLOCK - LEFT), 0, LEFT + RIGHT)
    chosen = (row_of[:, None] == jnp.arange(LEFT + RIGHT + 1)[None, :]).astype(table.dtype)
    return jnp.dot(chosen, table, preferred_element_type=F32).astype(table.dtype)


def fold_table(extended):
    slots = jnp.arange(SPAN)
    signed = jnp.where(slots < SPAN - BLOCK + 1, slots, slots - SPAN)
    row_of = jnp.clip(signed - (BLOCK - LEFT), 0, LEFT + RIGHT)
    ends = jnp.repeat(jnp.asarray([0, LEFT + RIGHT]), 8)
    row_of = jnp.concatenate([row_of, ends])
    chosen = (jnp.arange(LEFT + RIGHT + 1)[:, None] == row_of[None, :]).astype(F32)
    return jnp.dot(chosen, extended, precision=lax.Precision.HIGHEST)


def column_facts(at, length, limit):
    column = lax.broadcasted_iota(jnp.int32, (1, length), 1)
    place = column + (at - BLOCK)
    key = jnp.where(place < 0, place + length, jnp.where(place >= length, place - length, place))
    return column, place, key, key < limit


def position_terms(query, table_ref, at, length):
    terms = matmul_nt(query, table_ref[...])
    rolled = pltpu.roll(terms, 0, 1, stride=1, stride_axis=0)
    column, place, key, _ = column_facts(at, length, length)
    far_left, far_right = terms[:, 0:1], terms[:, SPAN - 2 * BLOCK:SPAN - 2 * BLOCK + 1]
    far = jnp.where(key < at, far_left, far_right)
    near = jnp.where((place[:, :WINDOW] >= 0) & (place[:, :WINDOW] < length), rolled[:, :WINDOW],
                     far[:, :WINDOW])
    return jnp.concatenate([near, far[:, WINDOW:]], axis=1)


def head_mask(group, head, rows):
    if group == HEAD_DIM:
        return None
    lane = lax.broadcasted_iota(jnp.int32, (rows, group), 1)
    return (lane >= head * HEAD_DIM) & (lane < (head + 1) * HEAD_DIM)


def masked(mask, values):
    return values if mask is None else jnp.where(mask, values, jnp.zeros_like(values))


def lanes(start, size):
    return pl.ds(start, size)


def duplicate(qkv_ref, width, group, keys, values):
    length = qkv_ref.shape[0]
    for part in range(width // group):
        base = part * group
        for copy in range(2):
            place = slice(copy * length, (copy + 1) * length)
            keys[part, place] = qkv_ref[:, lanes(width + base, group)]
            values[part, place] = qkv_ref[:, lanes(2 * width + base, group)]


def attend_blocks(first, blocks, width, group, limit, qkv_ref, table_ref, keys, values, context_ref,
                  log_ref):
    length = qkv_ref.shape[0]
    heads = group // HEAD_DIM
    scale = 1.0 / math.sqrt(HEAD_DIM)

    def block(index, carry):
        at = pl.multiple_of((first + index) * BLOCK, BLOCK)
        rows = pl.ds(at, BLOCK)
        from_row = pl.multiple_of(lax.rem(at + length - BLOCK, length), BLOCK)
        _, _, _, allowed = column_facts(at, length, limit)
        for part in range(width // group):
            base = part * group
            key_rows = keys[part, pl.ds(from_row, length)]
            value_rows = values[part, pl.ds(from_row, length)]
            query_rows = qkv_ref[rows, lanes(base, group)] * jnp.asarray(scale, BF16)
            result = None
            for head in range(heads):
                mask = head_mask(group, head, BLOCK)
                query = masked(mask, query_rows)
                scores = matmul_nt(query, key_rows) + position_terms(query, table_ref, at, length)
                scores = jnp.where(allowed, scores, NEG_FILL)
                peak = jnp.max(scores, axis=1, keepdims=True)
                weights = jnp.exp(scores - peak)
                total = jnp.sum(weights, axis=1, keepdims=True)
                piece = matmul(weights.astype(BF16), value_rows) * (1.0 / total)
                result = piece if result is None else jnp.where(mask, piece, result)
                slot = part * heads + head
                log_ref[rows, slot:slot + 1] = peak + jnp.log(total)
            context_ref[rows, lanes(base, group)] = result.astype(BF16)
        return carry

    lax.fori_loop(0, blocks, block, 0)


def attention_main(count, gain_row, wire, ins, outs, scratch):
    limit_ref, resid, keep_ref, gains_ref, weights, table_ref = ins
    after_ref, squares_ref, rows_ref, qkv_ref, context_ref, log_ref = outs
    keys, values, part, got = scratch
    width = context_ref.shape[1]
    group = keys.shape[2]
    wire.greet()
    wire.begin()
    norm_rows(wire, count, resid, gains_ref[gain_row:gain_row + 1], rows_ref)
    spread = Spread(wire, rows_ref, count)
    spread.start()
    collect = Collect(wire, got)
    spread.relay()
    wire.early()
    chunks = []
    for chunk, slot in spread.arrivals(relay=False):
        chunks.append((chunk, slot))
        rows = tile(chunk, count)
        left = rows_ref[rows]

        def project(cols, index):
            qkv_ref[rows, cols] = matmul(left, weights[:, cols]).astype(BF16)

        block_loop(3 * width, project)
    wire.middle()
    duplicate(qkv_ref, width, group, keys, values)
    limit = limit_ref[0]
    size = max(count, BLOCK)
    for chunk, slot in reversed(chunks):
        first = chunk * count // BLOCK
        attend_blocks(first, size // BLOCK, width, group, limit, qkv_ref, table_ref, keys, values,
                      context_ref, log_ref)
        target = part.at[wire.n - 1 if slot is None else slot]
        left = context_ref[tile(chunk, count)]

        def leave(cols, index):
            target[:, cols] = matmul_nt(left, weights[cols, 3 * width:]).astype(BF16)

        block_loop(weights.shape[0], leave)
        if slot is not None:
            collect.send(target, chunk, slot)
    collect.wait()
    residual(wire, count, 1.0, part.at[wire.n - 1], got, resid, keep_ref, after_ref, squares_ref)
    spread.finish()
    wire.end()


def attention(sizes, name, collective_id, gain_row, limit, resid, keep, gains, weights, table, **side):
    n, m = sizes
    count, full = resid.shape
    length, width = n * count, weights.shape[1] // 4
    group = min(2 * HEAD_DIM, width)
    return comm_call(
        name, collective_id, sizes, functools.partial(attention_main, count, gain_row),
        [(limit, pl.BlockSpec(memory_space=pltpu.SMEM))]
        + [(item, vmem()) for item in (resid, keep, gains, weights, table)],
        [
            ((count, full), F32, vmem()),
            ((16, full), F32, vmem()),
            ((length, full), BF16, vmem()),
            ((length, 3 * width), BF16, vmem()),
            ((length, width), BF16, vmem()),
            ((length, max(8, width // HEAD_DIM)), F32, vmem()),
        ],
        [
            pltpu.VMEM((width // group, 2 * length, group), BF16),
            pltpu.VMEM((width // group, 2 * length, group), BF16),
            pltpu.VMEM((n, count, full), BF16),
            pltpu.VMEM((n - 1, count, full), BF16),
        ],
        cost=20 * 10**9, **side,
    )


def attend_back_core(width, group, limit, qkv_ref, table_ref, log_ref, grad_ref, out_ref,
                     table_grad_ref, keys, values, key_grad, value_grad):
    length = qkv_ref.shape[0]
    heads = group // HEAD_DIM
    scale = 1.0 / math.sqrt(HEAD_DIM)
    duplicate(qkv_ref, width, group, keys, values)
    table_grad_ref[...] = jnp.zeros_like(table_grad_ref)
    down = lax.broadcasted_iota(jnp.int32, (BLOCK, BLOCK), 0)
    across = lax.broadcasted_iota(jnp.int32, (BLOCK, BLOCK), 1)
    reverse = jnp.where(down + across == BLOCK - 1, 1.0, 0.0).astype(BF16)
    first_row = table_ref[0:1].astype(F32)
    last_row = table_ref[SPAN - 2 * BLOCK:SPAN - 2 * BLOCK + 1].astype(F32)
    for part in range(width // group):
        base = part * group
        key_grad[...] = jnp.zeros_like(key_grad)
        value_grad[...] = jnp.zeros_like(value_grad)

        def block(index, carry, base=base, part=part):
            at = pl.multiple_of(index * BLOCK, BLOCK)
            rows = pl.ds(at, BLOCK)
            from_row = pl.multiple_of(lax.rem(at + length - BLOCK, length), BLOCK)
            window = pl.ds(from_row, length)
            key_rows = keys[part, window]
            value_rows = values[part, window]
            query_rows = qkv_ref[rows, lanes(base, group)] * jnp.asarray(scale, BF16)
            grad_rows = grad_ref[rows, lanes(base, group)]
            column, place, key, allowed = column_facts(at, length, limit)
            near = (place[:, :WINDOW] >= 0) & (place[:, :WINDOW] < length)
            is_left = key < at
            result = None
            for head in range(heads):
                mask = head_mask(group, head, BLOCK)
                query = masked(mask, query_rows)
                grad = masked(mask, grad_rows)
                slot = part * heads + head
                scores = matmul_nt(query, key_rows) + position_terms(query, table_ref, at, length)
                scores = jnp.where(allowed, scores, NEG_FILL)
                probs = jnp.exp(scores - log_ref[rows, slot:slot + 1])
                prob_grad = matmul_nt(grad, value_rows)
                row_dot = jnp.sum(probs * prob_grad, axis=1, keepdims=True)
                score_grad = (probs * (prob_grad - row_dot)).astype(BF16)
                value_grad[window] += matmul_tn(probs.astype(BF16), grad)
                key_grad[window] += matmul_tn(score_grad, query)
                wide = score_grad.astype(F32)
                near_grad = jnp.where(near, score_grad[:, :WINDOW], jnp.asarray(0.0, BF16))
                far_grad = jnp.concatenate(
                    [jnp.where(near, 0.0, wide[:, :WINDOW]), wide[:, WINDOW:]], axis=1
                )
                left_sum = jnp.sum(jnp.where(is_left, far_grad, 0.0), axis=1, keepdims=True)
                right_sum = jnp.sum(jnp.where(is_left, 0.0, far_grad), axis=1, keepdims=True)
                turned = jnp.concatenate(
                    [matmul(reverse, near_grad), jnp.zeros((BLOCK, SPAN - WINDOW), F32)], axis=1
                )
                turned = pltpu.roll(
                    turned, SPAN - (BLOCK - 1), 1, stride=1, stride_axis=0
                ).astype(BF16)
                near_term = matmul(turned, table_ref[...])
                high = near_term.astype(BF16)
                low = (near_term - high.astype(F32)).astype(BF16)
                far_term = left_sum * first_row + right_sum * last_row
                piece = (
                    matmul(score_grad, key_rows) + matmul(reverse, high) + matmul(reverse, low)
                    + far_term
                ) * scale
                result = piece if result is None else jnp.where(mask, piece, result)
                table_grad_ref[0:SPAN] += matmul_tn(turned, matmul(reverse, query).astype(BF16))
                query_wide = query.astype(F32)
                table_grad_ref[SPAN:SPAN + 8] += fold8(left_sum * query_wide)
                table_grad_ref[SPAN + 8:SPAN + 16] += fold8(right_sum * query_wide)
            out_ref[rows, lanes(base, group)] = result.astype(BF16)
            return carry

        lax.fori_loop(0, length // BLOCK, block, 0)
        out_ref[:, lanes(width + base, group)] = (
            key_grad[0:length] + key_grad[length:2 * length]
        ).astype(BF16)
        out_ref[:, lanes(2 * width + base, group)] = (
            value_grad[0:length] + value_grad[length:2 * length]
        ).astype(BF16)


def attention_back_main(count, gain_row, wire, ins, outs, scratch):
    limit_ref, grad_ref, resid, gains_ref, weights, table_ref, rows_ref, qkv_ref, context_ref, log_ref = ins
    gain_grad_ref, wide_ref, table_grad_ref, new_grad_ref = outs
    grads, context_grad, qkv_grad, keys, values, key_grad, value_grad, part, got = scratch
    width = context_ref.shape[1]
    group = keys.shape[2]
    wire.greet()
    wire.begin()
    cast_rows(wire, count, grad_ref, 1.0, grads)
    spread = Spread(wire, grads, count)
    spread.start()
    collect = Collect(wire, got)
    spread.relay()
    wire.early()
    chunks = []
    for chunk, slot in spread.arrivals(relay=False):
        chunks.append((chunk, slot))
        rows = tile(chunk, count)
        context_grad[rows] = matmul(grads[rows], weights[:, 3 * width:]).astype(BF16)
    wire.middle()
    attend_back_core(width, group, limit_ref[0], qkv_ref, table_ref, log_ref, context_grad, qkv_grad,
                     table_grad_ref, keys, values, key_grad, value_grad)
    for chunk, slot in reversed(chunks):
        target = part.at[wire.n - 1 if slot is None else slot]
        left = qkv_grad[tile(chunk, count)]

        def back(cols, index):
            target[:, cols] = matmul_nt(left, weights[cols, :3 * width]).astype(BF16)

        block_loop(weights.shape[0], back)
        if slot is not None:
            collect.send(target, chunk, slot)

    def weight_grads(rows, index):
        wide_ref[rows, :3 * width] = matmul_tn(rows_ref[:, rows], qkv_grad[...]).astype(BF16)
        wide_ref[rows, 3 * width:] = matmul_tn(grads[:, rows], context_ref[...]).astype(BF16)

    block_loop(weights.shape[0], weight_grads)
    collect.wait()
    residual_back(wire, count, part.at[wire.n - 1], got, grad_ref, resid,
                  gains_ref[gain_row:gain_row + 1], new_grad_ref, gain_grad_ref)
    spread.finish()
    wire.end()


def attention_back(sizes, name, collective_id, gain_row, limit, grad, resid, gains, weights, table, rows,
                   qkv, context, log_total, **side):
    n, m = sizes
    count, full = resid.shape
    length, width = context.shape
    group = min(2 * HEAD_DIM, width)
    return comm_call(
        name, collective_id, sizes, functools.partial(attention_back_main, count, gain_row),
        [(limit, pl.BlockSpec(memory_space=pltpu.SMEM))]
        + [(item, vmem()) for item in (grad, resid, gains, weights, table, rows, qkv, context, log_total)],
        [
            ((8, full), F32, vmem()),
            ((full, 4 * width), BF16, vmem()),
            ((SPAN + 16, group), F32, vmem()),
            ((count, full), F32, vmem()),
        ],
        [
            pltpu.VMEM((length, full), BF16),
            pltpu.VMEM((length, width), BF16),
            pltpu.VMEM((length, 3 * width), BF16),
            pltpu.VMEM((width // group, 2 * length, group), BF16),
            pltpu.VMEM((width // group, 2 * length, group), BF16),
            pltpu.VMEM((2 * length, group), F32),
            pltpu.VMEM((2 * length, group), F32),
            pltpu.VMEM((n, count, full), BF16),
            pltpu.VMEM((n - 1, count, full), BF16),
        ],
        cost=50 * 10**9, **side,
    )


PAD = 32
ROWS = 64


def shifted_sets(held, low, high, size):
    for residue in range(8):
        shifts = [shift for shift in range(low, high + 1) if shift % 8 == residue]
        if shifts:
            extent = shifts[-1] - residue + size
            moved = held[residue:residue + extent]
            for shift in shifts:
                yield shift, moved[shift - residue:shift - residue + size]


def stat_rows(blocks, first, second, stats_ref):
    lane = lax.broadcasted_iota(jnp.int32, (BLOCK, BLOCK), 1)
    both = jnp.where(lane == 0, first, jnp.where(lane == 1, second, 0.0))
    stats_ref[:, blocks] = both.T[0:8]


def stat_columns(stats):
    both = jnp.concatenate([stats, jnp.zeros((BLOCK - 8, BLOCK), F32)], axis=0).T
    return both[:, 0:1], both[:, 1:2]


class Stats:
    def __init__(self, wire, mine, got):
        self.wire, self.mine, self.got = wire, mine, got
        self.copies = [
            wire.remote(mine, got.at[step - 1], "col", lax.rem(wire.me + step, wire.n))
            for step in range(1, wire.n)
        ]

    def total(self):
        for copy in self.copies:
            copy.start()
        for copy in self.copies:
            copy.wait()
        total = self.mine[...]
        for step in range(self.wire.n - 1):
            total = total + self.got[step]
        return total


def token_blocks(length, body):
    def step(index, carry):
        body(tile(index, BLOCK), index)
        return carry

    lax.fori_loop(0, length // BLOCK, step, 0)


def convolution_main(count, gain_row, taps, wire, ins, outs, scratch):
    resid, keep_ref, keep_all, gains_ref, weights, kernel_ref, depth_ref = ins
    after_ref, squares_ref, rows_ref, pre_ref, mixed_ref, stats_ref = outs
    padded, stats_mine, stats_got, act, part, got = scratch
    length, width = mixed_ref.shape
    full = gains_ref.shape[1]
    wire.greet()
    wire.begin()
    norm_rows(wire, count, resid, gains_ref[gain_row:gain_row + 1], rows_ref)
    spread = Spread(wire, rows_ref, count)
    spread.start()
    collect = Collect(wire, got)
    stats = Stats(wire, stats_mine, stats_got)
    padded[0:PAD] = jnp.zeros((PAD, width), F32)
    spread.relay()
    wire.early()
    chunks = []
    for chunk, slot in spread.arrivals(relay=False):
        chunks.append((chunk, slot))
        rows = tile(chunk, count)
        left = rows_ref[rows]
        value_pre = matmul(left, weights[:, 0:width])
        gate_pre = matmul(left, weights[:, width:2 * width])
        pre_ref[rows, 0:width] = value_pre.astype(BF16)
        pre_ref[rows, width:2 * width] = gate_pre.astype(BF16)
        at = pl.multiple_of(chunk * count + PAD, PAD)
        padded[pl.ds(at, count)] = value_pre * jax.nn.sigmoid(gate_pre) * keep_all[rows]
    wire.middle()

    def mix(index, carry):
        held = padded[pl.ds(pl.multiple_of(index * ROWS, ROWS), ROWS + PAD)]
        total = jnp.zeros((ROWS, width), F32)
        for shift, moved in shifted_sets(held, PAD - taps + 1, PAD, ROWS):
            tap = shift - (PAD - taps + 1)
            total = total + moved * kernel_ref[tap:tap + 1]
        mixed_ref[tile(index, ROWS)] = total
        return carry

    lax.fori_loop(0, length // ROWS, mix, 0)

    def sums(rows, index):
        mixed = mixed_ref[rows]
        stat_rows(rows, jnp.sum(mixed, axis=1, keepdims=True),
                  jnp.sum(mixed * mixed, axis=1, keepdims=True), stats_mine)

    token_blocks(length, sums)
    total = stats.total() * (1.0 / full)
    inverse = lax.rsqrt(total[1:2] - total[0:1] * total[0:1] + EPSILON)
    stats_ref[...] = jnp.concatenate([total[0:1], inverse, total[2:]], axis=0)

    def activate(rows, index):
        mean, scale = stat_columns(stats_ref[:, rows])
        scaled = (mixed_ref[rows] - mean) * scale * depth_ref[...]
        act[rows] = (scaled * jax.nn.sigmoid(scaled)).astype(BF16)

    token_blocks(length, activate)
    for chunk, slot in reversed(chunks):
        target = part.at[wire.n - 1 if slot is None else slot]
        left = act[tile(chunk, count)]

        def leave(cols, index):
            target[:, cols] = matmul_nt(left, weights[cols, 2 * width:]).astype(BF16)

        block_loop(weights.shape[0], leave)
        if slot is not None:
            collect.send(target, chunk, slot)
    collect.wait()
    residual(wire, count, 1.0, part.at[wire.n - 1], got, resid, keep_ref, after_ref, squares_ref)
    spread.finish()
    wire.end()


def convolution(sizes, name, collective_id, gain_row, resid, keep, keep_all, gains, weights, kernel,
                depth_gain, **side):
    n, m = sizes
    count, full = resid.shape
    length, width = n * count, weights.shape[1] // 3
    return comm_call(
        name, collective_id, sizes,
        functools.partial(convolution_main, count, gain_row, kernel.shape[0]),
        [(item, vmem()) for item in (resid, keep, keep_all, gains, weights, kernel, depth_gain)],
        [
            ((count, full), F32, vmem()),
            ((16, full), F32, vmem()),
            ((length, full), BF16, vmem()),
            ((length, 2 * width), BF16, vmem()),
            ((length, width), F32, vmem()),
            ((8, length), F32, vmem()),
        ],
        [
            pltpu.VMEM((length + PAD, width), F32),
            pltpu.VMEM((8, length), F32),
            pltpu.VMEM((n - 1, 8, length), F32),
            pltpu.VMEM((length, width), BF16),
            pltpu.VMEM((n, count, full), BF16),
            pltpu.VMEM((n - 1, count, full), BF16),
        ],
        cost=15 * 10**9, **side,
    )


def convolution_back_main(count, gain_row, taps, wire, ins, outs, scratch):
    (grad_ref, resid, keep_all, gains_ref, weights, kernel_ref, depth_ref, rows_ref, pre_ref, mixed_ref,
     stats_ref) = ins
    gain_grad_ref, wide_ref, kernel_grad_ref, depth_grad_ref, new_grad_ref = outs
    (grads, padded, padded_grad, stats_mine, stats_got, sums_ref, act, pre_grad, part, got) = scratch
    length, width = mixed_ref.shape
    full = gains_ref.shape[1]
    wire.greet()
    wire.begin()
    cast_rows(wire, count, grad_ref, 1.0, grads)
    spread = Spread(wire, grads, count)
    spread.start()
    collect = Collect(wire, got)
    stats = Stats(wire, stats_mine, stats_got)
    padded[0:PAD] = jnp.zeros((PAD, width), F32)
    padded_grad[length:] = jnp.zeros((PAD, width), F32)
    sums_ref[...] = jnp.zeros_like(sums_ref)
    depth_grad_ref[...] = jnp.zeros_like(depth_grad_ref)
    spread.relay()

    def regate(rows, index):
        value_pre = pre_ref[rows, 0:width].astype(F32)
        gate_pre = pre_ref[rows, width:2 * width].astype(F32)
        at = pl.multiple_of(index * BLOCK + PAD, PAD)
        padded[pl.ds(at, BLOCK)] = value_pre * jax.nn.sigmoid(gate_pre) * keep_all[rows]

    token_blocks(length, regate)
    wire.early()
    chunks = []
    for chunk, slot in spread.arrivals(relay=False):
        chunks.append((chunk, slot))
        rows = tile(chunk, count)
        padded_grad[rows] = matmul(grads[rows], weights[:, 2 * width:])
    wire.middle()

    def first(rows, index):
        mean, scale = stat_columns(stats_ref[:, rows])
        normed = (mixed_ref[rows] - mean) * scale
        scaled = normed * depth_ref[...]
        sig = jax.nn.sigmoid(scaled)
        act[rows] = (scaled * sig).astype(BF16)
        scaled_grad = padded_grad[rows] * (sig + scaled * sig * (1.0 - sig))
        depth_grad_ref[...] += fold8(scaled_grad * normed)
        weighted = scaled_grad * depth_ref[...]
        padded_grad[rows] = weighted
        stat_rows(rows, jnp.sum(weighted, axis=1, keepdims=True),
                  jnp.sum(weighted * normed, axis=1, keepdims=True), stats_mine)

    token_blocks(length, first)
    total = stats.total() * (1.0 / full)
    stats_mine[...] = total

    def second(rows, index):
        mean, scale = stat_columns(stats_ref[:, rows])
        normed = (mixed_ref[rows] - mean) * scale
        one, two = stat_columns(stats_mine[:, rows])
        padded_grad[rows] = scale * (padded_grad[rows] - one - normed * two)

    token_blocks(length, second)

    def unmix(index, carry):
        rows = tile(index, ROWS)
        around = pl.ds(pl.multiple_of(index * ROWS, ROWS), ROWS + PAD)
        ahead = padded_grad[around]
        total = jnp.zeros((ROWS, width), F32)
        for shift, moved in shifted_sets(ahead, 0, taps - 1, ROWS):
            tap = taps - 1 - shift
            total = total + moved * kernel_ref[tap:tap + 1]
        here = ahead[0:ROWS]
        for shift, moved in shifted_sets(padded[around], PAD - taps + 1, PAD, ROWS):
            tap = shift - (PAD - taps + 1)
            sums_ref[tap * 8:(tap + 1) * 8] += fold8(here * moved)
        gate = jax.nn.sigmoid(pre_ref[rows, width:2 * width].astype(F32))
        through = total * keep_all[rows] * gate
        pre_grad[rows, 0:width] = through.astype(BF16)
        pre_grad[rows, width:2 * width] = (
            through * pre_ref[rows, 0:width].astype(F32) * (1.0 - gate)
        ).astype(BF16)
        return carry

    lax.fori_loop(0, length // ROWS, unmix, 0)
    for tap in range(taps):
        kernel_grad_ref[tap:tap + 1] = jnp.sum(sums_ref[tap * 8:(tap + 1) * 8], axis=0, keepdims=True)
    for chunk, slot in reversed(chunks):
        target = part.at[wire.n - 1 if slot is None else slot]
        left = pre_grad[tile(chunk, count)]

        def back(cols, index):
            target[:, cols] = matmul_nt(left, weights[cols, :2 * width]).astype(BF16)

        block_loop(weights.shape[0], back)
        if slot is not None:
            collect.send(target, chunk, slot)

    def weight_grads(rows, index):
        wide_ref[rows, :2 * width] = matmul_tn(rows_ref[:, rows], pre_grad[...]).astype(BF16)
        wide_ref[rows, 2 * width:] = matmul_tn(grads[:, rows], act[...]).astype(BF16)

    block_loop(weights.shape[0], weight_grads)
    collect.wait()
    residual_back(wire, count, part.at[wire.n - 1], got, grad_ref, resid,
                  gains_ref[gain_row:gain_row + 1], new_grad_ref, gain_grad_ref)
    spread.finish()
    wire.end()


def convolution_back(sizes, name, collective_id, gain_row, grad, resid, keep_all, gains, weights, kernel,
                     depth_gain, rows, pre, mixed, stats, **side):
    n, m = sizes
    count, full = resid.shape
    length, width = mixed.shape
    taps = kernel.shape[0]
    return comm_call(
        name, collective_id, sizes,
        functools.partial(convolution_back_main, count, gain_row, taps),
        [(item, vmem()) for item in (grad, resid, keep_all, gains, weights, kernel, depth_gain, rows, pre,
                                     mixed, stats)],
        [
            ((8, full), F32, vmem()),
            ((full, 3 * width), BF16, vmem()),
            ((taps, width), F32, vmem()),
            ((8, width), F32, vmem()),
            ((count, full), F32, vmem()),
        ],
        [
            pltpu.VMEM((length, full), BF16),
            pltpu.VMEM((length + PAD, width), F32),
            pltpu.VMEM((length + PAD, width), F32),
            pltpu.VMEM((8, length), F32),
            pltpu.VMEM((n - 1, 8, length), F32),
            pltpu.VMEM((8 * taps, width), F32),
            pltpu.VMEM((length, width), BF16),
            pltpu.VMEM((length, 2 * width), BF16),
            pltpu.VMEM((n, count, full), BF16),
            pltpu.VMEM((n - 1, count, full), BF16),
        ],
        cost=20 * 10**9, **side,
    )


def body(
    layer_input,
    clip_lengths,
    first_gain,
    first_up,
    first_down,
    attend_gain,
    query_weight,
    key_weight,
    value_weight,
    output_weight,
    distance_table,
    conv_gain,
    pointwise_value,
    pointwise_gate,
    depthwise_kernel,
    depthwise_gain,
    pointwise_out,
    second_gain,
    second_up,
    second_down,
    final_gain,
    output_cotangent,
):
    n = lax.axis_size("col")
    me = lax.axis_index("col")
    width, length = layer_input.shape
    full = n * width
    count = length // n

    sizes = (n, lax.axis_size("row"))
    attend_shard = jnp.concatenate([query_weight, key_weight, value_weight, output_weight.T], axis=1)
    conv_shard = jnp.concatenate([pointwise_value, pointwise_gate, pointwise_out.T], axis=1)

    keep_all = (jnp.arange(length)[:, None] < clip_lengths).astype(F32)
    keep = (jnp.arange(count)[:, None] + me * count < clip_lengths).astype(F32)
    blank = jnp.zeros_like(first_gain)
    gain_stack = jnp.stack(
        [first_gain, attend_gain, conv_gain, second_gain, final_gain, blank, blank, blank]
    )
    table_wide = extend_table(distance_table)
    group = min(2 * HEAD_DIM, width)
    table_wide = jnp.tile(table_wide, (1, group // HEAD_DIM))
    taps = depthwise_kernel.astype(F32)

    (start, cot, gains, up_first, down_first, attend_weights, after_first, squares_first, rows_first,
     pre_first) = feed_forward(
        sizes, "first", 1, 0, first_up, first_down.T, keep,
        enter=(layer_input.T, output_cotangent.T, gain_stack, attend_shard),
    )

    (after_attend, squares_attend, rows_attend, qkv, context, log_total, conv_weights,
     up_second) = attention(
        sizes, "attend", 2, 1, clip_lengths, after_first, keep, gains, attend_weights, table_wide,
        gathers=[conv_shard, second_up],
    )
    depth_row = depthwise_gain[None]
    (after_conv, squares_conv, rows_conv, conv_pre, mixed, stats, down_second) = convolution(
        sizes, "convolve", 3, 2, after_attend, keep, keep_all, gains, conv_weights, taps, depth_row,
        gathers=[second_down.T],
    )

    (grad_second, final_part, out_tokens, _, squares_second, rows_second, pre_second) = feed_forward(
        sizes, "second", 4, 3, up_second, down_second, keep, resid=after_conv, gains=gains, turn=cot
    )

    second_part, second_up_wide, second_down_wide, grad_conv = feed_forward_back(
        sizes, "second_back", 5, 3, grad_second, after_conv, gains, up_second, down_second,
        rows_second, pre_second,
    )

    (conv_part, conv_wide, kernel_part, depth_part, grad_attend, second_up_grad,
     second_down_grad) = convolution_back(
        sizes, "convolve_back", 6, 2, grad_conv, after_attend, keep_all, gains, conv_weights, taps,
        depth_row, rows_conv, conv_pre, mixed, stats, reduces=[second_up_wide, second_down_wide],
    )
    depth_part = jnp.sum(depth_part, axis=0)
    attend_part, attend_wide, table_part, grad_first, conv_grads = attention_back(
        sizes, "attend_back", 7, 1, clip_lengths, grad_attend, after_first, gains, attend_weights,
        table_wide, rows_attend, qkv, context, log_total, reduces=[conv_wide],
    )

    table_part = sum(
        table_part[:, at:at + HEAD_DIM] for at in range(0, group, HEAD_DIM)
    )
    table_part = fold_table(table_part)
    squares = jnp.stack(
        [
            jnp.sum(piece[at:at + 8])
            for at in (0, 8)
            for piece in (squares_first, squares_attend, squares_conv, squares_second)
        ]
    )
    lengths_sum = jnp.sum(clip_lengths).astype(F32) * (me == 0).astype(F32)
    token_parts = jnp.stack(
        [jnp.sum(piece, axis=0) for piece in (attend_part, conv_part, second_part, final_part)]
    )
    token_parts = jnp.pad(token_parts, ((0, 4), (0, 0))).reshape(8, n, width).transpose(1, 0, 2)
    loose = jnp.concatenate([table_part.reshape(-1), squares, lengths_sum[None]])
    loose_rows = -(-loose.shape[0] // (8 * width)) * 8
    loose = jnp.pad(loose, (0, loose_rows * width - loose.shape[0])).reshape(loose_rows, width)
    tap_count = kernel_part.shape[0]
    kept = jnp.concatenate([kernel_part, depth_part[None]])
    kept = jnp.pad(kept, ((0, -kept.shape[0] % 8), (0, 0)))

    (first_sum, first_up_grad, first_down_grad, grad_tokens, sums, attend_grads) = feed_forward_back(
        sizes, "first_back", 0, 0, grad_first, start, gains, up_first, down_first, rows_first,
        pre_first, leave=(token_parts, loose, kept), reduces=[attend_wide],
    )
    first_down_grad, second_down_grad = first_down_grad.T, second_down_grad.T
    mine = sums[:8]
    kept = sums[8 + loose_rows:]
    loose = sums[8:8 + loose_rows].reshape(-1)
    table_size = table_part.size
    table_sum = loose[:table_size].reshape(table_part.shape)
    square_sums = loose[table_size:table_size + 8]
    masked_rms = jnp.sqrt(square_sums / (loose[table_size + 8] * full))

    return (
        out_tokens.T,
        grad_tokens.T.astype(F32),
        jnp.sum(first_sum, axis=0),
        first_up_grad,
        first_down_grad,
        mine[0],
        attend_grads[:, :width],
        attend_grads[:, width:2 * width],
        attend_grads[:, 2 * width:3 * width],
        attend_grads[:, 3 * width:].T,
        table_sum,
        mine[1],
        conv_grads[:, :width],
        conv_grads[:, width:2 * width],
        kept[:tap_count],
        kept[tap_count],
        conv_grads[:, 2 * width:].T,
        mine[2],
        second_up_grad,
        second_down_grad,
        mine[3],
        masked_rms,
    )


def solution(mesh):
    in_specs = (
        P("col", "row"),
        P("row"),
        P("col"),
        P("row", "col"),
        P("col", "row"),
        P("col"),
        P("row", "col"),
        P("row", "col"),
        P("row", "col"),
        P("col", "row"),
        P(),
        P("col"),
        P("row", "col"),
        P("row", "col"),
        P(None, "col"),
        P("col"),
        P("col", "row"),
        P("col"),
        P("row", "col"),
        P("col", "row"),
        P("col"),
        P("col", "row"),
    )
    out_specs = (
        P("col", "row"),
        P("col", "row"),
        P("col"),
        P("row", "col"),
        P("col", "row"),
        P("col"),
        P("row", "col"),
        P("row", "col"),
        P("row", "col"),
        P("col", "row"),
        P(),
        P("col"),
        P("row", "col"),
        P("row", "col"),
        P(None, "col"),
        P("col"),
        P("col", "row"),
        P("col"),
        P("row", "col"),
        P("col", "row"),
        P("col"),
        P(),
    )
    return jax.shard_map(body, mesh=mesh, in_specs=in_specs, out_specs=out_specs, check_vma=False)
```

```python
import functools
import math

import jax
import jax.numpy as jnp
from jax import lax
from jax.experimental import pallas as pl
from jax.experimental.pallas import tpu as pltpu
from jax.sharding import PartitionSpec as P

HEAD_DIM = 64
LEFT = 64
RIGHT = 8
EPSILON = 1e-05
NEG_FILL = -1e30
BF16 = jnp.bfloat16
F32 = jnp.float32
MESH = pl.DeviceIdType.MESH
BLOCK = 128
WINDOW = 384
SPAN = 512
VMEM_LIMIT = 60 * 1024 * 1024
MARGIN = 6 * 1024 * 1024


def matmul(left, right):
    return jnp.dot(left, right, preferred_element_type=F32)


def matmul_nt(left, right):
    return lax.dot_general(left, right, (((1,), (1,)), ((), ())), preferred_element_type=F32)


def matmul_tn(left, right):
    return lax.dot_general(left, right, (((0,), (0,)), ((), ())), preferred_element_type=F32)


def vmem():
    return pl.BlockSpec(memory_space=pltpu.VMEM)


def smem():
    return pl.BlockSpec(memory_space=pltpu.SMEM)


def hbm():
    return pl.BlockSpec(memory_space=pltpu.HBM)


def padded_bytes(shape, dtype):
    size = jnp.dtype(dtype).itemsize
    rows = 8 * 4 // size
    shape = (1,) * (2 - len(shape)) + tuple(shape)
    held = -(-shape[-1] // 128) * 128 * -(-shape[-2] // rows) * rows
    return math.prod(shape[:-2]) * held * size


def comm_params(collective_id, held):
    return pltpu.CompilerParams(
        collective_id=collective_id, has_side_effects=True,
        vmem_limit_bytes=max(VMEM_LIMIT, held + MARGIN),
    )


def tile(index, size):
    return pl.ds(pl.multiple_of(index * size, size), size)


class Wire:
    def __init__(self, sizes, send_sem, recv_sem, local_sem, side, col_on=True, row_on=False):
        self.n, self.m = sizes
        self.me = lax.axis_index("col")
        self.row = lax.axis_index("row")
        self.send_sem, self.recv_sem, self.local_sem = send_sem, recv_sem, local_sem
        self.used = 0
        self.used_local = 0
        self.core = lax.rem(self.row, 2)
        self.layer = self.row // 2
        self.partner = self.row + 1 - 2 * self.core
        self.layers = self.m // 2
        self.col_on = col_on
        self.loads, self.stores, self.stored = [], [], []
        self.row_on = row_on or bool(side)
        self.side = [job(self) for job in side]

    def layer_peer(self, step):
        return lax.rem(self.layer + step, self.layers) * 2 + self.core

    def greet(self):
        barrier = pltpu.get_barrier_semaphore()
        waits = 0
        if self.col_on:
            for step in range(1, self.n):
                pl.semaphore_signal(
                    barrier, inc=1, device_id={"col": lax.rem(self.me + step, self.n)},
                    device_id_type=MESH,
                )
            waits += self.n - 1
        if self.row_on:
            for step in range(1, self.layers):
                pl.semaphore_signal(
                    barrier, inc=1, device_id={"row": self.layer_peer(step)}, device_id_type=MESH
                )
            pl.semaphore_signal(
                barrier, inc=1, device_id={"row": self.partner}, device_id_type=MESH
            )
            waits += self.layers
        pl.semaphore_wait(barrier, waits)

    def remote(self, source, target, axis, peer):
        slot = self.used
        self.used += 1
        return pltpu.make_async_remote_copy(
            src_ref=source, dst_ref=target, send_sem=self.send_sem.at[slot],
            recv_sem=self.recv_sem.at[slot], device_id={axis: peer}, device_id_type=MESH,
        )

    def local(self, source, target):
        slot = self.used_local
        self.used_local += 1
        return pltpu.make_async_copy(source, target, self.local_sem.at[slot])

    def to_all(self, source_of, target):
        copies = [
            self.remote(source_of(lax.rem(self.me + step, self.n)), target, "col",
                        lax.rem(self.me + step, self.n))
            for step in range(1, self.n)
        ]
        for copy in copies:
            copy.start()
        return copies

    def loaded(self):
        for copy in self.loads:
            copy.wait()

    def store(self, copies):
        for copy in copies:
            copy.start()
        self.stored += copies

    def flush(self):
        self.store(self.stores)

    def settle(self):
        for copy in self.stored:
            copy.wait()

    def begin(self):
        for job in self.side:
            job.begin()

    def early(self):
        for job in self.side:
            job.early()

    def middle(self):
        for job in self.side:
            job.middle()

    def end(self):
        for job in self.side:
            job.end()

    def peers(self):
        if self.n == 4:
            across = self.me + 1 - 2 * lax.rem(self.me, 2)
            along = lax.rem(self.me + 2, 4)
            return [(across, 0), (along, 1), (3 - self.me, 2)]
        return [
            (lax.rem(self.me + self.n - step, self.n), self.n - step - 1)
            for step in range(1, self.n)
        ]


class Spread:
    def __init__(self, wire, ref, count):
        self.wire, self.ref, self.count = wire, ref, count
        me = wire.me
        if wire.n != 4:
            self.copies = [
                wire.remote(self.part(me), self.part(me), "col", lax.rem(me + step, wire.n))
                for step in range(1, wire.n)
            ]
            return
        (across, _), (along, _), (far, _) = wire.peers()
        self.across = [wire.remote(self.part(me, q), self.part(me, q), "col", across) for q in range(4)]
        self.along = [wire.remote(self.part(me, q), self.part(me, q), "col", along) for q in range(4)]
        self.onward = [
            wire.remote(self.part(across, q), self.part(across, q), "col", along) for q in (0, 1)
        ] + [wire.remote(self.part(along, q), self.part(along, q), "col", across) for q in (2, 3)]

    def part(self, chunk, quarter=None):
        if quarter is None:
            return self.ref.at[tile(chunk, self.count)]
        size = self.count // 4
        return self.ref.at[tile(chunk * 4 + quarter, size)]

    def start(self):
        if self.wire.n != 4:
            for copy in self.copies:
                copy.start()
            return
        for first, second in ((0, 2), (1, 3), (2, 0), (3, 1)):
            self.across[first].start()
            self.along[second].start()

    def relay(self):
        if self.wire.n != 4:
            return
        for turn in range(2):
            self.across[turn].wait_recv()
            self.onward[turn].start()
            self.along[2 + turn].wait_recv()
            self.onward[2 + turn].start()

    def arrivals(self, relay=True):
        wire = self.wire
        yield wire.me, None
        if wire.n != 4:
            for step, (peer, slot) in zip(range(1, wire.n), wire.peers()):
                self.copies[step - 1].wait_recv()
                yield peer, slot
            return
        if relay:
            self.relay()
        for (peer, slot), copies in zip(
            wire.peers(), (self.across[2:], self.along[:2], self.onward)
        ):
            for copy in copies:
                copy.wait_recv()
            yield peer, slot

    def finish(self):
        copies = self.copies if self.wire.n != 4 else self.across + self.along + self.onward
        for copy in copies:
            copy.wait_send()


class Collect:
    def __init__(self, wire, part, got):
        self.wire, self.part, self.got = wire, part, got
        self.relayed = wire.n == 4
        self.count = part.shape[1]
        if not self.relayed:
            self.copies = {
                slot: wire.remote(part.at[slot], got.at[slot], "col", owner)
                for owner, slot in wire.peers()
            }
            return
        (across, _), (along, _), _ = wire.peers()
        half = self.count // 2
        first, second = pl.ds(0, half), pl.ds(half, half)
        places = [got.at[place // 2, (first, second)[place % 2]] for place in range(6)]
        self.far = [
            wire.remote(part.at[2, first], places[0], "col", across),
            wire.remote(part.at[2, second], places[1], "col", along),
        ]
        self.direct = {
            0: wire.remote(part.at[0, first], places[2], "col", across),
            1: wire.remote(part.at[1, second], places[4], "col", along),
        }
        self.onward = [
            wire.remote(part.at[0, second], places[3], "col", across),
            wire.remote(part.at[1, first], places[5], "col", along),
        ]

    def send(self, slot):
        if not self.relayed:
            self.copies[slot].start()
        elif slot == 2:
            for copy in self.far:
                copy.start()
        else:
            self.direct[slot].start()

    def combine(self):
        if not self.relayed:
            return
        half = self.count // 2
        for copy, slot, at, onward in (
            (self.far[1], 0, half, self.onward[0]), (self.far[0], 1, 0, self.onward[1])
        ):
            copy.wait_recv()
            place = 1 - slot

            def add(rows, index):
                mine = pl.ds(pl.multiple_of(at + index * 32, 32), 32)
                came = pl.ds(pl.multiple_of((half if place else 0) + index * 32, 32), 32)
                self.part[slot, mine] = (
                    self.part[slot, mine].astype(F32) + self.got[0, came].astype(F32)
                ).astype(BF16)

            row_loop(half, add)
            onward.start()

    def wait(self):
        if not self.relayed:
            for copy in self.copies.values():
                copy.wait()
            return
        for copy in self.far:
            copy.wait_send()
        for copy in list(self.direct.values()) + self.onward:
            copy.wait()

    def sum_loop(self, body):
        part, got, last = self.part, self.got, self.wire.n - 1
        if not self.relayed:
            def step(rows, index):
                total = part[last, rows].astype(F32)
                for slot in range(last):
                    total = total + got[slot, rows].astype(F32)
                body(rows, total)

            row_loop(self.count, step)
            return
        half = self.count // 2
        for at, sources in ((0, ((1, 0), (2, half))), (half, ((1, half), (2, 0)))):
            def step(rows, index, at=at, sources=sources):
                mine = pl.ds(pl.multiple_of(at + index * 32, 32), 32)
                total = part[last, mine].astype(F32)
                for slot, start in sources:
                    total = total + got[
                        slot, pl.ds(pl.multiple_of(start + index * 32, 32), 32)
                    ].astype(F32)
                body(mine, total)

            row_loop(half, step)


class RowChain:
    def __init__(self, shard, full, wire):
        self.wire, self.shard, self.full = wire, shard, full
        self.count = shard.shape[0]
        self.steps = wire.layers - 1
        self.base = wire.used
        wire.used += 4 * self.steps
        mine = full.at[tile(wire.row, self.count)]
        self.own = [wire.local(shard, mine), wire.remote(shard, mine, "row", wire.partner)]

    def block(self, layer):
        return self.full.at[tile(layer * 2 + self.wire.core, self.count)]

    def copy(self, kind, step, layer, peer):
        slot = self.base + kind * self.steps + step
        wire = self.wire
        source = self.shard if kind < 2 and step == 0 else self.block(layer)
        return pltpu.make_async_remote_copy(
            src_ref=source, dst_ref=self.block(layer), send_sem=wire.send_sem.at[slot],
            recv_sem=wire.recv_sem.at[slot], device_id={"row": peer}, device_id_type=MESH,
        )

    def up(self, step):
        wire = self.wire
        return self.copy(0, step, wire.layer - step, wire.row + 2)

    def down(self, step):
        wire = self.wire
        return self.copy(1, step, wire.layer + step, wire.row - 2)

    def begin(self):
        wire = self.wire
        pl.when(wire.layer + 1 < wire.layers)(lambda: self.up(0).start())
        pl.when(wire.layer > 0)(lambda: self.down(0).start())
        for copy in self.own:
            copy.start()

    def advance(self, step):
        wire = self.wire

        @pl.when(wire.layer - 1 - step >= 0)
        def _():
            self.copy(0, step, wire.layer - 1 - step, wire.row).wait_recv()
            if step + 1 < self.steps:
                pl.when(wire.layer + 1 < wire.layers)(lambda: self.up(step + 1).start())
            self.copy(2, step, wire.layer - 1 - step, wire.partner).start()

        @pl.when(wire.layer + 1 + step < wire.layers)
        def _():
            self.copy(1, step, wire.layer + 1 + step, wire.row).wait_recv()
            if step + 1 < self.steps:
                pl.when(wire.layer > 0)(lambda: self.down(step + 1).start())
            self.copy(3, step, wire.layer + 1 + step, wire.partner).start()

    def end(self):
        wire = self.wire
        for step in range(self.steps):
            pl.when((wire.layer + 1 < wire.layers) & (wire.layer - step >= 0))(
                lambda step=step: self.up(step).wait_send()
            )
            pl.when((wire.layer > 0) & (wire.layer + step < wire.layers))(
                lambda step=step: self.down(step).wait_send()
            )
            pl.when(wire.layer - 1 - step >= 0)(
                lambda step=step: self.copy(2, step, wire.layer - 1 - step, wire.partner).wait()
            )
            pl.when(wire.layer + 1 + step < wire.layers)(
                lambda step=step: self.copy(3, step, wire.layer + 1 + step, wire.partner).wait()
            )
        for copy in self.own:
            copy.wait()


class RowGather:
    def __init__(self, shard, full, wire):
        self.wire = wire
        count = shard.shape[0]
        mine = full.at[tile(wire.row, count)]
        self.first = [wire.local(shard, mine), wire.remote(shard, mine, "row", wire.partner)]
        self.along = [
            wire.remote(shard, mine, "row", wire.layer_peer(step))
            for step in range(1, wire.layers)
        ]
        self.onward = []
        for step in range(1, wire.layers):
            block = full.at[tile(wire.layer_peer(wire.layers - step), count)]
            self.onward.append(wire.remote(block, block, "row", wire.partner))

    def begin(self):
        for copy in self.along + self.first:
            copy.start()

    def early(self):
        pass

    def middle(self):
        for copy, onward in zip(self.along, self.onward):
            copy.wait_recv()
            onward.start()

    def end(self):
        for copy in self.along:
            copy.wait_send()
        for copy in self.first:
            copy.wait()
        for copy in self.onward:
            copy.wait()


class RowReduce:
    def __init__(self, grads, pieces, outs, held, pair, got, total, *rest, load=True):
        *parts, wire = rest
        self.wire, self.out, self.grads = wire, total, grads
        self.pieces = pieces
        self.parts = parts or [total]
        self.keep = [wire.local(part, out) for part, out in zip(self.parts, outs)]
        self.held, self.pair, self.got = held, pair, got
        self.count = held.shape[1]
        other = 1 - wire.core
        self.load = []
        if load:
            self.load = [
                wire.local(grads.at[tile(layer * 2 + wire.core, self.count)], held.at[layer])
                for layer in range(wire.layers)
            ]
        self.swap = [
            wire.remote(grads.at[tile(layer * 2 + other, self.count)], pair.at[layer], "row",
                        wire.partner)
            for layer in range(wire.layers)
        ]
        self.along = []
        for step in range(1, wire.layers):
            layer = lax.rem(wire.layer + step, wire.layers)
            self.along.append(
                wire.remote(held.at[layer], got.at[step - 1], "row", wire.layer_peer(step))
            )

    def begin(self):
        for copy in self.swap + self.load:
            copy.start()

    def early(self):
        for copy in self.load + self.swap:
            copy.wait()
        size = min(32, self.count)
        for layer in range(self.wire.layers):
            def add(rows, index, layer=layer):
                if self.load:
                    mine = self.held[layer, rows]
                else:
                    at = (layer * 2 + self.wire.core) * self.count + index * size
                    mine = self.grads[pl.ds(pl.multiple_of(at, size), size)]
                self.held[layer, rows] = (
                    mine.astype(F32) + self.pair[layer, rows].astype(F32)
                ).astype(BF16)

            row_loop(self.count, add)
        for copy in self.along:
            copy.start()

    def middle(self):
        pass

    def end(self):
        for copy in self.along:
            copy.wait()

        def add(rows, index):
            total = self.held[self.wire.layer, rows].astype(F32)
            for step in range(self.wire.layers - 1):
                total = total + self.got[step, rows].astype(F32)
            self.out[rows] = total

        row_loop(self.count, add)
        if len(self.parts) > 1 or self.pieces[0][1]:
            at = 0
            for part, (width, flip) in zip(self.parts, self.pieces):
                piece = self.out[:, at:at + width]
                part[...] = piece.T if flip else piece
                at += width
        self.wire.store(self.keep)


def piece_shapes(count, pieces):
    return [(width, count) if flip else (count, width) for width, flip in pieces]


def reduce_scratch(layers, count, width, pieces):
    apart = len(pieces) > 1 or pieces[0][1]
    parts = [pltpu.VMEM(shape, F32) for shape in piece_shapes(count, pieces)] if apart else []
    return parts_last(layers, count, width) + parts


def parts_last(layers, count, width):
    return [
        pltpu.VMEM((layers, count, width), BF16),
        pltpu.VMEM((layers, count, width), BF16),
        pltpu.VMEM((max(1, layers - 1), count, width), BF16),
        pltpu.VMEM((count, width), F32),
    ]


class SumItem:
    def __init__(self, kind, source, out, got, packed, got_row, wire):
        self.wire, self.kind, self.source, self.out = wire, kind, source, out
        self.got, self.packed, self.got_row = got, packed, got_row
        self.col = []
        if kind != "own":
            for step in range(1, wire.n):
                peer = lax.rem(wire.me + step, wire.n)
                piece = source.at[peer] if kind == "piece" else source
                self.col.append(wire.remote(piece, got.at[step - 1], "col", peer))
        self.swap = wire.remote(packed.at[0], got_row.at[0], "row", wire.partner)
        self.along = [
            wire.remote(packed.at[1], got_row.at[step], "row", wire.layer_peer(step))
            for step in range(1, wire.layers)
        ]

    def begin(self):
        for copy in self.col:
            copy.start()

    def early(self):
        for copy in self.col:
            copy.wait()
        total = self.source[self.wire.me] if self.kind == "piece" else self.source[...]
        if self.kind != "own":
            for step in range(self.wire.n - 1):
                total = total + self.got[step]
        self.packed[0] = total
        self.swap.start()

    def middle(self):
        self.swap.wait()
        self.packed[1] = self.packed[0] + self.got_row[0]
        for copy in self.along:
            copy.start()

    def end(self):
        for copy in self.along:
            copy.wait()
        total = self.packed[1]
        for step in range(1, self.wire.layers):
            total = total + self.got_row[step]
        self.out[...] = total


def sum_scratch(n, layers, shape):
    return [
        pltpu.VMEM(shape, F32),
        pltpu.VMEM((n - 1,) + shape, F32),
        pltpu.VMEM((2,) + shape, F32),
        pltpu.VMEM((layers,) + shape, F32),
    ]


def join(pieces, target):
    at = 0
    for ref, flip in pieces:
        width = ref.shape[0] if flip else ref.shape[1]
        target[:, at:at + width] = ref[...].T if flip else ref[...]
        at += width


def joined_shape(pieces):
    rows = {array.shape[1] if flip else array.shape[0] for array, flip in pieces}
    return rows.pop(), sum(array.shape[0] if flip else array.shape[1] for array, flip in pieces)


def row_loop(count, body):
    size = min(32, count)

    def step(index, carry):
        body(tile(index, size), index)
        return carry

    lax.fori_loop(0, count // size, step, 0)


def block_loop(extent, body):
    size = min(256, extent)

    def step(index, carry):
        body(tile(index, size), index)
        return carry

    lax.fori_loop(0, extent // size, step, 0)


def fold8(values):
    return jnp.sum(values.reshape(values.shape[0] // 8, 8, values.shape[1]), axis=0)


def normalize(values):
    average = jnp.mean(values, axis=1, keepdims=True)
    centered = values - average
    inverse = lax.rsqrt(jnp.mean(centered * centered, axis=1, keepdims=True) + EPSILON)
    return centered * inverse, inverse


def norm_back(grad_in, normed, inverse, gains):
    scaled = grad_in * gains
    first = jnp.mean(scaled, axis=1, keepdims=True)
    second = jnp.mean(scaled * normed, axis=1, keepdims=True)
    return inverse * (scaled - first - normed * second)


def comm_call(name, collective_id, sizes, main, ins, outs, scratch, gathers=(), reduces=(), cost=10**9,
              col_on=True, more_slots=0, row_on=False):
    n, m = sizes
    layers = m // 2
    gather_pieces = [piece for pieces in gathers for piece in pieces]
    in_arrays = [item[0] for item in ins] + [array for array, _ in gather_pieces]
    in_arrays += [grads for grads, _ in reduces]
    in_specs = [hbm() if item[1] == "load" else item[1] for item in ins]
    in_specs += [vmem()] * len(gather_pieces) + [hbm()] * len(reduces)
    out_shapes = [jax.ShapeDtypeStruct(item[0], item[1]) for item in outs]
    out_specs = [hbm() if item[2] == "store" else item[2] for item in outs]
    copied = [pltpu.VMEM(item[0].shape, item[0].dtype) for item in ins if item[1] == "load"]
    copied += [pltpu.VMEM(item[0], item[1]) for item in outs if item[2] == "store"]
    side_scratch = []
    for pieces in gathers:
        rows, width = joined_shape(pieces)
        out_shapes.append(jax.ShapeDtypeStruct((m * rows, width), BF16))
        out_specs.append(hbm())
        side_scratch.append(pltpu.VMEM((rows, width), BF16))
    reduce_counts = []
    for grads, pieces in reduces:
        count, width = grads.shape[0] // m, grads.shape[1]
        for shape in piece_shapes(count, pieces):
            out_shapes.append(jax.ShapeDtypeStruct(shape, F32))
            out_specs.append(hbm())
        made = reduce_scratch(layers, count, width, pieces)
        reduce_counts.append(len(made))
        side_scratch += made
    every_scratch = copied + list(scratch) + side_scratch
    held = sum(padded_bytes(item.shape, item.dtype) for item in every_scratch)
    remote_slots = 8 * n + 16 + len(gathers) * 2 * layers + len(reduces) * 2 * layers + more_slots
    local_slots = 12 + len(copied) + len(gathers) + len(reduces) * (layers + 4) + more_slots

    def kernel(*refs):
        at = 0

        def take(count):
            nonlocal at
            at += count
            return refs[at - count:at]

        main_ins = list(take(len(ins)))
        gather_ins = [
            [(ref, flip) for ref, (_, flip) in zip(take(len(pieces)), pieces)] for pieces in gathers
        ]
        reduce_ins = take(len(reduces))
        main_outs = list(take(len(outs)))
        gather_outs = take(len(gathers))
        reduce_outs = [take(len(pieces)) for _, pieces in reduces]
        loads, stores = [], []
        for place, item in enumerate(ins):
            if item[1] == "load":
                (held_ref,) = take(1)
                loads.append((main_ins[place], held_ref))
                main_ins[place] = held_ref
        for place, item in enumerate(outs):
            if item[2] == "store":
                (held_ref,) = take(1)
                stores.append((held_ref, main_outs[place]))
                main_outs[place] = held_ref
        main_scratch = take(len(scratch))
        side = []
        for pieces, full in zip(gather_ins, gather_outs):
            (shard,) = take(1)
            join(pieces, shard)
            side.append(functools.partial(RowGather, shard, full))
        for grads, out, (_, pieces), size in zip(reduce_ins, reduce_outs, reduces, reduce_counts):
            side.append(functools.partial(RowReduce, grads, pieces, out, *take(size)))
        send_sem, recv_sem, local_sem = take(3)
        wire = Wire(sizes, send_sem, recv_sem, local_sem, side, col_on, row_on)
        wire.loads = [wire.local(*pair) for pair in loads]
        wire.stores = [wire.local(*pair) for pair in stores]
        for copy in wire.loads:
            copy.start()
        main(wire, main_ins, main_outs, main_scratch)
        wire.settle()

    return pl.pallas_call(
        kernel,
        name=name,
        out_shape=tuple(out_shapes),
        in_specs=in_specs,
        out_specs=tuple(out_specs),
        scratch_shapes=every_scratch + [
            pltpu.SemaphoreType.DMA((remote_slots,)),
            pltpu.SemaphoreType.DMA((remote_slots,)),
            pltpu.SemaphoreType.DMA((local_slots,)),
        ],
        compiler_params=comm_params(collective_id, held),
        cost_estimate=pl.CostEstimate(flops=cost, bytes_accessed=10**8, transcendentals=0),
    )(*in_arrays)


def norm_rows(wire, count, source, gains, rows_ref):
    base = wire.me * count

    def work(rows, index):
        normed, _ = normalize(source[rows])
        size = min(32, count)
        rows_ref[pl.ds(pl.multiple_of(base + index * size, size), size)] = (normed * gains).astype(BF16)

    row_loop(count, work)


def cast_rows(wire, count, source, factor, rows_ref):
    base = wire.me * count

    def work(rows, index):
        size = min(32, count)
        rows_ref[pl.ds(pl.multiple_of(base + index * size, size), size)] = (
            factor * source[rows]
        ).astype(BF16)

    row_loop(count, work)


def keep_rows(limit, start, rows):
    place = lax.broadcasted_iota(jnp.int32, (rows, 1), 0) + start
    return jnp.where(place < limit, 1.0, 0.0)


def residual(collect, factor, resid, limit, after_ref, squares_ref):
    squares_ref[...] = jnp.zeros_like(squares_ref)
    base = collect.wire.me * collect.count

    def work(rows, branch):
        after = resid[rows] + factor * branch
        after_ref[rows] = after
        keep = keep_rows(limit, base + rows.start, branch.shape[0])
        squares_ref[0:8] += fold8(branch * branch * keep)
        squares_ref[8:16] += fold8(after * after * keep)

    collect.sum_loop(work)


def residual_back(collect, grad_ref, resid, gains, new_grad_ref, gain_grad_ref):
    gain_grad_ref[...] = jnp.zeros_like(gain_grad_ref)

    def work(rows, rows_grad):
        normed, inverse = normalize(resid[rows])
        new_grad_ref[rows] = grad_ref[rows] + norm_back(rows_grad, normed, inverse, gains)
        gain_grad_ref[...] += fold8(rows_grad * normed)

    collect.sum_loop(work)


def send_pieces(wire, count, source, pieces, out_ref):
    width = pieces.shape[2]

    def split(rows, index):
        result = source[rows].astype(BF16)
        for part in range(wire.n):
            pieces[part, rows] = result[:, part * width:(part + 1) * width]

    row_loop(count, split)
    mine = out_ref.at[tile(wire.me, count)]
    copies = wire.to_all(lambda peer: pieces.at[peer], mine)
    here = wire.local(pieces.at[wire.me], mine)
    here.start()
    return copies + [here]


def feed_forward_first(count, chunk, rows_ref, up, pre_ref, act):
    rows = tile(chunk, count)
    left = rows_ref[rows]

    def first(cols, index):
        pre = matmul(left, up[:, cols])
        pre_ref[rows, cols] = pre.astype(BF16)
        act[:, cols] = (pre * jax.nn.sigmoid(pre)).astype(BF16)

    block_loop(up.shape[1], first)


def feed_forward_second(act, down_t, target):
    hidden = act[...]

    def second(cols, index):
        target[:, cols] = matmul_nt(hidden, down_t[cols]).astype(BF16)

    block_loop(down_t.shape[0], second)


def feed_forward_main(count, gain_row, factor, enter, turn, wire, ins, outs, scratch):
    ins, outs, scratch = list(ins), list(outs), list(scratch)
    if enter:
        limit_ref, tokens_ref, cot_in = ins[:3]
        gain_ins = ins[3:8]
        up_shard, down_ref = ins[8:10]
        next_pieces = [(ref, flip) for ref, flip in zip(ins[10:], enter)]
        ins = []
        resid, cot_out, gains_ref, up, down_t, next_full = outs[:6]
        outs = outs[6:]
        arrived, arrived_cot, arrived_gain, gain_in, down_shard, next_shard = scratch[:6]
        scratch = scratch[6:]
    else:
        limit_ref, resid, gains_ref = ins[:3]
        ins = ins[3:]
    if enter:
        for place, ref in enumerate(gain_ins):
            gain_in[place:place + 1] = ref[...]
        gain_in[len(gain_ins):] = jnp.zeros((8 - len(gain_ins), gain_in.shape[1]), F32)
        join([(down_ref, True)], down_shard)
        join(next_pieces, next_shard)
    else:
        up, down_t = ins[:2]
        ins = ins[2:]
    if turn:
        (cot_ref,) = ins
        grad_ref, gain_grad_ref, out_ref = outs[:3]
        outs = outs[3:]
        pieces, after_ref = scratch[:2]
        scratch = scratch[2:]
    else:
        after_ref = outs.pop(0)
    squares_ref, rows_ref, pre_ref = outs
    act, part, got = scratch
    wire.greet()
    wire.begin()
    if enter:
        up_job = RowChain(up_shard, up, wire)
        down_job = RowChain(down_shard, down_t, wire)
        next_job = RowChain(next_shard, next_full, wire)
        up_job.begin()
        width = arrived_gain.shape[2]
        turned = tokens_ref.shape[0] == width

        def share(ref, peer):
            return ref.at[:, tile(peer, count)] if turned else ref.at[tile(peer, count)]

        def settle(came, target):
            for piece in range(wire.n):
                cols = slice(piece * width, (piece + 1) * width)
                if turned:
                    target[:, cols] = came[piece].astype(F32).T
                else:
                    target[:, cols] = came[piece].astype(F32)

        mine = [
            wire.local(share(tokens_ref, wire.me), arrived.at[wire.me]),
            wire.local(gain_in, arrived_gain.at[wire.me]),
            wire.local(share(cot_in, wire.me), arrived_cot.at[wire.me]),
        ]
        copies = wire.to_all(lambda peer: share(tokens_ref, peer), arrived.at[wire.me])
        copies += wire.to_all(lambda peer: gain_in, arrived_gain.at[wire.me])
        for copy in mine:
            copy.start()
        for copy in mine + copies:
            copy.wait()
        for piece in range(wire.n):
            gains_ref[:, piece * width:(piece + 1) * width] = arrived_gain[piece]

        settle(arrived, resid)
    gains = gains_ref[gain_row:gain_row + 1]
    norm_rows(wire, count, resid, gains, rows_ref)
    spread = Spread(wire, rows_ref, count)
    spread.start()
    wire.loaded()
    collect = Collect(wire, part, got)
    cot_copies = []
    if enter:
        cot_copies = wire.to_all(
            lambda peer: share(cot_in, peer), arrived_cot.at[wire.me]
        )
    wire.early()
    if enter:
        up_job.advance(0)
        spread.relay()
        for step in range(1, up_job.steps):
            up_job.advance(step)
        down_job.begin()
        up_job.end()
        chunks = []
        for chunk, slot in spread.arrivals(relay=False):
            chunks.append((chunk, slot))
            feed_forward_first(count, chunk, rows_ref, up, pre_ref, act.at[len(chunks) - 1])
            if len(chunks) - 1 < down_job.steps:
                down_job.advance(len(chunks) - 1)
        for copy in cot_copies:
            copy.wait()

        settle(arrived_cot, cot_out)
        next_job.begin()
        down_job.end()
        for place, (chunk, slot) in reversed(list(enumerate(chunks))):
            target = part.at[wire.n - 1 if slot is None else slot]
            feed_forward_second(act.at[place], down_t, target)
            if slot is not None:
                collect.send(slot)
            if len(chunks) - 1 - place < next_job.steps:
                next_job.advance(len(chunks) - 1 - place)
        collect.combine()
        for step in range(len(chunks), next_job.steps):
            next_job.advance(step)
    else:
        for chunk, slot in spread.arrivals():
            target = part.at[wire.n - 1 if slot is None else slot]
            feed_forward_first(count, chunk, rows_ref, up, pre_ref, act.at[0])
            feed_forward_second(act.at[0], down_t, target)
            if slot is not None:
                collect.send(slot)
        collect.combine()
    wire.middle()
    wire.flush()
    collect.wait()
    residual(collect, factor, resid, limit_ref[0], after_ref, squares_ref)
    late = []
    if turn:
        final_gains = gains_ref[gain_row + 1:gain_row + 2]
        gain_grad_ref[...] = jnp.zeros_like(gain_grad_ref)

        def final(rows, index):
            normed, inverse = normalize(after_ref[rows])
            cot = cot_ref[rows]
            grad_ref[rows] = norm_back(cot, normed, inverse, final_gains)
            gain_grad_ref[...] += fold8(cot * normed)
            after_ref[rows] = normed * final_gains

        row_loop(count, final)
        late = send_pieces(wire, count, after_ref, pieces, out_ref)
    spread.finish()
    for copy in late:
        copy.wait()
    if enter:
        next_job.end()
    wire.end()


def feed_forward(sizes, name, collective_id, gain_row, up, down_t, limit, resid=None, gains=None,
                 enter=None, turn=None, **side):
    n, m = sizes
    hidden = up.shape[1]
    full = up.shape[0] * (m if enter else 1)
    next_pieces = None
    if enter:
        tokens, cotangent, gain_parts, next_pieces = enter
        turned = tokens.shape[0] * n == full
        width, length = tokens.shape if turned else tokens.shape[::-1]
        count = length // n
        came = (n, width, count) if turned else (n, count, width)
        ins = [(limit, smem()), (tokens, vmem()), (cotangent, vmem())]
        ins += [(part, vmem()) for part in gain_parts] + [(up, vmem()), (down_t, vmem())]
        ins += [(array, vmem()) for array, _ in next_pieces]
        down_shape, next_shape = (full // m, hidden), joined_shape(next_pieces)
        outs = [((count, full), F32, "store"), ((count, full), F32, "store"), ((8, full), F32, vmem())]
        scratch = [
            pltpu.VMEM(came, BF16),
            pltpu.VMEM(came, BF16),
            pltpu.VMEM((n, 8, width), F32),
            pltpu.VMEM((8, width), F32),
            pltpu.VMEM(down_shape, BF16),
            pltpu.VMEM(next_shape, BF16),
        ]
        for shape, spec in ((down_shape, "store"), (down_shape, "store"), (next_shape, hbm())):
            outs.append(((m * shape[0], shape[1]), BF16, spec))
        side = dict(side, more_slots=6 * m, row_on=True)
    else:
        count = resid.shape[0]
        ins = [(limit, smem()), (resid, vmem()), (gains, vmem())]
        outs, scratch = [], []
        ins += [(up, "load"), (down_t, "load")]
    if turn is not None:
        ins.append((turn, "load"))
        outs += [
            ((count, full), F32, vmem()),
            ((8, full), F32, vmem()),
            ((n * count, full // n), BF16, hbm()),
        ]
        scratch.append(pltpu.VMEM((n, count, full // n), BF16))
    if turn is None:
        outs.append(((count, full), F32, vmem()))
    else:
        scratch.append(pltpu.VMEM((count, full), F32))
    outs += [
        ((16, full), F32, vmem()),
        ((n * count, full), BF16, "store"),
        ((n * count, hidden), BF16, "store"),
    ]
    scratch += [
        pltpu.VMEM((n if enter else 1, count, hidden), BF16),
        pltpu.VMEM((n, count, full), BF16),
        pltpu.VMEM((n - 1, count, full), BF16),
    ]
    return comm_call(
        name, collective_id, sizes,
        functools.partial(
            feed_forward_main, count, gain_row, 0.5, enter and [flip for _, flip in next_pieces],
            turn is not None,
        ),
        ins, outs, scratch, **side,
    )


def lane_sum(values):
    total = values[:, 0:BLOCK]
    for at in range(BLOCK, values.shape[1], BLOCK):
        total = total + values[:, at:at + BLOCK]
    return total


def feed_forward_back_main(count, gain_row, leave, wire, ins, outs, scratch):
    grad_ref, resid, gains_ref, up, down_t, rows_ref, pre_ref = ins[:7]
    ins = ins[7:]
    grads, pre_grad, act, part, got = scratch[:5]
    scratch = list(scratch[5:])
    hidden = up.shape[1]
    full = up.shape[0]

    def take(size):
        taken, scratch[:size] = scratch[:size], []
        return taken

    if leave:
        up_width, down_pieces, reduce_sizes = leave
        limit_ref = ins[0]
        gain_parts, squares, table_part, tap_part, depth_part = ins[1:5], ins[5:9], *ins[9:12]
        gain_outs, table_out, rms_out, tap_out, depth_out = outs[:5], *outs[5:9]
        up_out, down_out, last_ref = outs[9:12]
        gain_grad_ref, up_grad_ref, down_grad_ref, new_grad_ref, pieces = take(5)
        width = pieces.shape[2]
        up_job = RowReduce(up_grad_ref, [(hidden, False)], [up_out], *take(reduce_sizes[0]), wire,
                           load=False)
        down_job = RowReduce(down_grad_ref, [(hidden, True)], [down_out], *take(reduce_sizes[1]), wire,
                             load=False)
        gain_pieces, square_parts, first_pieces = take(3)
        items = [
            SumItem(kind, source, *take(4), wire)
            for kind, source in (
                ("piece", gain_pieces), ("all", table_part), ("all", square_parts),
                ("own", tap_part), ("own", depth_part),
            )
        ]
        gain_item = SumItem("piece", first_pieces, *take(4), wire)
    else:
        (tokens_ref,) = ins
        gain_grad_ref, up_grad_ref, down_grad_ref, last_ref, turned_ref = outs
        new_grad_ref = last_ref
        items = []
    gains = gains_ref[gain_row:gain_row + 1]
    wire.greet()
    wire.begin()
    cast_rows(wire, count, grad_ref, 0.5, grads)
    spread = Spread(wire, grads, count)
    spread.start()
    if leave:
        gain_pieces[...] = jnp.zeros_like(gain_pieces)
        square_parts[...] = jnp.zeros_like(square_parts)
        for place, ref in enumerate(gain_parts):
            row = jnp.sum(ref[...], axis=0, keepdims=True)
            for piece in range(wire.n):
                gain_pieces[piece, place:place + 1] = row[:, piece * width:(piece + 1) * width]
        for place, ref in enumerate(squares):
            for at in (0, 1):
                rows = ref[at * 8:(at + 1) * 8]
                square_parts[at * 4 + place:at * 4 + place + 1] = lane_sum(
                    jnp.sum(rows, axis=0, keepdims=True)
                )
        lane = lax.broadcasted_iota(jnp.int32, (1, BLOCK), 1)
        once = jnp.where(wire.me == 0, limit_ref[0], 0)
        square_parts[8:9] = jnp.where(lane == 0, once, 0).astype(F32)
        for item in items:
            item.begin()
    wire.loaded()
    collect = Collect(wire, part, got)
    for chunk, slot in spread.arrivals():
        rows = tile(chunk, count)
        target = part.at[wire.n - 1 if slot is None else slot]
        left = grads[rows]

        def first(cols, index):
            act_grad = matmul(left, down_t[:, cols])
            pre = pre_ref[rows, cols].astype(F32)
            sig = jax.nn.sigmoid(pre)
            act[rows, cols] = (pre * sig).astype(BF16)
            pre_grad[rows, cols] = (act_grad * (sig + pre * sig * (1.0 - sig))).astype(BF16)

        block_loop(hidden, first)
        through = pre_grad[rows]

        def second(cols, index):
            target[:, cols] = matmul_nt(through, up[cols]).astype(BF16)

        block_loop(full, second)
        if slot is not None:
            collect.send(slot)
        if slot is None:
            wire.early()
            for item in items:
                item.early()
            if not leave:
                turned_ref[...] = tokens_ref[...].T
        elif slot == 0:
            for item in items:
                item.middle()
    wire.middle()
    size = min(256, hidden)

    def weight_grad(left_ref, right_ref, out):
        for start in range(0, hidden, size):
            cols = slice(start, start + size)

            def block(rows, index):
                out[rows, cols] = matmul_tn(left_ref[:, rows], right_ref[:, cols]).astype(BF16)

            block_loop(full, block)

    weight_grad(grads, act, down_grad_ref)
    if leave:
        down_job.begin()
    collect.combine()
    weight_grad(rows_ref, pre_grad, up_grad_ref)
    if leave:
        up_job.begin()
        down_job.early()
    wire.flush()
    collect.wait()
    residual_back(collect, grad_ref, resid, gains, new_grad_ref, gain_grad_ref)
    if leave:
        for piece in range(wire.n):
            first_pieces[piece] = gain_grad_ref[:, piece * width:(piece + 1) * width]
        gain_item.begin()
        late = send_pieces(wire, count, new_grad_ref, pieces, last_ref)
        up_job.early()
        gain_item.early()
        for item in items:
            item.end()
        gain_item.middle()
        totals = [item.out for item in items]
        for place, ref in enumerate(gain_outs[1:]):
            ref[...] = totals[0][place:place + 1]
        table = totals[1][...]
        for at in range(HEAD_DIM, table.shape[1], HEAD_DIM):
            table = table[:, 0:HEAD_DIM] + table[:, at:at + HEAD_DIM]
        table_out[...] = table[0:LEFT + RIGHT + 1]
        sums = jnp.sum(totals[2][...], axis=1, keepdims=True)
        rms_out[...] = jnp.broadcast_to(jnp.sqrt(sums[0:8] / (sums[8:9] * full)), rms_out.shape)
        tap_out[...] = totals[3][0:tap_out.shape[0]]
        depth_out[...] = jnp.sum(totals[4][...], axis=0, keepdims=True)
        for copy in late:
            copy.wait()
        wire.end()
        down_job.end()
        gain_item.end()
        gain_outs[0][...] = jnp.sum(gain_item.out[...], axis=0, keepdims=True)
        up_job.end()
    spread.finish()
    if not leave:
        wire.end()


def feed_forward_back(sizes, name, collective_id, gain_row, grad, resid, gains, up, down_t, rows, pre,
                      leave=None, tokens=None, taps=0, **side):
    n, m = sizes
    full, hidden = up.shape
    count = resid.shape[0]
    width = full // n
    ins = [(grad, vmem()), (resid, "load"), (gains, vmem())]
    ins += [(item, "load") for item in (up, down_t, rows, pre)]
    scratch = [
        pltpu.VMEM((n * count, full), BF16),
        pltpu.VMEM((n * count, hidden), BF16),
        pltpu.VMEM((n * count, hidden), BF16),
        pltpu.VMEM((n, count, full), BF16),
        pltpu.VMEM((n - 1, count, full), BF16),
    ]
    extra = None
    if leave:
        limit, gain_parts, squares, table_part, tap_part, depth_part = leave
        layers = m // 2
        ins.append((limit, smem()))
        ins += [(item, vmem()) for item in (*gain_parts, *squares, table_part, tap_part, depth_part)]
        outs = [((1, width), F32, vmem())] * 5
        outs += [
            ((LEFT + RIGHT + 1, HEAD_DIM), F32, vmem()),
            ((8, BLOCK), F32, vmem()),
            ((taps, width), F32, vmem()),
            ((1, width), F32, vmem()),
            ((full // m, hidden), F32, hbm()),
            ((hidden, full // m), F32, hbm()),
            ((n * count, width), BF16, hbm()),
        ]
        scratch += [
            pltpu.VMEM((8, full), F32),
            pltpu.VMEM((full, hidden), BF16),
            pltpu.VMEM((full, hidden), BF16),
            pltpu.VMEM((count, full), F32),
            pltpu.VMEM((n, count, width), BF16),
        ]
        reduces = [
            reduce_scratch(layers, full // m, hidden, [(hidden, flip)]) for flip in (False, True)
        ]
        scratch += reduces[0] + reduces[1]
        extra = (hidden, None, [len(made) for made in reduces])
        scratch += [
            pltpu.VMEM((n, 8, width), F32), pltpu.VMEM((16, BLOCK), F32), pltpu.VMEM((n, 8, width), F32)
        ]
        for shape in ((8, width), table_part.shape, (16, BLOCK), tap_part.shape, depth_part.shape,
                      (8, width)):
            scratch += sum_scratch(n, layers, shape)
        side = dict(side, more_slots=16 * m + 8 * n, row_on=True)
    else:
        ins.append((tokens, "load"))
        outs = [
            ((8, full), F32, vmem()),
            ((full, hidden), BF16, "store"),
            ((full, hidden), BF16, "store"),
            ((count, full), F32, vmem()),
            ((tokens.shape[1], tokens.shape[0]), BF16, "store"),
        ]
    return comm_call(
        name, collective_id, sizes,
        functools.partial(feed_forward_back_main, count, gain_row, extra),
        ins, outs, scratch, **side,
    )


def slot_rows(axis):
    slots = lax.broadcasted_iota(jnp.int32, (LEFT + RIGHT + 8, SPAN), axis)
    signed = jnp.where(slots < SPAN - BLOCK + 1, slots, slots - SPAN)
    return jnp.clip(signed - (BLOCK - LEFT), 0, LEFT + RIGHT)


def extend_table(table, copies):
    slots = jnp.arange(SPAN)
    signed = jnp.where(slots < SPAN - BLOCK + 1, slots, slots - SPAN)
    row_of = jnp.clip(signed - (BLOCK - LEFT), 0, LEFT + RIGHT)
    chosen = (row_of[:, None] == jnp.arange(LEFT + RIGHT + 1)[None, :]).astype(table.dtype)
    return jnp.tile(matmul(chosen, table).astype(table.dtype), (1, copies))


def fill_far(far_ref, table_ref, limit):
    blocks, length, _ = far_ref.shape
    lane = lax.broadcasted_iota(jnp.int32, (1, BLOCK), 1)

    def row(at, mark):
        ends = table_ref[at:at + 1].astype(F32)
        if ends.shape[1] < BLOCK:
            ends = jnp.concatenate([ends, jnp.zeros((1, BLOCK - ends.shape[1]), F32)], axis=1)
        return jnp.where(lane < HEAD_DIM, ends, jnp.where(lane == mark, 1.0, 0.0))

    first = row(0, HEAD_DIM + 1)
    last = row(SPAN - 2 * BLOCK, HEAD_DIM + 2)

    def block(step, carry):
        index, piece = step // (length // BLOCK), lax.rem(step, length // BLOCK)
        at = index * BLOCK
        column = lax.broadcasted_iota(jnp.int32, (BLOCK, 1), 0) + piece * BLOCK
        place = column + at - BLOCK
        key = jnp.where(place < 0, place + length, jnp.where(place >= length, place - length, place))
        near = (column < WINDOW) & (place >= 0) & (place < length)
        left = jnp.where(near | (key >= at), 0.0, 1.0)
        right = jnp.where(near | (key < at), 0.0, 1.0)
        bias = jnp.where(key < limit, 0.0, NEG_FILL)
        terms = left * first + right * last + jnp.where(lane == HEAD_DIM, bias, 0.0)
        far_ref[index, tile(piece, BLOCK)] = terms.astype(BF16)
        return carry

    lax.fori_loop(0, blocks * (length // BLOCK), block, 0)


def duplicate(qkv_ref, width, group, keys, values):
    length = qkv_ref.shape[0]
    for part in range(width // group):
        base = part * group
        for copy in range(2):
            place = slice(copy * length, (copy + 1) * length)
            keys[part, place] = qkv_ref[:, width + base:width + base + group]
            values[part, place] = qkv_ref[:, 2 * width + base:2 * width + base + group]


def by_head(values, group):
    if group == HEAD_DIM:
        return values
    lane = lax.broadcasted_iota(jnp.int32, (BLOCK, group), 1)
    zero = jnp.zeros_like(values)
    return jnp.concatenate(
        [
            jnp.where((lane >= at) & (lane < at + HEAD_DIM), values, zero)
            for at in range(0, group, HEAD_DIM)
        ],
        axis=0,
    )


def own_lanes(values, group):
    if group == HEAD_DIM:
        return values
    lane = lax.broadcasted_iota(jnp.int32, (BLOCK, group), 1)
    return jnp.where(lane < HEAD_DIM, values[0:BLOCK], values[BLOCK:2 * BLOCK])


def far_queries(values, group):
    wide = values.astype(F32)
    if group == HEAD_DIM:
        lane = lax.broadcasted_iota(jnp.int32, (BLOCK, BLOCK - HEAD_DIM), 1)
        return jnp.concatenate([wide, jnp.where(lane == 0, 1.0, 0.0)], axis=1).astype(BF16)
    lane = lax.broadcasted_iota(jnp.int32, (BLOCK, BLOCK), 1)
    rest = jnp.where(lane == HEAD_DIM, 1.0, 0.0)
    return jnp.concatenate(
        [
            jnp.where(lane < HEAD_DIM, wide, rest),
            jnp.where(lane < HEAD_DIM, pltpu.roll(wide, HEAD_DIM, 1), rest),
        ],
        axis=0,
    ).astype(BF16)


def near_mask(at, length):
    place = lax.broadcasted_iota(jnp.int32, (1, WINDOW), 1) + (at - BLOCK)
    return (place >= 0) & (place < length)


def near_terms(query, table, at, length):
    terms = matmul_nt(query, table)
    halves = [
        pltpu.roll(terms[start:start + BLOCK], 0, 1, stride=1, stride_axis=0)[:, :WINDOW]
        for start in range(0, query.shape[0], BLOCK)
    ]
    return jnp.where(near_mask(at, length), jnp.concatenate(halves, axis=0), 0.0)


def attend_blocks(first, blocks, width, group, qkv_ref, table_ref, far_ref, keys, values, context_ref,
                  log_ref):
    length = qkv_ref.shape[0]
    heads = group // HEAD_DIM
    parts = width // group
    scale = 1.0 / math.sqrt(HEAD_DIM)

    def block(step, carry):
        index, part = first + step // parts, lax.rem(step, parts)
        at = pl.multiple_of(index * BLOCK, BLOCK)
        rows = pl.ds(at, BLOCK)
        cols = tile(part, group) if parts > 1 else slice(0, group)
        window = pl.ds(pl.multiple_of(lax.rem(at + length - BLOCK, length), BLOCK), length)
        query_rows = qkv_ref[rows, cols] * jnp.asarray(scale, BF16)
        query = by_head(query_rows, group)
        extra = far_queries(query_rows, group)
        if group == 2 * HEAD_DIM:
            scores = matmul_nt(
                jnp.concatenate([query, extra], axis=1),
                jnp.concatenate([keys[part, window], far_ref[index]], axis=1),
            )
        else:
            scores = matmul_nt(query, keys[part, window]) + matmul_nt(extra, far_ref[index])
        near = scores[:, :WINDOW] + near_terms(query, table_ref[...], at, length)
        scores = jnp.concatenate([near, scores[:, WINDOW:]], axis=1)
        peak = jnp.max(scores, axis=1, keepdims=True)
        weights = jnp.exp(scores - peak)
        total = jnp.sum(weights, axis=1, keepdims=True)
        mixed = matmul(weights.astype(BF16), values[part, window]) * (1.0 / total)
        context_ref[rows, cols] = own_lanes(mixed, group).astype(BF16)
        log = peak + jnp.log(total)
        lane = lax.broadcasted_iota(jnp.int32, (BLOCK, BLOCK), 1)
        square = jnp.where(lane == 0, log[0:BLOCK], 0.0)
        for head in range(1, heads):
            square = jnp.where(lane == head, log[head * BLOCK:(head + 1) * BLOCK], square)
        log_ref[part, :, rows] = square.T[0:8]
        return carry

    lax.fori_loop(0, blocks * parts, block, 0)


def attend_back_core(width, group, qkv_ref, table_ref, far_ref, log_ref, grad_ref, out_ref,
                     table_grad_ref, keys, values, key_grad, value_grad, slot_grad, end_grad):
    length = qkv_ref.shape[0]
    heads = group // HEAD_DIM
    parts = width // group
    scale = 1.0 / math.sqrt(HEAD_DIM)
    duplicate(qkv_ref, width, group, keys, values)
    slot_grad[...] = jnp.zeros_like(slot_grad)
    end_grad[...] = jnp.zeros_like(end_grad)
    key_grad[...] = jnp.zeros_like(key_grad)
    value_grad[...] = jnp.zeros_like(value_grad)
    down = lax.broadcasted_iota(jnp.int32, (BLOCK, BLOCK), 0)
    across = lax.broadcasted_iota(jnp.int32, (BLOCK, BLOCK), 1)
    reverse = jnp.where(down + across == BLOCK - 1, 1.0, 0.0).astype(BF16)

    def flip(values_in):
        return jnp.concatenate(
            [
                matmul(reverse, values_in[start:start + BLOCK])
                for start in range(0, heads * BLOCK, BLOCK)
            ],
            axis=0,
        )

    def block(step, carry):
        index, part = step // parts, lax.rem(step, parts)
        at = pl.multiple_of(index * BLOCK, BLOCK)
        rows = pl.ds(at, BLOCK)
        cols = tile(part, group) if parts > 1 else slice(0, group)
        window = pl.ds(pl.multiple_of(lax.rem(at + length - BLOCK, length), BLOCK), length)
        key_rows = keys[part, window]
        far_rows = far_ref[index]
        query_rows = qkv_ref[rows, cols] * jnp.asarray(scale, BF16)
        query = by_head(query_rows, group)
        extra = far_queries(query_rows, group)
        grad = by_head(grad_ref[rows, cols], group)
        if group == 2 * HEAD_DIM:
            key_wide = jnp.concatenate([key_rows, far_rows], axis=1)
            scores = matmul_nt(key_wide, jnp.concatenate([query, extra], axis=1))
        else:
            scores = matmul_nt(key_rows, query) + matmul_nt(far_rows, extra)
        near = scores[:WINDOW] + near_terms(query, table_ref[...], at, length).T
        scores = jnp.concatenate([near, scores[WINDOW:]], axis=0)
        log = jnp.concatenate([log_ref[part, head:head + 1, rows] for head in range(heads)], axis=1)
        probs = jnp.exp(scores - log)
        prob_grad = matmul_nt(values[part, window], grad)
        row_dot = jnp.sum(probs * prob_grad, axis=0, keepdims=True)
        score_grad = (probs * (prob_grad - row_dot)).astype(BF16)
        value_grad[part, window] += matmul(probs.astype(BF16), grad)
        key_grad[part, window] += matmul(score_grad, query)
        turned_back = score_grad.T
        if group == 2 * HEAD_DIM:
            both = matmul(turned_back, key_wide)
            direct, ends = both[:, :group], both[:, group:]
        else:
            direct, ends = matmul(turned_back, key_rows), matmul(turned_back, far_rows)
        left_sum, right_sum = ends[:, HEAD_DIM + 1:HEAD_DIM + 2], ends[:, HEAD_DIM + 2:HEAD_DIM + 3]
        query_wide = query.astype(F32)
        end_grad[0:8] += fold8(left_sum * query_wide)
        end_grad[8:16] += fold8(right_sum * query_wide)
        near_grad = jnp.where(
            near_mask(at, length), turned_back[:, :WINDOW], jnp.asarray(0.0, BF16)
        )
        flipped = flip(near_grad)
        skewed = []
        for start in range(0, heads * BLOCK, BLOCK):
            padded = jnp.concatenate(
                [flipped[start:start + BLOCK], jnp.zeros((BLOCK, SPAN - WINDOW), F32)], axis=1
            )
            skewed.append(pltpu.roll(padded, SPAN - (BLOCK - 1), 1, stride=1, stride_axis=0))
        straight = jnp.concatenate(skewed, axis=0).astype(BF16)
        term = matmul(straight, table_ref[...])
        high = term.astype(BF16)
        low = (term - high.astype(F32)).astype(BF16)
        direct = direct + flip(high) + flip(low)
        result = own_lanes(direct, group)
        if heads == 1:
            result = result + ends[:, :HEAD_DIM]
        else:
            lane = lax.broadcasted_iota(jnp.int32, (BLOCK, BLOCK), 1)
            result = result + jnp.where(
                lane < HEAD_DIM, ends[0:BLOCK], pltpu.roll(ends[BLOCK:2 * BLOCK], HEAD_DIM, 1)
            )
        out_ref[rows, cols] = (result * scale).astype(BF16)
        slot_grad[...] += matmul_tn(flip(query).astype(BF16), straight)
        return carry

    lax.fori_loop(0, length // BLOCK * parts, block, 0)
    for part in range(parts):
        base = width + part * group
        out_ref[:, base:base + group] = (
            key_grad[part, 0:length] + key_grad[part, length:2 * length]
        ).astype(BF16)
        out_ref[:, width + base:width + base + group] = (
            value_grad[part, 0:length] + value_grad[part, length:2 * length]
        ).astype(BF16)
    chosen = jnp.where(
        slot_rows(1) == lax.broadcasted_iota(jnp.int32, (LEFT + RIGHT + 8, SPAN), 0), 1.0, 0.0
    )
    table_grad_ref[...] = lax.dot_general(
        chosen, slot_grad[...], (((1,), (1,)), ((), ())), precision=lax.Precision.HIGHEST,
        preferred_element_type=F32,
    )
    table_grad_ref[0:1] += jnp.sum(end_grad[0:8], axis=0, keepdims=True)
    table_grad_ref[LEFT + RIGHT:LEFT + RIGHT + 1] += jnp.sum(end_grad[8:16], axis=0, keepdims=True)


def attention_main(count, gain_row, wire, ins, outs, scratch):
    limit_ref, resid, gains_ref, weights, table_ref = ins
    after_ref, squares_ref, rows_ref, qkv_ref, context_ref, log_ref = outs
    far_ref, keys, values, part, got = scratch
    width = context_ref.shape[1]
    group = keys.shape[2]
    wire.greet()
    wire.begin()
    norm_rows(wire, count, resid, gains_ref[gain_row:gain_row + 1], rows_ref)
    spread = Spread(wire, rows_ref, count)
    spread.start()
    wire.loaded()
    collect = Collect(wire, part, got)
    spread.relay()
    wire.early()
    fill_far(far_ref, table_ref, limit_ref[0])
    chunks = []
    for chunk, slot in spread.arrivals(relay=False):
        chunks.append((chunk, slot))
        rows = tile(chunk, count)
        left = rows_ref[rows]

        def project(cols, index):
            qkv_ref[rows, cols] = matmul(left, weights[:, cols]).astype(BF16)

        block_loop(3 * width, project)
    duplicate(qkv_ref, width, group, keys, values)
    size = max(count, BLOCK)
    for chunk, slot in reversed(chunks):
        first = chunk * count // BLOCK
        attend_blocks(first, size // BLOCK, width, group, qkv_ref, table_ref, far_ref, keys, values,
                      context_ref, log_ref)
        target = part.at[wire.n - 1 if slot is None else slot]
        left = context_ref[tile(chunk, count)]

        def leave(cols, index):
            target[:, cols] = matmul_nt(left, weights[cols, 3 * width:]).astype(BF16)

        block_loop(weights.shape[0], leave)
        if slot is not None:
            collect.send(slot)
        if slot == 0:
            collect.combine()
            wire.middle()
    wire.flush()
    collect.wait()
    residual(collect, 1.0, resid, limit_ref[0], after_ref, squares_ref)
    spread.finish()
    wire.end()


def attention(sizes, name, collective_id, gain_row, limit, resid, gains, weights, table, **side):
    n, m = sizes
    count, full = resid.shape
    length, width = n * count, weights.shape[1] // 4
    group = min(2 * HEAD_DIM, width)
    return comm_call(
        name, collective_id, sizes, functools.partial(attention_main, count, gain_row),
        [(limit, smem()), (resid, vmem()), (gains, vmem()), (weights, "load"), (table, "load")],
        [
            ((count, full), F32, vmem()),
            ((16, full), F32, vmem()),
            ((length, full), BF16, "store"),
            ((length, 3 * width), BF16, "store"),
            ((length, width), BF16, "store"),
            ((width // group, 8, length), F32, "store"),
        ],
        [
            pltpu.VMEM((length // BLOCK, length, BLOCK), BF16),
            pltpu.VMEM((width // group, 2 * length, group), BF16),
            pltpu.VMEM((width // group, 2 * length, group), BF16),
            pltpu.VMEM((n, count, full), BF16),
            pltpu.VMEM((n - 1, count, full), BF16),
        ],
        cost=20 * 10**9, **side,
    )


def attention_back_main(count, gain_row, wire, ins, outs, scratch):
    (limit_ref, grad_ref, resid, gains_ref, weights, table_ref, rows_ref, qkv_ref, context_ref,
     log_ref) = ins
    gain_grad_ref, wide_ref, table_grad_ref, new_grad_ref = outs
    (far_ref, grads, context_grad, qkv_grad, keys, values, key_grad, value_grad, slot_grad, end_grad, part,
     got) = scratch
    width = context_ref.shape[1]
    group = keys.shape[2]
    wire.greet()
    wire.begin()
    cast_rows(wire, count, grad_ref, 1.0, grads)
    spread = Spread(wire, grads, count)
    spread.start()
    wire.loaded()
    collect = Collect(wire, part, got)
    spread.relay()
    wire.early()
    fill_far(far_ref, table_ref, limit_ref[0])
    chunks = []
    for chunk, slot in spread.arrivals(relay=False):
        chunks.append((chunk, slot))
        rows = tile(chunk, count)
        context_grad[rows] = matmul(grads[rows], weights[:, 3 * width:]).astype(BF16)
    wire.middle()
    attend_back_core(width, group, qkv_ref, table_ref, far_ref, log_ref, context_grad, qkv_grad,
                     table_grad_ref, keys, values, key_grad, value_grad, slot_grad, end_grad)
    for chunk, slot in reversed(chunks):
        target = part.at[wire.n - 1 if slot is None else slot]
        left = qkv_grad[tile(chunk, count)]

        def back(cols, index):
            target[:, cols] = matmul_nt(left, weights[cols, :3 * width]).astype(BF16)

        block_loop(weights.shape[0], back)
        if slot is not None:
            collect.send(slot)
    collect.combine()

    def weight_grads(rows, index):
        wide_ref[rows, :3 * width] = matmul_tn(rows_ref[:, rows], qkv_grad[...]).astype(BF16)
        wide_ref[rows, 3 * width:] = matmul_tn(grads[:, rows], context_ref[...]).astype(BF16)

    block_loop(weights.shape[0], weight_grads)
    wire.flush()
    wire.end()
    collect.wait()
    residual_back(collect, grad_ref, resid, gains_ref[gain_row:gain_row + 1], new_grad_ref,
                  gain_grad_ref)
    spread.finish()


def attention_back(sizes, name, collective_id, gain_row, limit, grad, resid, gains, weights, table, rows,
                   qkv, context, log_total, **side):
    n, m = sizes
    count, full = resid.shape
    length, width = context.shape
    group = min(2 * HEAD_DIM, width)
    return comm_call(
        name, collective_id, sizes, functools.partial(attention_back_main, count, gain_row),
        [(limit, smem()), (grad, vmem()), (resid, "load"), (gains, vmem())]
        + [(item, "load") for item in (weights, table, rows, qkv, context, log_total)],
        [
            ((8, full), F32, vmem()),
            ((full, 4 * width), BF16, "store"),
            ((LEFT + RIGHT + 8, group), F32, vmem()),
            ((count, full), F32, vmem()),
        ],
        [
            pltpu.VMEM((length // BLOCK, length, BLOCK), BF16),
            pltpu.VMEM((length, full), BF16),
            pltpu.VMEM((length, width), BF16),
            pltpu.VMEM((length, 3 * width), BF16),
            pltpu.VMEM((width // group, 2 * length, group), BF16),
            pltpu.VMEM((width // group, 2 * length, group), BF16),
            pltpu.VMEM((width // group, 2 * length, group), F32),
            pltpu.VMEM((width // group, 2 * length, group), F32),
            pltpu.VMEM((group, SPAN), F32),
            pltpu.VMEM((16, group), F32),
            pltpu.VMEM((n, count, full), BF16),
            pltpu.VMEM((n - 1, count, full), BF16),
        ],
        cost=50 * 10**9, **side,
    )


PAD = 32
ROWS = 64


def shifted_sets(held, low, high, size):
    for residue in range(8):
        shifts = [shift for shift in range(low, high + 1) if shift % 8 == residue]
        if shifts:
            extent = shifts[-1] - residue + size
            moved = held[residue:residue + extent]
            for shift in shifts:
                yield shift, moved[shift - residue:shift - residue + size]


def stat_rows(blocks, first, second, stats_ref):
    lane = lax.broadcasted_iota(jnp.int32, (BLOCK, BLOCK), 1)
    both = jnp.where(lane == 0, first, jnp.where(lane == 1, second, 0.0))
    stats_ref[:, blocks] = both.T[0:8]


def stat_columns(stats):
    both = jnp.concatenate([stats, jnp.zeros((BLOCK - 8, BLOCK), F32)], axis=0).T
    return both[:, 0:1], both[:, 1:2]


class Stats:
    def __init__(self, wire, mine, got):
        self.wire, self.mine, self.got = wire, mine, got
        self.copies = [
            wire.remote(mine, got.at[step - 1], "col", lax.rem(wire.me + step, wire.n))
            for step in range(1, wire.n)
        ]

    def total(self):
        for copy in self.copies:
            copy.start()
        for copy in self.copies:
            copy.wait()
        total = self.mine[...]
        for step in range(self.wire.n - 1):
            total = total + self.got[step]
        return total


def token_blocks(length, body):
    def step(index, carry):
        body(tile(index, BLOCK), index)
        return carry

    lax.fori_loop(0, length // BLOCK, step, 0)


def convolution_main(count, gain_row, taps, wire, ins, outs, scratch):
    limit_ref, resid, gains_ref, weights, taps_ref, depth_ref = ins
    after_ref, squares_ref, rows_ref, pre_ref, mixed_ref, stats_ref = outs
    kernel_ref, padded, stats_mine, stats_got, act, part, got = scratch
    length, width = mixed_ref.shape
    full = gains_ref.shape[1]
    wire.greet()
    wire.begin()
    norm_rows(wire, count, resid, gains_ref[gain_row:gain_row + 1], rows_ref)
    spread = Spread(wire, rows_ref, count)
    spread.start()
    wire.loaded()
    collect = Collect(wire, part, got)
    stats = Stats(wire, stats_mine, stats_got)
    padded[0:PAD] = jnp.zeros((PAD, width), F32)
    kernel_ref[0:taps] = taps_ref[...].astype(F32)
    spread.relay()
    wire.early()
    chunks = []
    for chunk, slot in spread.arrivals(relay=False):
        chunks.append((chunk, slot))
        rows = tile(chunk, count)
        left = rows_ref[rows]
        value_pre = matmul(left, weights[:, 0:width])
        gate_pre = matmul(left, weights[:, width:2 * width])
        pre_ref[rows, 0:width] = value_pre.astype(BF16)
        pre_ref[rows, width:2 * width] = gate_pre.astype(BF16)
        at = pl.multiple_of(chunk * count + PAD, PAD)
        keep = keep_rows(limit_ref[0], chunk * count, count)
        padded[pl.ds(at, count)] = value_pre * jax.nn.sigmoid(gate_pre) * keep

    def mix(index, carry):
        held = padded[pl.ds(pl.multiple_of(index * ROWS, ROWS), ROWS + PAD)]
        total = jnp.zeros((ROWS, width), F32)
        for shift, moved in shifted_sets(held, PAD - taps + 1, PAD, ROWS):
            tap = shift - (PAD - taps + 1)
            total = total + moved * kernel_ref[tap:tap + 1]
        mixed_ref[tile(index, ROWS)] = total
        return carry

    lax.fori_loop(0, length // ROWS, mix, 0)

    def sums(rows, index):
        mixed = mixed_ref[rows]
        stat_rows(rows, jnp.sum(mixed, axis=1, keepdims=True),
                  jnp.sum(mixed * mixed, axis=1, keepdims=True), stats_mine)

    token_blocks(length, sums)
    total = stats.total() * (1.0 / full)
    inverse = lax.rsqrt(total[1:2] - total[0:1] * total[0:1] + EPSILON)
    stats_ref[...] = jnp.concatenate([total[0:1], inverse, total[2:]], axis=0)

    def activate(rows, index):
        mean, scale = stat_columns(stats_ref[:, rows])
        scaled = (mixed_ref[rows] - mean) * scale * depth_ref[...]
        act[rows] = (scaled * jax.nn.sigmoid(scaled)).astype(BF16)

    token_blocks(length, activate)
    wire.middle()
    for chunk, slot in reversed(chunks):
        target = part.at[wire.n - 1 if slot is None else slot]
        left = act[tile(chunk, count)]

        def leave(cols, index):
            target[:, cols] = matmul_nt(left, weights[cols, 2 * width:]).astype(BF16)

        block_loop(weights.shape[0], leave)
        if slot is not None:
            collect.send(slot)
    collect.combine()
    wire.flush()
    collect.wait()
    residual(collect, 1.0, resid, limit_ref[0], after_ref, squares_ref)
    spread.finish()
    wire.end()


def convolution(sizes, name, collective_id, gain_row, limit, resid, gains, weights, kernel, depth_gain,
                **side):
    n, m = sizes
    count, full = resid.shape
    length, width = n * count, weights.shape[1] // 3
    return comm_call(
        name, collective_id, sizes,
        functools.partial(convolution_main, count, gain_row, kernel.shape[0]),
        [(limit, smem()), (resid, vmem()), (gains, vmem()), (weights, "load"), (kernel, vmem()),
         (depth_gain, vmem())],
        [
            ((count, full), F32, vmem()),
            ((16, full), F32, vmem()),
            ((length, full), BF16, "store"),
            ((length, 2 * width), BF16, "store"),
            ((length, width), F32, "store"),
            ((8, length), F32, "store"),
        ],
        [
            pltpu.VMEM((PAD, width), F32),
            pltpu.VMEM((length + PAD, width), F32),
            pltpu.VMEM((8, length), F32),
            pltpu.VMEM((n - 1, 8, length), F32),
            pltpu.VMEM((length, width), BF16),
            pltpu.VMEM((n, count, full), BF16),
            pltpu.VMEM((n - 1, count, full), BF16),
        ],
        cost=15 * 10**9, **side,
    )


def convolution_back_main(count, gain_row, taps, wire, ins, outs, scratch):
    (limit_ref, grad_ref, resid, gains_ref, weights, taps_ref, depth_ref, rows_ref, pre_ref, mixed_ref,
     stats_ref) = ins
    gain_grad_ref, wide_ref, kernel_grad_ref, depth_grad_ref, new_grad_ref = outs
    (kernel_ref, grads, padded, padded_grad, stats_mine, stats_got, sums_ref, act, pre_grad, part, got) = scratch
    length, width = mixed_ref.shape
    full = gains_ref.shape[1]
    wire.greet()
    wire.begin()
    cast_rows(wire, count, grad_ref, 1.0, grads)
    spread = Spread(wire, grads, count)
    spread.start()
    wire.loaded()
    collect = Collect(wire, part, got)
    stats = Stats(wire, stats_mine, stats_got)
    padded[0:PAD] = jnp.zeros((PAD, width), F32)
    padded_grad[length:] = jnp.zeros((PAD, width), F32)
    sums_ref[...] = jnp.zeros_like(sums_ref)
    depth_grad_ref[...] = jnp.zeros_like(depth_grad_ref)
    kernel_ref[0:taps] = taps_ref[...].astype(F32)
    kernel_grad_ref[...] = jnp.zeros_like(kernel_grad_ref)
    spread.relay()

    def regate(rows, index):
        value_pre = pre_ref[rows, 0:width].astype(F32)
        gate_pre = pre_ref[rows, width:2 * width].astype(F32)
        at = pl.multiple_of(index * BLOCK + PAD, PAD)
        keep = keep_rows(limit_ref[0], index * BLOCK, BLOCK)
        padded[pl.ds(at, BLOCK)] = value_pre * jax.nn.sigmoid(gate_pre) * keep

    token_blocks(length, regate)
    wire.early()
    chunks = []
    for chunk, slot in spread.arrivals(relay=False):
        chunks.append((chunk, slot))
        rows = tile(chunk, count)
        padded_grad[rows] = matmul(grads[rows], weights[:, 2 * width:])
    wire.middle()

    def first(rows, index):
        mean, scale = stat_columns(stats_ref[:, rows])
        normed = (mixed_ref[rows] - mean) * scale
        scaled = normed * depth_ref[...]
        sig = jax.nn.sigmoid(scaled)
        act[rows] = (scaled * sig).astype(BF16)
        scaled_grad = padded_grad[rows] * (sig + scaled * sig * (1.0 - sig))
        depth_grad_ref[...] += fold8(scaled_grad * normed)
        weighted = scaled_grad * depth_ref[...]
        padded_grad[rows] = weighted
        stat_rows(rows, jnp.sum(weighted, axis=1, keepdims=True),
                  jnp.sum(weighted * normed, axis=1, keepdims=True), stats_mine)

    token_blocks(length, first)
    total = stats.total() * (1.0 / full)
    stats_mine[...] = total

    def second(rows, index):
        mean, scale = stat_columns(stats_ref[:, rows])
        normed = (mixed_ref[rows] - mean) * scale
        one, two = stat_columns(stats_mine[:, rows])
        padded_grad[rows] = scale * (padded_grad[rows] - one - normed * two)

    token_blocks(length, second)

    def unmix(index, carry):
        rows = tile(index, ROWS)
        around = pl.ds(pl.multiple_of(index * ROWS, ROWS), ROWS + PAD)
        ahead = padded_grad[around]
        total = jnp.zeros((ROWS, width), F32)
        for shift, moved in shifted_sets(ahead, 0, taps - 1, ROWS):
            tap = taps - 1 - shift
            total = total + moved * kernel_ref[tap:tap + 1]
        here = ahead[0:ROWS]
        for shift, moved in shifted_sets(padded[around], PAD - taps + 1, PAD, ROWS):
            tap = shift - (PAD - taps + 1)
            sums_ref[tap * 8:(tap + 1) * 8] += fold8(here * moved)
        gate = jax.nn.sigmoid(pre_ref[rows, width:2 * width].astype(F32))
        through = total * keep_rows(limit_ref[0], index * ROWS, ROWS) * gate
        pre_grad[rows, 0:width] = through.astype(BF16)
        pre_grad[rows, width:2 * width] = (
            through * pre_ref[rows, 0:width].astype(F32) * (1.0 - gate)
        ).astype(BF16)
        return carry

    lax.fori_loop(0, length // ROWS, unmix, 0)
    for tap in range(taps):
        kernel_grad_ref[tap:tap + 1] = jnp.sum(sums_ref[tap * 8:(tap + 1) * 8], axis=0, keepdims=True)
    for chunk, slot in reversed(chunks):
        target = part.at[wire.n - 1 if slot is None else slot]
        left = pre_grad[tile(chunk, count)]

        def back(cols, index):
            target[:, cols] = matmul_nt(left, weights[cols, :2 * width]).astype(BF16)

        block_loop(weights.shape[0], back)
        if slot is not None:
            collect.send(slot)
    collect.combine()

    def weight_grads(rows, index):
        wide_ref[rows, :2 * width] = matmul_tn(rows_ref[:, rows], pre_grad[...]).astype(BF16)
        wide_ref[rows, 2 * width:] = matmul_tn(grads[:, rows], act[...]).astype(BF16)

    block_loop(weights.shape[0], weight_grads)
    wire.flush()
    wire.end()
    collect.wait()
    residual_back(collect, grad_ref, resid, gains_ref[gain_row:gain_row + 1], new_grad_ref,
                  gain_grad_ref)
    spread.finish()


def convolution_back(sizes, name, collective_id, gain_row, limit, grad, resid, gains, weights, kernel,
                     depth_gain, rows, pre, mixed, stats, **side):
    n, m = sizes
    count, full = resid.shape
    length, width = mixed.shape
    taps = kernel.shape[0]
    return comm_call(
        name, collective_id, sizes,
        functools.partial(convolution_back_main, count, gain_row, taps),
        [(limit, smem()), (grad, vmem()), (resid, "load"), (gains, vmem()), (weights, "load"),
         (kernel, vmem()), (depth_gain, vmem())]
        + [(item, "load") for item in (rows, pre, mixed, stats)],
        [
            ((8, full), F32, vmem()),
            ((full, 3 * width), BF16, "store"),
            ((PAD, width), F32, vmem()),
            ((8, width), F32, vmem()),
            ((count, full), F32, vmem()),
        ],
        [
            pltpu.VMEM((PAD, width), F32),
            pltpu.VMEM((length, full), BF16),
            pltpu.VMEM((length + PAD, width), F32),
            pltpu.VMEM((length + PAD, width), F32),
            pltpu.VMEM((8, length), F32),
            pltpu.VMEM((n - 1, 8, length), F32),
            pltpu.VMEM((8 * taps, width), F32),
            pltpu.VMEM((length, width), BF16),
            pltpu.VMEM((length, 2 * width), BF16),
            pltpu.VMEM((n, count, full), BF16),
            pltpu.VMEM((n - 1, count, full), BF16),
        ],
        cost=20 * 10**9, **side,
    )


def results_kernel(*refs):
    sources, targets = refs[:len(refs) // 2], refs[len(refs) // 2:]
    for source, target in zip(sources, targets):
        if source.shape != target.shape:
            target[...] = source[...].astype(target.dtype).T
        else:
            target[...] = source[...]


def results(arrays, shapes):
    return pl.pallas_call(
        results_kernel,
        name="results",
        out_shape=tuple(shapes),
        in_specs=[vmem()] * len(arrays),
        out_specs=tuple(vmem() for _ in arrays),
        compiler_params=pltpu.CompilerParams(vmem_limit_bytes=VMEM_LIMIT),
    )(*arrays)


def body(
    layer_input,
    clip_lengths,
    first_gain,
    first_up,
    first_down,
    attend_gain,
    query_weight,
    key_weight,
    value_weight,
    output_weight,
    distance_table,
    conv_gain,
    pointwise_value,
    pointwise_gate,
    depthwise_kernel,
    depthwise_gain,
    pointwise_out,
    second_gain,
    second_up,
    second_down,
    final_gain,
    output_cotangent,
):
    n = lax.axis_size("col")
    me = lax.axis_index("col")
    width, length = layer_input.shape
    full = n * width
    count = length // n

    sizes = (n, lax.axis_size("row"))
    group = min(2 * HEAD_DIM, width)
    table_wide = extend_table(distance_table, group // HEAD_DIM)
    limit = clip_lengths
    tap_count = depthwise_kernel.shape[0]
    gain_parts = [
        gain[None] for gain in (first_gain, attend_gain, conv_gain, second_gain, final_gain)
    ]
    attend_pieces = [
        (query_weight, False), (key_weight, False), (value_weight, False), (output_weight, True)
    ]
    conv_pieces = [(pointwise_value, False), (pointwise_gate, False), (pointwise_out, True)]
    hidden = first_up.shape[1]
    tokens_in = (layer_input, output_cotangent)
    if count % BLOCK:
        tokens_in = (layer_input.T, output_cotangent.T)

    (start, cot, gains, up_first, down_first, attend_weights, after_first, squares_first, rows_first,
     pre_first) = feed_forward(
        sizes, "first", 1, 0, first_up, first_down, limit,
        enter=(*tokens_in, gain_parts, attend_pieces),
    )
    (after_attend, squares_attend, rows_attend, qkv, context, log_total, conv_weights,
     up_second) = attention(
        sizes, "attend", 2, 1, limit, after_first, gains, attend_weights, table_wide,
        gathers=[conv_pieces, [(second_up, False)]],
    )
    depth_row = depthwise_gain[None]
    (after_conv, squares_conv, rows_conv, conv_pre, mixed, stats, down_second) = convolution(
        sizes, "convolve", 3, 2, limit, after_attend, gains, conv_weights, depthwise_kernel, depth_row,
        gathers=[[(second_down, True)]],
    )
    (grad_second, final_part, out_tokens, squares_second, rows_second, pre_second) = feed_forward(
        sizes, "second", 4, 3, up_second, down_second, limit, resid=after_conv, gains=gains, turn=cot
    )

    second_part, second_up_wide, second_down_wide, grad_conv, layer_output = feed_forward_back(
        sizes, "second_back", 5, 3, grad_second, after_conv, gains, up_second, down_second,
        rows_second, pre_second, tokens=out_tokens,
    )
    conv_part, conv_wide, kernel_part, depth_part, grad_attend, second_up_grad = convolution_back(
        sizes, "convolve_back", 6, 2, limit, grad_conv, after_attend, gains, conv_weights,
        depthwise_kernel, depth_row, rows_conv, conv_pre, mixed, stats,
        reduces=[(second_up_wide, [(hidden, False)])],
    )
    (attend_part, attend_wide, table_part, grad_first, second_down_grad, value_grad, gate_grad,
     out_grad) = attention_back(
        sizes, "attend_back", 7, 1, limit, grad_attend, after_first, gains, attend_weights,
        table_wide, rows_attend, qkv, context, log_total,
        reduces=[
            (second_down_wide, [(hidden, True)]),
            (conv_wide, [(width, False), (width, False), (width, True)]),
        ],
    )
    (first_sum, attend_sum, conv_sum, second_sum, final_sum, table_sum, masked_rms, kernel_sum,
     depth_sum, first_up_grad, first_down_grad, grad_tokens, query_grad, key_grad, attend_value_grad,
     output_grad) = feed_forward_back(
        sizes, "first_back", 0, 0, grad_first, start, gains, up_first, down_first, rows_first,
        pre_first, taps=tap_count,
        leave=(
            limit, (attend_part, conv_part, second_part, final_part),
            (squares_first, squares_attend, squares_conv, squares_second), table_part, kernel_part,
            depth_part,
        ),
        reduces=[(attend_wide, [(width, False), (width, False), (width, False), (width, True)])],
    )

    arrays = [
        layer_output, grad_tokens, first_sum, first_up_grad, first_down_grad, attend_sum, query_grad,
        key_grad, attend_value_grad, output_grad, table_sum, conv_sum, value_grad, gate_grad, kernel_sum,
        depth_sum, out_grad, second_sum, second_up_grad, second_down_grad, final_sum, masked_rms,
    ]
    shapes = [jax.ShapeDtypeStruct(array.shape, array.dtype) for array in arrays]
    shapes[1] = jax.ShapeDtypeStruct(grad_tokens.shape[::-1], F32)
    arrays = results(arrays, shapes)
    outputs = [array[0] if array.shape[0] == 1 else array for array in arrays]
    return (*outputs[:-1], outputs[-1][:, 0])


def solution(mesh):
    in_specs = (
        P("col", "row"),
        P("row"),
        P("col"),
        P("row", "col"),
        P("col", "row"),
        P("col"),
        P("row", "col"),
        P("row", "col"),
        P("row", "col"),
        P("col", "row"),
        P(),
        P("col"),
        P("row", "col"),
        P("row", "col"),
        P(None, "col"),
        P("col"),
        P("col", "row"),
        P("col"),
        P("row", "col"),
        P("col", "row"),
        P("col"),
        P("col", "row"),
    )
    out_specs = (
        P("col", "row"),
        P("col", "row"),
        P("col"),
        P("row", "col"),
        P("col", "row"),
        P("col"),
        P("row", "col"),
        P("row", "col"),
        P("row", "col"),
        P("col", "row"),
        P(),
        P("col"),
        P("row", "col"),
        P("row", "col"),
        P(None, "col"),
        P("col"),
        P("col", "row"),
        P("col"),
        P("row", "col"),
        P("col", "row"),
        P("col"),
        P(),
    )
    return jax.shard_map(body, mesh=mesh, in_specs=in_specs, out_specs=out_specs, check_vma=False)
```

```python
import functools
import math

import jax
import jax.numpy as jnp
from jax import lax
from jax.experimental import pallas as pl
from jax.experimental.pallas import tpu as pltpu
from jax.sharding import PartitionSpec as P

HEAD_DIM = 64
LEFT = 64
RIGHT = 8
EPSILON = 1e-05
NEG_FILL = -1e30
BF16 = jnp.bfloat16
F32 = jnp.float32
MESH = pl.DeviceIdType.MESH
BLOCK = 128
WINDOW = 384
SPAN = 512
VMEM_LIMIT = 60 * 1024 * 1024
MARGIN = 6 * 1024 * 1024


def matmul(left, right):
    return jnp.dot(left, right, preferred_element_type=F32)


def matmul_nt(left, right):
    return lax.dot_general(left, right, (((1,), (1,)), ((), ())), preferred_element_type=F32)


def matmul_tn(left, right):
    return lax.dot_general(left, right, (((0,), (0,)), ((), ())), preferred_element_type=F32)


def vmem():
    return pl.BlockSpec(memory_space=pltpu.VMEM)


def smem():
    return pl.BlockSpec(memory_space=pltpu.SMEM)


def hbm():
    return pl.BlockSpec(memory_space=pltpu.HBM)


def padded_bytes(shape, dtype):
    size = jnp.dtype(dtype).itemsize
    rows = 8 * 4 // size
    shape = (1,) * (2 - len(shape)) + tuple(shape)
    held = -(-shape[-1] // 128) * 128 * -(-shape[-2] // rows) * rows
    return math.prod(shape[:-2]) * held * size


def comm_params(collective_id, held):
    return pltpu.CompilerParams(
        collective_id=collective_id, has_side_effects=True,
        vmem_limit_bytes=max(VMEM_LIMIT, held + MARGIN),
    )


def tile(index, size):
    return pl.ds(pl.multiple_of(index * size, size), size)


class Wire:
    def __init__(self, sizes, send_sem, recv_sem, local_sem, side, col_on=True, row_on=False):
        self.n, self.m = sizes
        self.me = lax.axis_index("col")
        self.row = lax.axis_index("row")
        self.send_sem, self.recv_sem, self.local_sem = send_sem, recv_sem, local_sem
        self.used = 0
        self.used_local = 0
        self.core = lax.rem(self.row, 2)
        self.layer = self.row // 2
        self.partner = self.row + 1 - 2 * self.core
        self.layers = self.m // 2
        self.col_on = col_on
        self.loads, self.stores, self.stored = [], [], []
        self.row_on = row_on or bool(side)
        self.side = [job(self) for job in side]

    def layer_peer(self, step):
        return lax.rem(self.layer + step, self.layers) * 2 + self.core

    def greet(self):
        barrier = pltpu.get_barrier_semaphore()
        waits = 0
        if self.col_on:
            for step in range(1, self.n):
                pl.semaphore_signal(
                    barrier, inc=1, device_id={"col": lax.rem(self.me + step, self.n)},
                    device_id_type=MESH,
                )
            waits += self.n - 1
        if self.row_on:
            for step in range(1, self.layers):
                pl.semaphore_signal(
                    barrier, inc=1, device_id={"row": self.layer_peer(step)}, device_id_type=MESH
                )
            pl.semaphore_signal(
                barrier, inc=1, device_id={"row": self.partner}, device_id_type=MESH
            )
            waits += self.layers
        pl.semaphore_wait(barrier, waits)

    def remote(self, source, target, axis, peer):
        slot = self.used
        self.used += 1
        return pltpu.make_async_remote_copy(
            src_ref=source, dst_ref=target, send_sem=self.send_sem.at[slot],
            recv_sem=self.recv_sem.at[slot], device_id={axis: peer}, device_id_type=MESH,
        )

    def local(self, source, target):
        slot = self.used_local
        self.used_local += 1
        return pltpu.make_async_copy(source, target, self.local_sem.at[slot])

    def to_all(self, source_of, target):
        copies = [
            self.remote(source_of(lax.rem(self.me + step, self.n)), target, "col",
                        lax.rem(self.me + step, self.n))
            for step in range(1, self.n)
        ]
        for copy in copies:
            copy.start()
        return copies

    def loaded(self):
        for copy in self.loads:
            copy.wait()

    def store(self, copies):
        for copy in copies:
            copy.start()
        self.stored += copies

    def flush(self):
        self.store(self.stores)

    def settle(self):
        for copy in self.stored:
            copy.wait()

    def begin(self):
        for job in self.side:
            job.begin()

    def early(self):
        for job in self.side:
            job.early()

    def middle(self):
        for job in self.side:
            job.middle()

    def end(self):
        for job in self.side:
            job.end()

    def peers(self):
        if self.n == 4:
            across = self.me + 1 - 2 * lax.rem(self.me, 2)
            along = lax.rem(self.me + 2, 4)
            return [(across, 0), (along, 1), (3 - self.me, 2)]
        return [
            (lax.rem(self.me + self.n - step, self.n), self.n - step - 1)
            for step in range(1, self.n)
        ]


class Spread:
    def __init__(self, wire, ref, count):
        self.wire, self.ref, self.count = wire, ref, count
        me = wire.me
        if wire.n != 4:
            self.copies = [
                wire.remote(self.part(me), self.part(me), "col", lax.rem(me + step, wire.n))
                for step in range(1, wire.n)
            ]
            return
        (across, _), (along, _), (far, _) = wire.peers()
        self.across = [wire.remote(self.part(me, q), self.part(me, q), "col", across) for q in range(4)]
        self.along = [wire.remote(self.part(me, q), self.part(me, q), "col", along) for q in range(4)]
        self.onward = [
            wire.remote(self.part(across, q), self.part(across, q), "col", along) for q in (0, 1)
        ] + [wire.remote(self.part(along, q), self.part(along, q), "col", across) for q in (2, 3)]

    def part(self, chunk, quarter=None):
        if quarter is None:
            return self.ref.at[tile(chunk, self.count)]
        size = self.count // 4
        return self.ref.at[tile(chunk * 4 + quarter, size)]

    def start(self):
        if self.wire.n != 4:
            for copy in self.copies:
                copy.start()
            return
        for first, second in ((0, 2), (1, 3), (2, 0), (3, 1)):
            self.across[first].start()
            self.along[second].start()

    def relay(self):
        if self.wire.n != 4:
            return
        for turn in range(2):
            self.across[turn].wait_recv()
            self.onward[turn].start()
            self.along[2 + turn].wait_recv()
            self.onward[2 + turn].start()

    def arrivals(self, relay=True):
        wire = self.wire
        yield wire.me, None
        if wire.n != 4:
            for step, (peer, slot) in zip(range(1, wire.n), wire.peers()):
                self.copies[step - 1].wait_recv()
                yield peer, slot
            return
        if relay:
            self.relay()
        for (peer, slot), copies in zip(
            wire.peers(), (self.across[2:], self.along[:2], self.onward)
        ):
            for copy in copies:
                copy.wait_recv()
            yield peer, slot

    def finish(self):
        copies = self.copies if self.wire.n != 4 else self.across + self.along + self.onward
        for copy in copies:
            copy.wait_send()


class Collect:
    def __init__(self, wire, part, got):
        self.wire, self.part, self.got = wire, part, got
        self.relayed = wire.n == 4
        self.count = part.shape[1]
        if not self.relayed:
            self.copies = {
                slot: wire.remote(part.at[slot], got.at[slot], "col", owner)
                for owner, slot in wire.peers()
            }
            return
        (across, _), (along, _), _ = wire.peers()
        half = self.count // 2
        first, second = pl.ds(0, half), pl.ds(half, half)
        places = [got.at[place // 2, (first, second)[place % 2]] for place in range(6)]
        self.far = [
            wire.remote(part.at[2, first], places[0], "col", across),
            wire.remote(part.at[2, second], places[1], "col", along),
        ]
        self.direct = {
            0: wire.remote(part.at[0, first], places[2], "col", across),
            1: wire.remote(part.at[1, second], places[4], "col", along),
        }
        self.onward = [
            wire.remote(part.at[0, second], places[3], "col", across),
            wire.remote(part.at[1, first], places[5], "col", along),
        ]

    def send(self, slot):
        if not self.relayed:
            self.copies[slot].start()
        elif slot == 2:
            for copy in self.far:
                copy.start()
        else:
            self.direct[slot].start()

    def combine(self):
        if not self.relayed:
            return
        half = self.count // 2
        for copy, slot, at, onward in (
            (self.far[1], 0, half, self.onward[0]), (self.far[0], 1, 0, self.onward[1])
        ):
            copy.wait_recv()
            place = 1 - slot

            def add(rows, index):
                mine = pl.ds(pl.multiple_of(at + index * 32, 32), 32)
                came = pl.ds(pl.multiple_of((half if place else 0) + index * 32, 32), 32)
                self.part[slot, mine] = (
                    self.part[slot, mine].astype(F32) + self.got[0, came].astype(F32)
                ).astype(BF16)

            row_loop(half, add)
            onward.start()

    def wait(self):
        if not self.relayed:
            for copy in self.copies.values():
                copy.wait()
            return
        for copy in self.far:
            copy.wait_send()
        for copy in list(self.direct.values()) + self.onward:
            copy.wait()

    def sum_loop(self, body):
        part, got, last = self.part, self.got, self.wire.n - 1
        if not self.relayed:
            def step(rows, index):
                total = part[last, rows].astype(F32)
                for slot in range(last):
                    total = total + got[slot, rows].astype(F32)
                body(rows, total)

            row_loop(self.count, step)
            return
        half = self.count // 2
        for at, sources in ((0, ((1, 0), (2, half))), (half, ((1, half), (2, 0)))):
            def step(rows, index, at=at, sources=sources):
                mine = pl.ds(pl.multiple_of(at + index * 32, 32), 32)
                total = part[last, mine].astype(F32)
                for slot, start in sources:
                    total = total + got[
                        slot, pl.ds(pl.multiple_of(start + index * 32, 32), 32)
                    ].astype(F32)
                body(mine, total)

            row_loop(half, step)


class RowChain:
    def __init__(self, shard, full, wire):
        self.wire, self.shard, self.full = wire, shard, full
        self.count = shard.shape[0]
        self.steps = wire.layers - 1
        self.base = wire.used
        wire.used += 4 * self.steps
        mine = full.at[tile(wire.row, self.count)]
        self.own = [wire.local(shard, mine), wire.remote(shard, mine, "row", wire.partner)]

    def block(self, layer):
        return self.full.at[tile(layer * 2 + self.wire.core, self.count)]

    def copy(self, kind, step, layer, peer):
        slot = self.base + kind * self.steps + step
        wire = self.wire
        source = self.shard if kind < 2 and step == 0 else self.block(layer)
        return pltpu.make_async_remote_copy(
            src_ref=source, dst_ref=self.block(layer), send_sem=wire.send_sem.at[slot],
            recv_sem=wire.recv_sem.at[slot], device_id={"row": peer}, device_id_type=MESH,
        )

    def up(self, step):
        wire = self.wire
        return self.copy(0, step, wire.layer - step, wire.row + 2)

    def down(self, step):
        wire = self.wire
        return self.copy(1, step, wire.layer + step, wire.row - 2)

    def begin(self):
        wire = self.wire
        pl.when(wire.layer + 1 < wire.layers)(lambda: self.up(0).start())
        pl.when(wire.layer > 0)(lambda: self.down(0).start())
        for copy in self.own:
            copy.start()

    def advance(self, step):
        wire = self.wire

        @pl.when(wire.layer - 1 - step >= 0)
        def _():
            self.copy(0, step, wire.layer - 1 - step, wire.row).wait_recv()
            if step + 1 < self.steps:
                pl.when(wire.layer + 1 < wire.layers)(lambda: self.up(step + 1).start())
            self.copy(2, step, wire.layer - 1 - step, wire.partner).start()

        @pl.when(wire.layer + 1 + step < wire.layers)
        def _():
            self.copy(1, step, wire.layer + 1 + step, wire.row).wait_recv()
            if step + 1 < self.steps:
                pl.when(wire.layer > 0)(lambda: self.down(step + 1).start())
            self.copy(3, step, wire.layer + 1 + step, wire.partner).start()

    def end(self):
        wire = self.wire
        for step in range(self.steps):
            pl.when((wire.layer + 1 < wire.layers) & (wire.layer - step >= 0))(
                lambda step=step: self.up(step).wait_send()
            )
            pl.when((wire.layer > 0) & (wire.layer + step < wire.layers))(
                lambda step=step: self.down(step).wait_send()
            )
            pl.when(wire.layer - 1 - step >= 0)(
                lambda step=step: self.copy(2, step, wire.layer - 1 - step, wire.partner).wait()
            )
            pl.when(wire.layer + 1 + step < wire.layers)(
                lambda step=step: self.copy(3, step, wire.layer + 1 + step, wire.partner).wait()
            )
        for copy in self.own:
            copy.wait()


class RowGather:
    def __init__(self, shard, full, wire):
        self.wire = wire
        count = shard.shape[0]
        mine = full.at[tile(wire.row, count)]
        self.first = [wire.local(shard, mine), wire.remote(shard, mine, "row", wire.partner)]
        self.along = [
            wire.remote(shard, mine, "row", wire.layer_peer(step))
            for step in range(1, wire.layers)
        ]
        self.onward = []
        for step in range(1, wire.layers):
            block = full.at[tile(wire.layer_peer(wire.layers - step), count)]
            self.onward.append(wire.remote(block, block, "row", wire.partner))

    def begin(self):
        for copy in self.along + self.first:
            copy.start()

    def early(self):
        pass

    def middle(self):
        for copy, onward in zip(self.along, self.onward):
            copy.wait_recv()
            onward.start()

    def end(self):
        for copy in self.along:
            copy.wait_send()
        for copy in self.first:
            copy.wait()
        for copy in self.onward:
            copy.wait()


class RowReduce:
    def __init__(self, grads, pieces, outs, held, pair, got, total, *rest, load=True):
        *parts, wire = rest
        self.wire, self.out, self.grads = wire, total, grads
        self.pieces = pieces
        self.parts = parts or [total]
        self.keep = [wire.local(part, out) for part, out in zip(self.parts, outs)]
        self.held, self.pair, self.got = held, pair, got
        self.count = held.shape[1]
        self.load = []
        if load:
            self.load = [
                wire.local(grads.at[tile(layer * 2 + wire.core, self.count)], held.at[layer])
                for layer in range(wire.layers)
            ]
        self.base = wire.used
        wire.used += 2 * wire.layers

    def layer_of(self, step):
        return lax.rem(self.wire.layer + 1 + step, self.wire.layers)

    def between(self, source, target, slot, peer):
        wire = self.wire
        return pltpu.make_async_remote_copy(
            src_ref=source, dst_ref=target, send_sem=wire.send_sem.at[self.base + slot],
            recv_sem=wire.recv_sem.at[self.base + slot], device_id={"row": peer}, device_id_type=MESH,
        )

    def swap(self, step):
        layer = self.layer_of(step)
        block = layer * 2 + 1 - self.wire.core
        return self.between(self.grads.at[tile(block, self.count)], self.pair.at[layer], step,
                            self.wire.partner)

    def along(self, step):
        layer = self.layer_of(step)
        return self.between(self.held.at[layer], self.got.at[step], self.wire.layers + step,
                            layer * 2 + self.wire.core)

    def begin_step(self, step):
        self.swap(step).start()

    def early_step(self, step):
        self.swap(step).wait()
        layer = self.layer_of(step)
        size = min(32, self.count)

        def add(rows, index):
            if self.load:
                mine = self.held[layer, rows]
            else:
                at = (layer * 2 + self.wire.core) * self.count + index * size
                mine = self.grads[pl.ds(pl.multiple_of(at, size), size)]
            self.held[layer, rows] = (
                mine.astype(F32) + self.pair[layer, rows].astype(F32)
            ).astype(BF16)

        row_loop(self.count, add)
        pl.when(step < self.wire.layers - 1)(lambda: self.along(step).start())

    def begin(self):
        for step in range(self.wire.layers):
            self.begin_step(step)
        for copy in self.load:
            copy.start()

    def early(self):
        for copy in self.load:
            copy.wait()

        def one(step, carry):
            self.early_step(step)
            return carry

        lax.fori_loop(0, self.wire.layers, one, 0)

    def middle(self):
        pass

    def end(self):
        for step in range(self.wire.layers - 1):
            self.along(step).wait()

        def add(rows, index):
            total = self.held[self.wire.layer, rows].astype(F32)
            for step in range(self.wire.layers - 1):
                total = total + self.got[step, rows].astype(F32)
            self.out[rows] = total

        row_loop(self.count, add)
        if len(self.parts) > 1 or self.pieces[0][1]:
            at = 0
            for part, (width, flip) in zip(self.parts, self.pieces):
                piece = self.out[:, at:at + width]
                part[...] = piece.T if flip else piece
                at += width
        self.wire.store(self.keep)


def piece_shapes(count, pieces):
    return [(width, count) if flip else (count, width) for width, flip in pieces]


def reduce_scratch(layers, count, width, pieces):
    apart = len(pieces) > 1 or pieces[0][1]
    parts = [pltpu.VMEM(shape, F32) for shape in piece_shapes(count, pieces)] if apart else []
    return parts_last(layers, count, width) + parts


def parts_last(layers, count, width):
    return [
        pltpu.VMEM((layers, count, width), BF16),
        pltpu.VMEM((layers, count, width), BF16),
        pltpu.VMEM((max(1, layers - 1), count, width), BF16),
        pltpu.VMEM((count, width), F32),
    ]


class SumItem:
    def __init__(self, kind, source, out, got, packed, got_row, wire):
        self.wire, self.kind, self.source, self.out = wire, kind, source, out
        self.got, self.packed, self.got_row = got, packed, got_row
        self.col = []
        if kind != "own":
            for step in range(1, wire.n):
                peer = lax.rem(wire.me + step, wire.n)
                piece = source.at[peer] if kind == "piece" else source
                self.col.append(wire.remote(piece, got.at[step - 1], "col", peer))
        self.swap = wire.remote(packed.at[0], got_row.at[0], "row", wire.partner)
        self.along = [
            wire.remote(packed.at[1], got_row.at[step], "row", wire.layer_peer(step))
            for step in range(1, wire.layers)
        ]

    def begin(self):
        for copy in self.col:
            copy.start()

    def early(self):
        for copy in self.col:
            copy.wait()
        total = self.source[self.wire.me] if self.kind == "piece" else self.source[...]
        if self.kind != "own":
            for step in range(self.wire.n - 1):
                total = total + self.got[step]
        self.packed[0] = total
        self.swap.start()

    def middle(self):
        self.swap.wait()
        self.packed[1] = self.packed[0] + self.got_row[0]
        for copy in self.along:
            copy.start()

    def end(self):
        for copy in self.along:
            copy.wait()
        total = self.packed[1]
        for step in range(1, self.wire.layers):
            total = total + self.got_row[step]
        self.out[...] = total


def sum_scratch(n, layers, shape):
    return [
        pltpu.VMEM(shape, F32),
        pltpu.VMEM((n - 1,) + shape, F32),
        pltpu.VMEM((2,) + shape, F32),
        pltpu.VMEM((layers,) + shape, F32),
    ]


def join(pieces, target):
    at = 0
    for ref, flip in pieces:
        width = ref.shape[0] if flip else ref.shape[1]
        target[:, at:at + width] = ref[...].T if flip else ref[...]
        at += width


def joined_shape(pieces):
    rows = {array.shape[1] if flip else array.shape[0] for array, flip in pieces}
    return rows.pop(), sum(array.shape[0] if flip else array.shape[1] for array, flip in pieces)


def row_loop(count, body):
    size = min(32, count)

    def step(index, carry):
        body(tile(index, size), index)
        return carry

    lax.fori_loop(0, count // size, step, 0)


def block_loop(extent, body):
    size = min(256, extent)

    def step(index, carry):
        body(tile(index, size), index)
        return carry

    lax.fori_loop(0, extent // size, step, 0)


def fold8(values):
    return jnp.sum(values.reshape(values.shape[0] // 8, 8, values.shape[1]), axis=0)


def normalize(values):
    average = jnp.mean(values, axis=1, keepdims=True)
    centered = values - average
    inverse = lax.rsqrt(jnp.mean(centered * centered, axis=1, keepdims=True) + EPSILON)
    return centered * inverse, inverse


def norm_back(grad_in, normed, inverse, gains):
    scaled = grad_in * gains
    first = jnp.mean(scaled, axis=1, keepdims=True)
    second = jnp.mean(scaled * normed, axis=1, keepdims=True)
    return inverse * (scaled - first - normed * second)


def comm_call(name, collective_id, sizes, main, ins, outs, scratch, gathers=(), reduces=(), cost=10**9,
              col_on=True, more_slots=0, row_on=False):
    n, m = sizes
    layers = m // 2
    gather_pieces = [piece for pieces in gathers for piece in pieces]
    in_arrays = [item[0] for item in ins] + [array for array, _ in gather_pieces]
    in_arrays += [grads for grads, _ in reduces]
    in_specs = [hbm() if item[1] == "load" else item[1] for item in ins]
    in_specs += [vmem()] * len(gather_pieces) + [hbm()] * len(reduces)
    out_shapes = [jax.ShapeDtypeStruct(item[0], item[1]) for item in outs]
    out_specs = [hbm() if item[2] == "store" else item[2] for item in outs]
    copied = [pltpu.VMEM(item[0].shape, item[0].dtype) for item in ins if item[1] == "load"]
    copied += [pltpu.VMEM(item[0], item[1]) for item in outs if item[2] == "store"]
    side_scratch = []
    for pieces in gathers:
        rows, width = joined_shape(pieces)
        out_shapes.append(jax.ShapeDtypeStruct((m * rows, width), BF16))
        out_specs.append(hbm())
        side_scratch.append(pltpu.VMEM((rows, width), BF16))
    reduce_counts = []
    for grads, pieces in reduces:
        count, width = grads.shape[0] // m, grads.shape[1]
        for shape in piece_shapes(count, pieces):
            out_shapes.append(jax.ShapeDtypeStruct(shape, F32))
            out_specs.append(hbm())
        made = reduce_scratch(layers, count, width, pieces)
        reduce_counts.append(len(made))
        side_scratch += made
    every_scratch = copied + list(scratch) + side_scratch
    held = sum(padded_bytes(item.shape, item.dtype) for item in every_scratch)
    remote_slots = 8 * n + 16 + len(gathers) * 2 * layers + len(reduces) * 2 * layers + more_slots
    local_slots = 12 + len(copied) + len(gathers) + len(reduces) * (layers + 4) + more_slots

    def kernel(*refs):
        at = 0

        def take(count):
            nonlocal at
            at += count
            return refs[at - count:at]

        main_ins = list(take(len(ins)))
        gather_ins = [
            [(ref, flip) for ref, (_, flip) in zip(take(len(pieces)), pieces)] for pieces in gathers
        ]
        reduce_ins = take(len(reduces))
        main_outs = list(take(len(outs)))
        gather_outs = take(len(gathers))
        reduce_outs = [take(len(pieces)) for _, pieces in reduces]
        loads, stores = [], []
        for place, item in enumerate(ins):
            if item[1] == "load":
                (held_ref,) = take(1)
                loads.append((main_ins[place], held_ref))
                main_ins[place] = held_ref
        for place, item in enumerate(outs):
            if item[2] == "store":
                (held_ref,) = take(1)
                stores.append((held_ref, main_outs[place]))
                main_outs[place] = held_ref
        main_scratch = take(len(scratch))
        side = []
        for pieces, full in zip(gather_ins, gather_outs):
            (shard,) = take(1)
            join(pieces, shard)
            side.append(functools.partial(RowGather, shard, full))
        for grads, out, (_, pieces), size in zip(reduce_ins, reduce_outs, reduces, reduce_counts):
            side.append(functools.partial(RowReduce, grads, pieces, out, *take(size)))
        send_sem, recv_sem, local_sem = take(3)
        wire = Wire(sizes, send_sem, recv_sem, local_sem, side, col_on, row_on)
        wire.loads = [wire.local(*pair) for pair in loads]
        wire.stores = [wire.local(*pair) for pair in stores]
        for copy in wire.loads:
            copy.start()
        main(wire, main_ins, main_outs, main_scratch)
        wire.settle()

    return pl.pallas_call(
        kernel,
        name=name,
        out_shape=tuple(out_shapes),
        in_specs=in_specs,
        out_specs=tuple(out_specs),
        scratch_shapes=every_scratch + [
            pltpu.SemaphoreType.DMA((remote_slots,)),
            pltpu.SemaphoreType.DMA((remote_slots,)),
            pltpu.SemaphoreType.DMA((local_slots,)),
        ],
        compiler_params=comm_params(collective_id, held),
        cost_estimate=pl.CostEstimate(flops=cost, bytes_accessed=10**8, transcendentals=0),
    )(*in_arrays)


def norm_rows(wire, count, source, gains, rows_ref):
    base = wire.me * count

    def work(rows, index):
        normed, _ = normalize(source[rows])
        size = min(32, count)
        rows_ref[pl.ds(pl.multiple_of(base + index * size, size), size)] = (normed * gains).astype(BF16)

    row_loop(count, work)


def cast_rows(wire, count, source, factor, rows_ref):
    base = wire.me * count

    def work(rows, index):
        size = min(32, count)
        rows_ref[pl.ds(pl.multiple_of(base + index * size, size), size)] = (
            factor * source[rows]
        ).astype(BF16)

    row_loop(count, work)


def keep_rows(limit, start, rows):
    place = lax.broadcasted_iota(jnp.int32, (rows, 1), 0) + start
    return jnp.where(place < limit, 1.0, 0.0)


def residual(collect, factor, resid, limit, after_ref, squares_ref):
    squares_ref[...] = jnp.zeros_like(squares_ref)
    base = collect.wire.me * collect.count

    def work(rows, branch):
        after = resid[rows] + factor * branch
        after_ref[rows] = after
        keep = keep_rows(limit, base + rows.start, branch.shape[0])
        squares_ref[0:8] += fold8(branch * branch * keep)
        squares_ref[8:16] += fold8(after * after * keep)

    collect.sum_loop(work)


def residual_back(collect, grad_ref, resid, gains, new_grad_ref, gain_grad_ref):
    gain_grad_ref[...] = jnp.zeros_like(gain_grad_ref)

    def work(rows, rows_grad):
        normed, inverse = normalize(resid[rows])
        new_grad_ref[rows] = grad_ref[rows] + norm_back(rows_grad, normed, inverse, gains)
        gain_grad_ref[...] += fold8(rows_grad * normed)

    collect.sum_loop(work)


def send_pieces(wire, count, source, pieces, out_ref):
    width = pieces.shape[2]

    def split(rows, index):
        result = source[rows].astype(BF16)
        for part in range(wire.n):
            pieces[part, rows] = result[:, part * width:(part + 1) * width]

    row_loop(count, split)
    mine = out_ref.at[tile(wire.me, count)]
    copies = wire.to_all(lambda peer: pieces.at[peer], mine)
    here = wire.local(pieces.at[wire.me], mine)
    here.start()
    return copies + [here]


def send_shares(wire, chunks, collect, share, last=None):
    part = collect.part
    if wire.n == 4:
        across_bit, along_bit = lax.rem(wire.me, 2), wire.me // 2

        def turn(step, carry):
            left = 3 - step
            flip_across, flip_along = lax.rem(left, 2), left // 2
            chunk = (
                across_bit + flip_across - 2 * across_bit * flip_across
                + 2 * (along_bit + flip_along - 2 * along_bit * flip_along)
            )
            share(chunk, part.at[lax.rem(left + 3, 4)])
            for place in range(3):
                pl.when(step == place)(lambda place=place: collect.send(2 - place))
            if last is not None:
                pl.when(step == 2)(last)
            return carry

        lax.fori_loop(0, 4, turn, 0)
    else:
        for chunk, slot in reversed(chunks):
            share(chunk, part.at[wire.n - 1 if slot is None else slot])
            if slot is not None:
                collect.send(slot)
        if last is not None:
            last()


def feed_forward_first(count, chunk, rows_ref, up, pre_ref, act):
    rows = tile(chunk, count)
    left = rows_ref[rows]

    def first(cols, index):
        pre = matmul(left, up[:, cols])
        pre_ref[rows, cols] = pre.astype(BF16)
        act[:, cols] = (pre * jax.nn.sigmoid(pre)).astype(BF16)

    block_loop(up.shape[1], first)


def feed_forward_second(act, down_t, target):
    hidden = act[...]

    def second(cols, index):
        target[:, cols] = matmul_nt(hidden, down_t[cols]).astype(BF16)

    block_loop(down_t.shape[0], second)


def feed_forward_main(count, gain_row, factor, enter, turn, wire, ins, outs, scratch):
    ins, outs, scratch = list(ins), list(outs), list(scratch)
    if enter:
        limit_ref, tokens_ref, cot_in = ins[:3]
        gain_ins = ins[3:8]
        up_shard, down_ref = ins[8:10]
        next_pieces = [(ref, flip) for ref, flip in zip(ins[10:], enter)]
        ins = []
        resid, cot_out, gains_ref, up, down_t, next_full = outs[:6]
        outs = outs[6:]
        arrived, arrived_cot, arrived_gain, gain_in, down_shard, next_shard = scratch[:6]
        scratch = scratch[6:]
    else:
        limit_ref, resid, gains_ref = ins[:3]
        ins = ins[3:]
    if enter:
        for place, ref in enumerate(gain_ins):
            gain_in[place:place + 1] = ref[...]
        gain_in[len(gain_ins):] = jnp.zeros((8 - len(gain_ins), gain_in.shape[1]), F32)
        join([(down_ref, True)], down_shard)
        join(next_pieces, next_shard)
    else:
        up, down_t = ins[:2]
        ins = ins[2:]
    if turn:
        (cot_ref,) = ins
        grad_ref, gain_grad_ref, out_ref = outs[:3]
        outs = outs[3:]
        pieces, after_ref = scratch[:2]
        scratch = scratch[2:]
    else:
        after_ref = outs.pop(0)
    squares_ref, rows_ref, pre_ref = outs
    act, part, got = scratch
    wire.greet()
    wire.begin()
    if enter:
        up_job = RowChain(up_shard, up, wire)
        down_job = RowChain(down_shard, down_t, wire)
        next_job = RowChain(next_shard, next_full, wire)
        up_job.begin()
        width = arrived_gain.shape[2]
        turned = tokens_ref.shape[0] == width

        def share(ref, peer):
            return ref.at[:, tile(peer, count)] if turned else ref.at[tile(peer, count)]

        def settle(came, target):
            for piece in range(wire.n):
                cols = slice(piece * width, (piece + 1) * width)
                if turned:
                    target[:, cols] = came[piece].astype(F32).T
                else:
                    target[:, cols] = came[piece].astype(F32)

        mine = [
            wire.local(share(tokens_ref, wire.me), arrived.at[wire.me]),
            wire.local(gain_in, arrived_gain.at[wire.me]),
            wire.local(share(cot_in, wire.me), arrived_cot.at[wire.me]),
        ]
        copies = wire.to_all(lambda peer: share(tokens_ref, peer), arrived.at[wire.me])
        copies += wire.to_all(lambda peer: gain_in, arrived_gain.at[wire.me])
        for copy in mine:
            copy.start()
        for copy in mine + copies:
            copy.wait()
        for piece in range(wire.n):
            gains_ref[:, piece * width:(piece + 1) * width] = arrived_gain[piece]

        settle(arrived, resid)
    gains = gains_ref[gain_row:gain_row + 1]
    norm_rows(wire, count, resid, gains, rows_ref)
    spread = Spread(wire, rows_ref, count)
    spread.start()
    wire.loaded()
    collect = Collect(wire, part, got)
    cot_copies = []
    if enter:
        cot_copies = wire.to_all(
            lambda peer: share(cot_in, peer), arrived_cot.at[wire.me]
        )
    wire.early()
    if enter:
        up_job.advance(0)
        spread.relay()
        for step in range(1, up_job.steps):
            up_job.advance(step)
        down_job.begin()
        up_job.end()
        chunks = []
        for chunk, slot in spread.arrivals(relay=False):
            chunks.append((chunk, slot))
            feed_forward_first(count, chunk, rows_ref, up, pre_ref, act.at[len(chunks) - 1])
            if len(chunks) - 1 < down_job.steps:
                down_job.advance(len(chunks) - 1)
        for copy in cot_copies:
            copy.wait()

        settle(arrived_cot, cot_out)
        next_job.begin()
        down_job.end()
        for place, (chunk, slot) in reversed(list(enumerate(chunks))):
            target = part.at[wire.n - 1 if slot is None else slot]
            feed_forward_second(act.at[place], down_t, target)
            if slot is not None:
                collect.send(slot)
            if len(chunks) - 1 - place < next_job.steps:
                next_job.advance(len(chunks) - 1 - place)
        collect.combine()
        for step in range(len(chunks), next_job.steps):
            next_job.advance(step)
    else:
        for chunk, slot in spread.arrivals():
            target = part.at[wire.n - 1 if slot is None else slot]
            feed_forward_first(count, chunk, rows_ref, up, pre_ref, act.at[0])
            feed_forward_second(act.at[0], down_t, target)
            if slot is not None:
                collect.send(slot)
        collect.combine()
    wire.middle()
    wire.flush()
    collect.wait()
    residual(collect, factor, resid, limit_ref[0], after_ref, squares_ref)
    late = []
    if turn:
        final_gains = gains_ref[gain_row + 1:gain_row + 2]
        gain_grad_ref[...] = jnp.zeros_like(gain_grad_ref)

        def final(rows, index):
            normed, inverse = normalize(after_ref[rows])
            cot = cot_ref[rows]
            grad_ref[rows] = norm_back(cot, normed, inverse, final_gains)
            gain_grad_ref[...] += fold8(cot * normed)
            after_ref[rows] = normed * final_gains

        row_loop(count, final)
        late = send_pieces(wire, count, after_ref, pieces, out_ref)
    spread.finish()
    for copy in late:
        copy.wait()
    if enter:
        next_job.end()
    wire.end()


def feed_forward(sizes, name, collective_id, gain_row, up, down_t, limit, resid=None, gains=None,
                 enter=None, turn=None, **side):
    n, m = sizes
    hidden = up.shape[1]
    full = up.shape[0] * (m if enter else 1)
    next_pieces = None
    if enter:
        tokens, cotangent, gain_parts, next_pieces = enter
        turned = tokens.shape[0] * n == full
        width, length = tokens.shape if turned else tokens.shape[::-1]
        count = length // n
        came = (n, width, count) if turned else (n, count, width)
        ins = [(limit, smem()), (tokens, vmem()), (cotangent, vmem())]
        ins += [(part, vmem()) for part in gain_parts] + [(up, vmem()), (down_t, vmem())]
        ins += [(array, vmem()) for array, _ in next_pieces]
        down_shape, next_shape = (full // m, hidden), joined_shape(next_pieces)
        outs = [((count, full), F32, "store"), ((count, full), F32, "store"), ((8, full), F32, vmem())]
        scratch = [
            pltpu.VMEM(came, BF16),
            pltpu.VMEM(came, BF16),
            pltpu.VMEM((n, 8, width), F32),
            pltpu.VMEM((8, width), F32),
            pltpu.VMEM(down_shape, BF16),
            pltpu.VMEM(next_shape, BF16),
        ]
        for shape, spec in ((down_shape, "store"), (down_shape, "store"), (next_shape, hbm())):
            outs.append(((m * shape[0], shape[1]), BF16, spec))
        side = dict(side, more_slots=6 * m, row_on=True)
    else:
        count = resid.shape[0]
        ins = [(limit, smem()), (resid, vmem()), (gains, vmem())]
        outs, scratch = [], []
        ins += [(up, "load"), (down_t, "load")]
    if turn is not None:
        ins.append((turn, "load"))
        outs += [
            ((count, full), F32, vmem()),
            ((8, full), F32, vmem()),
            ((n * count, full // n), BF16, hbm()),
        ]
        scratch.append(pltpu.VMEM((n, count, full // n), BF16))
    if turn is None:
        outs.append(((count, full), F32, vmem()))
    else:
        scratch.append(pltpu.VMEM((count, full), F32))
    outs += [
        ((16, full), F32, vmem()),
        ((n * count, full), BF16, "store"),
        ((n * count, hidden), BF16, "store"),
    ]
    scratch += [
        pltpu.VMEM((n if enter else 1, count, hidden), BF16),
        pltpu.VMEM((n, count, full), BF16),
        pltpu.VMEM((n - 1, count, full), BF16),
    ]
    return comm_call(
        name, collective_id, sizes,
        functools.partial(
            feed_forward_main, count, gain_row, 0.5, enter and [flip for _, flip in next_pieces],
            turn is not None,
        ),
        ins, outs, scratch, **side,
    )


def lane_sum(values):
    total = values[:, 0:BLOCK]
    for at in range(BLOCK, values.shape[1], BLOCK):
        total = total + values[:, at:at + BLOCK]
    return total


def feed_forward_back_main(count, gain_row, leave, wire, ins, outs, scratch):
    grad_ref, resid, gains_ref, up, down_t, rows_ref, pre_ref = ins[:7]
    ins = ins[7:]
    grads, pre_grad, act, part, got = scratch[:5]
    scratch = list(scratch[5:])
    hidden = up.shape[1]
    full = up.shape[0]

    def take(size):
        taken, scratch[:size] = scratch[:size], []
        return taken

    if leave:
        up_width, down_pieces, reduce_sizes = leave
        limit_ref = ins[0]
        gain_parts, squares, table_part, tap_part, depth_part = ins[1:5], ins[5:9], *ins[9:12]
        gain_outs, table_out, rms_out, tap_out, depth_out = outs[:5], *outs[5:9]
        up_out, down_out, last_ref = outs[9:12]
        gain_grad_ref, up_grad_ref, down_grad_ref, new_grad_ref, pieces = take(5)
        width = pieces.shape[2]
        up_job = RowReduce(up_grad_ref, [(hidden, False)], [up_out], *take(reduce_sizes[0]), wire,
                           load=False)
        down_job = RowReduce(down_grad_ref, [(hidden, True)], [down_out], *take(reduce_sizes[1]), wire,
                             load=False)
        gain_pieces, square_parts, first_pieces = take(3)
        items = [
            SumItem(kind, source, *take(4), wire)
            for kind, source in (
                ("piece", gain_pieces), ("all", table_part), ("all", square_parts),
                ("own", tap_part), ("own", depth_part),
            )
        ]
        gain_item = SumItem("piece", first_pieces, *take(4), wire)
    else:
        (tokens_ref,) = ins
        gain_grad_ref, up_grad_ref, down_grad_ref, last_ref, turned_ref = outs
        new_grad_ref = last_ref
        items = []
        down_job = up_job = None
    gains = gains_ref[gain_row:gain_row + 1]
    wire.greet()
    wire.begin()
    cast_rows(wire, count, grad_ref, 0.5, grads)
    spread = Spread(wire, grads, count)
    spread.start()
    if leave:
        gain_pieces[...] = jnp.zeros_like(gain_pieces)
        square_parts[...] = jnp.zeros_like(square_parts)
        for place, ref in enumerate(gain_parts):
            row = jnp.sum(ref[...], axis=0, keepdims=True)
            for piece in range(wire.n):
                gain_pieces[piece, place:place + 1] = row[:, piece * width:(piece + 1) * width]
        for place, ref in enumerate(squares):
            for at in (0, 1):
                rows = ref[at * 8:(at + 1) * 8]
                square_parts[at * 4 + place:at * 4 + place + 1] = lane_sum(
                    jnp.sum(rows, axis=0, keepdims=True)
                )
        lane = lax.broadcasted_iota(jnp.int32, (1, BLOCK), 1)
        once = jnp.where(wire.me == 0, limit_ref[0], 0)
        square_parts[8:9] = jnp.where(lane == 0, once, 0).astype(F32)
        for item in items:
            item.begin()
    wire.loaded()
    collect = Collect(wire, part, got)
    def first_leg(chunk):
        rows = tile(chunk, count)
        left = grads[rows]

        def first(cols, index):
            act_grad = matmul(left, down_t[:, cols])
            pre = pre_ref[rows, cols].astype(F32)
            sig = jax.nn.sigmoid(pre)
            act[rows, cols] = (pre * sig).astype(BF16)
            pre_grad[rows, cols] = (act_grad * (sig + pre * sig * (1.0 - sig))).astype(BF16)

        block_loop(hidden, first)

    def second_leg(chunk, slot):
        target = part.at[wire.n - 1 if slot is None else slot]
        through = pre_grad[tile(chunk, count)]

        def second(cols, index):
            target[:, cols] = matmul_nt(through, up[cols]).astype(BF16)

        block_loop(full, second)
        if slot is not None:
            collect.send(slot)

    def weight_rows(left_ref, right_ref, out, rows):
        left = left_ref[:, rows]

        def piece(cols, index):
            out[rows, cols] = matmul_tn(left, right_ref[:, cols]).astype(BF16)

        block_loop(hidden, piece)

    def weight_grad(left_ref, right_ref, out, job=None):
        if job is None:
            block_loop(full, lambda rows, index: weight_rows(left_ref, right_ref, out, rows))
            return

        def layer(step, carry):
            weight_rows(left_ref, right_ref, out, tile(job.layer_of(step), 2 * job.count))
            job.begin_step(step)
            pl.when(step > 0)(lambda: job.early_step(step - 1))
            return carry

        lax.fori_loop(0, wire.layers, layer, 0)
        job.early_step(wire.layers - 1)

    late_leg = None
    for place, (chunk, slot) in enumerate(spread.arrivals()):
        first_leg(chunk)
        if leave and place == wire.n - 1:
            late_leg = (chunk, slot)
        else:
            second_leg(chunk, slot)
        if slot is None:
            wire.early()
            for item in items:
                item.early()
            if not leave:
                turned_ref[...] = tokens_ref[...].T
        elif slot == 0:
            for item in items:
                item.middle()
    wire.middle()
    weight_grad(grads, act, down_grad_ref, down_job)
    if leave:
        second_leg(*late_leg)
        weight_grad(rows_ref, pre_grad, up_grad_ref, up_job)
        collect.combine()
    else:
        collect.combine()
        weight_grad(rows_ref, pre_grad, up_grad_ref)
    wire.flush()
    collect.wait()
    residual_back(collect, grad_ref, resid, gains, new_grad_ref, gain_grad_ref)
    if leave:
        for piece in range(wire.n):
            first_pieces[piece] = gain_grad_ref[:, piece * width:(piece + 1) * width]
        gain_item.begin()
        late = send_pieces(wire, count, new_grad_ref, pieces, last_ref)
        gain_item.early()
        for item in items:
            item.end()
        gain_item.middle()
        totals = [item.out for item in items]
        for place, ref in enumerate(gain_outs[1:]):
            ref[...] = totals[0][place:place + 1]
        table = totals[1][...]
        for at in range(HEAD_DIM, table.shape[1], HEAD_DIM):
            table = table[:, 0:HEAD_DIM] + table[:, at:at + HEAD_DIM]
        table_out[...] = table[0:LEFT + RIGHT + 1]
        sums = jnp.sum(totals[2][...], axis=1, keepdims=True)
        rms_out[...] = jnp.broadcast_to(jnp.sqrt(sums[0:8] / (sums[8:9] * full)), rms_out.shape)
        tap_out[...] = totals[3][0:tap_out.shape[0]]
        depth_out[...] = jnp.sum(totals[4][...], axis=0, keepdims=True)
        for copy in late:
            copy.wait()
        wire.end()
        down_job.end()
        gain_item.end()
        gain_outs[0][...] = jnp.sum(gain_item.out[...], axis=0, keepdims=True)
        up_job.end()
    spread.finish()
    if not leave:
        wire.end()


def feed_forward_back(sizes, name, collective_id, gain_row, grad, resid, gains, up, down_t, rows, pre,
                      leave=None, tokens=None, taps=0, **side):
    n, m = sizes
    full, hidden = up.shape
    count = resid.shape[0]
    width = full // n
    ins = [(grad, vmem()), (resid, "load"), (gains, vmem())]
    ins += [(item, "load") for item in (up, down_t, rows, pre)]
    scratch = [
        pltpu.VMEM((n * count, full), BF16),
        pltpu.VMEM((n * count, hidden), BF16),
        pltpu.VMEM((n * count, hidden), BF16),
        pltpu.VMEM((n, count, full), BF16),
        pltpu.VMEM((n - 1, count, full), BF16),
    ]
    extra = None
    if leave:
        limit, gain_parts, squares, table_part, tap_part, depth_part = leave
        layers = m // 2
        ins.append((limit, smem()))
        ins += [(item, vmem()) for item in (*gain_parts, *squares, table_part, tap_part, depth_part)]
        outs = [((1, width), F32, vmem())] * 5
        outs += [
            ((LEFT + RIGHT + 1, HEAD_DIM), F32, vmem()),
            ((8, BLOCK), F32, vmem()),
            ((taps, width), F32, vmem()),
            ((1, width), F32, vmem()),
            ((full // m, hidden), F32, hbm()),
            ((hidden, full // m), F32, hbm()),
            ((n * count, width), BF16, hbm()),
        ]
        scratch += [
            pltpu.VMEM((8, full), F32),
            pltpu.VMEM((full, hidden), BF16),
            pltpu.VMEM((full, hidden), BF16),
            pltpu.VMEM((count, full), F32),
            pltpu.VMEM((n, count, width), BF16),
        ]
        reduces = [
            reduce_scratch(layers, full // m, hidden, [(hidden, flip)]) for flip in (False, True)
        ]
        scratch += reduces[0] + reduces[1]
        extra = (hidden, None, [len(made) for made in reduces])
        scratch += [
            pltpu.VMEM((n, 8, width), F32), pltpu.VMEM((16, BLOCK), F32), pltpu.VMEM((n, 8, width), F32)
        ]
        for shape in ((8, width), table_part.shape, (16, BLOCK), tap_part.shape, depth_part.shape,
                      (8, width)):
            scratch += sum_scratch(n, layers, shape)
        side = dict(side, more_slots=16 * m + 8 * n, row_on=True)
    else:
        ins.append((tokens, "load"))
        outs = [
            ((8, full), F32, vmem()),
            ((full, hidden), BF16, "store"),
            ((full, hidden), BF16, "store"),
            ((count, full), F32, vmem()),
            ((tokens.shape[1], tokens.shape[0]), BF16, "store"),
        ]
    return comm_call(
        name, collective_id, sizes,
        functools.partial(feed_forward_back_main, count, gain_row, extra),
        ins, outs, scratch, **side,
    )


def slot_rows(axis):
    slots = lax.broadcasted_iota(jnp.int32, (LEFT + RIGHT + 8, SPAN), axis)
    signed = jnp.where(slots < SPAN - BLOCK + 1, slots, slots - SPAN)
    return jnp.clip(signed - (BLOCK - LEFT), 0, LEFT + RIGHT)


def extend_table(table, copies):
    slots = jnp.arange(SPAN)
    signed = jnp.where(slots < SPAN - BLOCK + 1, slots, slots - SPAN)
    row_of = jnp.clip(signed - (BLOCK - LEFT), 0, LEFT + RIGHT)
    chosen = (row_of[:, None] == jnp.arange(LEFT + RIGHT + 1)[None, :]).astype(table.dtype)
    return jnp.tile(matmul(chosen, table).astype(table.dtype), (1, copies))


def fill_far(far_ref, table_ref, limit):
    blocks, length, _ = far_ref.shape
    lane = lax.broadcasted_iota(jnp.int32, (1, BLOCK), 1)

    def row(at, mark):
        ends = table_ref[at:at + 1].astype(F32)
        if ends.shape[1] < BLOCK:
            ends = jnp.concatenate([ends, jnp.zeros((1, BLOCK - ends.shape[1]), F32)], axis=1)
        return jnp.where(lane < HEAD_DIM, ends, jnp.where(lane == mark, 1.0, 0.0))

    first = row(0, HEAD_DIM + 1)
    last = row(SPAN - 2 * BLOCK, HEAD_DIM + 2)

    def block(step, carry):
        index, piece = step // (length // BLOCK), lax.rem(step, length // BLOCK)
        at = index * BLOCK
        column = lax.broadcasted_iota(jnp.int32, (BLOCK, 1), 0) + piece * BLOCK
        place = column + at - BLOCK
        key = jnp.where(place < 0, place + length, jnp.where(place >= length, place - length, place))
        near = (column < WINDOW) & (place >= 0) & (place < length)
        left = jnp.where(near | (key >= at), 0.0, 1.0)
        right = jnp.where(near | (key < at), 0.0, 1.0)
        bias = jnp.where(key < limit, 0.0, NEG_FILL)
        terms = left * first + right * last + jnp.where(lane == HEAD_DIM, bias, 0.0)
        far_ref[index, tile(piece, BLOCK)] = terms.astype(BF16)
        return carry

    lax.fori_loop(0, blocks * (length // BLOCK), block, 0)


def duplicate(qkv_ref, width, group, keys, values):
    length = qkv_ref.shape[0]
    for part in range(width // group):
        base = part * group
        for copy in range(2):
            place = slice(copy * length, (copy + 1) * length)
            keys[part, place] = qkv_ref[:, width + base:width + base + group]
            values[part, place] = qkv_ref[:, 2 * width + base:2 * width + base + group]


def by_head(values, group):
    if group == HEAD_DIM:
        return values
    lane = lax.broadcasted_iota(jnp.int32, (BLOCK, group), 1)
    zero = jnp.zeros_like(values)
    return jnp.concatenate(
        [
            jnp.where((lane >= at) & (lane < at + HEAD_DIM), values, zero)
            for at in range(0, group, HEAD_DIM)
        ],
        axis=0,
    )


def own_lanes(values, group):
    if group == HEAD_DIM:
        return values
    lane = lax.broadcasted_iota(jnp.int32, (BLOCK, group), 1)
    return jnp.where(lane < HEAD_DIM, values[0:BLOCK], values[BLOCK:2 * BLOCK])


def far_queries(values, group):
    wide = values.astype(F32)
    if group == HEAD_DIM:
        lane = lax.broadcasted_iota(jnp.int32, (BLOCK, BLOCK - HEAD_DIM), 1)
        return jnp.concatenate([wide, jnp.where(lane == 0, 1.0, 0.0)], axis=1).astype(BF16)
    lane = lax.broadcasted_iota(jnp.int32, (BLOCK, BLOCK), 1)
    rest = jnp.where(lane == HEAD_DIM, 1.0, 0.0)
    return jnp.concatenate(
        [
            jnp.where(lane < HEAD_DIM, wide, rest),
            jnp.where(lane < HEAD_DIM, pltpu.roll(wide, HEAD_DIM, 1), rest),
        ],
        axis=0,
    ).astype(BF16)


def near_mask(at, length):
    place = lax.broadcasted_iota(jnp.int32, (1, WINDOW), 1) + (at - BLOCK)
    return (place >= 0) & (place < length)


def near_terms(query, table, at, length):
    terms = matmul_nt(query, table)
    halves = [
        pltpu.roll(terms[start:start + BLOCK], 0, 1, stride=1, stride_axis=0)[:, :WINDOW]
        for start in range(0, query.shape[0], BLOCK)
    ]
    return jnp.where(near_mask(at, length), jnp.concatenate(halves, axis=0), 0.0)


def attend_blocks(first, blocks, width, group, qkv_ref, table_ref, far_ref, keys, values, context_ref,
                  log_ref, weights):
    length = qkv_ref.shape[0]
    heads = group // HEAD_DIM
    parts = width // group
    scale = 1.0 / math.sqrt(HEAD_DIM)

    def block(step, carry):
        index, part = first + step // parts, lax.rem(step, parts)
        at = pl.multiple_of(index * BLOCK, BLOCK)
        rows = pl.ds(at, BLOCK)
        cols = tile(part, group) if parts > 1 else slice(0, group)
        window = pl.ds(pl.multiple_of(lax.rem(at + length - BLOCK, length), BLOCK), length)
        query_rows = qkv_ref[rows, cols] * jnp.asarray(scale, BF16)
        query = by_head(query_rows, group)
        extra = far_queries(query_rows, group)
        if group == 2 * HEAD_DIM:
            scores = matmul_nt(
                jnp.concatenate([query, extra], axis=1),
                jnp.concatenate([keys[part, window], far_ref[index]], axis=1),
            )
        else:
            scores = matmul_nt(query, keys[part, window]) + matmul_nt(extra, far_ref[index])
        near = near_terms(query, table_ref[...], at, length)
        size = 32
        peaks, totals = [], []
        for start in range(0, heads * BLOCK, size):
            some = slice(start, start + size)
            first_part = scores[some, :WINDOW] + near[some]
            last_part = scores[some, WINDOW:]
            peak = jnp.maximum(
                jnp.max(first_part, axis=1, keepdims=True), jnp.max(last_part, axis=1, keepdims=True)
            )
            first_part = jnp.exp(first_part - peak)
            last_part = jnp.exp(last_part - peak)
            weights[some, :WINDOW] = first_part.astype(BF16)
            weights[some, WINDOW:] = last_part.astype(BF16)
            peaks.append(peak)
            totals.append(
                jnp.sum(first_part, axis=1, keepdims=True) + jnp.sum(last_part, axis=1, keepdims=True)
            )
        total = jnp.concatenate(totals, axis=0)
        mixed = matmul(weights[...], values[part, window]) * (1.0 / total)
        context_ref[rows, cols] = own_lanes(mixed, group).astype(BF16)
        log = jnp.concatenate(peaks, axis=0) + jnp.log(total)
        lane = lax.broadcasted_iota(jnp.int32, (BLOCK, BLOCK), 1)
        square = jnp.where(lane == 0, log[0:BLOCK], 0.0)
        for head in range(1, heads):
            square = jnp.where(lane == head, log[head * BLOCK:(head + 1) * BLOCK], square)
        log_ref[part, :, rows] = square.T[0:8]
        return carry

    lax.fori_loop(0, blocks * parts, block, 0)


def attend_back_core(width, group, qkv_ref, table_ref, far_ref, log_ref, grad_ref, out_ref,
                     table_grad_ref, keys, values, key_grad, value_grad, slot_grad, end_grad, probs,
                     prob_grads, back):
    length = qkv_ref.shape[0]
    heads = group // HEAD_DIM
    parts = width // group
    scale = 1.0 / math.sqrt(HEAD_DIM)
    duplicate(qkv_ref, width, group, keys, values)
    slot_grad[...] = jnp.zeros_like(slot_grad)
    end_grad[...] = jnp.zeros_like(end_grad)
    key_grad[...] = jnp.zeros_like(key_grad)
    value_grad[...] = jnp.zeros_like(value_grad)
    down = lax.broadcasted_iota(jnp.int32, (BLOCK, BLOCK), 0)
    across = lax.broadcasted_iota(jnp.int32, (BLOCK, BLOCK), 1)
    reverse = jnp.where(down + across == BLOCK - 1, 1.0, 0.0).astype(BF16)

    def flip(values_in):
        return jnp.concatenate(
            [
                matmul(reverse, values_in[start:start + BLOCK])
                for start in range(0, heads * BLOCK, BLOCK)
            ],
            axis=0,
        )

    def block(step, carry):
        index, part = step // parts, lax.rem(step, parts)
        at = pl.multiple_of(index * BLOCK, BLOCK)
        rows = pl.ds(at, BLOCK)
        cols = tile(part, group) if parts > 1 else slice(0, group)
        window = pl.ds(pl.multiple_of(lax.rem(at + length - BLOCK, length), BLOCK), length)
        key_rows = keys[part, window]
        far_rows = far_ref[index]
        query_rows = qkv_ref[rows, cols] * jnp.asarray(scale, BF16)
        query = by_head(query_rows, group)
        extra = far_queries(query_rows, group)
        grad = by_head(grad_ref[rows, cols], group)
        query_wide = [query, extra]
        if group == 2 * HEAD_DIM:
            query_wide = [jnp.concatenate(query_wide, axis=1)]
            key_wide = [jnp.concatenate([key_rows, far_rows], axis=1)]
        else:
            key_wide = [key_rows, far_rows]
        near = near_terms(query, table_ref[...], at, length)
        log = jnp.concatenate([log_ref[part, head:head + 1, rows] for head in range(heads)], axis=1)
        value_rows = values[part, window]
        row_dot = jnp.zeros((8, heads * BLOCK), F32)
        for start in range(0, length, BLOCK):
            some = slice(start, start + BLOCK)
            scores = sum(
                matmul_nt(left[some], right) for left, right in zip(key_wide, query_wide)
            )
            if start < WINDOW:
                scores = scores + near[:, some].T
            prob = jnp.exp(scores - log)
            prob_grad = matmul_nt(value_rows[some], grad)
            row_dot = row_dot + fold8(prob * prob_grad)
            probs[some] = prob
            prob_grads[some] = prob_grad
        row_dot = jnp.sum(row_dot, axis=0, keepdims=True)
        for start in range(0, length, BLOCK):
            some = slice(start, start + BLOCK)
            there = pl.ds(pl.multiple_of(window.start + start, BLOCK), BLOCK)
            prob = probs[some]
            score_grad = (prob * (prob_grads[some] - row_dot)).astype(BF16)
            value_grad[part, there] += matmul(prob.astype(BF16), grad)
            key_grad[part, there] += matmul(score_grad, query)
            back[:, some] = score_grad.T
        turned_back = back[...]
        if group == 2 * HEAD_DIM:
            both = matmul(turned_back, key_wide[0])
            direct, ends = both[:, :group], both[:, group:]
        else:
            direct, ends = matmul(turned_back, key_rows), matmul(turned_back, far_rows)
        left_sum, right_sum = ends[:, HEAD_DIM + 1:HEAD_DIM + 2], ends[:, HEAD_DIM + 2:HEAD_DIM + 3]
        query_full = query.astype(F32)
        end_grad[0:8] += fold8(left_sum * query_full)
        end_grad[8:16] += fold8(right_sum * query_full)
        near_grad = jnp.where(
            near_mask(at, length), turned_back[:, :WINDOW], jnp.asarray(0.0, BF16)
        )
        flipped = flip(near_grad)
        skewed = []
        for start in range(0, heads * BLOCK, BLOCK):
            padded = jnp.concatenate(
                [flipped[start:start + BLOCK], jnp.zeros((BLOCK, SPAN - WINDOW), F32)], axis=1
            )
            skewed.append(pltpu.roll(padded, SPAN - (BLOCK - 1), 1, stride=1, stride_axis=0))
        straight = jnp.concatenate(skewed, axis=0).astype(BF16)
        term = matmul(straight, table_ref[...])
        high = term.astype(BF16)
        low = (term - high.astype(F32)).astype(BF16)
        direct = direct + flip(high) + flip(low)
        result = own_lanes(direct, group)
        if heads == 1:
            result = result + ends[:, :HEAD_DIM]
        else:
            lane = lax.broadcasted_iota(jnp.int32, (BLOCK, BLOCK), 1)
            result = result + jnp.where(
                lane < HEAD_DIM, ends[0:BLOCK], pltpu.roll(ends[BLOCK:2 * BLOCK], HEAD_DIM, 1)
            )
        out_ref[rows, cols] = (result * scale).astype(BF16)
        slot_grad[...] += matmul_tn(flip(query).astype(BF16), straight)
        return carry

    lax.fori_loop(0, length // BLOCK * parts, block, 0)
    for part in range(parts):
        base = width + part * group
        out_ref[:, base:base + group] = (
            key_grad[part, 0:length] + key_grad[part, length:2 * length]
        ).astype(BF16)
        out_ref[:, width + base:width + base + group] = (
            value_grad[part, 0:length] + value_grad[part, length:2 * length]
        ).astype(BF16)
    chosen = jnp.where(
        slot_rows(1) == lax.broadcasted_iota(jnp.int32, (LEFT + RIGHT + 8, SPAN), 0), 1.0, 0.0
    )
    table_grad_ref[...] = lax.dot_general(
        chosen, slot_grad[...], (((1,), (1,)), ((), ())), precision=lax.Precision.HIGHEST,
        preferred_element_type=F32,
    )
    table_grad_ref[0:1] += jnp.sum(end_grad[0:8], axis=0, keepdims=True)
    table_grad_ref[LEFT + RIGHT:LEFT + RIGHT + 1] += jnp.sum(end_grad[8:16], axis=0, keepdims=True)


def attention_main(count, gain_row, wire, ins, outs, scratch):
    limit_ref, resid, gains_ref, weights, table_ref = ins
    after_ref, squares_ref, rows_ref, qkv_ref, context_ref, log_ref = outs
    far_ref, keys, values, weights_ref, part, got = scratch
    width = context_ref.shape[1]
    group = keys.shape[2]
    wire.greet()
    wire.begin()
    norm_rows(wire, count, resid, gains_ref[gain_row:gain_row + 1], rows_ref)
    spread = Spread(wire, rows_ref, count)
    spread.start()
    wire.loaded()
    collect = Collect(wire, part, got)
    spread.relay()
    wire.early()
    fill_far(far_ref, table_ref, limit_ref[0])
    chunks = []
    for chunk, slot in spread.arrivals(relay=False):
        chunks.append((chunk, slot))
        rows = tile(chunk, count)
        left = rows_ref[rows]

        def project(cols, index):
            qkv_ref[rows, cols] = matmul(left, weights[:, cols]).astype(BF16)

        block_loop(3 * width, project)
    duplicate(qkv_ref, width, group, keys, values)
    wire.side[0].middle()
    size = max(count, BLOCK)

    def share(chunk, target):
        attend_blocks(chunk * count // BLOCK, size // BLOCK, width, group, qkv_ref, table_ref, far_ref,
                      keys, values, context_ref, log_ref, weights_ref)
        left = context_ref[tile(chunk, count)]

        def leave(cols, index):
            target[:, cols] = matmul_nt(left, weights[cols, 3 * width:]).astype(BF16)

        block_loop(weights.shape[0], leave)

    def last():
        collect.combine()
        wire.side[1].middle()

    send_shares(wire, chunks, collect, share, last)
    wire.flush()
    collect.wait()
    residual(collect, 1.0, resid, limit_ref[0], after_ref, squares_ref)
    spread.finish()
    wire.end()


def attention(sizes, name, collective_id, gain_row, limit, resid, gains, weights, table, **side):
    n, m = sizes
    count, full = resid.shape
    length, width = n * count, weights.shape[1] // 4
    group = min(2 * HEAD_DIM, width)
    return comm_call(
        name, collective_id, sizes, functools.partial(attention_main, count, gain_row),
        [(limit, smem()), (resid, vmem()), (gains, vmem()), (weights, "load"), (table, "load")],
        [
            ((count, full), F32, vmem()),
            ((16, full), F32, vmem()),
            ((length, full), BF16, "store"),
            ((length, 3 * width), BF16, "store"),
            ((length, width), BF16, "store"),
            ((width // group, 8, length), F32, "store"),
        ],
        [
            pltpu.VMEM((length // BLOCK, length, BLOCK), BF16),
            pltpu.VMEM((width // group, 2 * length, group), BF16),
            pltpu.VMEM((width // group, 2 * length, group), BF16),
            pltpu.VMEM((group // HEAD_DIM * BLOCK, length), BF16),
            pltpu.VMEM((n, count, full), BF16),
            pltpu.VMEM((n - 1, count, full), BF16),
        ],
        cost=20 * 10**9, **side,
    )


def attention_back_main(count, gain_row, wire, ins, outs, scratch):
    (limit_ref, grad_ref, resid, gains_ref, weights, table_ref, rows_ref, qkv_ref, context_ref,
     log_ref) = ins
    gain_grad_ref, wide_ref, table_grad_ref, new_grad_ref = outs
    (far_ref, grads, context_grad, qkv_grad, keys, values, key_grad, value_grad, slot_grad, end_grad,
     probs, prob_grads, back, part, got) = scratch
    width = context_ref.shape[1]
    group = keys.shape[2]
    wire.greet()
    wire.begin()
    cast_rows(wire, count, grad_ref, 1.0, grads)
    spread = Spread(wire, grads, count)
    spread.start()
    wire.loaded()
    collect = Collect(wire, part, got)
    spread.relay()
    wire.early()
    fill_far(far_ref, table_ref, limit_ref[0])
    chunks = []
    for chunk, slot in spread.arrivals(relay=False):
        chunks.append((chunk, slot))
        rows = tile(chunk, count)
        context_grad[rows] = matmul(grads[rows], weights[:, 3 * width:]).astype(BF16)
    wire.middle()
    attend_back_core(width, group, qkv_ref, table_ref, far_ref, log_ref, context_grad, qkv_grad,
                     table_grad_ref, keys, values, key_grad, value_grad, slot_grad, end_grad, probs,
                     prob_grads, back)
    def share(chunk, target):
        left = qkv_grad[tile(chunk, count)]

        def back(cols, index):
            target[:, cols] = matmul_nt(left, weights[cols, :3 * width]).astype(BF16)

        block_loop(weights.shape[0], back)

    send_shares(wire, chunks, collect, share)
    collect.combine()

    def weight_grads(rows, index):
        wide_ref[rows, :3 * width] = matmul_tn(rows_ref[:, rows], qkv_grad[...]).astype(BF16)
        wide_ref[rows, 3 * width:] = matmul_tn(grads[:, rows], context_ref[...]).astype(BF16)

    block_loop(weights.shape[0], weight_grads)
    wire.flush()
    wire.end()
    collect.wait()
    residual_back(collect, grad_ref, resid, gains_ref[gain_row:gain_row + 1], new_grad_ref,
                  gain_grad_ref)
    spread.finish()


def attention_back(sizes, name, collective_id, gain_row, limit, grad, resid, gains, weights, table, rows,
                   qkv, context, log_total, **side):
    n, m = sizes
    count, full = resid.shape
    length, width = context.shape
    group = min(2 * HEAD_DIM, width)
    return comm_call(
        name, collective_id, sizes, functools.partial(attention_back_main, count, gain_row),
        [(limit, smem()), (grad, vmem()), (resid, "load"), (gains, vmem())]
        + [(item, "load") for item in (weights, table, rows, qkv, context, log_total)],
        [
            ((8, full), F32, vmem()),
            ((full, 4 * width), BF16, "store"),
            ((LEFT + RIGHT + 8, group), F32, vmem()),
            ((count, full), F32, vmem()),
        ],
        [
            pltpu.VMEM((length // BLOCK, length, BLOCK), BF16),
            pltpu.VMEM((length, full), BF16),
            pltpu.VMEM((length, width), BF16),
            pltpu.VMEM((length, 3 * width), BF16),
            pltpu.VMEM((width // group, 2 * length, group), BF16),
            pltpu.VMEM((width // group, 2 * length, group), BF16),
            pltpu.VMEM((width // group, 2 * length, group), F32),
            pltpu.VMEM((width // group, 2 * length, group), F32),
            pltpu.VMEM((group, SPAN), F32),
            pltpu.VMEM((16, group), F32),
            pltpu.VMEM((length, group // HEAD_DIM * BLOCK), F32),
            pltpu.VMEM((length, group // HEAD_DIM * BLOCK), F32),
            pltpu.VMEM((group // HEAD_DIM * BLOCK, length), BF16),
            pltpu.VMEM((n, count, full), BF16),
            pltpu.VMEM((n - 1, count, full), BF16),
        ],
        cost=50 * 10**9, **side,
    )


PAD = 32
ROWS = 64


def shifted_sets(held, low, high, size):
    for residue in range(8):
        shifts = [shift for shift in range(low, high + 1) if shift % 8 == residue]
        if shifts:
            extent = shifts[-1] - residue + size
            moved = held[residue:residue + extent]
            for shift in shifts:
                yield shift, moved[shift - residue:shift - residue + size]


def stat_rows(blocks, first, second, stats_ref):
    lane = lax.broadcasted_iota(jnp.int32, (BLOCK, BLOCK), 1)
    both = jnp.where(lane == 0, first, jnp.where(lane == 1, second, 0.0))
    stats_ref[:, blocks] = both.T[0:8]


def stat_columns(stats):
    both = jnp.concatenate([stats, jnp.zeros((BLOCK - 8, stats.shape[1]), F32)], axis=0).T
    return both[:, 0:1], both[:, 1:2]


class Stats:
    def __init__(self, wire, mine, got):
        self.wire, self.mine, self.got = wire, mine, got
        self.copies = [
            wire.remote(mine, got.at[step - 1], "col", lax.rem(wire.me + step, wire.n))
            for step in range(1, wire.n)
        ]

    def total(self):
        for copy in self.copies:
            copy.start()
        for copy in self.copies:
            copy.wait()
        total = self.mine[...]
        for step in range(self.wire.n - 1):
            total = total + self.got[step]
        return total


def token_blocks(length, body):
    def step(index, carry):
        body(tile(index, BLOCK), index)
        return carry

    lax.fori_loop(0, length // BLOCK, step, 0)


def convolution_main(count, gain_row, taps, wire, ins, outs, scratch):
    limit_ref, resid, gains_ref, weights, taps_ref, depth_ref = ins
    after_ref, squares_ref, rows_ref, pre_ref, mixed_ref, stats_ref = outs
    kernel_ref, padded, stats_mine, stats_got, act, part, got = scratch
    length, width = mixed_ref.shape
    full = gains_ref.shape[1]
    wire.greet()
    wire.begin()
    norm_rows(wire, count, resid, gains_ref[gain_row:gain_row + 1], rows_ref)
    spread = Spread(wire, rows_ref, count)
    spread.start()
    wire.loaded()
    collect = Collect(wire, part, got)
    stats = Stats(wire, stats_mine, stats_got)
    padded[0:PAD] = jnp.zeros((PAD, width), F32)
    kernel_ref[0:taps] = taps_ref[...].astype(F32)
    spread.relay()
    wire.early()
    chunks = []
    for chunk, slot in spread.arrivals(relay=False):
        chunks.append((chunk, slot))
        rows = tile(chunk, count)
        left = rows_ref[rows]
        value_pre = matmul(left, weights[:, 0:width])
        gate_pre = matmul(left, weights[:, width:2 * width])
        pre_ref[rows, 0:width] = value_pre.astype(BF16)
        pre_ref[rows, width:2 * width] = gate_pre.astype(BF16)
        at = pl.multiple_of(chunk * count + PAD, PAD)
        keep = keep_rows(limit_ref[0], chunk * count, count)
        padded[pl.ds(at, count)] = value_pre * jax.nn.sigmoid(gate_pre) * keep

    def mix(index, carry):
        held = padded[pl.ds(pl.multiple_of(index * ROWS, ROWS), ROWS + PAD)]
        total = jnp.zeros((ROWS, width), F32)
        for shift, moved in shifted_sets(held, PAD - taps + 1, PAD, ROWS):
            tap = shift - (PAD - taps + 1)
            total = total + moved * kernel_ref[tap:tap + 1]
        mixed_ref[tile(index, ROWS)] = total
        return carry

    lax.fori_loop(0, length // ROWS, mix, 0)

    def sums(rows, index):
        mixed = mixed_ref[rows]
        stat_rows(rows, jnp.sum(mixed, axis=1, keepdims=True),
                  jnp.sum(mixed * mixed, axis=1, keepdims=True), stats_mine)

    token_blocks(length, sums)
    total = stats.total() * (1.0 / full)
    inverse = lax.rsqrt(total[1:2] - total[0:1] * total[0:1] + EPSILON)
    stats_ref[...] = jnp.concatenate([total[0:1], inverse, total[2:]], axis=0)

    def share(chunk, target):
        def activate(index, carry):
            rows = tile(chunk * count // BLOCK + index, BLOCK)
            mean, scale = stat_columns(stats_ref[:, rows])
            scaled = (mixed_ref[rows] - mean) * scale * depth_ref[...]
            act[tile(index, BLOCK)] = (scaled * jax.nn.sigmoid(scaled)).astype(BF16)
            return carry

        lax.fori_loop(0, -(-count // BLOCK), activate, 0)
        if count % BLOCK:
            at = lax.rem(chunk * count, BLOCK)
            left = act[pl.ds(pl.multiple_of(at, count), count)]
        else:
            left = act[...]

        def leave(cols, index):
            target[:, cols] = matmul_nt(left, weights[cols, 2 * width:]).astype(BF16)

        block_loop(weights.shape[0], leave)

    send_shares(wire, chunks, collect, share, collect.combine)
    wire.middle()
    wire.flush()
    collect.wait()
    residual(collect, 1.0, resid, limit_ref[0], after_ref, squares_ref)
    spread.finish()
    wire.end()


def convolution(sizes, name, collective_id, gain_row, limit, resid, gains, weights, kernel, depth_gain,
                **side):
    n, m = sizes
    count, full = resid.shape
    length, width = n * count, weights.shape[1] // 3
    return comm_call(
        name, collective_id, sizes,
        functools.partial(convolution_main, count, gain_row, kernel.shape[0]),
        [(limit, smem()), (resid, vmem()), (gains, vmem()), (weights, "load"), (kernel, vmem()),
         (depth_gain, vmem())],
        [
            ((count, full), F32, vmem()),
            ((16, full), F32, vmem()),
            ((length, full), BF16, "store"),
            ((length, 2 * width), BF16, "store"),
            ((length, width), F32, "store"),
            ((8, length), F32, "store"),
        ],
        [
            pltpu.VMEM((PAD, width), F32),
            pltpu.VMEM((length + PAD, width), F32),
            pltpu.VMEM((8, length), F32),
            pltpu.VMEM((n - 1, 8, length), F32),
            pltpu.VMEM((max(count, BLOCK), width), BF16),
            pltpu.VMEM((n, count, full), BF16),
            pltpu.VMEM((n - 1, count, full), BF16),
        ],
        cost=15 * 10**9, **side,
    )


def convolution_back_main(count, gain_row, taps, wire, ins, outs, scratch):
    (limit_ref, grad_ref, resid, gains_ref, weights, taps_ref, depth_ref, rows_ref, pre_ref, mixed_ref,
     stats_ref) = ins
    gain_grad_ref, wide_ref, kernel_grad_ref, depth_grad_ref, new_grad_ref = outs
    (kernel_ref, grads, padded, padded_grad, stats_mine, stats_got, sums_ref, act, pre_grad, part, got) = scratch
    length, width = mixed_ref.shape
    full = gains_ref.shape[1]
    wire.greet()
    wire.begin()
    cast_rows(wire, count, grad_ref, 1.0, grads)
    spread = Spread(wire, grads, count)
    spread.start()
    wire.loaded()
    collect = Collect(wire, part, got)
    stats = Stats(wire, stats_mine, stats_got)
    padded[0:PAD] = jnp.zeros((PAD, width), F32)
    padded_grad[length:] = jnp.zeros((PAD, width), F32)
    sums_ref[...] = jnp.zeros_like(sums_ref)
    depth_grad_ref[...] = jnp.zeros_like(depth_grad_ref)
    kernel_ref[0:taps] = taps_ref[...].astype(F32)
    kernel_grad_ref[...] = jnp.zeros_like(kernel_grad_ref)
    spread.relay()

    def regate(rows, index):
        value_pre = pre_ref[rows, 0:width].astype(F32)
        gate_pre = pre_ref[rows, width:2 * width].astype(F32)
        at = pl.multiple_of(index * BLOCK + PAD, PAD)
        keep = keep_rows(limit_ref[0], index * BLOCK, BLOCK)
        padded[pl.ds(at, BLOCK)] = value_pre * jax.nn.sigmoid(gate_pre) * keep

    token_blocks(length, regate)
    wire.early()
    chunks = []
    for chunk, slot in spread.arrivals(relay=False):
        chunks.append((chunk, slot))
        rows = tile(chunk, count)
        padded_grad[rows] = matmul(grads[rows], weights[:, 2 * width:])
    wire.middle()

    def first(rows, index):
        mean, scale = stat_columns(stats_ref[:, rows])
        normed = (mixed_ref[rows] - mean) * scale
        scaled = normed * depth_ref[...]
        sig = jax.nn.sigmoid(scaled)
        act[rows] = (scaled * sig).astype(BF16)
        scaled_grad = padded_grad[rows] * (sig + scaled * sig * (1.0 - sig))
        depth_grad_ref[...] += fold8(scaled_grad * normed)
        weighted = scaled_grad * depth_ref[...]
        padded_grad[rows] = weighted
        stat_rows(rows, jnp.sum(weighted, axis=1, keepdims=True),
                  jnp.sum(weighted * normed, axis=1, keepdims=True), stats_mine)

    token_blocks(length, first)
    total = stats.total() * (1.0 / full)
    stats_mine[...] = total

    def second(rows, index):
        mean, scale = stat_columns(stats_ref[:, rows])
        normed = (mixed_ref[rows] - mean) * scale
        one, two = stat_columns(stats_mine[:, rows])
        padded_grad[rows] = scale * (padded_grad[rows] - one - normed * two)

    token_blocks(length, second)

    def share(chunk, target):
        def unmix(index, carry):
            start = chunk * count + index * ROWS
            rows = pl.ds(pl.multiple_of(start, ROWS), ROWS)
            ahead = padded_grad[pl.ds(pl.multiple_of(start, ROWS), ROWS + PAD)]
            total = jnp.zeros((ROWS, width), F32)
            for shift, moved in shifted_sets(ahead, 0, taps - 1, ROWS):
                tap = taps - 1 - shift
                total = total + moved * kernel_ref[tap:tap + 1]
            gate = jax.nn.sigmoid(pre_ref[rows, width:2 * width].astype(F32))
            through = total * keep_rows(limit_ref[0], start, ROWS) * gate
            pre_grad[rows, 0:width] = through.astype(BF16)
            pre_grad[rows, width:2 * width] = (
                through * pre_ref[rows, 0:width].astype(F32) * (1.0 - gate)
            ).astype(BF16)
            return carry

        lax.fori_loop(0, count // ROWS, unmix, 0)
        left = pre_grad[tile(chunk, count)]

        def back(cols, index):
            target[:, cols] = matmul_nt(left, weights[cols, :2 * width]).astype(BF16)

        block_loop(weights.shape[0], back)

    send_shares(wire, chunks, collect, share)
    collect.combine()

    def tap_grads(index, carry):
        here = padded_grad[tile(index, ROWS)]
        around = pl.ds(pl.multiple_of(index * ROWS, ROWS), ROWS + PAD)
        for shift, moved in shifted_sets(padded[around], PAD - taps + 1, PAD, ROWS):
            tap = shift - (PAD - taps + 1)
            sums_ref[tap * 8:(tap + 1) * 8] += fold8(here * moved)
        return carry

    lax.fori_loop(0, length // ROWS, tap_grads, 0)
    for tap in range(taps):
        kernel_grad_ref[tap:tap + 1] = jnp.sum(sums_ref[tap * 8:(tap + 1) * 8], axis=0, keepdims=True)

    def weight_grads(rows, index):
        wide_ref[rows, :2 * width] = matmul_tn(rows_ref[:, rows], pre_grad[...]).astype(BF16)
        wide_ref[rows, 2 * width:] = matmul_tn(grads[:, rows], act[...]).astype(BF16)

    block_loop(weights.shape[0], weight_grads)
    wire.flush()
    wire.end()
    collect.wait()
    residual_back(collect, grad_ref, resid, gains_ref[gain_row:gain_row + 1], new_grad_ref,
                  gain_grad_ref)
    spread.finish()


def convolution_back(sizes, name, collective_id, gain_row, limit, grad, resid, gains, weights, kernel,
                     depth_gain, rows, pre, mixed, stats, **side):
    n, m = sizes
    count, full = resid.shape
    length, width = mixed.shape
    taps = kernel.shape[0]
    return comm_call(
        name, collective_id, sizes,
        functools.partial(convolution_back_main, count, gain_row, taps),
        [(limit, smem()), (grad, vmem()), (resid, "load"), (gains, vmem()), (weights, "load"),
         (kernel, vmem()), (depth_gain, vmem())]
        + [(item, "load") for item in (rows, pre, mixed, stats)],
        [
            ((8, full), F32, vmem()),
            ((full, 3 * width), BF16, "store"),
            ((PAD, width), F32, vmem()),
            ((8, width), F32, vmem()),
            ((count, full), F32, vmem()),
        ],
        [
            pltpu.VMEM((PAD, width), F32),
            pltpu.VMEM((length, full), BF16),
            pltpu.VMEM((length + PAD, width), F32),
            pltpu.VMEM((length + PAD, width), F32),
            pltpu.VMEM((8, length), F32),
            pltpu.VMEM((n - 1, 8, length), F32),
            pltpu.VMEM((8 * taps, width), F32),
            pltpu.VMEM((length, width), BF16),
            pltpu.VMEM((length, 2 * width), BF16),
            pltpu.VMEM((n, count, full), BF16),
            pltpu.VMEM((n - 1, count, full), BF16),
        ],
        cost=20 * 10**9, **side,
    )


def results_kernel(*refs):
    sources, targets = refs[:len(refs) // 2], refs[len(refs) // 2:]
    for source, target in zip(sources, targets):
        if target.shape[0] == 1 and source.shape[0] == 8:
            target[...] = source[...].T[0:1]
        elif source.shape != target.shape:
            target[...] = source[...].astype(target.dtype).T
        else:
            target[...] = source[...]


def results(arrays, shapes):
    return pl.pallas_call(
        results_kernel,
        name="results",
        out_shape=tuple(shapes),
        in_specs=[vmem()] * len(arrays),
        out_specs=tuple(vmem() for _ in arrays),
        compiler_params=pltpu.CompilerParams(vmem_limit_bytes=VMEM_LIMIT),
    )(*arrays)


def body(
    layer_input,
    clip_lengths,
    first_gain,
    first_up,
    first_down,
    attend_gain,
    query_weight,
    key_weight,
    value_weight,
    output_weight,
    distance_table,
    conv_gain,
    pointwise_value,
    pointwise_gate,
    depthwise_kernel,
    depthwise_gain,
    pointwise_out,
    second_gain,
    second_up,
    second_down,
    final_gain,
    output_cotangent,
):
    n = lax.axis_size("col")
    me = lax.axis_index("col")
    width, length = layer_input.shape
    full = n * width
    count = length // n

    sizes = (n, lax.axis_size("row"))
    group = min(2 * HEAD_DIM, width)
    table_wide = extend_table(distance_table, group // HEAD_DIM)
    limit = clip_lengths
    tap_count = depthwise_kernel.shape[0]
    gain_parts = [
        gain[None] for gain in (first_gain, attend_gain, conv_gain, second_gain, final_gain)
    ]
    attend_pieces = [
        (query_weight, False), (key_weight, False), (value_weight, False), (output_weight, True)
    ]
    conv_pieces = [(pointwise_value, False), (pointwise_gate, False), (pointwise_out, True)]
    hidden = first_up.shape[1]
    tokens_in = (layer_input, output_cotangent)
    if count % BLOCK:
        tokens_in = (layer_input.T, output_cotangent.T)

    (start, cot, gains, up_first, down_first, attend_weights, after_first, squares_first, rows_first,
     pre_first) = feed_forward(
        sizes, "first", 1, 0, first_up, first_down, limit,
        enter=(*tokens_in, gain_parts, attend_pieces),
    )
    (after_attend, squares_attend, rows_attend, qkv, context, log_total, conv_weights,
     up_second) = attention(
        sizes, "attend", 2, 1, limit, after_first, gains, attend_weights, table_wide,
        gathers=[conv_pieces, [(second_up, False)]],
    )
    depth_row = depthwise_gain[None]
    (after_conv, squares_conv, rows_conv, conv_pre, mixed, stats, down_second) = convolution(
        sizes, "convolve", 3, 2, limit, after_attend, gains, conv_weights, depthwise_kernel, depth_row,
        gathers=[[(second_down, True)]],
    )
    (grad_second, final_part, out_tokens, squares_second, rows_second, pre_second) = feed_forward(
        sizes, "second", 4, 3, up_second, down_second, limit, resid=after_conv, gains=gains, turn=cot
    )

    second_part, second_up_wide, second_down_wide, grad_conv, layer_output = feed_forward_back(
        sizes, "second_back", 5, 3, grad_second, after_conv, gains, up_second, down_second,
        rows_second, pre_second, tokens=out_tokens,
    )
    conv_part, conv_wide, kernel_part, depth_part, grad_attend, second_up_grad = convolution_back(
        sizes, "convolve_back", 6, 2, limit, grad_conv, after_attend, gains, conv_weights,
        depthwise_kernel, depth_row, rows_conv, conv_pre, mixed, stats,
        reduces=[(second_up_wide, [(hidden, False)])],
    )
    (attend_part, attend_wide, table_part, grad_first, second_down_grad, value_grad, gate_grad,
     out_grad) = attention_back(
        sizes, "attend_back", 7, 1, limit, grad_attend, after_first, gains, attend_weights,
        table_wide, rows_attend, qkv, context, log_total,
        reduces=[
            (second_down_wide, [(hidden, True)]),
            (conv_wide, [(width, False), (width, False), (width, True)]),
        ],
    )
    (first_sum, attend_sum, conv_sum, second_sum, final_sum, table_sum, masked_rms, kernel_sum,
     depth_sum, first_up_grad, first_down_grad, grad_tokens, query_grad, key_grad, attend_value_grad,
     output_grad) = feed_forward_back(
        sizes, "first_back", 0, 0, grad_first, start, gains, up_first, down_first, rows_first,
        pre_first, taps=tap_count,
        leave=(
            limit, (attend_part, conv_part, second_part, final_part),
            (squares_first, squares_attend, squares_conv, squares_second), table_part, kernel_part,
            depth_part,
        ),
        reduces=[(attend_wide, [(width, False), (width, False), (width, False), (width, True)])],
    )

    arrays = [
        layer_output, grad_tokens, first_sum, first_up_grad, first_down_grad, attend_sum, query_grad,
        key_grad, attend_value_grad, output_grad, table_sum, conv_sum, value_grad, gate_grad, kernel_sum,
        depth_sum, out_grad, second_sum, second_up_grad, second_down_grad, final_sum, masked_rms,
    ]
    shapes = [jax.ShapeDtypeStruct(array.shape, array.dtype) for array in arrays]
    shapes[1] = jax.ShapeDtypeStruct(grad_tokens.shape[::-1], F32)
    shapes[-1] = jax.ShapeDtypeStruct((1, 8), F32)
    arrays = results(arrays, shapes)
    return tuple(array[0] if array.shape[0] == 1 else array for array in arrays)


def solution(mesh):
    in_specs = (
        P("col", "row"),
        P("row"),
        P("col"),
        P("row", "col"),
        P("col", "row"),
        P("col"),
        P("row", "col"),
        P("row", "col"),
        P("row", "col"),
        P("col", "row"),
        P(),
        P("col"),
        P("row", "col"),
        P("row", "col"),
        P(None, "col"),
        P("col"),
        P("col", "row"),
        P("col"),
        P("row", "col"),
        P("col", "row"),
        P("col"),
        P("col", "row"),
    )
    out_specs = (
        P("col", "row"),
        P("col", "row"),
        P("col"),
        P("row", "col"),
        P("col", "row"),
        P("col"),
        P("row", "col"),
        P("row", "col"),
        P("row", "col"),
        P("col", "row"),
        P(),
        P("col"),
        P("row", "col"),
        P("row", "col"),
        P(None, "col"),
        P("col"),
        P("col", "row"),
        P("col"),
        P("row", "col"),
        P("col", "row"),
        P("col"),
        P(),
    )
    return jax.shard_map(body, mesh=mesh, in_specs=in_specs, out_specs=out_specs, check_vma=False)
```

```python
import functools
import math

import jax
import jax.numpy as jnp
from jax import lax
from jax.experimental import pallas as pl
from jax.experimental.pallas import tpu as pltpu
from jax.sharding import PartitionSpec as P

HEAD_DIM = 64
LEFT = 64
RIGHT = 8
EPSILON = 1e-05
NEG_FILL = -1e30
BF16 = jnp.bfloat16
F32 = jnp.float32
MESH = pl.DeviceIdType.MESH
BLOCK = 128
WINDOW = 384
SPAN = 512
VMEM_LIMIT = 60 * 1024 * 1024
MARGIN = 6 * 1024 * 1024


def matmul(left, right):
    return jnp.dot(left, right, preferred_element_type=F32)


def matmul_nt(left, right):
    return lax.dot_general(left, right, (((1,), (1,)), ((), ())), preferred_element_type=F32)


def matmul_tn(left, right):
    return lax.dot_general(left, right, (((0,), (0,)), ((), ())), preferred_element_type=F32)


def vmem():
    return pl.BlockSpec(memory_space=pltpu.VMEM)


def smem():
    return pl.BlockSpec(memory_space=pltpu.SMEM)


def hbm():
    return pl.BlockSpec(memory_space=pltpu.HBM)


def padded_bytes(shape, dtype):
    size = jnp.dtype(dtype).itemsize
    rows = 8 * 4 // size
    shape = (1,) * (2 - len(shape)) + tuple(shape)
    held = -(-shape[-1] // 128) * 128 * -(-shape[-2] // rows) * rows
    return math.prod(shape[:-2]) * held * size


def comm_params(collective_id, held):
    return pltpu.CompilerParams(
        collective_id=collective_id, has_side_effects=True,
        vmem_limit_bytes=max(VMEM_LIMIT, held + MARGIN),
    )


def tile(index, size):
    return pl.ds(pl.multiple_of(index * size, size), size)


class Wire:
    def __init__(self, sizes, send_sem, recv_sem, local_sem, side, col_on=True, row_on=False):
        self.n, self.m = sizes
        self.me = lax.axis_index("col")
        self.row = lax.axis_index("row")
        self.send_sem, self.recv_sem, self.local_sem = send_sem, recv_sem, local_sem
        self.used = 0
        self.used_local = 0
        self.core = lax.rem(self.row, 2)
        self.layer = self.row // 2
        self.partner = self.row + 1 - 2 * self.core
        self.layers = self.m // 2
        self.col_on = col_on
        self.loads, self.stores, self.stored = [], [], []
        self.row_on = row_on or bool(side)
        self.side = [job(self) for job in side]

    def layer_peer(self, step):
        return lax.rem(self.layer + step, self.layers) * 2 + self.core

    def greet(self):
        barrier = pltpu.get_barrier_semaphore()
        waits = 0
        if self.col_on:
            for step in range(1, self.n):
                pl.semaphore_signal(
                    barrier, inc=1, device_id={"col": lax.rem(self.me + step, self.n)},
                    device_id_type=MESH,
                )
            waits += self.n - 1
        if self.row_on:
            for step in range(1, self.layers):
                pl.semaphore_signal(
                    barrier, inc=1, device_id={"row": self.layer_peer(step)}, device_id_type=MESH
                )
            pl.semaphore_signal(
                barrier, inc=1, device_id={"row": self.partner}, device_id_type=MESH
            )
            waits += self.layers
        pl.semaphore_wait(barrier, waits)

    def remote(self, source, target, axis, peer):
        slot = self.used
        self.used += 1
        return pltpu.make_async_remote_copy(
            src_ref=source, dst_ref=target, send_sem=self.send_sem.at[slot],
            recv_sem=self.recv_sem.at[slot], device_id={axis: peer}, device_id_type=MESH,
        )

    def local(self, source, target):
        slot = self.used_local
        self.used_local += 1
        return pltpu.make_async_copy(source, target, self.local_sem.at[slot])

    def to_all(self, source_of, target):
        copies = [
            self.remote(source_of(lax.rem(self.me + step, self.n)), target, "col",
                        lax.rem(self.me + step, self.n))
            for step in range(1, self.n)
        ]
        for copy in copies:
            copy.start()
        return copies

    def loaded(self):
        for copy in self.loads:
            copy.wait()

    def store(self, copies):
        for copy in copies:
            copy.start()
        self.stored += copies

    def flush(self):
        self.store(self.stores)

    def settle(self):
        for copy in self.stored:
            copy.wait()

    def begin(self):
        for job in self.side:
            job.begin()

    def early(self):
        for job in self.side:
            job.early()

    def middle(self):
        for job in self.side:
            job.middle()

    def end(self):
        for job in self.side:
            job.end()

    def peers(self):
        if self.n == 4:
            across = self.me + 1 - 2 * lax.rem(self.me, 2)
            along = lax.rem(self.me + 2, 4)
            return [(across, 0), (along, 1), (3 - self.me, 2)]
        return [
            (lax.rem(self.me + self.n - step, self.n), self.n - step - 1)
            for step in range(1, self.n)
        ]


class Spread:
    def __init__(self, wire, ref, count):
        self.wire, self.ref, self.count = wire, ref, count
        me = wire.me
        if wire.n != 4:
            self.copies = [
                wire.remote(self.part(me), self.part(me), "col", lax.rem(me + step, wire.n))
                for step in range(1, wire.n)
            ]
            return
        (across, _), (along, _), (far, _) = wire.peers()
        self.across = [wire.remote(self.part(me, q), self.part(me, q), "col", across) for q in range(4)]
        self.along = [wire.remote(self.part(me, q), self.part(me, q), "col", along) for q in range(4)]
        self.onward = [
            wire.remote(self.part(across, q), self.part(across, q), "col", along) for q in (0, 1)
        ] + [wire.remote(self.part(along, q), self.part(along, q), "col", across) for q in (2, 3)]

    def part(self, chunk, quarter=None):
        if quarter is None:
            return self.ref.at[tile(chunk, self.count)]
        size = self.count // 4
        return self.ref.at[tile(chunk * 4 + quarter, size)]

    def start(self):
        if self.wire.n != 4:
            for copy in self.copies:
                copy.start()
            return
        for first, second in ((0, 2), (1, 3), (2, 0), (3, 1)):
            self.across[first].start()
            self.along[second].start()

    def relay(self):
        if self.wire.n != 4:
            return
        for turn in range(2):
            self.relay_turn(turn)

    def relay_turn(self, turn):
        self.across[turn].wait_recv()
        self.onward[turn].start()
        self.along[2 + turn].wait_recv()
        self.onward[2 + turn].start()

    def wait_place(self, place):
        for copy in (self.across[2:], self.along[:2], self.onward)[place - 1]:
            copy.wait_recv()

    def arrivals(self, relay=True):
        wire = self.wire
        yield wire.me, None
        if wire.n != 4:
            for step, (peer, slot) in zip(range(1, wire.n), wire.peers()):
                self.copies[step - 1].wait_recv()
                yield peer, slot
            return
        if relay:
            self.relay()
        for place, (peer, slot) in enumerate(wire.peers()):
            self.wait_place(place + 1)
            yield peer, slot

    def finish(self):
        copies = self.copies if self.wire.n != 4 else self.across + self.along + self.onward
        for copy in copies:
            copy.wait_send()


class Collect:
    def __init__(self, wire, part, got):
        self.wire, self.part, self.got = wire, part, got
        self.relayed = wire.n == 4
        self.count = part.shape[1]
        if not self.relayed:
            self.copies = {
                slot: wire.remote(part.at[slot], got.at[slot], "col", owner)
                for owner, slot in wire.peers()
            }
            return
        (across, _), (along, _), _ = wire.peers()
        half = self.count // 2
        first, second = pl.ds(0, half), pl.ds(half, half)
        places = [got.at[place // 2, (first, second)[place % 2]] for place in range(6)]
        self.far = [
            wire.remote(part.at[2, first], places[0], "col", across),
            wire.remote(part.at[2, second], places[1], "col", along),
        ]
        self.direct = {
            0: wire.remote(part.at[0, first], places[2], "col", across),
            1: wire.remote(part.at[1, second], places[4], "col", along),
        }
        self.onward = [
            wire.remote(part.at[0, second], places[3], "col", across),
            wire.remote(part.at[1, first], places[5], "col", along),
        ]

    def send(self, slot):
        if not self.relayed:
            self.copies[slot].start()
        elif slot == 2:
            for copy in self.far:
                copy.start()
        else:
            self.direct[slot].start()

    def combine(self):
        if not self.relayed:
            return
        half = self.count // 2
        for copy, slot, at, onward in (
            (self.far[1], 0, half, self.onward[0]), (self.far[0], 1, 0, self.onward[1])
        ):
            copy.wait_recv()
            place = 1 - slot

            def add(rows, index):
                mine = pl.ds(pl.multiple_of(at + index * 32, 32), 32)
                came = pl.ds(pl.multiple_of((half if place else 0) + index * 32, 32), 32)
                self.part[slot, mine] = (
                    self.part[slot, mine].astype(F32) + self.got[0, came].astype(F32)
                ).astype(BF16)

            row_loop(half, add)
            onward.start()

    def wait(self):
        if not self.relayed:
            for copy in self.copies.values():
                copy.wait()
            return
        for copy in self.far:
            copy.wait_send()
        for copy in list(self.direct.values()) + self.onward:
            copy.wait()

    def sum_loop(self, body):
        part, got, last = self.part, self.got, self.wire.n - 1
        if not self.relayed:
            def step(rows, index):
                total = part[last, rows].astype(F32)
                for slot in range(last):
                    total = total + got[slot, rows].astype(F32)
                body(rows, total)

            row_loop(self.count, step)
            return
        half = self.count // 2
        for at, sources in ((0, ((1, 0), (2, half))), (half, ((1, half), (2, 0)))):
            def step(rows, index, at=at, sources=sources):
                mine = pl.ds(pl.multiple_of(at + index * 32, 32), 32)
                total = part[last, mine].astype(F32)
                for slot, start in sources:
                    total = total + got[
                        slot, pl.ds(pl.multiple_of(start + index * 32, 32), 32)
                    ].astype(F32)
                body(mine, total)

            row_loop(half, step)


class RowChain:
    def __init__(self, shard, full, wire):
        self.wire, self.shard, self.full = wire, shard, full
        self.count = shard.shape[0]
        self.steps = wire.layers - 1
        self.base = wire.used
        wire.used += 4 * self.steps
        mine = full.at[tile(wire.row, self.count)]
        self.own = [wire.local(shard, mine), wire.remote(shard, mine, "row", wire.partner)]

    def block(self, layer):
        return self.full.at[tile(layer * 2 + self.wire.core, self.count)]

    def copy(self, kind, step, layer, peer):
        slot = self.base + kind * self.steps + step
        wire = self.wire
        source = self.shard if kind < 2 and step == 0 else self.block(layer)
        return pltpu.make_async_remote_copy(
            src_ref=source, dst_ref=self.block(layer), send_sem=wire.send_sem.at[slot],
            recv_sem=wire.recv_sem.at[slot], device_id={"row": peer}, device_id_type=MESH,
        )

    def up(self, step):
        wire = self.wire
        return self.copy(0, step, wire.layer - step, wire.row + 2)

    def down(self, step):
        wire = self.wire
        return self.copy(1, step, wire.layer + step, wire.row - 2)

    def begin(self):
        wire = self.wire
        pl.when(wire.layer + 1 < wire.layers)(lambda: self.up(0).start())
        pl.when(wire.layer > 0)(lambda: self.down(0).start())
        for copy in self.own:
            copy.start()

    def advance(self, step):
        wire = self.wire

        @pl.when(wire.layer - 1 - step >= 0)
        def _():
            self.copy(0, step, wire.layer - 1 - step, wire.row).wait_recv()
            if step + 1 < self.steps:
                pl.when(wire.layer + 1 < wire.layers)(lambda: self.up(step + 1).start())
            self.copy(2, step, wire.layer - 1 - step, wire.partner).start()

        @pl.when(wire.layer + 1 + step < wire.layers)
        def _():
            self.copy(1, step, wire.layer + 1 + step, wire.row).wait_recv()
            if step + 1 < self.steps:
                pl.when(wire.layer > 0)(lambda: self.down(step + 1).start())
            self.copy(3, step, wire.layer + 1 + step, wire.partner).start()

    def end(self):
        wire = self.wire
        for step in range(self.steps):
            pl.when((wire.layer + 1 < wire.layers) & (wire.layer - step >= 0))(
                lambda step=step: self.up(step).wait_send()
            )
            pl.when((wire.layer > 0) & (wire.layer + step < wire.layers))(
                lambda step=step: self.down(step).wait_send()
            )
            pl.when(wire.layer - 1 - step >= 0)(
                lambda step=step: self.copy(2, step, wire.layer - 1 - step, wire.partner).wait()
            )
            pl.when(wire.layer + 1 + step < wire.layers)(
                lambda step=step: self.copy(3, step, wire.layer + 1 + step, wire.partner).wait()
            )
        for copy in self.own:
            copy.wait()


class RowGather:
    def __init__(self, shard, full, wire):
        self.wire = wire
        count = shard.shape[0]
        mine = full.at[tile(wire.row, count)]
        self.first = [wire.local(shard, mine), wire.remote(shard, mine, "row", wire.partner)]
        self.along = [
            wire.remote(shard, mine, "row", wire.layer_peer(step))
            for step in range(1, wire.layers)
        ]
        self.onward = []
        for step in range(1, wire.layers):
            block = full.at[tile(wire.layer_peer(wire.layers - step), count)]
            self.onward.append(wire.remote(block, block, "row", wire.partner))

    def begin(self):
        for copy in self.along + self.first:
            copy.start()

    def early(self):
        pass

    def middle(self):
        for copy, onward in zip(self.along, self.onward):
            copy.wait_recv()
            onward.start()

    def end(self):
        for copy in self.along:
            copy.wait_send()
        for copy in self.first:
            copy.wait()
        for copy in self.onward:
            copy.wait()


class RowReduce:
    def __init__(self, grads, pieces, outs, held, pair, got, total, *rest, load=True):
        *parts, wire = rest
        self.wire, self.out, self.grads = wire, total, grads
        self.pieces = pieces
        self.parts = parts or [total]
        self.keep = [wire.local(part, out) for part, out in zip(self.parts, outs)]
        self.held, self.pair, self.got = held, pair, got
        self.count = held.shape[1]
        self.load = []
        if load:
            self.load = [
                wire.local(grads.at[tile(layer * 2 + wire.core, self.count)], held.at[layer])
                for layer in range(wire.layers)
            ]
        self.base = wire.used
        wire.used += 2 * wire.layers

    def layer_of(self, step):
        return lax.rem(self.wire.layer + 1 + step, self.wire.layers)

    def between(self, source, target, slot, peer):
        wire = self.wire
        return pltpu.make_async_remote_copy(
            src_ref=source, dst_ref=target, send_sem=wire.send_sem.at[self.base + slot],
            recv_sem=wire.recv_sem.at[self.base + slot], device_id={"row": peer}, device_id_type=MESH,
        )

    def swap(self, step):
        layer = self.layer_of(step)
        block = layer * 2 + 1 - self.wire.core
        return self.between(self.grads.at[tile(block, self.count)], self.pair.at[layer], step,
                            self.wire.partner)

    def along(self, step):
        layer = self.layer_of(step)
        return self.between(self.held.at[layer], self.got.at[step], self.wire.layers + step,
                            layer * 2 + self.wire.core)

    def begin_step(self, step):
        self.swap(step).start()

    def early_step(self, step):
        self.swap(step).wait()
        layer = self.layer_of(step)
        size = min(32, self.count)

        def add(rows, index):
            if self.load:
                mine = self.held[layer, rows]
            else:
                at = (layer * 2 + self.wire.core) * self.count + index * size
                mine = self.grads[pl.ds(pl.multiple_of(at, size), size)]
            self.held[layer, rows] = (
                mine.astype(F32) + self.pair[layer, rows].astype(F32)
            ).astype(BF16)

        row_loop(self.count, add)
        pl.when(step < self.wire.layers - 1)(lambda: self.along(step).start())

    def begin(self):
        for step in range(self.wire.layers):
            self.begin_step(step)
        for copy in self.load:
            copy.start()

    def early(self):
        for copy in self.load:
            copy.wait()

        def one(step, carry):
            self.early_step(step)
            return carry

        lax.fori_loop(0, self.wire.layers, one, 0)

    def middle(self):
        pass

    def end(self):
        for step in range(self.wire.layers - 1):
            self.along(step).wait()

        def add(rows, index):
            total = self.held[self.wire.layer, rows].astype(F32)
            for step in range(self.wire.layers - 1):
                total = total + self.got[step, rows].astype(F32)
            self.out[rows] = total

        row_loop(self.count, add)
        if len(self.parts) > 1 or self.pieces[0][1]:
            at = 0
            for part, (width, flip) in zip(self.parts, self.pieces):
                piece = self.out[:, at:at + width]
                part[...] = piece.T if flip else piece
                at += width
        self.wire.store(self.keep)


def piece_shapes(count, pieces):
    return [(width, count) if flip else (count, width) for width, flip in pieces]


def reduce_scratch(layers, count, width, pieces):
    apart = len(pieces) > 1 or pieces[0][1]
    parts = [pltpu.VMEM(shape, F32) for shape in piece_shapes(count, pieces)] if apart else []
    return parts_last(layers, count, width) + parts


def parts_last(layers, count, width):
    return [
        pltpu.VMEM((layers, count, width), BF16),
        pltpu.VMEM((layers, count, width), BF16),
        pltpu.VMEM((max(1, layers - 1), count, width), BF16),
        pltpu.VMEM((count, width), F32),
    ]


class SumItem:
    def __init__(self, kind, source, out, got, packed, got_row, wire):
        self.wire, self.kind, self.source, self.out = wire, kind, source, out
        self.got, self.packed, self.got_row = got, packed, got_row
        self.col = []
        if kind != "own":
            for step in range(1, wire.n):
                peer = lax.rem(wire.me + step, wire.n)
                piece = source.at[peer] if kind == "piece" else source
                self.col.append(wire.remote(piece, got.at[step - 1], "col", peer))
        self.swap = wire.remote(packed.at[0], got_row.at[0], "row", wire.partner)
        self.along = [
            wire.remote(packed.at[1], got_row.at[step], "row", wire.layer_peer(step))
            for step in range(1, wire.layers)
        ]

    def begin(self):
        for copy in self.col:
            copy.start()

    def early(self):
        for copy in self.col:
            copy.wait()
        total = self.source[self.wire.me] if self.kind == "piece" else self.source[...]
        if self.kind != "own":
            for step in range(self.wire.n - 1):
                total = total + self.got[step]
        self.packed[0] = total
        self.swap.start()

    def middle(self):
        self.swap.wait()
        self.packed[1] = self.packed[0] + self.got_row[0]
        for copy in self.along:
            copy.start()

    def end(self):
        for copy in self.along:
            copy.wait()
        total = self.packed[1]
        for step in range(1, self.wire.layers):
            total = total + self.got_row[step]
        self.out[...] = total


def sum_scratch(n, layers, shape):
    return [
        pltpu.VMEM(shape, F32),
        pltpu.VMEM((n - 1,) + shape, F32),
        pltpu.VMEM((2,) + shape, F32),
        pltpu.VMEM((layers,) + shape, F32),
    ]


def join(pieces, target):
    at = 0
    for ref, flip in pieces:
        width = ref.shape[0] if flip else ref.shape[1]
        target[:, at:at + width] = ref[...].T if flip else ref[...]
        at += width


def joined_shape(pieces):
    rows = {array.shape[1] if flip else array.shape[0] for array, flip in pieces}
    return rows.pop(), sum(array.shape[0] if flip else array.shape[1] for array, flip in pieces)


def row_loop(count, body):
    size = min(32, count)

    def step(index, carry):
        body(tile(index, size), index)
        return carry

    lax.fori_loop(0, count // size, step, 0)


def block_loop(extent, body):
    size = min(256, extent)

    def step(index, carry):
        body(tile(index, size), index)
        return carry

    lax.fori_loop(0, extent // size, step, 0)


def fold8(values):
    return jnp.sum(values.reshape(values.shape[0] // 8, 8, values.shape[1]), axis=0)


def normalize(values):
    average = jnp.mean(values, axis=1, keepdims=True)
    centered = values - average
    inverse = lax.rsqrt(jnp.mean(centered * centered, axis=1, keepdims=True) + EPSILON)
    return centered * inverse, inverse


def norm_back(grad_in, normed, inverse, gains):
    scaled = grad_in * gains
    first = jnp.mean(scaled, axis=1, keepdims=True)
    second = jnp.mean(scaled * normed, axis=1, keepdims=True)
    return inverse * (scaled - first - normed * second)


def comm_call(name, collective_id, sizes, main, ins, outs, scratch, gathers=(), reduces=(), cost=10**9,
              col_on=True, more_slots=0, row_on=False):
    n, m = sizes
    layers = m // 2
    gather_pieces = [piece for pieces in gathers for piece in pieces]
    in_arrays = [item[0] for item in ins] + [array for array, _ in gather_pieces]
    in_arrays += [grads for grads, _ in reduces]
    in_specs = [hbm() if item[1] == "load" else item[1] for item in ins]
    in_specs += [vmem()] * len(gather_pieces) + [hbm()] * len(reduces)
    out_shapes = [jax.ShapeDtypeStruct(item[0], item[1]) for item in outs]
    out_specs = [hbm() if item[2] == "store" else item[2] for item in outs]
    copied = [pltpu.VMEM(item[0].shape, item[0].dtype) for item in ins if item[1] == "load"]
    copied += [pltpu.VMEM(item[0], item[1]) for item in outs if item[2] == "store"]
    side_scratch = []
    for pieces in gathers:
        rows, width = joined_shape(pieces)
        out_shapes.append(jax.ShapeDtypeStruct((m * rows, width), BF16))
        out_specs.append(hbm())
        side_scratch.append(pltpu.VMEM((rows, width), BF16))
    reduce_counts = []
    for grads, pieces in reduces:
        count, width = grads.shape[0] // m, grads.shape[1]
        for shape in piece_shapes(count, pieces):
            out_shapes.append(jax.ShapeDtypeStruct(shape, F32))
            out_specs.append(hbm())
        made = reduce_scratch(layers, count, width, pieces)
        reduce_counts.append(len(made))
        side_scratch += made
    every_scratch = copied + list(scratch) + side_scratch
    held = sum(padded_bytes(item.shape, item.dtype) for item in every_scratch)
    remote_slots = 8 * n + 16 + len(gathers) * 2 * layers + len(reduces) * 2 * layers + more_slots
    local_slots = 12 + len(copied) + len(gathers) + len(reduces) * (layers + 4) + more_slots

    def kernel(*refs):
        at = 0

        def take(count):
            nonlocal at
            at += count
            return refs[at - count:at]

        main_ins = list(take(len(ins)))
        gather_ins = [
            [(ref, flip) for ref, (_, flip) in zip(take(len(pieces)), pieces)] for pieces in gathers
        ]
        reduce_ins = take(len(reduces))
        main_outs = list(take(len(outs)))
        gather_outs = take(len(gathers))
        reduce_outs = [take(len(pieces)) for _, pieces in reduces]
        loads, stores = [], []
        for place, item in enumerate(ins):
            if item[1] == "load":
                (held_ref,) = take(1)
                loads.append((main_ins[place], held_ref))
                main_ins[place] = held_ref
        for place, item in enumerate(outs):
            if item[2] == "store":
                (held_ref,) = take(1)
                stores.append((held_ref, main_outs[place]))
                main_outs[place] = held_ref
        main_scratch = take(len(scratch))
        side = []
        for pieces, full in zip(gather_ins, gather_outs):
            (shard,) = take(1)
            join(pieces, shard)
            side.append(functools.partial(RowGather, shard, full))
        for grads, out, (_, pieces), size in zip(reduce_ins, reduce_outs, reduces, reduce_counts):
            side.append(functools.partial(RowReduce, grads, pieces, out, *take(size)))
        send_sem, recv_sem, local_sem = take(3)
        wire = Wire(sizes, send_sem, recv_sem, local_sem, side, col_on, row_on)
        wire.loads = [wire.local(*pair) for pair in loads]
        wire.stores = [wire.local(*pair) for pair in stores]
        for copy in wire.loads:
            copy.start()
        main(wire, main_ins, main_outs, main_scratch)
        wire.settle()

    return pl.pallas_call(
        kernel,
        name=name,
        out_shape=tuple(out_shapes),
        in_specs=in_specs,
        out_specs=tuple(out_specs),
        scratch_shapes=every_scratch + [
            pltpu.SemaphoreType.DMA((remote_slots,)),
            pltpu.SemaphoreType.DMA((remote_slots,)),
            pltpu.SemaphoreType.DMA((local_slots,)),
        ],
        compiler_params=comm_params(collective_id, held),
        cost_estimate=pl.CostEstimate(flops=cost, bytes_accessed=10**8, transcendentals=0),
    )(*in_arrays)


def norm_rows(wire, count, source, gains, rows_ref):
    base = wire.me * count

    def work(rows, index):
        normed, _ = normalize(source[rows])
        size = min(32, count)
        rows_ref[pl.ds(pl.multiple_of(base + index * size, size), size)] = (normed * gains).astype(BF16)

    row_loop(count, work)


def cast_rows(wire, count, source, factor, rows_ref):
    base = wire.me * count

    def work(rows, index):
        size = min(32, count)
        rows_ref[pl.ds(pl.multiple_of(base + index * size, size), size)] = (
            factor * source[rows]
        ).astype(BF16)

    row_loop(count, work)


def keep_rows(limit, start, rows):
    place = lax.broadcasted_iota(jnp.int32, (rows, 1), 0) + start
    return jnp.where(place < limit, 1.0, 0.0)


def residual(collect, factor, resid, limit, after_ref, squares_ref):
    squares_ref[...] = jnp.zeros_like(squares_ref)
    base = collect.wire.me * collect.count

    def work(rows, branch):
        after = resid[rows] + factor * branch
        after_ref[rows] = after
        keep = keep_rows(limit, base + rows.start, branch.shape[0])
        squares_ref[0:8] += fold8(branch * branch * keep)
        squares_ref[8:16] += fold8(after * after * keep)

    collect.sum_loop(work)


def residual_back(collect, grad_ref, resid, gains, new_grad_ref, gain_grad_ref):
    gain_grad_ref[...] = jnp.zeros_like(gain_grad_ref)

    def work(rows, rows_grad):
        normed, inverse = normalize(resid[rows])
        new_grad_ref[rows] = grad_ref[rows] + norm_back(rows_grad, normed, inverse, gains)
        gain_grad_ref[...] += fold8(rows_grad * normed)

    collect.sum_loop(work)


def send_pieces(wire, count, source, pieces, out_ref):
    width = pieces.shape[2]

    def split(rows, index):
        result = source[rows].astype(BF16)
        for part in range(wire.n):
            pieces[part, rows] = result[:, part * width:(part + 1) * width]

    row_loop(count, split)
    mine = out_ref.at[tile(wire.me, count)]
    copies = wire.to_all(lambda peer: pieces.at[peer], mine)
    here = wire.local(pieces.at[wire.me], mine)
    here.start()
    return copies + [here]


def flipped(wire, place):
    flip_across, flip_along = lax.rem(place, 2), place // 2
    across_bit, along_bit = lax.rem(wire.me, 2), wire.me // 2
    return (
        across_bit + flip_across - 2 * across_bit * flip_across
        + 2 * (along_bit + flip_along - 2 * along_bit * flip_along)
    )


def send_shares(wire, chunks, collect, share, last=None):
    part = collect.part
    if wire.n == 4:
        def turn(step, carry):
            left = 3 - step
            share(flipped(wire, left), part.at[lax.rem(left + 3, 4)])
            for place in range(3):
                pl.when(step == place)(lambda place=place: collect.send(2 - place))
            if last is not None:
                pl.when(step == 2)(last)
            return carry

        lax.fori_loop(0, 4, turn, 0)
    else:
        for chunk, slot in reversed(chunks):
            share(chunk, part.at[wire.n - 1 if slot is None else slot])
            if slot is not None:
                collect.send(slot)
        if last is not None:
            last()


def feed_forward_first(count, chunk, rows_ref, up, pre_ref, act):
    rows = tile(chunk, count)
    left = rows_ref[rows]

    def first(cols, index):
        pre = matmul(left, up[:, cols])
        pre_ref[rows, cols] = pre.astype(BF16)
        act[:, cols] = (pre * jax.nn.sigmoid(pre)).astype(BF16)

    block_loop(up.shape[1], first)


def feed_forward_second(act, down_t, target):
    hidden = act[...]

    def second(cols, index):
        target[:, cols] = matmul_nt(hidden, down_t[cols]).astype(BF16)

    block_loop(down_t.shape[0], second)


def feed_forward_main(count, gain_row, factor, enter, turn, wire, ins, outs, scratch):
    ins, outs, scratch = list(ins), list(outs), list(scratch)
    if enter:
        limit_ref, tokens_ref, cot_in = ins[:3]
        gain_ins = ins[3:8]
        up_shard, down_ref = ins[8:10]
        next_pieces = [(ref, flip) for ref, flip in zip(ins[10:], enter)]
        ins = []
        resid, cot_out, gains_ref, up, down_t, next_full = outs[:6]
        outs = outs[6:]
        arrived, arrived_cot, arrived_gain, gain_in, down_shard, next_shard = scratch[:6]
        scratch = scratch[6:]
    else:
        limit_ref, resid, gains_ref = ins[:3]
        ins = ins[3:]
    if enter:
        for place, ref in enumerate(gain_ins):
            gain_in[place:place + 1] = ref[...]
        gain_in[len(gain_ins):] = jnp.zeros((8 - len(gain_ins), gain_in.shape[1]), F32)
        join([(down_ref, True)], down_shard)
        join(next_pieces, next_shard)
    else:
        up, down_t = ins[:2]
        ins = ins[2:]
    if turn:
        (cot_ref,) = ins
        grad_ref, gain_grad_ref, out_ref = outs[:3]
        outs = outs[3:]
        pieces, after_ref = scratch[:2]
        scratch = scratch[2:]
    else:
        after_ref = outs.pop(0)
    squares_ref, rows_ref, pre_ref = outs
    act, part, got = scratch
    wire.greet()
    wire.begin()
    if enter:
        up_job = RowChain(up_shard, up, wire)
        down_job = RowChain(down_shard, down_t, wire)
        next_job = RowChain(next_shard, next_full, wire)
        up_job.begin()
        width = arrived_gain.shape[2]
        turned = tokens_ref.shape[0] == width

        def share(ref, peer):
            return ref.at[:, tile(peer, count)] if turned else ref.at[tile(peer, count)]

        def settle(came, target):
            for piece in range(wire.n):
                cols = slice(piece * width, (piece + 1) * width)
                if turned:
                    target[:, cols] = came[piece].astype(F32).T
                else:
                    target[:, cols] = came[piece].astype(F32)

        mine = [
            wire.local(share(tokens_ref, wire.me), arrived.at[wire.me]),
            wire.local(gain_in, arrived_gain.at[wire.me]),
            wire.local(share(cot_in, wire.me), arrived_cot.at[wire.me]),
        ]
        copies = wire.to_all(lambda peer: share(tokens_ref, peer), arrived.at[wire.me])
        copies += wire.to_all(lambda peer: gain_in, arrived_gain.at[wire.me])
        for copy in mine:
            copy.start()
        for copy in mine + copies:
            copy.wait()
        for piece in range(wire.n):
            gains_ref[:, piece * width:(piece + 1) * width] = arrived_gain[piece]

        settle(arrived, resid)
    gains = gains_ref[gain_row:gain_row + 1]
    norm_rows(wire, count, resid, gains, rows_ref)
    spread = Spread(wire, rows_ref, count)
    spread.start()
    wire.loaded()
    collect = Collect(wire, part, got)
    cot_copies = []
    if enter:
        cot_copies = wire.to_all(
            lambda peer: share(cot_in, peer), arrived_cot.at[wire.me]
        )
    wire.early()
    if enter:
        up_job.advance(0)
        spread.relay()
        for step in range(1, up_job.steps):
            up_job.advance(step)
        down_job.begin()
        up_job.end()
        chunks = []
        for chunk, slot in spread.arrivals(relay=False):
            chunks.append((chunk, slot))
            feed_forward_first(count, chunk, rows_ref, up, pre_ref, act.at[len(chunks) - 1])
            if len(chunks) - 1 < down_job.steps:
                down_job.advance(len(chunks) - 1)
        for copy in cot_copies:
            copy.wait()

        settle(arrived_cot, cot_out)
        next_job.begin()
        down_job.end()
        for place, (chunk, slot) in reversed(list(enumerate(chunks))):
            target = part.at[wire.n - 1 if slot is None else slot]
            feed_forward_second(act.at[place], down_t, target)
            if slot is not None:
                collect.send(slot)
            if len(chunks) - 1 - place < next_job.steps:
                next_job.advance(len(chunks) - 1 - place)
        collect.combine()
        for step in range(len(chunks), next_job.steps):
            next_job.advance(step)
    else:
        for chunk, slot in spread.arrivals():
            target = part.at[wire.n - 1 if slot is None else slot]
            feed_forward_first(count, chunk, rows_ref, up, pre_ref, act.at[0])
            feed_forward_second(act.at[0], down_t, target)
            if slot is not None:
                collect.send(slot)
        collect.combine()
    wire.middle()
    wire.flush()
    collect.wait()
    residual(collect, factor, resid, limit_ref[0], after_ref, squares_ref)
    late = []
    if turn:
        final_gains = gains_ref[gain_row + 1:gain_row + 2]
        gain_grad_ref[...] = jnp.zeros_like(gain_grad_ref)

        def final(rows, index):
            normed, inverse = normalize(after_ref[rows])
            cot = cot_ref[rows]
            grad_ref[rows] = norm_back(cot, normed, inverse, final_gains)
            gain_grad_ref[...] += fold8(cot * normed)
            after_ref[rows] = normed * final_gains

        row_loop(count, final)
        late = send_pieces(wire, count, after_ref, pieces, out_ref)
    spread.finish()
    for copy in late:
        copy.wait()
    if enter:
        next_job.end()
    wire.end()


def feed_forward(sizes, name, collective_id, gain_row, up, down_t, limit, resid=None, gains=None,
                 enter=None, turn=None, **side):
    n, m = sizes
    hidden = up.shape[1]
    full = up.shape[0] * (m if enter else 1)
    next_pieces = None
    if enter:
        tokens, cotangent, gain_parts, next_pieces = enter
        turned = tokens.shape[0] * n == full
        width, length = tokens.shape if turned else tokens.shape[::-1]
        count = length // n
        came = (n, width, count) if turned else (n, count, width)
        ins = [(limit, smem()), (tokens, vmem()), (cotangent, vmem())]
        ins += [(part, vmem()) for part in gain_parts] + [(up, vmem()), (down_t, vmem())]
        ins += [(array, vmem()) for array, _ in next_pieces]
        down_shape, next_shape = (full // m, hidden), joined_shape(next_pieces)
        outs = [((count, full), F32, "store"), ((count, full), F32, "store"), ((8, full), F32, vmem())]
        scratch = [
            pltpu.VMEM(came, BF16),
            pltpu.VMEM(came, BF16),
            pltpu.VMEM((n, 8, width), F32),
            pltpu.VMEM((8, width), F32),
            pltpu.VMEM(down_shape, BF16),
            pltpu.VMEM(next_shape, BF16),
        ]
        for shape, spec in ((down_shape, "store"), (down_shape, "store"), (next_shape, hbm())):
            outs.append(((m * shape[0], shape[1]), BF16, spec))
        side = dict(side, more_slots=6 * m, row_on=True)
    else:
        count = resid.shape[0]
        ins = [(limit, smem()), (resid, vmem()), (gains, vmem())]
        outs, scratch = [], []
        ins += [(up, "load"), (down_t, "load")]
    if turn is not None:
        ins.append((turn, "load"))
        outs += [
            ((count, full), F32, vmem()),
            ((8, full), F32, vmem()),
            ((n * count, full // n), BF16, hbm()),
        ]
        scratch.append(pltpu.VMEM((n, count, full // n), BF16))
    if turn is None:
        outs.append(((count, full), F32, vmem()))
    else:
        scratch.append(pltpu.VMEM((count, full), F32))
    outs += [
        ((16, full), F32, vmem()),
        ((n * count, full), BF16, "store"),
        ((n * count, hidden), BF16, "store"),
    ]
    scratch += [
        pltpu.VMEM((n if enter else 1, count, hidden), BF16),
        pltpu.VMEM((n, count, full), BF16),
        pltpu.VMEM((n - 1, count, full), BF16),
    ]
    return comm_call(
        name, collective_id, sizes,
        functools.partial(
            feed_forward_main, count, gain_row, 0.5, enter and [flip for _, flip in next_pieces],
            turn is not None,
        ),
        ins, outs, scratch, **side,
    )


def lane_sum(values):
    total = values[:, 0:BLOCK]
    for at in range(BLOCK, values.shape[1], BLOCK):
        total = total + values[:, at:at + BLOCK]
    return total


def feed_forward_back_main(count, gain_row, leave, wire, ins, outs, scratch):
    grad_ref, resid, gains_ref, up, down_t, rows_ref, pre_ref = ins[:7]
    ins = ins[7:]
    grads, pre_grad, act, part, got = scratch[:5]
    scratch = list(scratch[5:])
    hidden = up.shape[1]
    full = up.shape[0]

    def take(size):
        taken, scratch[:size] = scratch[:size], []
        return taken

    if leave:
        up_width, down_pieces, reduce_sizes = leave
        limit_ref = ins[0]
        gain_parts, squares, table_part, tap_part, depth_part = ins[1:5], ins[5:9], *ins[9:12]
        gain_outs, table_out, rms_out, tap_out, depth_out = outs[:5], *outs[5:9]
        up_out, down_out, last_ref = outs[9:12]
        gain_grad_ref, up_grad_ref, down_grad_ref, new_grad_ref, pieces = take(5)
        width = pieces.shape[2]
        up_job = RowReduce(up_grad_ref, [(hidden, False)], [up_out], *take(reduce_sizes[0]), wire,
                           load=False)
        down_job = RowReduce(down_grad_ref, [(hidden, True)], [down_out], *take(reduce_sizes[1]), wire,
                             load=False)
        gain_pieces, square_parts, first_pieces = take(3)
        items = [
            SumItem(kind, source, *take(4), wire)
            for kind, source in (
                ("piece", gain_pieces), ("all", table_part), ("all", square_parts),
                ("own", tap_part), ("own", depth_part),
            )
        ]
        gain_item = SumItem("piece", first_pieces, *take(4), wire)
    else:
        (tokens_ref,) = ins
        gain_grad_ref, up_grad_ref, down_grad_ref, last_ref, turned_ref = outs
        new_grad_ref = last_ref
        items = []
        down_job = up_job = None
    gains = gains_ref[gain_row:gain_row + 1]
    wire.greet()
    wire.begin()
    cast_rows(wire, count, grad_ref, 0.5, grads)
    spread = Spread(wire, grads, count)
    spread.start()
    if leave:
        gain_pieces[...] = jnp.zeros_like(gain_pieces)
        square_parts[...] = jnp.zeros_like(square_parts)
        for place, ref in enumerate(gain_parts):
            row = jnp.sum(ref[...], axis=0, keepdims=True)
            for piece in range(wire.n):
                gain_pieces[piece, place:place + 1] = row[:, piece * width:(piece + 1) * width]
        for place, ref in enumerate(squares):
            for at in (0, 1):
                rows = ref[at * 8:(at + 1) * 8]
                square_parts[at * 4 + place:at * 4 + place + 1] = lane_sum(
                    jnp.sum(rows, axis=0, keepdims=True)
                )
        lane = lax.broadcasted_iota(jnp.int32, (1, BLOCK), 1)
        once = jnp.where(wire.me == 0, limit_ref[0], 0)
        square_parts[8:9] = jnp.where(lane == 0, once, 0).astype(F32)
        for item in items:
            item.begin()
    wire.loaded()
    collect = Collect(wire, part, got)
    def first_leg(chunk):
        rows = tile(chunk, count)
        left = grads[rows]

        def first(cols, index):
            act_grad = matmul(left, down_t[:, cols])
            pre = pre_ref[rows, cols].astype(F32)
            sig = jax.nn.sigmoid(pre)
            act[rows, cols] = (pre * sig).astype(BF16)
            pre_grad[rows, cols] = (act_grad * (sig + pre * sig * (1.0 - sig))).astype(BF16)

        block_loop(hidden, first)

    def second_leg(chunk, slot):
        target = part.at[wire.n - 1 if slot is None else slot]
        through = pre_grad[tile(chunk, count)]

        def second(cols, index):
            target[:, cols] = matmul_nt(through, up[cols]).astype(BF16)

        block_loop(full, second)
        if slot is not None:
            collect.send(slot)

    def weight_rows(left_ref, right_ref, out, rows):
        left = left_ref[:, rows]

        def piece(cols, index):
            out[rows, cols] = matmul_tn(left, right_ref[:, cols]).astype(BF16)

        block_loop(hidden, piece)

    def weight_grad(left_ref, right_ref, out, job=None):
        if job is None:
            block_loop(full, lambda rows, index: weight_rows(left_ref, right_ref, out, rows))
            return

        def layer(step, carry):
            weight_rows(left_ref, right_ref, out, tile(job.layer_of(step), 2 * job.count))
            job.begin_step(step)
            pl.when(step > 0)(lambda: job.early_step(step - 1))
            return carry

        lax.fori_loop(0, wire.layers, layer, 0)
        job.early_step(wire.layers - 1)

    late_leg = None
    for place, (chunk, slot) in enumerate(spread.arrivals()):
        first_leg(chunk)
        if leave and place == wire.n - 1:
            late_leg = (chunk, slot)
        else:
            second_leg(chunk, slot)
        if slot is None:
            wire.early()
            for item in items:
                item.early()
            if not leave:
                turned_ref[...] = tokens_ref[...].T
        elif slot == 0:
            for item in items:
                item.middle()
    wire.middle()
    weight_grad(grads, act, down_grad_ref, down_job)
    if leave:
        second_leg(*late_leg)
        weight_grad(rows_ref, pre_grad, up_grad_ref, up_job)
        collect.combine()
    else:
        collect.combine()
        weight_grad(rows_ref, pre_grad, up_grad_ref)
    wire.flush()
    collect.wait()
    residual_back(collect, grad_ref, resid, gains, new_grad_ref, gain_grad_ref)
    if leave:
        for piece in range(wire.n):
            first_pieces[piece] = gain_grad_ref[:, piece * width:(piece + 1) * width]
        gain_item.begin()
        late = send_pieces(wire, count, new_grad_ref, pieces, last_ref)
        gain_item.early()
        for item in items:
            item.end()
        gain_item.middle()
        totals = [item.out for item in items]
        for place, ref in enumerate(gain_outs[1:]):
            ref[...] = totals[0][place:place + 1]
        table = totals[1][...]
        for at in range(HEAD_DIM, table.shape[1], HEAD_DIM):
            table = table[:, 0:HEAD_DIM] + table[:, at:at + HEAD_DIM]
        table_out[...] = table[0:LEFT + RIGHT + 1]
        sums = jnp.sum(totals[2][...], axis=1, keepdims=True)
        rms_out[...] = jnp.broadcast_to(jnp.sqrt(sums[0:8] / (sums[8:9] * full)), rms_out.shape)
        tap_out[...] = totals[3][0:tap_out.shape[0]]
        depth_out[...] = jnp.sum(totals[4][...], axis=0, keepdims=True)
        for copy in late:
            copy.wait()
        wire.end()
        down_job.end()
        gain_item.end()
        gain_outs[0][...] = jnp.sum(gain_item.out[...], axis=0, keepdims=True)
        up_job.end()
    spread.finish()
    if not leave:
        wire.end()


def feed_forward_back(sizes, name, collective_id, gain_row, grad, resid, gains, up, down_t, rows, pre,
                      leave=None, tokens=None, taps=0, **side):
    n, m = sizes
    full, hidden = up.shape
    count = resid.shape[0]
    width = full // n
    ins = [(grad, vmem()), (resid, "load"), (gains, vmem())]
    ins += [(item, "load") for item in (up, down_t, rows, pre)]
    scratch = [
        pltpu.VMEM((n * count, full), BF16),
        pltpu.VMEM((n * count, hidden), BF16),
        pltpu.VMEM((n * count, hidden), BF16),
        pltpu.VMEM((n, count, full), BF16),
        pltpu.VMEM((n - 1, count, full), BF16),
    ]
    extra = None
    if leave:
        limit, gain_parts, squares, table_part, tap_part, depth_part = leave
        layers = m // 2
        ins.append((limit, smem()))
        ins += [(item, vmem()) for item in (*gain_parts, *squares, table_part, tap_part, depth_part)]
        outs = [((1, width), F32, vmem())] * 5
        outs += [
            ((LEFT + RIGHT + 1, HEAD_DIM), F32, vmem()),
            ((8, BLOCK), F32, vmem()),
            ((taps, width), F32, vmem()),
            ((1, width), F32, vmem()),
            ((full // m, hidden), F32, hbm()),
            ((hidden, full // m), F32, hbm()),
            ((n * count, width), BF16, hbm()),
        ]
        scratch += [
            pltpu.VMEM((8, full), F32),
            pltpu.VMEM((full, hidden), BF16),
            pltpu.VMEM((full, hidden), BF16),
            pltpu.VMEM((count, full), F32),
            pltpu.VMEM((n, count, width), BF16),
        ]
        reduces = [
            reduce_scratch(layers, full // m, hidden, [(hidden, flip)]) for flip in (False, True)
        ]
        scratch += reduces[0] + reduces[1]
        extra = (hidden, None, [len(made) for made in reduces])
        scratch += [
            pltpu.VMEM((n, 8, width), F32), pltpu.VMEM((16, BLOCK), F32), pltpu.VMEM((n, 8, width), F32)
        ]
        for shape in ((8, width), table_part.shape, (16, BLOCK), tap_part.shape, depth_part.shape,
                      (8, width)):
            scratch += sum_scratch(n, layers, shape)
        side = dict(side, more_slots=16 * m + 8 * n, row_on=True)
    else:
        ins.append((tokens, "load"))
        outs = [
            ((8, full), F32, vmem()),
            ((full, hidden), BF16, "store"),
            ((full, hidden), BF16, "store"),
            ((count, full), F32, vmem()),
            ((tokens.shape[1], tokens.shape[0]), BF16, "store"),
        ]
    return comm_call(
        name, collective_id, sizes,
        functools.partial(feed_forward_back_main, count, gain_row, extra),
        ins, outs, scratch, **side,
    )


def slot_rows(axis):
    slots = lax.broadcasted_iota(jnp.int32, (LEFT + RIGHT + 8, SPAN), axis)
    signed = jnp.where(slots < SPAN - BLOCK + 1, slots, slots - SPAN)
    return jnp.clip(signed - (BLOCK - LEFT), 0, LEFT + RIGHT)


def extend_table(table, copies):
    slots = jnp.arange(SPAN)
    signed = jnp.where(slots < SPAN - BLOCK + 1, slots, slots - SPAN)
    row_of = jnp.clip(signed - (BLOCK - LEFT), 0, LEFT + RIGHT)
    chosen = (row_of[:, None] == jnp.arange(LEFT + RIGHT + 1)[None, :]).astype(table.dtype)
    return jnp.tile(matmul(chosen, table).astype(table.dtype), (1, copies))


def fill_far(far_ref, table_ref, limit):
    blocks, length, _ = far_ref.shape
    lane = lax.broadcasted_iota(jnp.int32, (1, BLOCK), 1)

    def row(at, mark):
        ends = table_ref[at:at + 1].astype(F32)
        if ends.shape[1] < BLOCK:
            ends = jnp.concatenate([ends, jnp.zeros((1, BLOCK - ends.shape[1]), F32)], axis=1)
        return jnp.where(lane < HEAD_DIM, ends, jnp.where(lane == mark, 1.0, 0.0))

    first = row(0, HEAD_DIM + 1)
    last = row(SPAN - 2 * BLOCK, HEAD_DIM + 2)

    def block(step, carry):
        index, piece = step // (length // BLOCK), lax.rem(step, length // BLOCK)
        at = index * BLOCK
        column = lax.broadcasted_iota(jnp.int32, (BLOCK, 1), 0) + piece * BLOCK
        place = column + at - BLOCK
        key = jnp.where(place < 0, place + length, jnp.where(place >= length, place - length, place))
        near = (column < WINDOW) & (place >= 0) & (place < length)
        left = jnp.where(near | (key >= at), 0.0, 1.0)
        right = jnp.where(near | (key < at), 0.0, 1.0)
        bias = jnp.where(key < limit, 0.0, NEG_FILL)
        terms = left * first + right * last + jnp.where(lane == HEAD_DIM, bias, 0.0)
        far_ref[index, tile(piece, BLOCK)] = terms.astype(BF16)
        return carry

    lax.fori_loop(0, blocks * (length // BLOCK), block, 0)


def duplicate(qkv_ref, width, group, keys, values):
    length = qkv_ref.shape[0]
    for part in range(width // group):
        base = part * group
        for copy in range(2):
            place = slice(copy * length, (copy + 1) * length)
            keys[part, place] = qkv_ref[:, width + base:width + base + group]
            values[part, place] = qkv_ref[:, 2 * width + base:2 * width + base + group]


def by_head(values, group):
    if group == HEAD_DIM:
        return values
    lane = lax.broadcasted_iota(jnp.int32, (BLOCK, group), 1)
    zero = jnp.zeros_like(values)
    return jnp.concatenate(
        [
            jnp.where((lane >= at) & (lane < at + HEAD_DIM), values, zero)
            for at in range(0, group, HEAD_DIM)
        ],
        axis=0,
    )


def own_lanes(values, group):
    if group == HEAD_DIM:
        return values
    lane = lax.broadcasted_iota(jnp.int32, (BLOCK, group), 1)
    return jnp.where(lane < HEAD_DIM, values[0:BLOCK], values[BLOCK:2 * BLOCK])


def far_queries(values, group):
    wide = values.astype(F32)
    if group == HEAD_DIM:
        lane = lax.broadcasted_iota(jnp.int32, (BLOCK, BLOCK - HEAD_DIM), 1)
        return jnp.concatenate([wide, jnp.where(lane == 0, 1.0, 0.0)], axis=1).astype(BF16)
    lane = lax.broadcasted_iota(jnp.int32, (BLOCK, BLOCK), 1)
    rest = jnp.where(lane == HEAD_DIM, 1.0, 0.0)
    return jnp.concatenate(
        [
            jnp.where(lane < HEAD_DIM, wide, rest),
            jnp.where(lane < HEAD_DIM, pltpu.roll(wide, HEAD_DIM, 1), rest),
        ],
        axis=0,
    ).astype(BF16)


def near_mask(at, length):
    place = lax.broadcasted_iota(jnp.int32, (1, WINDOW), 1) + (at - BLOCK)
    return (place >= 0) & (place < length)


def near_terms(query, table, at, length):
    terms = matmul_nt(query, table)
    halves = [
        pltpu.roll(terms[start:start + BLOCK], 0, 1, stride=1, stride_axis=0)[:, :WINDOW]
        for start in range(0, query.shape[0], BLOCK)
    ]
    return jnp.where(near_mask(at, length), jnp.concatenate(halves, axis=0), 0.0)


def attend_blocks(first, blocks, width, group, qkv_ref, table_ref, far_ref, keys, values, context_ref,
                  log_ref, weights):
    length = qkv_ref.shape[0]
    heads = group // HEAD_DIM
    parts = width // group
    scale = 1.0 / math.sqrt(HEAD_DIM)

    def block(step, carry):
        index, part = first + step // parts, lax.rem(step, parts)
        at = pl.multiple_of(index * BLOCK, BLOCK)
        rows = pl.ds(at, BLOCK)
        cols = tile(part, group) if parts > 1 else slice(0, group)
        window = pl.ds(pl.multiple_of(lax.rem(at + length - BLOCK, length), BLOCK), length)
        query_rows = qkv_ref[rows, cols] * jnp.asarray(scale, BF16)
        query = by_head(query_rows, group)
        extra = far_queries(query_rows, group)
        if group == 2 * HEAD_DIM:
            scores = matmul_nt(
                jnp.concatenate([query, extra], axis=1),
                jnp.concatenate([keys[part, window], far_ref[index]], axis=1),
            )
        else:
            scores = matmul_nt(query, keys[part, window]) + matmul_nt(extra, far_ref[index])
        near = near_terms(query, table_ref[...], at, length)
        size = 32
        peaks, totals = [], []
        for start in range(0, heads * BLOCK, size):
            some = slice(start, start + size)
            first_part = scores[some, :WINDOW] + near[some]
            last_part = scores[some, WINDOW:]
            peak = jnp.maximum(
                jnp.max(first_part, axis=1, keepdims=True), jnp.max(last_part, axis=1, keepdims=True)
            )
            first_part = jnp.exp(first_part - peak)
            last_part = jnp.exp(last_part - peak)
            weights[some, :WINDOW] = first_part.astype(BF16)
            weights[some, WINDOW:] = last_part.astype(BF16)
            peaks.append(peak)
            totals.append(
                jnp.sum(first_part, axis=1, keepdims=True) + jnp.sum(last_part, axis=1, keepdims=True)
            )
        total = jnp.concatenate(totals, axis=0)
        mixed = matmul(weights[...], values[part, window]) * (1.0 / total)
        context_ref[rows, cols] = own_lanes(mixed, group).astype(BF16)
        log = jnp.concatenate(peaks, axis=0) + jnp.log(total)
        lane = lax.broadcasted_iota(jnp.int32, (BLOCK, BLOCK), 1)
        square = jnp.where(lane == 0, log[0:BLOCK], 0.0)
        for head in range(1, heads):
            square = jnp.where(lane == head, log[head * BLOCK:(head + 1) * BLOCK], square)
        log_ref[part, :, rows] = square.T[0:8]
        return carry

    lax.fori_loop(0, blocks * parts, block, 0)


def attend_back_core(width, group, qkv_ref, table_ref, far_ref, log_ref, grad_ref, out_ref,
                     table_grad_ref, keys, values, key_grad, value_grad, slot_grad, end_grad, probs,
                     prob_grads, back, blocks_in_turn):
    length = qkv_ref.shape[0]
    heads = group // HEAD_DIM
    parts = width // group
    scale = 1.0 / math.sqrt(HEAD_DIM)
    duplicate(qkv_ref, width, group, keys, values)
    slot_grad[...] = jnp.zeros_like(slot_grad)
    end_grad[...] = jnp.zeros_like(end_grad)
    key_grad[...] = jnp.zeros_like(key_grad)
    value_grad[...] = jnp.zeros_like(value_grad)
    down = lax.broadcasted_iota(jnp.int32, (BLOCK, BLOCK), 0)
    across = lax.broadcasted_iota(jnp.int32, (BLOCK, BLOCK), 1)
    reverse = jnp.where(down + across == BLOCK - 1, 1.0, 0.0).astype(BF16)

    def flip(values_in):
        return jnp.concatenate(
            [
                matmul(reverse, values_in[start:start + BLOCK])
                for start in range(0, heads * BLOCK, BLOCK)
            ],
            axis=0,
        )

    def block(index, part):
        at = pl.multiple_of(index * BLOCK, BLOCK)
        rows = pl.ds(at, BLOCK)
        cols = tile(part, group) if parts > 1 else slice(0, group)
        window = pl.ds(pl.multiple_of(lax.rem(at + length - BLOCK, length), BLOCK), length)
        key_rows = keys[part, window]
        far_rows = far_ref[index]
        query_rows = qkv_ref[rows, cols] * jnp.asarray(scale, BF16)
        query = by_head(query_rows, group)
        extra = far_queries(query_rows, group)
        grad = by_head(grad_ref[rows, cols], group)
        query_wide = [query, extra]
        if group == 2 * HEAD_DIM:
            query_wide = [jnp.concatenate(query_wide, axis=1)]
            key_wide = [jnp.concatenate([key_rows, far_rows], axis=1)]
        else:
            key_wide = [key_rows, far_rows]
        near = near_terms(query, table_ref[...], at, length)
        log = jnp.concatenate([log_ref[part, head:head + 1, rows] for head in range(heads)], axis=1)
        value_rows = values[part, window]
        row_dot = jnp.zeros((8, heads * BLOCK), F32)
        for start in range(0, length, BLOCK):
            some = slice(start, start + BLOCK)
            scores = sum(
                matmul_nt(left[some], right) for left, right in zip(key_wide, query_wide)
            )
            if start < WINDOW:
                scores = scores + near[:, some].T
            prob = jnp.exp(scores - log)
            prob_grad = matmul_nt(value_rows[some], grad)
            row_dot = row_dot + fold8(prob * prob_grad)
            probs[some] = prob
            prob_grads[some] = prob_grad
        row_dot = jnp.sum(row_dot, axis=0, keepdims=True)
        for start in range(0, length, BLOCK):
            some = slice(start, start + BLOCK)
            there = pl.ds(pl.multiple_of(window.start + start, BLOCK), BLOCK)
            prob = probs[some]
            score_grad = (prob * (prob_grads[some] - row_dot)).astype(BF16)
            value_grad[part, there] += matmul(prob.astype(BF16), grad)
            key_grad[part, there] += matmul(score_grad, query)
            back[:, some] = score_grad.T
        turned_back = back[...]
        if group == 2 * HEAD_DIM:
            both = matmul(turned_back, key_wide[0])
            direct, ends = both[:, :group], both[:, group:]
        else:
            direct, ends = matmul(turned_back, key_rows), matmul(turned_back, far_rows)
        left_sum, right_sum = ends[:, HEAD_DIM + 1:HEAD_DIM + 2], ends[:, HEAD_DIM + 2:HEAD_DIM + 3]
        query_full = query.astype(F32)
        end_grad[0:8] += fold8(left_sum * query_full)
        end_grad[8:16] += fold8(right_sum * query_full)
        near_grad = jnp.where(
            near_mask(at, length), turned_back[:, :WINDOW], jnp.asarray(0.0, BF16)
        )
        flipped = flip(near_grad)
        skewed = []
        for start in range(0, heads * BLOCK, BLOCK):
            padded = jnp.concatenate(
                [flipped[start:start + BLOCK], jnp.zeros((BLOCK, SPAN - WINDOW), F32)], axis=1
            )
            skewed.append(pltpu.roll(padded, SPAN - (BLOCK - 1), 1, stride=1, stride_axis=0))
        straight = jnp.concatenate(skewed, axis=0).astype(BF16)
        term = matmul(straight, table_ref[...])
        high = term.astype(BF16)
        low = (term - high.astype(F32)).astype(BF16)
        direct = direct + flip(high) + flip(low)
        result = own_lanes(direct, group)
        if heads == 1:
            result = result + ends[:, :HEAD_DIM]
        else:
            lane = lax.broadcasted_iota(jnp.int32, (BLOCK, BLOCK), 1)
            result = result + jnp.where(
                lane < HEAD_DIM, ends[0:BLOCK], pltpu.roll(ends[BLOCK:2 * BLOCK], HEAD_DIM, 1)
            )
        out_ref[rows, cols] = (result * scale).astype(BF16)
        slot_grad[...] += matmul_tn(flip(query).astype(BF16), straight)

    blocks_in_turn(block, parts)
    for part in range(parts):
        base = width + part * group
        out_ref[:, base:base + group] = (
            key_grad[part, 0:length] + key_grad[part, length:2 * length]
        ).astype(BF16)
        out_ref[:, width + base:width + base + group] = (
            value_grad[part, 0:length] + value_grad[part, length:2 * length]
        ).astype(BF16)
    chosen = jnp.where(
        slot_rows(1) == lax.broadcasted_iota(jnp.int32, (LEFT + RIGHT + 8, SPAN), 0), 1.0, 0.0
    )
    table_grad_ref[...] = lax.dot_general(
        chosen, slot_grad[...], (((1,), (1,)), ((), ())), precision=lax.Precision.HIGHEST,
        preferred_element_type=F32,
    )
    table_grad_ref[0:1] += jnp.sum(end_grad[0:8], axis=0, keepdims=True)
    table_grad_ref[LEFT + RIGHT:LEFT + RIGHT + 1] += jnp.sum(end_grad[8:16], axis=0, keepdims=True)


def attention_main(count, gain_row, wire, ins, outs, scratch):
    limit_ref, resid, gains_ref, weights, table_ref = ins
    after_ref, squares_ref, rows_ref, qkv_ref, context_ref, log_ref = outs
    far_ref, keys, values, weights_ref, part, got = scratch
    width = context_ref.shape[1]
    group = keys.shape[2]
    wire.greet()
    wire.begin()
    norm_rows(wire, count, resid, gains_ref[gain_row:gain_row + 1], rows_ref)
    spread = Spread(wire, rows_ref, count)
    spread.start()
    wire.loaded()
    collect = Collect(wire, part, got)
    spread.relay()
    wire.early()
    fill_far(far_ref, table_ref, limit_ref[0])
    chunks = []
    for chunk, slot in spread.arrivals(relay=False):
        chunks.append((chunk, slot))
        rows = tile(chunk, count)
        left = rows_ref[rows]

        def project(cols, index):
            qkv_ref[rows, cols] = matmul(left, weights[:, cols]).astype(BF16)

        block_loop(3 * width, project)
    duplicate(qkv_ref, width, group, keys, values)
    wire.side[0].middle()
    size = max(count, BLOCK)

    def share(chunk, target):
        attend_blocks(chunk * count // BLOCK, size // BLOCK, width, group, qkv_ref, table_ref, far_ref,
                      keys, values, context_ref, log_ref, weights_ref)
        left = context_ref[tile(chunk, count)]

        def leave(cols, index):
            target[:, cols] = matmul_nt(left, weights[cols, 3 * width:]).astype(BF16)

        block_loop(weights.shape[0], leave)

    def last():
        collect.combine()
        wire.side[1].middle()

    send_shares(wire, chunks, collect, share, last)
    wire.flush()
    collect.wait()
    residual(collect, 1.0, resid, limit_ref[0], after_ref, squares_ref)
    spread.finish()
    wire.end()


def attention(sizes, name, collective_id, gain_row, limit, resid, gains, weights, table, **side):
    n, m = sizes
    count, full = resid.shape
    length, width = n * count, weights.shape[1] // 4
    group = min(2 * HEAD_DIM, width)
    return comm_call(
        name, collective_id, sizes, functools.partial(attention_main, count, gain_row),
        [(limit, smem()), (resid, vmem()), (gains, vmem()), (weights, "load"), (table, "load")],
        [
            ((count, full), F32, vmem()),
            ((16, full), F32, vmem()),
            ((length, full), BF16, "store"),
            ((length, 3 * width), BF16, "store"),
            ((length, width), BF16, "store"),
            ((width // group, 8, length), F32, "store"),
        ],
        [
            pltpu.VMEM((length // BLOCK, length, BLOCK), BF16),
            pltpu.VMEM((width // group, 2 * length, group), BF16),
            pltpu.VMEM((width // group, 2 * length, group), BF16),
            pltpu.VMEM((group // HEAD_DIM * BLOCK, length), BF16),
            pltpu.VMEM((n, count, full), BF16),
            pltpu.VMEM((n - 1, count, full), BF16),
        ],
        cost=20 * 10**9, **side,
    )


def attention_back_main(count, gain_row, wire, ins, outs, scratch):
    (limit_ref, grad_ref, resid, gains_ref, weights, table_ref, rows_ref, qkv_ref, context_ref,
     log_ref) = ins
    gain_grad_ref, wide_ref, table_grad_ref, new_grad_ref = outs
    (far_ref, grads, context_grad, qkv_grad, keys, values, key_grad, value_grad, slot_grad, end_grad,
     probs, prob_grads, back, part, got) = scratch
    width = context_ref.shape[1]
    group = keys.shape[2]
    wire.greet()
    wire.begin()
    cast_rows(wire, count, grad_ref, 1.0, grads)
    spread = Spread(wire, grads, count)
    spread.start()
    wire.loaded()
    collect = Collect(wire, part, got)
    fill_far(far_ref, table_ref, limit_ref[0])
    chunks = []
    per_chunk = max(count, BLOCK) // BLOCK

    def down_gradient(chunk):
        rows = tile(chunk, count)
        context_grad[rows] = matmul(grads[rows], weights[:, 3 * width:]).astype(BF16)

    def in_turn(block, parts):
        if wire.n == 4:
            def turn(place, carry):
                pl.when(place == 1)(wire.early)
                for at in (1, 2, 3):
                    pl.when(place == at)(lambda at=at: spread.wait_place(at))
                chunk = flipped(wire, place)
                down_gradient(chunk)

                def one(step, carry):
                    block(chunk * per_chunk + step // parts, lax.rem(step, parts))
                    final = per_chunk * parts - 1
                    for turn_of, after in ((0, min(1, final)), (1, final)):
                        pl.when((place == 0) & (step == after))(
                            lambda turn_of=turn_of: spread.relay_turn(turn_of)
                        )
                    return carry

                lax.fori_loop(0, per_chunk * parts, one, 0)
                return carry

            lax.fori_loop(0, 4, turn, 0)
            return
        wire.early()
        for chunk, slot in spread.arrivals():
            chunks.append((chunk, slot))
            down_gradient(chunk)

        def one(step, carry):
            block(step // parts, lax.rem(step, parts))
            return carry

        lax.fori_loop(0, wire.n * count // BLOCK * parts, one, 0)

    attend_back_core(width, group, qkv_ref, table_ref, far_ref, log_ref, context_grad, qkv_grad,
                     table_grad_ref, keys, values, key_grad, value_grad, slot_grad, end_grad, probs,
                     prob_grads, back, in_turn)
    wire.middle()

    def share(chunk, target):
        left = qkv_grad[tile(chunk, count)]

        def back(cols, index):
            target[:, cols] = matmul_nt(left, weights[cols, :3 * width]).astype(BF16)

        block_loop(weights.shape[0], back)

    send_shares(wire, chunks, collect, share)
    collect.combine()

    def weight_grads(rows, index):
        wide_ref[rows, :3 * width] = matmul_tn(rows_ref[:, rows], qkv_grad[...]).astype(BF16)
        wide_ref[rows, 3 * width:] = matmul_tn(grads[:, rows], context_ref[...]).astype(BF16)

    block_loop(weights.shape[0], weight_grads)
    wire.flush()
    wire.end()
    collect.wait()
    residual_back(collect, grad_ref, resid, gains_ref[gain_row:gain_row + 1], new_grad_ref,
                  gain_grad_ref)
    spread.finish()


def attention_back(sizes, name, collective_id, gain_row, limit, grad, resid, gains, weights, table, rows,
                   qkv, context, log_total, **side):
    n, m = sizes
    count, full = resid.shape
    length, width = context.shape
    group = min(2 * HEAD_DIM, width)
    return comm_call(
        name, collective_id, sizes, functools.partial(attention_back_main, count, gain_row),
        [(limit, smem()), (grad, vmem()), (resid, "load"), (gains, vmem())]
        + [(item, "load") for item in (weights, table, rows, qkv, context, log_total)],
        [
            ((8, full), F32, vmem()),
            ((full, 4 * width), BF16, "store"),
            ((LEFT + RIGHT + 8, group), F32, vmem()),
            ((count, full), F32, vmem()),
        ],
        [
            pltpu.VMEM((length // BLOCK, length, BLOCK), BF16),
            pltpu.VMEM((length, full), BF16),
            pltpu.VMEM((length, width), BF16),
            pltpu.VMEM((length, 3 * width), BF16),
            pltpu.VMEM((width // group, 2 * length, group), BF16),
            pltpu.VMEM((width // group, 2 * length, group), BF16),
            pltpu.VMEM((width // group, 2 * length, group), F32),
            pltpu.VMEM((width // group, 2 * length, group), F32),
            pltpu.VMEM((group, SPAN), F32),
            pltpu.VMEM((16, group), F32),
            pltpu.VMEM((length, group // HEAD_DIM * BLOCK), F32),
            pltpu.VMEM((length, group // HEAD_DIM * BLOCK), F32),
            pltpu.VMEM((group // HEAD_DIM * BLOCK, length), BF16),
            pltpu.VMEM((n, count, full), BF16),
            pltpu.VMEM((n - 1, count, full), BF16),
        ],
        cost=50 * 10**9, **side,
    )


PAD = 32
ROWS = 64


def shifted_sets(held, low, high, size):
    for residue in range(8):
        shifts = [shift for shift in range(low, high + 1) if shift % 8 == residue]
        if shifts:
            extent = shifts[-1] - residue + size
            moved = held[residue:residue + extent]
            for shift in shifts:
                yield shift, moved[shift - residue:shift - residue + size]


def stat_rows(blocks, first, second, stats_ref):
    lane = lax.broadcasted_iota(jnp.int32, (BLOCK, BLOCK), 1)
    both = jnp.where(lane == 0, first, jnp.where(lane == 1, second, 0.0))
    stats_ref[:, blocks] = both.T[0:8]


def stat_columns(stats):
    both = jnp.concatenate([stats, jnp.zeros((BLOCK - 8, stats.shape[1]), F32)], axis=0).T
    return both[:, 0:1], both[:, 1:2]


class Stats:
    def __init__(self, wire, mine, got):
        self.wire, self.mine, self.got = wire, mine, got
        self.copies = [
            wire.remote(mine, got.at[step - 1], "col", lax.rem(wire.me + step, wire.n))
            for step in range(1, wire.n)
        ]

    def total(self):
        for copy in self.copies:
            copy.start()
        for copy in self.copies:
            copy.wait()
        total = self.mine[...]
        for step in range(self.wire.n - 1):
            total = total + self.got[step]
        return total


def token_blocks(length, body):
    def step(index, carry):
        body(tile(index, BLOCK), index)
        return carry

    lax.fori_loop(0, length // BLOCK, step, 0)


def convolution_main(count, gain_row, taps, wire, ins, outs, scratch):
    limit_ref, resid, gains_ref, weights, taps_ref, depth_ref = ins
    after_ref, squares_ref, rows_ref, pre_ref, mixed_ref, stats_ref = outs
    kernel_ref, padded, stats_mine, stats_got, act, part, got = scratch
    length, width = mixed_ref.shape
    full = gains_ref.shape[1]
    wire.greet()
    wire.begin()
    norm_rows(wire, count, resid, gains_ref[gain_row:gain_row + 1], rows_ref)
    spread = Spread(wire, rows_ref, count)
    spread.start()
    wire.loaded()
    collect = Collect(wire, part, got)
    stats = Stats(wire, stats_mine, stats_got)
    padded[0:PAD] = jnp.zeros((PAD, width), F32)
    kernel_ref[0:taps] = taps_ref[...].astype(F32)
    spread.relay()
    wire.early()
    chunks = []
    for chunk, slot in spread.arrivals(relay=False):
        chunks.append((chunk, slot))
        rows = tile(chunk, count)
        left = rows_ref[rows]
        value_pre = matmul(left, weights[:, 0:width])
        gate_pre = matmul(left, weights[:, width:2 * width])
        pre_ref[rows, 0:width] = value_pre.astype(BF16)
        pre_ref[rows, width:2 * width] = gate_pre.astype(BF16)
        at = pl.multiple_of(chunk * count + PAD, PAD)
        keep = keep_rows(limit_ref[0], chunk * count, count)
        padded[pl.ds(at, count)] = value_pre * jax.nn.sigmoid(gate_pre) * keep

    def mix(index, carry):
        held = padded[pl.ds(pl.multiple_of(index * ROWS, ROWS), ROWS + PAD)]
        total = jnp.zeros((ROWS, width), F32)
        for shift, moved in shifted_sets(held, PAD - taps + 1, PAD, ROWS):
            tap = shift - (PAD - taps + 1)
            total = total + moved * kernel_ref[tap:tap + 1]
        mixed_ref[tile(index, ROWS)] = total
        return carry

    lax.fori_loop(0, length // ROWS, mix, 0)

    def sums(rows, index):
        mixed = mixed_ref[rows]
        stat_rows(rows, jnp.sum(mixed, axis=1, keepdims=True),
                  jnp.sum(mixed * mixed, axis=1, keepdims=True), stats_mine)

    token_blocks(length, sums)
    total = stats.total() * (1.0 / full)
    inverse = lax.rsqrt(total[1:2] - total[0:1] * total[0:1] + EPSILON)
    stats_ref[...] = jnp.concatenate([total[0:1], inverse, total[2:]], axis=0)

    def share(chunk, target):
        def activate(index, carry):
            rows = tile(chunk * count // BLOCK + index, BLOCK)
            mean, scale = stat_columns(stats_ref[:, rows])
            scaled = (mixed_ref[rows] - mean) * scale * depth_ref[...]
            act[tile(index, BLOCK)] = (scaled * jax.nn.sigmoid(scaled)).astype(BF16)
            return carry

        lax.fori_loop(0, -(-count // BLOCK), activate, 0)
        if count % BLOCK:
            at = lax.rem(chunk * count, BLOCK)
            left = act[pl.ds(pl.multiple_of(at, count), count)]
        else:
            left = act[...]

        def leave(cols, index):
            target[:, cols] = matmul_nt(left, weights[cols, 2 * width:]).astype(BF16)

        block_loop(weights.shape[0], leave)

    send_shares(wire, chunks, collect, share, collect.combine)
    wire.middle()
    wire.flush()
    collect.wait()
    residual(collect, 1.0, resid, limit_ref[0], after_ref, squares_ref)
    spread.finish()
    wire.end()


def convolution(sizes, name, collective_id, gain_row, limit, resid, gains, weights, kernel, depth_gain,
                **side):
    n, m = sizes
    count, full = resid.shape
    length, width = n * count, weights.shape[1] // 3
    return comm_call(
        name, collective_id, sizes,
        functools.partial(convolution_main, count, gain_row, kernel.shape[0]),
        [(limit, smem()), (resid, vmem()), (gains, vmem()), (weights, "load"), (kernel, vmem()),
         (depth_gain, vmem())],
        [
            ((count, full), F32, vmem()),
            ((16, full), F32, vmem()),
            ((length, full), BF16, "store"),
            ((length, 2 * width), BF16, "store"),
            ((length, width), F32, "store"),
            ((8, length), F32, "store"),
        ],
        [
            pltpu.VMEM((PAD, width), F32),
            pltpu.VMEM((length + PAD, width), F32),
            pltpu.VMEM((8, length), F32),
            pltpu.VMEM((n - 1, 8, length), F32),
            pltpu.VMEM((max(count, BLOCK), width), BF16),
            pltpu.VMEM((n, count, full), BF16),
            pltpu.VMEM((n - 1, count, full), BF16),
        ],
        cost=15 * 10**9, **side,
    )


def convolution_back_main(count, gain_row, taps, wire, ins, outs, scratch):
    (limit_ref, grad_ref, resid, gains_ref, weights, taps_ref, depth_ref, rows_ref, pre_ref, mixed_ref,
     stats_ref) = ins
    gain_grad_ref, wide_ref, kernel_grad_ref, depth_grad_ref, new_grad_ref = outs
    (kernel_ref, grads, padded, padded_grad, stats_mine, stats_got, sums_ref, act, pre_grad, part, got) = scratch
    length, width = mixed_ref.shape
    full = gains_ref.shape[1]
    wire.greet()
    wire.begin()
    cast_rows(wire, count, grad_ref, 1.0, grads)
    spread = Spread(wire, grads, count)
    spread.start()
    wire.loaded()
    collect = Collect(wire, part, got)
    stats = Stats(wire, stats_mine, stats_got)
    padded[0:PAD] = jnp.zeros((PAD, width), F32)
    padded_grad[length:] = jnp.zeros((PAD, width), F32)
    sums_ref[...] = jnp.zeros_like(sums_ref)
    depth_grad_ref[...] = jnp.zeros_like(depth_grad_ref)
    kernel_ref[0:taps] = taps_ref[...].astype(F32)
    kernel_grad_ref[...] = jnp.zeros_like(kernel_grad_ref)
    spread.relay()

    def regate(rows, index):
        value_pre = pre_ref[rows, 0:width].astype(F32)
        gate_pre = pre_ref[rows, width:2 * width].astype(F32)
        at = pl.multiple_of(index * BLOCK + PAD, PAD)
        keep = keep_rows(limit_ref[0], index * BLOCK, BLOCK)
        padded[pl.ds(at, BLOCK)] = value_pre * jax.nn.sigmoid(gate_pre) * keep

    token_blocks(length, regate)
    wire.early()
    def first(rows, index):
        mean, scale = stat_columns(stats_ref[:, rows])
        normed = (mixed_ref[rows] - mean) * scale
        scaled = normed * depth_ref[...]
        sig = jax.nn.sigmoid(scaled)
        act[rows] = (scaled * sig).astype(BF16)
        scaled_grad = padded_grad[rows] * (sig + scaled * sig * (1.0 - sig))
        depth_grad_ref[...] += fold8(scaled_grad * normed)
        weighted = scaled_grad * depth_ref[...]
        padded_grad[rows] = weighted
        stat_rows(rows, jnp.sum(weighted, axis=1, keepdims=True),
                  jnp.sum(weighted * normed, axis=1, keepdims=True), stats_mine)

    chunks = []
    for chunk, slot in spread.arrivals(relay=False):
        chunks.append((chunk, slot))
        rows = tile(chunk, count)
        padded_grad[rows] = matmul(grads[rows], weights[:, 2 * width:])
        if count % BLOCK == 0:
            def some(index, carry):
                first(tile(chunk * (count // BLOCK) + index, BLOCK), index)
                return carry

            lax.fori_loop(0, count // BLOCK, some, 0)
    wire.middle()
    if count % BLOCK:
        token_blocks(length, first)
    total = stats.total() * (1.0 / full)
    stats_mine[...] = total

    def second(rows, index):
        mean, scale = stat_columns(stats_ref[:, rows])
        normed = (mixed_ref[rows] - mean) * scale
        one, two = stat_columns(stats_mine[:, rows])
        padded_grad[rows] = scale * (padded_grad[rows] - one - normed * two)

    token_blocks(length, second)

    def share(chunk, target):
        def unmix(index, carry):
            start = chunk * count + index * ROWS
            rows = pl.ds(pl.multiple_of(start, ROWS), ROWS)
            ahead = padded_grad[pl.ds(pl.multiple_of(start, ROWS), ROWS + PAD)]
            total = jnp.zeros((ROWS, width), F32)
            for shift, moved in shifted_sets(ahead, 0, taps - 1, ROWS):
                tap = taps - 1 - shift
                total = total + moved * kernel_ref[tap:tap + 1]
            gate = jax.nn.sigmoid(pre_ref[rows, width:2 * width].astype(F32))
            through = total * keep_rows(limit_ref[0], start, ROWS) * gate
            pre_grad[rows, 0:width] = through.astype(BF16)
            pre_grad[rows, width:2 * width] = (
                through * pre_ref[rows, 0:width].astype(F32) * (1.0 - gate)
            ).astype(BF16)
            return carry

        lax.fori_loop(0, count // ROWS, unmix, 0)
        left = pre_grad[tile(chunk, count)]

        def back(cols, index):
            target[:, cols] = matmul_nt(left, weights[cols, :2 * width]).astype(BF16)

        block_loop(weights.shape[0], back)

    send_shares(wire, chunks, collect, share)
    collect.combine()

    def tap_grads(index, carry):
        here = padded_grad[tile(index, ROWS)]
        around = pl.ds(pl.multiple_of(index * ROWS, ROWS), ROWS + PAD)
        for shift, moved in shifted_sets(padded[around], PAD - taps + 1, PAD, ROWS):
            tap = shift - (PAD - taps + 1)
            sums_ref[tap * 8:(tap + 1) * 8] += fold8(here * moved)
        return carry

    lax.fori_loop(0, length // ROWS, tap_grads, 0)
    for tap in range(taps):
        kernel_grad_ref[tap:tap + 1] = jnp.sum(sums_ref[tap * 8:(tap + 1) * 8], axis=0, keepdims=True)

    def weight_grads(rows, index):
        wide_ref[rows, :2 * width] = matmul_tn(rows_ref[:, rows], pre_grad[...]).astype(BF16)
        wide_ref[rows, 2 * width:] = matmul_tn(grads[:, rows], act[...]).astype(BF16)

    block_loop(weights.shape[0], weight_grads)
    wire.flush()
    wire.end()
    collect.wait()
    residual_back(collect, grad_ref, resid, gains_ref[gain_row:gain_row + 1], new_grad_ref,
                  gain_grad_ref)
    spread.finish()


def convolution_back(sizes, name, collective_id, gain_row, limit, grad, resid, gains, weights, kernel,
                     depth_gain, rows, pre, mixed, stats, **side):
    n, m = sizes
    count, full = resid.shape
    length, width = mixed.shape
    taps = kernel.shape[0]
    return comm_call(
        name, collective_id, sizes,
        functools.partial(convolution_back_main, count, gain_row, taps),
        [(limit, smem()), (grad, vmem()), (resid, "load"), (gains, vmem()), (weights, "load"),
         (kernel, vmem()), (depth_gain, vmem())]
        + [(item, "load") for item in (rows, pre, mixed, stats)],
        [
            ((8, full), F32, vmem()),
            ((full, 3 * width), BF16, "store"),
            ((PAD, width), F32, vmem()),
            ((8, width), F32, vmem()),
            ((count, full), F32, vmem()),
        ],
        [
            pltpu.VMEM((PAD, width), F32),
            pltpu.VMEM((length, full), BF16),
            pltpu.VMEM((length + PAD, width), F32),
            pltpu.VMEM((length + PAD, width), F32),
            pltpu.VMEM((8, length), F32),
            pltpu.VMEM((n - 1, 8, length), F32),
            pltpu.VMEM((8 * taps, width), F32),
            pltpu.VMEM((length, width), BF16),
            pltpu.VMEM((length, 2 * width), BF16),
            pltpu.VMEM((n, count, full), BF16),
            pltpu.VMEM((n - 1, count, full), BF16),
        ],
        cost=20 * 10**9, **side,
    )


def results_kernel(*refs):
    sources, targets = refs[:len(refs) // 2], refs[len(refs) // 2:]
    for source, target in zip(sources, targets):
        if target.shape[0] == 1 and source.shape[0] == 8:
            target[...] = source[...].T[0:1]
        elif source.shape != target.shape:
            target[...] = source[...].astype(target.dtype).T
        else:
            target[...] = source[...]


def results(arrays, shapes):
    return pl.pallas_call(
        results_kernel,
        name="results",
        out_shape=tuple(shapes),
        in_specs=[vmem()] * len(arrays),
        out_specs=tuple(vmem() for _ in arrays),
        compiler_params=pltpu.CompilerParams(vmem_limit_bytes=VMEM_LIMIT),
    )(*arrays)


def body(
    layer_input,
    clip_lengths,
    first_gain,
    first_up,
    first_down,
    attend_gain,
    query_weight,
    key_weight,
    value_weight,
    output_weight,
    distance_table,
    conv_gain,
    pointwise_value,
    pointwise_gate,
    depthwise_kernel,
    depthwise_gain,
    pointwise_out,
    second_gain,
    second_up,
    second_down,
    final_gain,
    output_cotangent,
):
    n = lax.axis_size("col")
    me = lax.axis_index("col")
    width, length = layer_input.shape
    full = n * width
    count = length // n

    sizes = (n, lax.axis_size("row"))
    group = min(2 * HEAD_DIM, width)
    table_wide = extend_table(distance_table, group // HEAD_DIM)
    limit = clip_lengths
    tap_count = depthwise_kernel.shape[0]
    gain_parts = [
        gain[None] for gain in (first_gain, attend_gain, conv_gain, second_gain, final_gain)
    ]
    attend_pieces = [
        (query_weight, False), (key_weight, False), (value_weight, False), (output_weight, True)
    ]
    conv_pieces = [(pointwise_value, False), (pointwise_gate, False), (pointwise_out, True)]
    hidden = first_up.shape[1]
    tokens_in = (layer_input, output_cotangent)
    if count % BLOCK:
        tokens_in = (layer_input.T, output_cotangent.T)

    (start, cot, gains, up_first, down_first, attend_weights, after_first, squares_first, rows_first,
     pre_first) = feed_forward(
        sizes, "first", 1, 0, first_up, first_down, limit,
        enter=(*tokens_in, gain_parts, attend_pieces),
    )
    (after_attend, squares_attend, rows_attend, qkv, context, log_total, conv_weights,
     up_second) = attention(
        sizes, "attend", 2, 1, limit, after_first, gains, attend_weights, table_wide,
        gathers=[conv_pieces, [(second_up, False)]],
    )
    depth_row = depthwise_gain[None]
    (after_conv, squares_conv, rows_conv, conv_pre, mixed, stats, down_second) = convolution(
        sizes, "convolve", 3, 2, limit, after_attend, gains, conv_weights, depthwise_kernel, depth_row,
        gathers=[[(second_down, True)]],
    )
    (grad_second, final_part, out_tokens, squares_second, rows_second, pre_second) = feed_forward(
        sizes, "second", 4, 3, up_second, down_second, limit, resid=after_conv, gains=gains, turn=cot
    )

    second_part, second_up_wide, second_down_wide, grad_conv, layer_output = feed_forward_back(
        sizes, "second_back", 5, 3, grad_second, after_conv, gains, up_second, down_second,
        rows_second, pre_second, tokens=out_tokens,
    )
    conv_part, conv_wide, kernel_part, depth_part, grad_attend, second_up_grad = convolution_back(
        sizes, "convolve_back", 6, 2, limit, grad_conv, after_attend, gains, conv_weights,
        depthwise_kernel, depth_row, rows_conv, conv_pre, mixed, stats,
        reduces=[(second_up_wide, [(hidden, False)])],
    )
    (attend_part, attend_wide, table_part, grad_first, second_down_grad, value_grad, gate_grad,
     out_grad) = attention_back(
        sizes, "attend_back", 7, 1, limit, grad_attend, after_first, gains, attend_weights,
        table_wide, rows_attend, qkv, context, log_total,
        reduces=[
            (second_down_wide, [(hidden, True)]),
            (conv_wide, [(width, False), (width, False), (width, True)]),
        ],
    )
    (first_sum, attend_sum, conv_sum, second_sum, final_sum, table_sum, masked_rms, kernel_sum,
     depth_sum, first_up_grad, first_down_grad, grad_tokens, query_grad, key_grad, attend_value_grad,
     output_grad) = feed_forward_back(
        sizes, "first_back", 0, 0, grad_first, start, gains, up_first, down_first, rows_first,
        pre_first, taps=tap_count,
        leave=(
            limit, (attend_part, conv_part, second_part, final_part),
            (squares_first, squares_attend, squares_conv, squares_second), table_part, kernel_part,
            depth_part,
        ),
        reduces=[(attend_wide, [(width, False), (width, False), (width, False), (width, True)])],
    )

    arrays = [
        layer_output, grad_tokens, first_sum, first_up_grad, first_down_grad, attend_sum, query_grad,
        key_grad, attend_value_grad, output_grad, table_sum, conv_sum, value_grad, gate_grad, kernel_sum,
        depth_sum, out_grad, second_sum, second_up_grad, second_down_grad, final_sum, masked_rms,
    ]
    shapes = [jax.ShapeDtypeStruct(array.shape, array.dtype) for array in arrays]
    shapes[1] = jax.ShapeDtypeStruct(grad_tokens.shape[::-1], F32)
    shapes[-1] = jax.ShapeDtypeStruct((1, 8), F32)
    arrays = results(arrays, shapes)
    return tuple(array[0] if array.shape[0] == 1 else array for array in arrays)


def solution(mesh):
    in_specs = (
        P("col", "row"),
        P("row"),
        P("col"),
        P("row", "col"),
        P("col", "row"),
        P("col"),
        P("row", "col"),
        P("row", "col"),
        P("row", "col"),
        P("col", "row"),
        P(),
        P("col"),
        P("row", "col"),
        P("row", "col"),
        P(None, "col"),
        P("col"),
        P("col", "row"),
        P("col"),
        P("row", "col"),
        P("col", "row"),
        P("col"),
        P("col", "row"),
    )
    out_specs = (
        P("col", "row"),
        P("col", "row"),
        P("col"),
        P("row", "col"),
        P("col", "row"),
        P("col"),
        P("row", "col"),
        P("row", "col"),
        P("row", "col"),
        P("col", "row"),
        P(),
        P("col"),
        P("row", "col"),
        P("row", "col"),
        P(None, "col"),
        P("col"),
        P("col", "row"),
        P("col"),
        P("row", "col"),
        P("col", "row"),
        P("col"),
        P(),
    )
    return jax.shard_map(body, mesh=mesh, in_specs=in_specs, out_specs=out_specs, check_vma=False)
```

```python
import functools
import math

import jax
import jax.numpy as jnp
from jax import lax
from jax.experimental import pallas as pl
from jax.experimental.pallas import tpu as pltpu
from jax.sharding import PartitionSpec as P

HEAD_DIM = 64
LEFT = 64
RIGHT = 8
EPSILON = 1e-05
NEG_FILL = -1e30
BF16 = jnp.bfloat16
F32 = jnp.float32
MESH = pl.DeviceIdType.MESH
BLOCK = 128
WINDOW = 384
SPAN = 512
VMEM_LIMIT = 60 * 1024 * 1024
MARGIN = 6 * 1024 * 1024


def matmul(left, right):
    return jnp.dot(left, right, preferred_element_type=F32)


def matmul_nt(left, right):
    return lax.dot_general(left, right, (((1,), (1,)), ((), ())), preferred_element_type=F32)


def matmul_tn(left, right):
    return lax.dot_general(left, right, (((0,), (0,)), ((), ())), preferred_element_type=F32)


def vmem():
    return pl.BlockSpec(memory_space=pltpu.VMEM)


def smem():
    return pl.BlockSpec(memory_space=pltpu.SMEM)


def hbm():
    return pl.BlockSpec(memory_space=pltpu.HBM)


def padded_bytes(shape, dtype):
    size = jnp.dtype(dtype).itemsize
    rows = 8 * 4 // size
    shape = (1,) * (2 - len(shape)) + tuple(shape)
    held = -(-shape[-1] // 128) * 128 * -(-shape[-2] // rows) * rows
    return math.prod(shape[:-2]) * held * size


def comm_params(collective_id, held):
    return pltpu.CompilerParams(
        collective_id=collective_id, has_side_effects=True,
        vmem_limit_bytes=max(VMEM_LIMIT, held + MARGIN),
    )


def tile(index, size):
    return pl.ds(pl.multiple_of(index * size, size), size)


class Wire:
    def __init__(self, sizes, send_sem, recv_sem, local_sem, side, col_on=True, row_on=False):
        self.n, self.m = sizes
        self.me = lax.axis_index("col")
        self.row = lax.axis_index("row")
        self.send_sem, self.recv_sem, self.local_sem = send_sem, recv_sem, local_sem
        self.used = 0
        self.used_local = 0
        self.core = lax.rem(self.row, 2)
        self.layer = self.row // 2
        self.partner = self.row + 1 - 2 * self.core
        self.layers = self.m // 2
        self.col_on = col_on
        self.loads, self.stores, self.stored = [], [], []
        self.row_on = row_on or bool(side)
        self.side = [job(self) for job in side]

    def layer_peer(self, step):
        return lax.rem(self.layer + step, self.layers) * 2 + self.core

    def greet(self):
        barrier = pltpu.get_barrier_semaphore()
        waits = 0
        if self.col_on:
            for step in range(1, self.n):
                pl.semaphore_signal(
                    barrier, inc=1, device_id={"col": lax.rem(self.me + step, self.n)},
                    device_id_type=MESH,
                )
            waits += self.n - 1
        if self.row_on:
            for step in range(1, self.layers):
                pl.semaphore_signal(
                    barrier, inc=1, device_id={"row": self.layer_peer(step)}, device_id_type=MESH
                )
            pl.semaphore_signal(
                barrier, inc=1, device_id={"row": self.partner}, device_id_type=MESH
            )
            waits += self.layers
        pl.semaphore_wait(barrier, waits)

    def remote(self, source, target, axis, peer):
        slot = self.used
        self.used += 1
        return pltpu.make_async_remote_copy(
            src_ref=source, dst_ref=target, send_sem=self.send_sem.at[slot],
            recv_sem=self.recv_sem.at[slot], device_id={axis: peer}, device_id_type=MESH,
        )

    def local(self, source, target):
        slot = self.used_local
        self.used_local += 1
        return pltpu.make_async_copy(source, target, self.local_sem.at[slot])

    def to_all(self, source_of, target):
        copies = [
            self.remote(source_of(lax.rem(self.me + step, self.n)), target, "col",
                        lax.rem(self.me + step, self.n))
            for step in range(1, self.n)
        ]
        for copy in copies:
            copy.start()
        return copies

    def loaded(self):
        for copy in self.loads:
            copy.wait()

    def store(self, copies):
        for copy in copies:
            copy.start()
        self.stored += copies

    def flush(self):
        self.store(self.stores)

    def settle(self):
        for copy in self.stored:
            copy.wait()

    def begin(self):
        for job in self.side:
            job.begin()

    def early(self):
        for job in self.side:
            job.early()

    def middle(self):
        for job in self.side:
            job.middle()

    def end(self):
        for job in self.side:
            job.end()

    def peers(self):
        if self.n == 4:
            across = self.me + 1 - 2 * lax.rem(self.me, 2)
            along = lax.rem(self.me + 2, 4)
            return [(across, 0), (along, 1), (3 - self.me, 2)]
        return [
            (lax.rem(self.me + self.n - step, self.n), self.n - step - 1)
            for step in range(1, self.n)
        ]


class Spread:
    def __init__(self, wire, ref, count):
        self.wire, self.ref, self.count = wire, ref, count
        me = wire.me
        if wire.n != 4:
            self.copies = [
                wire.remote(self.part(me), self.part(me), "col", lax.rem(me + step, wire.n))
                for step in range(1, wire.n)
            ]
            return
        (across, _), (along, _), (far, _) = wire.peers()
        self.across = [wire.remote(self.part(me, q), self.part(me, q), "col", across) for q in range(4)]
        self.along = [wire.remote(self.part(me, q), self.part(me, q), "col", along) for q in range(4)]
        self.onward = [
            wire.remote(self.part(across, q), self.part(across, q), "col", along) for q in (0, 1)
        ] + [wire.remote(self.part(along, q), self.part(along, q), "col", across) for q in (2, 3)]

    def part(self, chunk, quarter=None):
        if quarter is None:
            return self.ref.at[tile(chunk, self.count)]
        size = self.count // 4
        return self.ref.at[tile(chunk * 4 + quarter, size)]

    def start(self):
        if self.wire.n != 4:
            for copy in self.copies:
                copy.start()
            return
        for first, second in ((0, 2), (1, 3), (2, 0), (3, 1)):
            self.across[first].start()
            self.along[second].start()

    def relay(self):
        if self.wire.n != 4:
            return
        for turn in range(2):
            self.relay_turn(turn)

    def relay_turn(self, turn):
        self.across[turn].wait_recv()
        self.onward[turn].start()
        self.along[2 + turn].wait_recv()
        self.onward[2 + turn].start()

    def wait_place(self, place):
        for copy in (self.across[2:], self.along[:2], self.onward)[place - 1]:
            copy.wait_recv()

    def arrivals(self, relay=True):
        wire = self.wire
        yield wire.me, None
        if wire.n != 4:
            for step, (peer, slot) in zip(range(1, wire.n), wire.peers()):
                self.copies[step - 1].wait_recv()
                yield peer, slot
            return
        if relay:
            self.relay()
        for place, (peer, slot) in enumerate(wire.peers()):
            self.wait_place(place + 1)
            yield peer, slot

    def finish(self):
        copies = self.copies if self.wire.n != 4 else self.across + self.along + self.onward
        for copy in copies:
            copy.wait_send()


class Collect:
    def __init__(self, wire, part, got):
        self.wire, self.part, self.got = wire, part, got
        self.relayed = wire.n == 4
        self.count = part.shape[1]
        if not self.relayed:
            self.copies = {
                slot: wire.remote(part.at[slot], got.at[slot], "col", owner)
                for owner, slot in wire.peers()
            }
            return
        (across, _), (along, _), _ = wire.peers()
        half = self.count // 2
        first, second = pl.ds(0, half), pl.ds(half, half)
        places = [got.at[place // 2, (first, second)[place % 2]] for place in range(6)]
        self.far = [
            wire.remote(part.at[2, first], places[0], "col", across),
            wire.remote(part.at[2, second], places[1], "col", along),
        ]
        self.direct = {
            0: wire.remote(part.at[0, first], places[2], "col", across),
            1: wire.remote(part.at[1, second], places[4], "col", along),
        }
        self.onward = [
            wire.remote(part.at[0, second], places[3], "col", across),
            wire.remote(part.at[1, first], places[5], "col", along),
        ]

    def send(self, slot):
        if not self.relayed:
            self.copies[slot].start()
        elif slot == 2:
            for copy in self.far:
                copy.start()
        else:
            self.direct[slot].start()

    def combine(self):
        if not self.relayed:
            return
        half = self.count // 2
        for copy, slot, at, onward in (
            (self.far[1], 0, half, self.onward[0]), (self.far[0], 1, 0, self.onward[1])
        ):
            copy.wait_recv()
            place = 1 - slot

            def add(rows, index):
                mine = pl.ds(pl.multiple_of(at + index * 32, 32), 32)
                came = pl.ds(pl.multiple_of((half if place else 0) + index * 32, 32), 32)
                self.part[slot, mine] = (
                    self.part[slot, mine].astype(F32) + self.got[0, came].astype(F32)
                ).astype(BF16)

            row_loop(half, add)
            onward.start()

    def wait(self):
        if not self.relayed:
            for copy in self.copies.values():
                copy.wait()
            return
        for copy in self.far:
            copy.wait_send()
        for copy in list(self.direct.values()) + self.onward:
            copy.wait()

    def sum_loop(self, body):
        part, got, last = self.part, self.got, self.wire.n - 1
        if not self.relayed:
            def step(rows, index):
                total = part[last, rows].astype(F32)
                for slot in range(last):
                    total = total + got[slot, rows].astype(F32)
                body(rows, total)

            row_loop(self.count, step)
            return
        half = self.count // 2
        for at, sources in ((0, ((1, 0), (2, half))), (half, ((1, half), (2, 0)))):
            def step(rows, index, at=at, sources=sources):
                mine = pl.ds(pl.multiple_of(at + index * 32, 32), 32)
                total = part[last, mine].astype(F32)
                for slot, start in sources:
                    total = total + got[
                        slot, pl.ds(pl.multiple_of(start + index * 32, 32), 32)
                    ].astype(F32)
                body(mine, total)

            row_loop(half, step)


class RowChain:
    def __init__(self, shard, full, wire):
        self.wire, self.shard, self.full = wire, shard, full
        self.count = shard.shape[0]
        self.steps = wire.layers - 1
        self.base = wire.used
        wire.used += 4 * self.steps
        mine = full.at[tile(wire.row, self.count)]
        self.own = [wire.local(shard, mine), wire.remote(shard, mine, "row", wire.partner)]

    def block(self, layer):
        return self.full.at[tile(layer * 2 + self.wire.core, self.count)]

    def copy(self, kind, step, layer, peer):
        slot = self.base + kind * self.steps + step
        wire = self.wire
        source = self.shard if kind < 2 and step == 0 else self.block(layer)
        return pltpu.make_async_remote_copy(
            src_ref=source, dst_ref=self.block(layer), send_sem=wire.send_sem.at[slot],
            recv_sem=wire.recv_sem.at[slot], device_id={"row": peer}, device_id_type=MESH,
        )

    def up(self, step):
        wire = self.wire
        return self.copy(0, step, wire.layer - step, wire.row + 2)

    def down(self, step):
        wire = self.wire
        return self.copy(1, step, wire.layer + step, wire.row - 2)

    def begin(self):
        wire = self.wire
        pl.when(wire.layer + 1 < wire.layers)(lambda: self.up(0).start())
        pl.when(wire.layer > 0)(lambda: self.down(0).start())
        for copy in self.own:
            copy.start()

    def advance(self, step):
        wire = self.wire

        @pl.when(wire.layer - 1 - step >= 0)
        def _():
            self.copy(0, step, wire.layer - 1 - step, wire.row).wait_recv()
            if step + 1 < self.steps:
                pl.when(wire.layer + 1 < wire.layers)(lambda: self.up(step + 1).start())
            self.copy(2, step, wire.layer - 1 - step, wire.partner).start()

        @pl.when(wire.layer + 1 + step < wire.layers)
        def _():
            self.copy(1, step, wire.layer + 1 + step, wire.row).wait_recv()
            if step + 1 < self.steps:
                pl.when(wire.layer > 0)(lambda: self.down(step + 1).start())
            self.copy(3, step, wire.layer + 1 + step, wire.partner).start()

    def end(self):
        wire = self.wire
        for step in range(self.steps):
            pl.when((wire.layer + 1 < wire.layers) & (wire.layer - step >= 0))(
                lambda step=step: self.up(step).wait_send()
            )
            pl.when((wire.layer > 0) & (wire.layer + step < wire.layers))(
                lambda step=step: self.down(step).wait_send()
            )
            pl.when(wire.layer - 1 - step >= 0)(
                lambda step=step: self.copy(2, step, wire.layer - 1 - step, wire.partner).wait()
            )
            pl.when(wire.layer + 1 + step < wire.layers)(
                lambda step=step: self.copy(3, step, wire.layer + 1 + step, wire.partner).wait()
            )
        for copy in self.own:
            copy.wait()


class RowGather:
    def __init__(self, shard, full, wire):
        self.wire = wire
        count = shard.shape[0]
        mine = full.at[tile(wire.row, count)]
        self.first = [wire.local(shard, mine), wire.remote(shard, mine, "row", wire.partner)]
        self.along = [
            wire.remote(shard, mine, "row", wire.layer_peer(step))
            for step in range(1, wire.layers)
        ]
        self.onward = []
        for step in range(1, wire.layers):
            block = full.at[tile(wire.layer_peer(wire.layers - step), count)]
            self.onward.append(wire.remote(block, block, "row", wire.partner))

    def begin(self):
        for copy in self.along + self.first:
            copy.start()

    def early(self):
        pass

    def middle(self):
        for copy, onward in zip(self.along, self.onward):
            copy.wait_recv()
            onward.start()

    def end(self):
        for copy in self.along:
            copy.wait_send()
        for copy in self.first:
            copy.wait()
        for copy in self.onward:
            copy.wait()


class RowReduce:
    def __init__(self, grads, pieces, outs, held, pair, got, total, *rest, load=True):
        *parts, wire = rest
        self.wire, self.out, self.grads = wire, total, grads
        self.pieces = pieces
        self.parts = parts or [total]
        self.keep = [wire.local(part, out) for part, out in zip(self.parts, outs)]
        self.held, self.pair, self.got = held, pair, got
        self.count = held.shape[1]
        self.load = []
        if load:
            self.load = [
                wire.local(grads.at[tile(layer * 2 + wire.core, self.count)], held.at[layer])
                for layer in range(wire.layers)
            ]
        self.base = wire.used
        wire.used += 2 * wire.layers

    def layer_of(self, step):
        return lax.rem(self.wire.layer + 1 + step, self.wire.layers)

    def between(self, source, target, slot, peer):
        wire = self.wire
        return pltpu.make_async_remote_copy(
            src_ref=source, dst_ref=target, send_sem=wire.send_sem.at[self.base + slot],
            recv_sem=wire.recv_sem.at[self.base + slot], device_id={"row": peer}, device_id_type=MESH,
        )

    def swap(self, step):
        layer = self.layer_of(step)
        block = layer * 2 + 1 - self.wire.core
        return self.between(self.grads.at[tile(block, self.count)], self.pair.at[layer], step,
                            self.wire.partner)

    def along(self, step):
        layer = self.layer_of(step)
        return self.between(self.held.at[layer], self.got.at[step], self.wire.layers + step,
                            layer * 2 + self.wire.core)

    def begin_step(self, step):
        self.swap(step).start()

    def early_step(self, step):
        self.swap(step).wait()
        layer = self.layer_of(step)
        size = min(32, self.count)

        def add(rows, index):
            if self.load:
                mine = self.held[layer, rows]
            else:
                at = (layer * 2 + self.wire.core) * self.count + index * size
                mine = self.grads[pl.ds(pl.multiple_of(at, size), size)]
            self.held[layer, rows] = (
                mine.astype(F32) + self.pair[layer, rows].astype(F32)
            ).astype(BF16)

        row_loop(self.count, add)
        pl.when(step < self.wire.layers - 1)(lambda: self.along(step).start())

    def begin(self):
        for step in range(self.wire.layers):
            self.begin_step(step)
        for copy in self.load:
            copy.start()

    def early(self):
        for copy in self.load:
            copy.wait()

        def one(step, carry):
            self.early_step(step)
            return carry

        lax.fori_loop(0, self.wire.layers, one, 0)

    def middle(self):
        pass

    def end(self):
        for step in range(self.wire.layers - 1):
            self.along(step).wait()

        def add(rows, index):
            total = self.held[self.wire.layer, rows].astype(F32)
            for step in range(self.wire.layers - 1):
                total = total + self.got[step, rows].astype(F32)
            self.out[rows] = total

        row_loop(self.count, add)
        if len(self.parts) > 1 or self.pieces[0][1]:
            at = 0
            for part, (width, flip) in zip(self.parts, self.pieces):
                piece = self.out[:, at:at + width]
                part[...] = piece.T if flip else piece
                at += width
        self.wire.store(self.keep)


def piece_shapes(count, pieces):
    return [(width, count) if flip else (count, width) for width, flip in pieces]


def reduce_scratch(layers, count, width, pieces):
    apart = len(pieces) > 1 or pieces[0][1]
    parts = [pltpu.VMEM(shape, F32) for shape in piece_shapes(count, pieces)] if apart else []
    return parts_last(layers, count, width) + parts


def parts_last(layers, count, width):
    return [
        pltpu.VMEM((layers, count, width), BF16),
        pltpu.VMEM((layers, count, width), BF16),
        pltpu.VMEM((max(1, layers - 1), count, width), BF16),
        pltpu.VMEM((count, width), F32),
    ]


class SumItem:
    def __init__(self, kind, source, out, got, packed, got_row, wire):
        self.wire, self.kind, self.source, self.out = wire, kind, source, out
        self.got, self.packed, self.got_row = got, packed, got_row
        self.col = []
        if kind != "own":
            for step in range(1, wire.n):
                peer = lax.rem(wire.me + step, wire.n)
                piece = source.at[peer] if kind == "piece" else source
                self.col.append(wire.remote(piece, got.at[step - 1], "col", peer))
        self.swap = wire.remote(packed.at[0], got_row.at[0], "row", wire.partner)
        self.along = [
            wire.remote(packed.at[1], got_row.at[step], "row", wire.layer_peer(step))
            for step in range(1, wire.layers)
        ]

    def begin(self):
        for copy in self.col:
            copy.start()

    def early(self):
        for copy in self.col:
            copy.wait()
        total = self.source[self.wire.me] if self.kind == "piece" else self.source[...]
        if self.kind != "own":
            for step in range(self.wire.n - 1):
                total = total + self.got[step]
        self.packed[0] = total
        self.swap.start()

    def middle(self):
        self.swap.wait()
        self.packed[1] = self.packed[0] + self.got_row[0]
        for copy in self.along:
            copy.start()

    def end(self):
        for copy in self.along:
            copy.wait()
        total = self.packed[1]
        for step in range(1, self.wire.layers):
            total = total + self.got_row[step]
        self.out[...] = total


def sum_scratch(n, layers, shape):
    return [
        pltpu.VMEM(shape, F32),
        pltpu.VMEM((n - 1,) + shape, F32),
        pltpu.VMEM((2,) + shape, F32),
        pltpu.VMEM((layers,) + shape, F32),
    ]


def join(pieces, target):
    at = 0
    for ref, flip in pieces:
        width = ref.shape[0] if flip else ref.shape[1]
        target[:, at:at + width] = ref[...].T if flip else ref[...]
        at += width


def joined_shape(pieces):
    rows = {array.shape[1] if flip else array.shape[0] for array, flip in pieces}
    return rows.pop(), sum(array.shape[0] if flip else array.shape[1] for array, flip in pieces)


def row_loop(count, body):
    size = min(32, count)

    def step(index, carry):
        body(tile(index, size), index)
        return carry

    lax.fori_loop(0, count // size, step, 0)


def block_loop(extent, body):
    size = min(256, extent)

    def step(index, carry):
        body(tile(index, size), index)
        return carry

    lax.fori_loop(0, extent // size, step, 0)


def fold8(values):
    return jnp.sum(values.reshape(values.shape[0] // 8, 8, values.shape[1]), axis=0)


def normalize(values):
    average = jnp.mean(values, axis=1, keepdims=True)
    centered = values - average
    inverse = lax.rsqrt(jnp.mean(centered * centered, axis=1, keepdims=True) + EPSILON)
    return centered * inverse, inverse


def norm_back(grad_in, normed, inverse, gains):
    scaled = grad_in * gains
    first = jnp.mean(scaled, axis=1, keepdims=True)
    second = jnp.mean(scaled * normed, axis=1, keepdims=True)
    return inverse * (scaled - first - normed * second)


def comm_call(name, collective_id, sizes, main, ins, outs, scratch, gathers=(), reduces=(), cost=10**9,
              col_on=True, more_slots=0, row_on=False):
    n, m = sizes
    layers = m // 2
    gather_pieces = [piece for pieces in gathers for piece in pieces]
    in_arrays = [item[0] for item in ins] + [array for array, _ in gather_pieces]
    in_arrays += [grads for grads, _ in reduces]
    in_specs = [hbm() if item[1] == "load" else item[1] for item in ins]
    in_specs += [vmem()] * len(gather_pieces) + [hbm()] * len(reduces)
    out_shapes = [jax.ShapeDtypeStruct(item[0], item[1]) for item in outs]
    out_specs = [hbm() if item[2] == "store" else item[2] for item in outs]
    copied = [pltpu.VMEM(item[0].shape, item[0].dtype) for item in ins if item[1] == "load"]
    copied += [pltpu.VMEM(item[0], item[1]) for item in outs if item[2] == "store"]
    side_scratch = []
    for pieces in gathers:
        rows, width = joined_shape(pieces)
        out_shapes.append(jax.ShapeDtypeStruct((m * rows, width), BF16))
        out_specs.append(hbm())
        side_scratch.append(pltpu.VMEM((rows, width), BF16))
    reduce_counts = []
    for grads, pieces in reduces:
        count, width = grads.shape[0] // m, grads.shape[1]
        for shape in piece_shapes(count, pieces):
            out_shapes.append(jax.ShapeDtypeStruct(shape, F32))
            out_specs.append(hbm())
        made = reduce_scratch(layers, count, width, pieces)
        reduce_counts.append(len(made))
        side_scratch += made
    every_scratch = copied + list(scratch) + side_scratch
    held = sum(padded_bytes(item.shape, item.dtype) for item in every_scratch)
    remote_slots = 8 * n + 16 + len(gathers) * 2 * layers + len(reduces) * 2 * layers + more_slots
    local_slots = 12 + len(copied) + len(gathers) + len(reduces) * (layers + 4) + more_slots

    def kernel(*refs):
        at = 0

        def take(count):
            nonlocal at
            at += count
            return refs[at - count:at]

        main_ins = list(take(len(ins)))
        gather_ins = [
            [(ref, flip) for ref, (_, flip) in zip(take(len(pieces)), pieces)] for pieces in gathers
        ]
        reduce_ins = take(len(reduces))
        main_outs = list(take(len(outs)))
        gather_outs = take(len(gathers))
        reduce_outs = [take(len(pieces)) for _, pieces in reduces]
        loads, stores = [], []
        for place, item in enumerate(ins):
            if item[1] == "load":
                (held_ref,) = take(1)
                loads.append((main_ins[place], held_ref))
                main_ins[place] = held_ref
        for place, item in enumerate(outs):
            if item[2] == "store":
                (held_ref,) = take(1)
                stores.append((held_ref, main_outs[place]))
                main_outs[place] = held_ref
        main_scratch = take(len(scratch))
        side = []
        for pieces, full in zip(gather_ins, gather_outs):
            (shard,) = take(1)
            join(pieces, shard)
            side.append(functools.partial(RowGather, shard, full))
        for grads, out, (_, pieces), size in zip(reduce_ins, reduce_outs, reduces, reduce_counts):
            side.append(functools.partial(RowReduce, grads, pieces, out, *take(size)))
        send_sem, recv_sem, local_sem = take(3)
        wire = Wire(sizes, send_sem, recv_sem, local_sem, side, col_on, row_on)
        wire.loads = [wire.local(*pair) for pair in loads]
        wire.stores = [wire.local(*pair) for pair in stores]
        for copy in wire.loads:
            copy.start()
        main(wire, main_ins, main_outs, main_scratch)
        wire.settle()

    return pl.pallas_call(
        kernel,
        name=name,
        out_shape=tuple(out_shapes),
        in_specs=in_specs,
        out_specs=tuple(out_specs),
        scratch_shapes=every_scratch + [
            pltpu.SemaphoreType.DMA((remote_slots,)),
            pltpu.SemaphoreType.DMA((remote_slots,)),
            pltpu.SemaphoreType.DMA((local_slots,)),
        ],
        compiler_params=comm_params(collective_id, held),
        cost_estimate=pl.CostEstimate(flops=cost, bytes_accessed=10**8, transcendentals=0),
    )(*in_arrays)


def norm_rows(wire, count, source, gains, rows_ref):
    base = wire.me * count

    def work(rows, index):
        normed, _ = normalize(source[rows])
        size = min(32, count)
        rows_ref[pl.ds(pl.multiple_of(base + index * size, size), size)] = (normed * gains).astype(BF16)

    row_loop(count, work)


def cast_rows(wire, count, source, factor, rows_ref):
    base = wire.me * count

    def work(rows, index):
        size = min(32, count)
        rows_ref[pl.ds(pl.multiple_of(base + index * size, size), size)] = (
            factor * source[rows]
        ).astype(BF16)

    row_loop(count, work)


def keep_rows(limit, start, rows):
    place = lax.broadcasted_iota(jnp.int32, (rows, 1), 0) + start
    return jnp.where(place < limit, 1.0, 0.0)


def residual(collect, factor, resid, limit, after_ref, squares_ref):
    squares_ref[...] = jnp.zeros_like(squares_ref)
    base = collect.wire.me * collect.count

    def work(rows, branch):
        after = resid[rows] + factor * branch
        after_ref[rows] = after
        keep = keep_rows(limit, base + rows.start, branch.shape[0])
        squares_ref[0:8] += fold8(branch * branch * keep)
        squares_ref[8:16] += fold8(after * after * keep)

    collect.sum_loop(work)


def residual_back(collect, grad_ref, resid, gains, new_grad_ref, gain_grad_ref):
    gain_grad_ref[...] = jnp.zeros_like(gain_grad_ref)

    def work(rows, rows_grad):
        normed, inverse = normalize(resid[rows])
        new_grad_ref[rows] = grad_ref[rows] + norm_back(rows_grad, normed, inverse, gains)
        gain_grad_ref[...] += fold8(rows_grad * normed)

    collect.sum_loop(work)


def split_pieces(wire, count, source, pieces):
    width = pieces.shape[2]

    def split(rows, index):
        result = source[rows].astype(BF16)
        for part in range(wire.n):
            pieces[part, rows] = result[:, part * width:(part + 1) * width]

    row_loop(count, split)


def send_pieces(wire, count, source, pieces, out_ref):
    split_pieces(wire, count, source, pieces)
    mine = out_ref.at[tile(wire.me, count)]
    copies = wire.to_all(lambda peer: pieces.at[peer], mine)
    here = wire.local(pieces.at[wire.me], mine)
    here.start()
    return copies + [here]


def flipped(wire, place):
    flip_across, flip_along = lax.rem(place, 2), place // 2
    across_bit, along_bit = lax.rem(wire.me, 2), wire.me // 2
    return (
        across_bit + flip_across - 2 * across_bit * flip_across
        + 2 * (along_bit + flip_along - 2 * along_bit * flip_along)
    )


def send_shares(wire, chunks, collect, share, last=None):
    part = collect.part
    if wire.n == 4:
        def turn(step, carry):
            left = 3 - step
            share(flipped(wire, left), part.at[lax.rem(left + 3, 4)])
            for place in range(3):
                pl.when(step == place)(lambda place=place: collect.send(2 - place))
            if last is not None:
                pl.when(step == 2)(last)
            return carry

        lax.fori_loop(0, 4, turn, 0)
    else:
        for chunk, slot in reversed(chunks):
            share(chunk, part.at[wire.n - 1 if slot is None else slot])
            if slot is not None:
                collect.send(slot)
        if last is not None:
            last()


def feed_forward_first(count, chunk, rows_ref, up, pre_ref, act):
    rows = tile(chunk, count)
    left = rows_ref[rows]

    def first(cols, index):
        pre = matmul(left, up[:, cols])
        pre_ref[rows, cols] = pre.astype(BF16)
        act[:, cols] = (pre * jax.nn.sigmoid(pre)).astype(BF16)

    block_loop(up.shape[1], first)


def feed_forward_second(act, down_t, target):
    hidden = act[...]

    def second(cols, index):
        target[:, cols] = matmul_nt(hidden, down_t[cols]).astype(BF16)

    block_loop(down_t.shape[0], second)


def feed_forward_main(count, gain_row, factor, enter, turn, wire, ins, outs, scratch):
    ins, outs, scratch = list(ins), list(outs), list(scratch)
    if enter:
        limit_ref, tokens_ref, cot_in = ins[:3]
        gain_ins = ins[3:8]
        up_shard, down_ref = ins[8:10]
        next_pieces = [(ref, flip) for ref, flip in zip(ins[10:], enter)]
        ins = []
        resid, cot_out, gains_ref, up, down_t, next_full = outs[:6]
        outs = outs[6:]
        arrived, arrived_cot, arrived_gain, gain_in, down_shard, next_shard = scratch[:6]
        scratch = scratch[6:]
    else:
        limit_ref, resid, gains_ref = ins[:3]
        ins = ins[3:]
    if enter:
        for place, ref in enumerate(gain_ins):
            gain_in[place:place + 1] = ref[...]
        gain_in[len(gain_ins):] = jnp.zeros((8 - len(gain_ins), gain_in.shape[1]), F32)
        join([(down_ref, True)], down_shard)
        join(next_pieces, next_shard)
    else:
        up, down_t = ins[:2]
        ins = ins[2:]
    if turn:
        (cot_ref,) = ins
        grad_ref, gain_grad_ref, out_ref = outs[:3]
        outs = outs[3:]
        pieces, after_ref = scratch[:2]
        scratch = scratch[2:]
    else:
        after_ref = outs.pop(0)
    squares_ref, rows_ref, pre_ref = outs
    act, part, got = scratch
    wire.greet()
    wire.begin()
    if enter:
        up_job = RowChain(up_shard, up, wire)
        down_job = RowChain(down_shard, down_t, wire)
        next_job = RowChain(next_shard, next_full, wire)
        up_job.begin()
        width = arrived_gain.shape[2]
        turned = tokens_ref.shape[0] == width

        def share(ref, peer):
            return ref.at[:, tile(peer, count)] if turned else ref.at[tile(peer, count)]

        def settle(came, target):
            for piece in range(wire.n):
                cols = slice(piece * width, (piece + 1) * width)
                if turned:
                    target[:, cols] = came[piece].astype(F32).T
                else:
                    target[:, cols] = came[piece].astype(F32)

        mine = [
            wire.local(share(tokens_ref, wire.me), arrived.at[wire.me]),
            wire.local(gain_in, arrived_gain.at[wire.me]),
            wire.local(share(cot_in, wire.me), arrived_cot.at[wire.me]),
        ]
        copies = wire.to_all(lambda peer: share(tokens_ref, peer), arrived.at[wire.me])
        copies += wire.to_all(lambda peer: gain_in, arrived_gain.at[wire.me])
        for copy in mine:
            copy.start()
        for copy in mine + copies:
            copy.wait()
        for piece in range(wire.n):
            gains_ref[:, piece * width:(piece + 1) * width] = arrived_gain[piece]

        settle(arrived, resid)
    gains = gains_ref[gain_row:gain_row + 1]
    norm_rows(wire, count, resid, gains, rows_ref)
    spread = Spread(wire, rows_ref, count)
    spread.start()
    wire.loaded()
    collect = Collect(wire, part, got)
    wire.early()
    if enter:
        up_job.advance(0)
        spread.relay()
        cot_copies = wire.to_all(lambda peer: share(cot_in, peer), arrived_cot.at[wire.me])
        for step in range(1, up_job.steps):
            up_job.advance(step)
        down_job.begin()
        up_job.end()
        chunks = []
        for chunk, slot in spread.arrivals(relay=False):
            chunks.append((chunk, slot))
            feed_forward_first(count, chunk, rows_ref, up, pre_ref, act.at[len(chunks) - 1])
            if len(chunks) - 1 < down_job.steps:
                down_job.advance(len(chunks) - 1)
        for copy in cot_copies:
            copy.wait()

        settle(arrived_cot, cot_out)
        next_job.begin()
        down_job.end()
        for place, (chunk, slot) in reversed(list(enumerate(chunks))):
            target = part.at[wire.n - 1 if slot is None else slot]
            feed_forward_second(act.at[place], down_t, target)
            if slot is not None:
                collect.send(slot)
            if len(chunks) - 1 - place < next_job.steps:
                next_job.advance(len(chunks) - 1 - place)
        collect.combine()
        for step in range(len(chunks), next_job.steps):
            next_job.advance(step)
    else:
        for chunk, slot in spread.arrivals():
            target = part.at[wire.n - 1 if slot is None else slot]
            feed_forward_first(count, chunk, rows_ref, up, pre_ref, act.at[0])
            feed_forward_second(act.at[0], down_t, target)
            if slot is not None:
                collect.send(slot)
        collect.combine()
    wire.middle()
    wire.flush()
    collect.wait()
    residual(collect, factor, resid, limit_ref[0], after_ref, squares_ref)
    if turn:
        final_gains = gains_ref[gain_row + 1:gain_row + 2]
        gain_grad_ref[...] = jnp.zeros_like(gain_grad_ref)

        def final(rows, index):
            normed, inverse = normalize(after_ref[rows])
            cot = cot_ref[rows]
            grad_ref[rows] = norm_back(cot, normed, inverse, final_gains)
            gain_grad_ref[...] += fold8(cot * normed)
            after_ref[rows] = normed * final_gains

        row_loop(count, final)
        split_pieces(wire, count, after_ref, pieces)
        wire.store([wire.local(pieces, out_ref)])
    spread.finish()
    if enter:
        next_job.end()
    wire.end()


def feed_forward(sizes, name, collective_id, gain_row, up, down_t, limit, resid=None, gains=None,
                 enter=None, turn=None, **side):
    n, m = sizes
    hidden = up.shape[1]
    full = up.shape[0] * (m if enter else 1)
    next_pieces = None
    if enter:
        tokens, cotangent, gain_parts, next_pieces = enter
        turned = tokens.shape[0] * n == full
        width, length = tokens.shape if turned else tokens.shape[::-1]
        count = length // n
        came = (n, width, count) if turned else (n, count, width)
        ins = [(limit, smem()), (tokens, vmem()), (cotangent, vmem())]
        ins += [(part, vmem()) for part in gain_parts] + [(up, vmem()), (down_t, vmem())]
        ins += [(array, vmem()) for array, _ in next_pieces]
        down_shape, next_shape = (full // m, hidden), joined_shape(next_pieces)
        outs = [((count, full), F32, "store"), ((count, full), F32, "store"), ((8, full), F32, vmem())]
        scratch = [
            pltpu.VMEM(came, BF16),
            pltpu.VMEM(came, BF16),
            pltpu.VMEM((n, 8, width), F32),
            pltpu.VMEM((8, width), F32),
            pltpu.VMEM(down_shape, BF16),
            pltpu.VMEM(next_shape, BF16),
        ]
        for shape, spec in ((down_shape, "store"), (down_shape, "store"), (next_shape, hbm())):
            outs.append(((m * shape[0], shape[1]), BF16, spec))
        side = dict(side, more_slots=6 * m, row_on=True)
    else:
        count = resid.shape[0]
        ins = [(limit, smem()), (resid, vmem()), (gains, vmem())]
        outs, scratch = [], []
        ins += [(up, "load"), (down_t, "load")]
    if turn is not None:
        ins.append((turn, "load"))
        outs += [
            ((count, full), F32, vmem()),
            ((8, full), F32, vmem()),
            ((n, count, full // n), BF16, hbm()),
        ]
        scratch.append(pltpu.VMEM((n, count, full // n), BF16))
    if turn is None:
        outs.append(((count, full), F32, vmem()))
    else:
        scratch.append(pltpu.VMEM((count, full), F32))
    outs += [
        ((16, full), F32, vmem()),
        ((n * count, full), BF16, "store"),
        ((n * count, hidden), BF16, "store"),
    ]
    scratch += [
        pltpu.VMEM((n if enter else 1, count, hidden), BF16),
        pltpu.VMEM((n, count, full), BF16),
        pltpu.VMEM((n - 1, count, full), BF16),
    ]
    return comm_call(
        name, collective_id, sizes,
        functools.partial(
            feed_forward_main, count, gain_row, 0.5, enter and [flip for _, flip in next_pieces],
            turn is not None,
        ),
        ins, outs, scratch, **side,
    )


def lane_sum(values):
    total = values[:, 0:BLOCK]
    for at in range(BLOCK, values.shape[1], BLOCK):
        total = total + values[:, at:at + BLOCK]
    return total


def feed_forward_back_main(count, gain_row, leave, wire, ins, outs, scratch):
    grad_ref, resid, gains_ref, up, down_t, rows_ref, pre_ref = ins[:7]
    ins = ins[7:]
    grads, pre_grad, act, part, got = scratch[:5]
    scratch = list(scratch[5:])
    hidden = up.shape[1]
    full = up.shape[0]

    def take(size):
        taken, scratch[:size] = scratch[:size], []
        return taken

    if leave:
        up_width, down_pieces, reduce_sizes = leave
        limit_ref = ins[0]
        gain_parts, squares, table_part, tap_part, depth_part = ins[1:5], ins[5:9], *ins[9:12]
        gain_outs, table_out, rms_out, tap_out, depth_out = outs[:5], *outs[5:9]
        up_out, down_out, last_ref = outs[9:12]
        gain_grad_ref, up_grad_ref, down_grad_ref, new_grad_ref, pieces = take(5)
        width = pieces.shape[2]
        up_job = RowReduce(up_grad_ref, [(hidden, False)], [up_out], *take(reduce_sizes[0]), wire,
                           load=False)
        down_job = RowReduce(down_grad_ref, [(hidden, True)], [down_out], *take(reduce_sizes[1]), wire,
                             load=False)
        gain_pieces, square_parts, first_pieces = take(3)
        items = [
            SumItem(kind, source, *take(4), wire)
            for kind, source in (
                ("piece", gain_pieces), ("all", table_part), ("all", square_parts),
                ("own", tap_part), ("own", depth_part),
            )
        ]
        gain_item = SumItem("piece", first_pieces, *take(4), wire)
    else:
        gain_grad_ref, up_grad_ref, down_grad_ref, last_ref = outs
        new_grad_ref = last_ref
        items = []
        down_job = up_job = None
    gains = gains_ref[gain_row:gain_row + 1]
    wire.greet()
    wire.begin()
    cast_rows(wire, count, grad_ref, 0.5, grads)
    spread = Spread(wire, grads, count)
    spread.start()
    if leave:
        gain_pieces[...] = jnp.zeros_like(gain_pieces)
        square_parts[...] = jnp.zeros_like(square_parts)
        for place, ref in enumerate(gain_parts):
            row = jnp.sum(ref[...], axis=0, keepdims=True)
            for piece in range(wire.n):
                gain_pieces[piece, place:place + 1] = row[:, piece * width:(piece + 1) * width]
        for place, ref in enumerate(squares):
            for at in (0, 1):
                rows = ref[at * 8:(at + 1) * 8]
                square_parts[at * 4 + place:at * 4 + place + 1] = lane_sum(
                    jnp.sum(rows, axis=0, keepdims=True)
                )
        lane = lax.broadcasted_iota(jnp.int32, (1, BLOCK), 1)
        once = jnp.where(wire.me == 0, limit_ref[0], 0)
        square_parts[8:9] = jnp.where(lane == 0, once, 0).astype(F32)
        for item in items:
            item.begin()
    wire.loaded()
    collect = Collect(wire, part, got)
    def first_leg(chunk):
        rows = tile(chunk, count)
        left = grads[rows]

        def first(cols, index):
            act_grad = matmul(left, down_t[:, cols])
            pre = pre_ref[rows, cols].astype(F32)
            sig = jax.nn.sigmoid(pre)
            act[rows, cols] = (pre * sig).astype(BF16)
            pre_grad[rows, cols] = (act_grad * (sig + pre * sig * (1.0 - sig))).astype(BF16)

        block_loop(hidden, first)

    def second_leg(chunk, slot):
        target = part.at[wire.n - 1 if slot is None else slot]
        through = pre_grad[tile(chunk, count)]

        def second(cols, index):
            target[:, cols] = matmul_nt(through, up[cols]).astype(BF16)

        block_loop(full, second)
        if slot is not None:
            collect.send(slot)

    def weight_rows(left_ref, right_ref, out, rows):
        left = left_ref[:, rows]

        def piece(cols, index):
            out[rows, cols] = matmul_tn(left, right_ref[:, cols]).astype(BF16)

        block_loop(hidden, piece)

    def weight_grad(left_ref, right_ref, out, job=None):
        if job is None:
            block_loop(full, lambda rows, index: weight_rows(left_ref, right_ref, out, rows))
            return

        def layer(step, carry):
            weight_rows(left_ref, right_ref, out, tile(job.layer_of(step), 2 * job.count))
            job.begin_step(step)
            pl.when(step > 0)(lambda: job.early_step(step - 1))
            return carry

        lax.fori_loop(0, wire.layers, layer, 0)
        job.early_step(wire.layers - 1)

    late_leg = None
    for place, (chunk, slot) in enumerate(spread.arrivals()):
        if leave and place == wire.n - 1:
            late_leg = (chunk, slot)
        else:
            first_leg(chunk)
            second_leg(chunk, slot)
        if leave and place == wire.n - 2:
            rows = tile(wire.peers()[-1][0], count)

            def activate(cols, index):
                pre = pre_ref[rows, cols].astype(F32)
                act[rows, cols] = (pre * jax.nn.sigmoid(pre)).astype(BF16)

            block_loop(hidden, activate)
        if slot is None:
            wire.early()
            for item in items:
                item.early()
        elif slot == 0:
            for item in items:
                item.middle()
    wire.middle()
    weight_grad(grads, act, down_grad_ref, down_job)
    if leave:
        first_leg(late_leg[0])
        second_leg(*late_leg)
        weight_grad(rows_ref, pre_grad, up_grad_ref, up_job)
        collect.combine()
    else:
        collect.combine()
        weight_grad(rows_ref, pre_grad, up_grad_ref)
    wire.flush()
    collect.wait()
    residual_back(collect, grad_ref, resid, gains, new_grad_ref, gain_grad_ref)
    if leave:
        for piece in range(wire.n):
            first_pieces[piece] = gain_grad_ref[:, piece * width:(piece + 1) * width]
        gain_item.begin()
        late = send_pieces(wire, count, new_grad_ref, pieces, last_ref)
        gain_item.early()
        for item in items:
            item.end()
        gain_item.middle()
        totals = [item.out for item in items]
        for place, ref in enumerate(gain_outs[1:]):
            ref[...] = totals[0][place:place + 1]
        table = totals[1][...]
        for at in range(HEAD_DIM, table.shape[1], HEAD_DIM):
            table = table[:, 0:HEAD_DIM] + table[:, at:at + HEAD_DIM]
        table_out[...] = table[0:LEFT + RIGHT + 1]
        sums = jnp.sum(totals[2][...], axis=1, keepdims=True)
        rms_out[...] = jnp.broadcast_to(jnp.sqrt(sums[0:8] / (sums[8:9] * full)), rms_out.shape)
        tap_out[...] = totals[3][0:tap_out.shape[0]]
        depth_out[...] = jnp.sum(totals[4][...], axis=0, keepdims=True)
        for copy in late:
            copy.wait()
        wire.end()
        down_job.end()
        gain_item.end()
        gain_outs[0][...] = jnp.sum(gain_item.out[...], axis=0, keepdims=True)
        up_job.end()
    spread.finish()
    if not leave:
        wire.end()


def feed_forward_back(sizes, name, collective_id, gain_row, grad, resid, gains, up, down_t, rows, pre,
                      leave=None, taps=0, **side):
    n, m = sizes
    full, hidden = up.shape
    count = resid.shape[0]
    width = full // n
    ins = [(grad, vmem()), (resid, "load"), (gains, vmem())]
    ins += [(item, "load") for item in (up, down_t, rows, pre)]
    scratch = [
        pltpu.VMEM((n * count, full), BF16),
        pltpu.VMEM((n * count, hidden), BF16),
        pltpu.VMEM((n * count, hidden), BF16),
        pltpu.VMEM((n, count, full), BF16),
        pltpu.VMEM((n - 1, count, full), BF16),
    ]
    extra = None
    if leave:
        limit, gain_parts, squares, table_part, tap_part, depth_part = leave
        layers = m // 2
        ins.append((limit, smem()))
        ins += [(item, vmem()) for item in (*gain_parts, *squares, table_part, tap_part, depth_part)]
        outs = [((1, width), F32, vmem())] * 5
        outs += [
            ((LEFT + RIGHT + 1, HEAD_DIM), F32, vmem()),
            ((8, BLOCK), F32, vmem()),
            ((taps, width), F32, vmem()),
            ((1, width), F32, vmem()),
            ((full // m, hidden), F32, hbm()),
            ((hidden, full // m), F32, hbm()),
            ((n * count, width), BF16, hbm()),
        ]
        scratch += [
            pltpu.VMEM((8, full), F32),
            pltpu.VMEM((full, hidden), BF16),
            pltpu.VMEM((full, hidden), BF16),
            pltpu.VMEM((count, full), F32),
            pltpu.VMEM((n, count, width), BF16),
        ]
        reduces = [
            reduce_scratch(layers, full // m, hidden, [(hidden, flip)]) for flip in (False, True)
        ]
        scratch += reduces[0] + reduces[1]
        extra = (hidden, None, [len(made) for made in reduces])
        scratch += [
            pltpu.VMEM((n, 8, width), F32), pltpu.VMEM((16, BLOCK), F32), pltpu.VMEM((n, 8, width), F32)
        ]
        for shape in ((8, width), table_part.shape, (16, BLOCK), tap_part.shape, depth_part.shape,
                      (8, width)):
            scratch += sum_scratch(n, layers, shape)
        side = dict(side, more_slots=16 * m + 8 * n, row_on=True)
    else:
        outs = [
            ((8, full), F32, vmem()),
            ((full, hidden), BF16, "store"),
            ((full, hidden), BF16, "store"),
            ((count, full), F32, vmem()),
        ]
    return comm_call(
        name, collective_id, sizes,
        functools.partial(feed_forward_back_main, count, gain_row, extra),
        ins, outs, scratch, **side,
    )


def slot_rows(axis):
    slots = lax.broadcasted_iota(jnp.int32, (LEFT + RIGHT + 8, SPAN), axis)
    signed = jnp.where(slots < SPAN - BLOCK + 1, slots, slots - SPAN)
    return jnp.clip(signed - (BLOCK - LEFT), 0, LEFT + RIGHT)


def extend_table(table, copies):
    slots = jnp.arange(SPAN)
    signed = jnp.where(slots < SPAN - BLOCK + 1, slots, slots - SPAN)
    row_of = jnp.clip(signed - (BLOCK - LEFT), 0, LEFT + RIGHT)
    chosen = (row_of[:, None] == jnp.arange(LEFT + RIGHT + 1)[None, :]).astype(table.dtype)
    return jnp.tile(matmul(chosen, table).astype(table.dtype), (1, copies))


def fill_far(far_ref, table_ref, limit):
    blocks, length, _ = far_ref.shape
    lane = lax.broadcasted_iota(jnp.int32, (1, BLOCK), 1)

    def row(at, mark):
        ends = table_ref[at:at + 1].astype(F32)
        if ends.shape[1] < BLOCK:
            ends = jnp.concatenate([ends, jnp.zeros((1, BLOCK - ends.shape[1]), F32)], axis=1)
        return jnp.where(lane < HEAD_DIM, ends, jnp.where(lane == mark, 1.0, 0.0))

    first = row(0, HEAD_DIM + 1)
    last = row(SPAN - 2 * BLOCK, HEAD_DIM + 2)

    def block(step, carry):
        index, piece = step // (length // BLOCK), lax.rem(step, length // BLOCK)
        at = index * BLOCK
        column = lax.broadcasted_iota(jnp.int32, (BLOCK, 1), 0) + piece * BLOCK
        place = column + at - BLOCK
        key = jnp.where(place < 0, place + length, jnp.where(place >= length, place - length, place))
        near = (column < WINDOW) & (place >= 0) & (place < length)
        left = jnp.where(near | (key >= at), 0.0, 1.0)
        right = jnp.where(near | (key < at), 0.0, 1.0)
        bias = jnp.where(key < limit, 0.0, NEG_FILL)
        terms = left * first + right * last + jnp.where(lane == HEAD_DIM, bias, 0.0)
        far_ref[index, tile(piece, BLOCK)] = terms.astype(BF16)
        return carry

    lax.fori_loop(0, blocks * (length // BLOCK), block, 0)


def duplicate(qkv_ref, width, group, keys, values):
    length = qkv_ref.shape[0]
    for part in range(width // group):
        base = part * group
        for copy in range(2):
            place = slice(copy * length, (copy + 1) * length)
            keys[part, place] = qkv_ref[:, width + base:width + base + group]
            values[part, place] = qkv_ref[:, 2 * width + base:2 * width + base + group]


def by_head(values, group):
    if group == HEAD_DIM:
        return values
    lane = lax.broadcasted_iota(jnp.int32, (BLOCK, group), 1)
    zero = jnp.zeros_like(values)
    return jnp.concatenate(
        [
            jnp.where((lane >= at) & (lane < at + HEAD_DIM), values, zero)
            for at in range(0, group, HEAD_DIM)
        ],
        axis=0,
    )


def own_lanes(values, group):
    if group == HEAD_DIM:
        return values
    lane = lax.broadcasted_iota(jnp.int32, (BLOCK, group), 1)
    return jnp.where(lane < HEAD_DIM, values[0:BLOCK], values[BLOCK:2 * BLOCK])


def far_queries(values, group):
    wide = values.astype(F32)
    if group == HEAD_DIM:
        lane = lax.broadcasted_iota(jnp.int32, (BLOCK, BLOCK - HEAD_DIM), 1)
        return jnp.concatenate([wide, jnp.where(lane == 0, 1.0, 0.0)], axis=1).astype(BF16)
    lane = lax.broadcasted_iota(jnp.int32, (BLOCK, BLOCK), 1)
    rest = jnp.where(lane == HEAD_DIM, 1.0, 0.0)
    return jnp.concatenate(
        [
            jnp.where(lane < HEAD_DIM, wide, rest),
            jnp.where(lane < HEAD_DIM, pltpu.roll(wide, HEAD_DIM, 1), rest),
        ],
        axis=0,
    ).astype(BF16)


def near_mask(at, length):
    place = lax.broadcasted_iota(jnp.int32, (1, WINDOW), 1) + (at - BLOCK)
    return (place >= 0) & (place < length)


def near_terms(query, table, at, length):
    terms = matmul_nt(query, table)
    halves = [
        pltpu.roll(terms[start:start + BLOCK], 0, 1, stride=1, stride_axis=0)[:, :WINDOW]
        for start in range(0, query.shape[0], BLOCK)
    ]
    return jnp.where(near_mask(at, length), jnp.concatenate(halves, axis=0), 0.0)


def attend_blocks(first, blocks, width, group, qkv_ref, table_ref, far_ref, keys, values, context_ref,
                  log_ref, weights):
    length = qkv_ref.shape[0]
    heads = group // HEAD_DIM
    parts = width // group
    scale = 1.0 / math.sqrt(HEAD_DIM)

    def block(step, carry):
        index, part = first + step // parts, lax.rem(step, parts)
        at = pl.multiple_of(index * BLOCK, BLOCK)
        rows = pl.ds(at, BLOCK)
        cols = tile(part, group) if parts > 1 else slice(0, group)
        window = pl.ds(pl.multiple_of(lax.rem(at + length - BLOCK, length), BLOCK), length)
        query_rows = qkv_ref[rows, cols] * jnp.asarray(scale, BF16)
        query = by_head(query_rows, group)
        extra = far_queries(query_rows, group)
        if group == 2 * HEAD_DIM:
            scores = matmul_nt(
                jnp.concatenate([query, extra], axis=1),
                jnp.concatenate([keys[part, window], far_ref[index]], axis=1),
            )
        else:
            scores = matmul_nt(query, keys[part, window]) + matmul_nt(extra, far_ref[index])
        near = near_terms(query, table_ref[...], at, length)
        size = 32
        peaks, totals = [], []
        for start in range(0, heads * BLOCK, size):
            some = slice(start, start + size)
            first_part = scores[some, :WINDOW] + near[some]
            last_part = scores[some, WINDOW:]
            peak = jnp.maximum(
                jnp.max(first_part, axis=1, keepdims=True), jnp.max(last_part, axis=1, keepdims=True)
            )
            first_part = jnp.exp(first_part - peak)
            last_part = jnp.exp(last_part - peak)
            weights[some, :WINDOW] = first_part.astype(BF16)
            weights[some, WINDOW:] = last_part.astype(BF16)
            peaks.append(peak)
            totals.append(
                jnp.sum(first_part, axis=1, keepdims=True) + jnp.sum(last_part, axis=1, keepdims=True)
            )
        total = jnp.concatenate(totals, axis=0)
        mixed = matmul(weights[...], values[part, window]) * (1.0 / total)
        context_ref[rows, cols] = own_lanes(mixed, group).astype(BF16)
        log = jnp.concatenate(peaks, axis=0) + jnp.log(total)
        lane = lax.broadcasted_iota(jnp.int32, (BLOCK, BLOCK), 1)
        square = jnp.where(lane == 0, log[0:BLOCK], 0.0)
        for head in range(1, heads):
            square = jnp.where(lane == head, log[head * BLOCK:(head + 1) * BLOCK], square)
        log_ref[part, :, rows] = square.T[0:8]
        return carry

    lax.fori_loop(0, blocks * parts, block, 0)


def attend_back_core(width, group, qkv_ref, table_ref, far_ref, log_ref, grad_ref, out_ref,
                     table_grad_ref, keys, values, key_grad, value_grad, slot_grad, end_grad, probs,
                     prob_grads, back, blocks_in_turn):
    length = qkv_ref.shape[0]
    heads = group // HEAD_DIM
    parts = width // group
    scale = 1.0 / math.sqrt(HEAD_DIM)
    duplicate(qkv_ref, width, group, keys, values)
    slot_grad[...] = jnp.zeros_like(slot_grad)
    end_grad[...] = jnp.zeros_like(end_grad)
    key_grad[...] = jnp.zeros_like(key_grad)
    value_grad[...] = jnp.zeros_like(value_grad)
    down = lax.broadcasted_iota(jnp.int32, (BLOCK, BLOCK), 0)
    across = lax.broadcasted_iota(jnp.int32, (BLOCK, BLOCK), 1)
    reverse = jnp.where(down + across == BLOCK - 1, 1.0, 0.0).astype(BF16)

    def flip(values_in):
        return jnp.concatenate(
            [
                matmul(reverse, values_in[start:start + BLOCK])
                for start in range(0, heads * BLOCK, BLOCK)
            ],
            axis=0,
        )

    def block(index, part):
        at = pl.multiple_of(index * BLOCK, BLOCK)
        rows = pl.ds(at, BLOCK)
        cols = tile(part, group) if parts > 1 else slice(0, group)
        window = pl.ds(pl.multiple_of(lax.rem(at + length - BLOCK, length), BLOCK), length)
        key_rows = keys[part, window]
        far_rows = far_ref[index]
        query_rows = qkv_ref[rows, cols] * jnp.asarray(scale, BF16)
        query = by_head(query_rows, group)
        extra = far_queries(query_rows, group)
        grad = by_head(grad_ref[rows, cols], group)
        query_wide = [query, extra]
        if group == 2 * HEAD_DIM:
            query_wide = [jnp.concatenate(query_wide, axis=1)]
            key_wide = [jnp.concatenate([key_rows, far_rows], axis=1)]
        else:
            key_wide = [key_rows, far_rows]
        near = near_terms(query, table_ref[...], at, length)
        log = jnp.concatenate([log_ref[part, head:head + 1, rows] for head in range(heads)], axis=1)
        value_rows = values[part, window]
        row_dot = jnp.zeros((8, heads * BLOCK), F32)
        for start in range(0, length, BLOCK):
            some = slice(start, start + BLOCK)
            scores = sum(
                matmul_nt(left[some], right) for left, right in zip(key_wide, query_wide)
            )
            if start < WINDOW:
                scores = scores + near[:, some].T
            prob = jnp.exp(scores - log)
            prob_grad = matmul_nt(value_rows[some], grad)
            row_dot = row_dot + fold8(prob * prob_grad)
            probs[some] = prob
            prob_grads[some] = prob_grad
        row_dot = jnp.sum(row_dot, axis=0, keepdims=True)
        for start in range(0, length, BLOCK):
            some = slice(start, start + BLOCK)
            there = pl.ds(pl.multiple_of(window.start + start, BLOCK), BLOCK)
            prob = probs[some]
            score_grad = (prob * (prob_grads[some] - row_dot)).astype(BF16)
            value_grad[part, there] += matmul(prob.astype(BF16), grad)
            key_grad[part, there] += matmul(score_grad, query)
            back[:, some] = score_grad.T
        turned_back = back[...]
        if group == 2 * HEAD_DIM:
            both = matmul(turned_back, key_wide[0])
            direct, ends = both[:, :group], both[:, group:]
        else:
            direct, ends = matmul(turned_back, key_rows), matmul(turned_back, far_rows)
        left_sum, right_sum = ends[:, HEAD_DIM + 1:HEAD_DIM + 2], ends[:, HEAD_DIM + 2:HEAD_DIM + 3]
        query_full = query.astype(F32)
        end_grad[0:8] += fold8(left_sum * query_full)
        end_grad[8:16] += fold8(right_sum * query_full)
        near_grad = jnp.where(
            near_mask(at, length), turned_back[:, :WINDOW], jnp.asarray(0.0, BF16)
        )
        flipped = flip(near_grad)
        skewed = []
        for start in range(0, heads * BLOCK, BLOCK):
            padded = jnp.concatenate(
                [flipped[start:start + BLOCK], jnp.zeros((BLOCK, SPAN - WINDOW), F32)], axis=1
            )
            skewed.append(pltpu.roll(padded, SPAN - (BLOCK - 1), 1, stride=1, stride_axis=0))
        straight = jnp.concatenate(skewed, axis=0).astype(BF16)
        term = matmul(straight, table_ref[...])
        high = term.astype(BF16)
        low = (term - high.astype(F32)).astype(BF16)
        direct = direct + flip(high) + flip(low)
        result = own_lanes(direct, group)
        if heads == 1:
            result = result + ends[:, :HEAD_DIM]
        else:
            lane = lax.broadcasted_iota(jnp.int32, (BLOCK, BLOCK), 1)
            result = result + jnp.where(
                lane < HEAD_DIM, ends[0:BLOCK], pltpu.roll(ends[BLOCK:2 * BLOCK], HEAD_DIM, 1)
            )
        out_ref[rows, cols] = (result * scale).astype(BF16)
        slot_grad[...] += matmul_tn(flip(query).astype(BF16), straight)

    blocks_in_turn(block, parts)
    for part in range(parts):
        base = width + part * group
        out_ref[:, base:base + group] = (
            key_grad[part, 0:length] + key_grad[part, length:2 * length]
        ).astype(BF16)
        out_ref[:, width + base:width + base + group] = (
            value_grad[part, 0:length] + value_grad[part, length:2 * length]
        ).astype(BF16)
    chosen = jnp.where(
        slot_rows(1) == lax.broadcasted_iota(jnp.int32, (LEFT + RIGHT + 8, SPAN), 0), 1.0, 0.0
    )
    table_grad_ref[...] = lax.dot_general(
        chosen, slot_grad[...], (((1,), (1,)), ((), ())), precision=lax.Precision.HIGHEST,
        preferred_element_type=F32,
    )
    table_grad_ref[0:1] += jnp.sum(end_grad[0:8], axis=0, keepdims=True)
    table_grad_ref[LEFT + RIGHT:LEFT + RIGHT + 1] += jnp.sum(end_grad[8:16], axis=0, keepdims=True)


def attention_main(count, gain_row, wire, ins, outs, scratch):
    limit_ref, resid, gains_ref, weights, table_ref = ins
    after_ref, squares_ref, rows_ref, qkv_ref, context_ref, log_ref = outs
    far_ref, keys, values, weights_ref, part, got = scratch
    width = context_ref.shape[1]
    group = keys.shape[2]
    wire.greet()
    wire.begin()
    norm_rows(wire, count, resid, gains_ref[gain_row:gain_row + 1], rows_ref)
    spread = Spread(wire, rows_ref, count)
    spread.start()
    wire.loaded()
    collect = Collect(wire, part, got)
    spread.relay()
    wire.early()
    fill_far(far_ref, table_ref, limit_ref[0])
    chunks = []
    for chunk, slot in spread.arrivals(relay=False):
        chunks.append((chunk, slot))
        rows = tile(chunk, count)
        left = rows_ref[rows]

        def project(cols, index):
            qkv_ref[rows, cols] = matmul(left, weights[:, cols]).astype(BF16)

        block_loop(3 * width, project)
    duplicate(qkv_ref, width, group, keys, values)
    wire.side[0].middle()
    size = max(count, BLOCK)

    def share(chunk, target):
        attend_blocks(chunk * count // BLOCK, size // BLOCK, width, group, qkv_ref, table_ref, far_ref,
                      keys, values, context_ref, log_ref, weights_ref)
        left = context_ref[tile(chunk, count)]

        def leave(cols, index):
            target[:, cols] = matmul_nt(left, weights[cols, 3 * width:]).astype(BF16)

        block_loop(weights.shape[0], leave)

    def last():
        collect.combine()
        wire.side[1].middle()

    send_shares(wire, chunks, collect, share, last)
    wire.flush()
    collect.wait()
    residual(collect, 1.0, resid, limit_ref[0], after_ref, squares_ref)
    spread.finish()
    wire.end()


def attention(sizes, name, collective_id, gain_row, limit, resid, gains, weights, table, **side):
    n, m = sizes
    count, full = resid.shape
    length, width = n * count, weights.shape[1] // 4
    group = min(2 * HEAD_DIM, width)
    return comm_call(
        name, collective_id, sizes, functools.partial(attention_main, count, gain_row),
        [(limit, smem()), (resid, vmem()), (gains, vmem()), (weights, "load"), (table, "load")],
        [
            ((count, full), F32, vmem()),
            ((16, full), F32, vmem()),
            ((length, full), BF16, "store"),
            ((length, 3 * width), BF16, "store"),
            ((length, width), BF16, "store"),
            ((width // group, 8, length), F32, "store"),
        ],
        [
            pltpu.VMEM((length // BLOCK, length, BLOCK), BF16),
            pltpu.VMEM((width // group, 2 * length, group), BF16),
            pltpu.VMEM((width // group, 2 * length, group), BF16),
            pltpu.VMEM((group // HEAD_DIM * BLOCK, length), BF16),
            pltpu.VMEM((n, count, full), BF16),
            pltpu.VMEM((n - 1, count, full), BF16),
        ],
        cost=20 * 10**9, **side,
    )


def attention_back_main(count, gain_row, wire, ins, outs, scratch):
    (limit_ref, grad_ref, resid, gains_ref, weights, table_ref, rows_ref, qkv_ref, context_ref,
     log_ref, pieces) = ins
    gain_grad_ref, wide_ref, table_grad_ref, new_grad_ref, result_ref = outs
    (far_ref, grads, context_grad, qkv_grad, keys, values, key_grad, value_grad, slot_grad, end_grad,
     probs, prob_grads, back, part, got, came) = scratch
    width = context_ref.shape[1]
    group = keys.shape[2]
    wire.greet()
    wire.begin()
    cast_rows(wire, count, grad_ref, 1.0, grads)
    spread = Spread(wire, grads, count)
    spread.start()
    wire.loaded()
    collect = Collect(wire, part, got)
    fill_far(far_ref, table_ref, limit_ref[0])
    chunks = []
    per_chunk = max(count, BLOCK) // BLOCK

    mine = came.at[tile(wire.me, count)]
    output_copies = [
        wire.remote(pieces.at[lax.rem(wire.me + step, wire.n)], mine, "col",
                    lax.rem(wire.me + step, wire.n))
        for step in range(1, wire.n)
    ]
    output_copies.append(wire.local(pieces.at[wire.me], mine))

    def send_output():
        for copy in output_copies:
            copy.start()

    def down_gradient(chunk):
        rows = tile(chunk, count)
        context_grad[rows] = matmul(grads[rows], weights[:, 3 * width:]).astype(BF16)

    def in_turn(block, parts):
        if wire.n == 4:
            def turn(place, carry):
                pl.when(place == 1)(wire.early)
                for at in (1, 2, 3):
                    pl.when(place == at)(lambda at=at: spread.wait_place(at))
                pl.when(place == 3)(send_output)
                chunk = flipped(wire, place)
                down_gradient(chunk)

                def one(step, carry):
                    block(chunk * per_chunk + step // parts, lax.rem(step, parts))
                    final = per_chunk * parts - 1
                    for turn_of, after in ((0, min(1, final)), (1, final)):
                        pl.when((place == 0) & (step == after))(
                            lambda turn_of=turn_of: spread.relay_turn(turn_of)
                        )
                    return carry

                lax.fori_loop(0, per_chunk * parts, one, 0)
                return carry

            lax.fori_loop(0, 4, turn, 0)
            return
        wire.early()
        for chunk, slot in spread.arrivals():
            chunks.append((chunk, slot))
            down_gradient(chunk)
        send_output()

        def one(step, carry):
            block(step // parts, lax.rem(step, parts))
            return carry

        lax.fori_loop(0, wire.n * count // BLOCK * parts, one, 0)

    attend_back_core(width, group, qkv_ref, table_ref, far_ref, log_ref, context_grad, qkv_grad,
                     table_grad_ref, keys, values, key_grad, value_grad, slot_grad, end_grad, probs,
                     prob_grads, back, in_turn)
    wire.middle()

    def share(chunk, target):
        left = qkv_grad[tile(chunk, count)]

        def back(cols, index):
            target[:, cols] = matmul_nt(left, weights[cols, :3 * width]).astype(BF16)

        block_loop(weights.shape[0], back)

    send_shares(wire, chunks, collect, share)
    collect.combine()
    for copy in output_copies:
        copy.wait()
    result_ref[...] = came[...].T

    def weight_grads(rows, index):
        wide_ref[rows, :3 * width] = matmul_tn(rows_ref[:, rows], qkv_grad[...]).astype(BF16)
        wide_ref[rows, 3 * width:] = matmul_tn(grads[:, rows], context_ref[...]).astype(BF16)

    block_loop(weights.shape[0], weight_grads)
    wire.flush()
    wire.end()
    collect.wait()
    residual_back(collect, grad_ref, resid, gains_ref[gain_row:gain_row + 1], new_grad_ref,
                  gain_grad_ref)
    spread.finish()


def attention_back(sizes, name, collective_id, gain_row, limit, grad, resid, gains, weights, table, rows,
                   qkv, context, log_total, pieces, **side):
    n, m = sizes
    count, full = resid.shape
    length, width = context.shape
    group = min(2 * HEAD_DIM, width)
    return comm_call(
        name, collective_id, sizes, functools.partial(attention_back_main, count, gain_row),
        [(limit, smem()), (grad, vmem()), (resid, "load"), (gains, vmem())]
        + [(item, "load") for item in (weights, table, rows, qkv, context, log_total, pieces)],
        [
            ((8, full), F32, vmem()),
            ((full, 4 * width), BF16, "store"),
            ((LEFT + RIGHT + 8, group), F32, vmem()),
            ((count, full), F32, vmem()),
            ((width, length), BF16, "store"),
        ],
        [
            pltpu.VMEM((length // BLOCK, length, BLOCK), BF16),
            pltpu.VMEM((length, full), BF16),
            pltpu.VMEM((length, width), BF16),
            pltpu.VMEM((length, 3 * width), BF16),
            pltpu.VMEM((width // group, 2 * length, group), BF16),
            pltpu.VMEM((width // group, 2 * length, group), BF16),
            pltpu.VMEM((width // group, 2 * length, group), F32),
            pltpu.VMEM((width // group, 2 * length, group), F32),
            pltpu.VMEM((group, SPAN), F32),
            pltpu.VMEM((16, group), F32),
            pltpu.VMEM((length, group // HEAD_DIM * BLOCK), F32),
            pltpu.VMEM((length, group // HEAD_DIM * BLOCK), F32),
            pltpu.VMEM((group // HEAD_DIM * BLOCK, length), BF16),
            pltpu.VMEM((n, count, full), BF16),
            pltpu.VMEM((n - 1, count, full), BF16),
            pltpu.VMEM((length, width), BF16),
        ],
        cost=50 * 10**9, **side,
    )


PAD = 32
ROWS = 64


def shifted_sets(held, low, high, size):
    for residue in range(8):
        shifts = [shift for shift in range(low, high + 1) if shift % 8 == residue]
        if shifts:
            extent = shifts[-1] - residue + size
            moved = held[residue:residue + extent]
            for shift in shifts:
                yield shift, moved[shift - residue:shift - residue + size]


def stat_rows(blocks, first, second, stats_ref):
    lane = lax.broadcasted_iota(jnp.int32, (BLOCK, BLOCK), 1)
    both = jnp.where(lane == 0, first, jnp.where(lane == 1, second, 0.0))
    stats_ref[:, blocks] = both.T[0:8]


def stat_columns(stats):
    both = jnp.concatenate([stats, jnp.zeros((BLOCK - 8, stats.shape[1]), F32)], axis=0).T
    return both[:, 0:1], both[:, 1:2]


class Stats:
    def __init__(self, wire, mine, got):
        self.wire, self.mine, self.got = wire, mine, got
        self.copies = [
            wire.remote(mine, got.at[step - 1], "col", lax.rem(wire.me + step, wire.n))
            for step in range(1, wire.n)
        ]

    def total(self):
        for copy in self.copies:
            copy.start()
        for copy in self.copies:
            copy.wait()
        total = self.mine[...]
        for step in range(self.wire.n - 1):
            total = total + self.got[step]
        return total


def token_blocks(length, body):
    def step(index, carry):
        body(tile(index, BLOCK), index)
        return carry

    lax.fori_loop(0, length // BLOCK, step, 0)


def convolution_main(count, gain_row, taps, wire, ins, outs, scratch):
    limit_ref, resid, gains_ref, weights, taps_ref, depth_ref = ins
    after_ref, squares_ref, rows_ref, pre_ref, mixed_ref, stats_ref = outs
    kernel_ref, padded, stats_mine, stats_got, act, part, got = scratch
    length, width = mixed_ref.shape
    full = gains_ref.shape[1]
    wire.greet()
    wire.begin()
    norm_rows(wire, count, resid, gains_ref[gain_row:gain_row + 1], rows_ref)
    spread = Spread(wire, rows_ref, count)
    spread.start()
    wire.loaded()
    collect = Collect(wire, part, got)
    stats = Stats(wire, stats_mine, stats_got)
    padded[0:PAD] = jnp.zeros((PAD, width), F32)
    kernel_ref[0:taps] = taps_ref[...].astype(F32)
    spread.relay()
    wire.early()
    chunks = []
    for chunk, slot in spread.arrivals(relay=False):
        chunks.append((chunk, slot))
        rows = tile(chunk, count)
        left = rows_ref[rows]
        value_pre = matmul(left, weights[:, 0:width])
        gate_pre = matmul(left, weights[:, width:2 * width])
        pre_ref[rows, 0:width] = value_pre.astype(BF16)
        pre_ref[rows, width:2 * width] = gate_pre.astype(BF16)
        at = pl.multiple_of(chunk * count + PAD, PAD)
        keep = keep_rows(limit_ref[0], chunk * count, count)
        padded[pl.ds(at, count)] = value_pre * jax.nn.sigmoid(gate_pre) * keep

    def mix(index, carry):
        held = padded[pl.ds(pl.multiple_of(index * ROWS, ROWS), ROWS + PAD)]
        total = jnp.zeros((ROWS, width), F32)
        for shift, moved in shifted_sets(held, PAD - taps + 1, PAD, ROWS):
            tap = shift - (PAD - taps + 1)
            total = total + moved * kernel_ref[tap:tap + 1]
        mixed_ref[tile(index, ROWS)] = total
        return carry

    lax.fori_loop(0, length // ROWS, mix, 0)

    def sums(rows, index):
        mixed = mixed_ref[rows]
        stat_rows(rows, jnp.sum(mixed, axis=1, keepdims=True),
                  jnp.sum(mixed * mixed, axis=1, keepdims=True), stats_mine)

    token_blocks(length, sums)
    total = stats.total() * (1.0 / full)
    inverse = lax.rsqrt(total[1:2] - total[0:1] * total[0:1] + EPSILON)
    stats_ref[...] = jnp.concatenate([total[0:1], inverse, total[2:]], axis=0)

    def share(chunk, target):
        def activate(index, carry):
            rows = tile(chunk * count // BLOCK + index, BLOCK)
            mean, scale = stat_columns(stats_ref[:, rows])
            scaled = (mixed_ref[rows] - mean) * scale * depth_ref[...]
            act[tile(index, BLOCK)] = (scaled * jax.nn.sigmoid(scaled)).astype(BF16)
            return carry

        lax.fori_loop(0, -(-count // BLOCK), activate, 0)
        if count % BLOCK:
            at = lax.rem(chunk * count, BLOCK)
            left = act[pl.ds(pl.multiple_of(at, count), count)]
        else:
            left = act[...]

        def leave(cols, index):
            target[:, cols] = matmul_nt(left, weights[cols, 2 * width:]).astype(BF16)

        block_loop(weights.shape[0], leave)

    send_shares(wire, chunks, collect, share, collect.combine)
    wire.middle()
    wire.flush()
    collect.wait()
    residual(collect, 1.0, resid, limit_ref[0], after_ref, squares_ref)
    spread.finish()
    wire.end()


def convolution(sizes, name, collective_id, gain_row, limit, resid, gains, weights, kernel, depth_gain,
                **side):
    n, m = sizes
    count, full = resid.shape
    length, width = n * count, weights.shape[1] // 3
    return comm_call(
        name, collective_id, sizes,
        functools.partial(convolution_main, count, gain_row, kernel.shape[0]),
        [(limit, smem()), (resid, vmem()), (gains, vmem()), (weights, "load"), (kernel, vmem()),
         (depth_gain, vmem())],
        [
            ((count, full), F32, vmem()),
            ((16, full), F32, vmem()),
            ((length, full), BF16, "store"),
            ((length, 2 * width), BF16, "store"),
            ((length, width), F32, "store"),
            ((8, length), F32, "store"),
        ],
        [
            pltpu.VMEM((PAD, width), F32),
            pltpu.VMEM((length + PAD, width), F32),
            pltpu.VMEM((8, length), F32),
            pltpu.VMEM((n - 1, 8, length), F32),
            pltpu.VMEM((max(count, BLOCK), width), BF16),
            pltpu.VMEM((n, count, full), BF16),
            pltpu.VMEM((n - 1, count, full), BF16),
        ],
        cost=15 * 10**9, **side,
    )


def convolution_back_main(count, gain_row, taps, wire, ins, outs, scratch):
    (limit_ref, grad_ref, resid, gains_ref, weights, taps_ref, depth_ref, rows_ref, pre_ref, mixed_ref,
     stats_ref) = ins
    gain_grad_ref, wide_ref, kernel_grad_ref, depth_grad_ref, new_grad_ref = outs
    (kernel_ref, grads, padded, padded_grad, stats_mine, stats_got, sums_ref, act, pre_grad, part, got) = scratch
    length, width = mixed_ref.shape
    full = gains_ref.shape[1]
    wire.greet()
    wire.begin()
    cast_rows(wire, count, grad_ref, 1.0, grads)
    spread = Spread(wire, grads, count)
    spread.start()
    wire.loaded()
    collect = Collect(wire, part, got)
    stats = Stats(wire, stats_mine, stats_got)
    padded[0:PAD] = jnp.zeros((PAD, width), F32)
    padded_grad[length:] = jnp.zeros((PAD, width), F32)
    sums_ref[...] = jnp.zeros_like(sums_ref)
    depth_grad_ref[...] = jnp.zeros_like(depth_grad_ref)
    kernel_ref[0:taps] = taps_ref[...].astype(F32)
    kernel_grad_ref[...] = jnp.zeros_like(kernel_grad_ref)
    spread.relay()

    def regate(rows, index):
        value_pre = pre_ref[rows, 0:width].astype(F32)
        gate_pre = pre_ref[rows, width:2 * width].astype(F32)
        at = pl.multiple_of(index * BLOCK + PAD, PAD)
        keep = keep_rows(limit_ref[0], index * BLOCK, BLOCK)
        padded[pl.ds(at, BLOCK)] = value_pre * jax.nn.sigmoid(gate_pre) * keep

    token_blocks(length, regate)
    wire.early()
    def first(rows, index):
        mean, scale = stat_columns(stats_ref[:, rows])
        normed = (mixed_ref[rows] - mean) * scale
        scaled = normed * depth_ref[...]
        sig = jax.nn.sigmoid(scaled)
        act[rows] = (scaled * sig).astype(BF16)
        scaled_grad = padded_grad[rows] * (sig + scaled * sig * (1.0 - sig))
        depth_grad_ref[...] += fold8(scaled_grad * normed)
        weighted = scaled_grad * depth_ref[...]
        padded_grad[rows] = weighted
        stat_rows(rows, jnp.sum(weighted, axis=1, keepdims=True),
                  jnp.sum(weighted * normed, axis=1, keepdims=True), stats_mine)

    chunks = []
    for chunk, slot in spread.arrivals(relay=False):
        chunks.append((chunk, slot))
        rows = tile(chunk, count)
        padded_grad[rows] = matmul(grads[rows], weights[:, 2 * width:])
        if count % BLOCK == 0:
            def some(index, carry):
                first(tile(chunk * (count // BLOCK) + index, BLOCK), index)
                return carry

            lax.fori_loop(0, count // BLOCK, some, 0)
    wire.middle()
    if count % BLOCK:
        token_blocks(length, first)
    total = stats.total() * (1.0 / full)
    stats_mine[...] = total

    def second(rows, index):
        mean, scale = stat_columns(stats_ref[:, rows])
        normed = (mixed_ref[rows] - mean) * scale
        one, two = stat_columns(stats_mine[:, rows])
        padded_grad[rows] = scale * (padded_grad[rows] - one - normed * two)

    token_blocks(length, second)

    def share(chunk, target):
        def unmix(index, carry):
            start = chunk * count + index * ROWS
            rows = pl.ds(pl.multiple_of(start, ROWS), ROWS)
            ahead = padded_grad[pl.ds(pl.multiple_of(start, ROWS), ROWS + PAD)]
            total = jnp.zeros((ROWS, width), F32)
            for shift, moved in shifted_sets(ahead, 0, taps - 1, ROWS):
                tap = taps - 1 - shift
                total = total + moved * kernel_ref[tap:tap + 1]
            gate = jax.nn.sigmoid(pre_ref[rows, width:2 * width].astype(F32))
            through = total * keep_rows(limit_ref[0], start, ROWS) * gate
            pre_grad[rows, 0:width] = through.astype(BF16)
            pre_grad[rows, width:2 * width] = (
                through * pre_ref[rows, 0:width].astype(F32) * (1.0 - gate)
            ).astype(BF16)
            return carry

        lax.fori_loop(0, count // ROWS, unmix, 0)
        left = pre_grad[tile(chunk, count)]

        def back(cols, index):
            target[:, cols] = matmul_nt(left, weights[cols, :2 * width]).astype(BF16)

        block_loop(weights.shape[0], back)

    send_shares(wire, chunks, collect, share)
    collect.combine()

    def tap_grads(index, carry):
        here = padded_grad[tile(index, ROWS)]
        around = pl.ds(pl.multiple_of(index * ROWS, ROWS), ROWS + PAD)
        for shift, moved in shifted_sets(padded[around], PAD - taps + 1, PAD, ROWS):
            tap = shift - (PAD - taps + 1)
            sums_ref[tap * 8:(tap + 1) * 8] += fold8(here * moved)
        return carry

    lax.fori_loop(0, length // ROWS, tap_grads, 0)
    for tap in range(taps):
        kernel_grad_ref[tap:tap + 1] = jnp.sum(sums_ref[tap * 8:(tap + 1) * 8], axis=0, keepdims=True)

    def weight_grads(rows, index):
        wide_ref[rows, :2 * width] = matmul_tn(rows_ref[:, rows], pre_grad[...]).astype(BF16)
        wide_ref[rows, 2 * width:] = matmul_tn(grads[:, rows], act[...]).astype(BF16)

    block_loop(weights.shape[0], weight_grads)
    wire.flush()
    wire.end()
    collect.wait()
    residual_back(collect, grad_ref, resid, gains_ref[gain_row:gain_row + 1], new_grad_ref,
                  gain_grad_ref)
    spread.finish()


def convolution_back(sizes, name, collective_id, gain_row, limit, grad, resid, gains, weights, kernel,
                     depth_gain, rows, pre, mixed, stats, **side):
    n, m = sizes
    count, full = resid.shape
    length, width = mixed.shape
    taps = kernel.shape[0]
    return comm_call(
        name, collective_id, sizes,
        functools.partial(convolution_back_main, count, gain_row, taps),
        [(limit, smem()), (grad, vmem()), (resid, "load"), (gains, vmem()), (weights, "load"),
         (kernel, vmem()), (depth_gain, vmem())]
        + [(item, "load") for item in (rows, pre, mixed, stats)],
        [
            ((8, full), F32, vmem()),
            ((full, 3 * width), BF16, "store"),
            ((PAD, width), F32, vmem()),
            ((8, width), F32, vmem()),
            ((count, full), F32, vmem()),
        ],
        [
            pltpu.VMEM((PAD, width), F32),
            pltpu.VMEM((length, full), BF16),
            pltpu.VMEM((length + PAD, width), F32),
            pltpu.VMEM((length + PAD, width), F32),
            pltpu.VMEM((8, length), F32),
            pltpu.VMEM((n - 1, 8, length), F32),
            pltpu.VMEM((8 * taps, width), F32),
            pltpu.VMEM((length, width), BF16),
            pltpu.VMEM((length, 2 * width), BF16),
            pltpu.VMEM((n, count, full), BF16),
            pltpu.VMEM((n - 1, count, full), BF16),
        ],
        cost=20 * 10**9, **side,
    )


def results_kernel(*refs):
    sources, targets = refs[:len(refs) // 2], refs[len(refs) // 2:]
    for source, target in zip(sources, targets):
        if target.shape[0] == 1 and source.shape[0] == 8:
            target[...] = source[...].T[0:1]
        elif source.shape != target.shape:
            target[...] = source[...].astype(target.dtype).T
        else:
            target[...] = source[...]


def results(arrays, shapes):
    return pl.pallas_call(
        results_kernel,
        name="results",
        out_shape=tuple(shapes),
        in_specs=[vmem()] * len(arrays),
        out_specs=tuple(vmem() for _ in arrays),
        compiler_params=pltpu.CompilerParams(vmem_limit_bytes=VMEM_LIMIT),
    )(*arrays)


def body(
    layer_input,
    clip_lengths,
    first_gain,
    first_up,
    first_down,
    attend_gain,
    query_weight,
    key_weight,
    value_weight,
    output_weight,
    distance_table,
    conv_gain,
    pointwise_value,
    pointwise_gate,
    depthwise_kernel,
    depthwise_gain,
    pointwise_out,
    second_gain,
    second_up,
    second_down,
    final_gain,
    output_cotangent,
):
    n = lax.axis_size("col")
    me = lax.axis_index("col")
    width, length = layer_input.shape
    full = n * width
    count = length // n

    sizes = (n, lax.axis_size("row"))
    group = min(2 * HEAD_DIM, width)
    table_wide = extend_table(distance_table, group // HEAD_DIM)
    limit = clip_lengths
    tap_count = depthwise_kernel.shape[0]
    gain_parts = [
        gain[None] for gain in (first_gain, attend_gain, conv_gain, second_gain, final_gain)
    ]
    attend_pieces = [
        (query_weight, False), (key_weight, False), (value_weight, False), (output_weight, True)
    ]
    conv_pieces = [(pointwise_value, False), (pointwise_gate, False), (pointwise_out, True)]
    hidden = first_up.shape[1]
    tokens_in = (layer_input, output_cotangent)
    if count % BLOCK:
        tokens_in = (layer_input.T, output_cotangent.T)

    (start, cot, gains, up_first, down_first, attend_weights, after_first, squares_first, rows_first,
     pre_first) = feed_forward(
        sizes, "first", 1, 0, first_up, first_down, limit,
        enter=(*tokens_in, gain_parts, attend_pieces),
    )
    (after_attend, squares_attend, rows_attend, qkv, context, log_total, conv_weights,
     up_second) = attention(
        sizes, "attend", 2, 1, limit, after_first, gains, attend_weights, table_wide,
        gathers=[conv_pieces, [(second_up, False)]],
    )
    depth_row = depthwise_gain[None]
    (after_conv, squares_conv, rows_conv, conv_pre, mixed, stats, down_second) = convolution(
        sizes, "convolve", 3, 2, limit, after_attend, gains, conv_weights, depthwise_kernel, depth_row,
        gathers=[[(second_down, True)]],
    )
    (grad_second, final_part, out_tokens, squares_second, rows_second, pre_second) = feed_forward(
        sizes, "second", 4, 3, up_second, down_second, limit, resid=after_conv, gains=gains, turn=cot
    )

    second_part, second_up_wide, second_down_wide, grad_conv = feed_forward_back(
        sizes, "second_back", 5, 3, grad_second, after_conv, gains, up_second, down_second,
        rows_second, pre_second,
    )
    conv_part, conv_wide, kernel_part, depth_part, grad_attend, second_up_grad = convolution_back(
        sizes, "convolve_back", 6, 2, limit, grad_conv, after_attend, gains, conv_weights,
        depthwise_kernel, depth_row, rows_conv, conv_pre, mixed, stats,
        reduces=[(second_up_wide, [(hidden, False)])],
    )
    (attend_part, attend_wide, table_part, grad_first, layer_output, second_down_grad, value_grad, gate_grad,
     out_grad) = attention_back(
        sizes, "attend_back", 7, 1, limit, grad_attend, after_first, gains, attend_weights,
        table_wide, rows_attend, qkv, context, log_total, out_tokens,
        reduces=[
            (second_down_wide, [(hidden, True)]),
            (conv_wide, [(width, False), (width, False), (width, True)]),
        ],
    )
    (first_sum, attend_sum, conv_sum, second_sum, final_sum, table_sum, masked_rms, kernel_sum,
     depth_sum, first_up_grad, first_down_grad, grad_tokens, query_grad, key_grad, attend_value_grad,
     output_grad) = feed_forward_back(
        sizes, "first_back", 0, 0, grad_first, start, gains, up_first, down_first, rows_first,
        pre_first, taps=tap_count,
        leave=(
            limit, (attend_part, conv_part, second_part, final_part),
            (squares_first, squares_attend, squares_conv, squares_second), table_part, kernel_part,
            depth_part,
        ),
        reduces=[(attend_wide, [(width, False), (width, False), (width, False), (width, True)])],
    )

    arrays = [
        layer_output, grad_tokens, first_sum, first_up_grad, first_down_grad, attend_sum, query_grad,
        key_grad, attend_value_grad, output_grad, table_sum, conv_sum, value_grad, gate_grad, kernel_sum,
        depth_sum, out_grad, second_sum, second_up_grad, second_down_grad, final_sum, masked_rms,
    ]
    shapes = [jax.ShapeDtypeStruct(array.shape, array.dtype) for array in arrays]
    shapes[1] = jax.ShapeDtypeStruct(grad_tokens.shape[::-1], F32)
    shapes[-1] = jax.ShapeDtypeStruct((1, 8), F32)
    arrays = results(arrays, shapes)
    return tuple(array[0] if array.shape[0] == 1 else array for array in arrays)


def solution(mesh):
    in_specs = (
        P("col", "row"),
        P("row"),
        P("col"),
        P("row", "col"),
        P("col", "row"),
        P("col"),
        P("row", "col"),
        P("row", "col"),
        P("row", "col"),
        P("col", "row"),
        P(),
        P("col"),
        P("row", "col"),
        P("row", "col"),
        P(None, "col"),
        P("col"),
        P("col", "row"),
        P("col"),
        P("row", "col"),
        P("col", "row"),
        P("col"),
        P("col", "row"),
    )
    out_specs = (
        P("col", "row"),
        P("col", "row"),
        P("col"),
        P("row", "col"),
        P("col", "row"),
        P("col"),
        P("row", "col"),
        P("row", "col"),
        P("row", "col"),
        P("col", "row"),
        P(),
        P("col"),
        P("row", "col"),
        P("row", "col"),
        P(None, "col"),
        P("col"),
        P("col", "row"),
        P("col"),
        P("row", "col"),
        P("col", "row"),
        P("col"),
        P(),
    )
    return jax.shard_map(body, mesh=mesh, in_specs=in_specs, out_specs=out_specs, check_vma=False)
```

```python
import functools
import math

import jax
import jax.numpy as jnp
from jax import lax
from jax.experimental import pallas as pl
from jax.experimental.pallas import tpu as pltpu
from jax.sharding import PartitionSpec as P

HEAD_DIM = 64
LEFT = 64
RIGHT = 8
EPSILON = 1e-05
NEG_FILL = -1e30
BF16 = jnp.bfloat16
F32 = jnp.float32
MESH = pl.DeviceIdType.MESH
BLOCK = 128
WINDOW = 384
SPAN = 512
VMEM_LIMIT = 60 * 1024 * 1024
MARGIN = 6 * 1024 * 1024


def matmul(left, right):
    return jnp.dot(left, right, preferred_element_type=F32)


def matmul_nt(left, right):
    return lax.dot_general(left, right, (((1,), (1,)), ((), ())), preferred_element_type=F32)


def matmul_tn(left, right):
    return lax.dot_general(left, right, (((0,), (0,)), ((), ())), preferred_element_type=F32)


def vmem():
    return pl.BlockSpec(memory_space=pltpu.VMEM)


def smem():
    return pl.BlockSpec(memory_space=pltpu.SMEM)


def hbm():
    return pl.BlockSpec(memory_space=pltpu.HBM)


def padded_bytes(shape, dtype):
    size = jnp.dtype(dtype).itemsize
    rows = 8 * 4 // size
    shape = (1,) * (2 - len(shape)) + tuple(shape)
    held = -(-shape[-1] // 128) * 128 * -(-shape[-2] // rows) * rows
    return math.prod(shape[:-2]) * held * size


def comm_params(collective_id, held):
    return pltpu.CompilerParams(
        collective_id=collective_id, has_side_effects=True,
        vmem_limit_bytes=max(VMEM_LIMIT, held + MARGIN),
    )


def tile(index, size):
    return pl.ds(pl.multiple_of(index * size, size), size)


class Wire:
    def __init__(self, sizes, send_sem, recv_sem, local_sem, side, col_on=True, row_on=False):
        self.n, self.m = sizes
        self.me = lax.axis_index("col")
        self.row = lax.axis_index("row")
        self.send_sem, self.recv_sem, self.local_sem = send_sem, recv_sem, local_sem
        self.used = 0
        self.used_local = 0
        self.core = lax.rem(self.row, 2)
        self.layer = self.row // 2
        self.partner = self.row + 1 - 2 * self.core
        self.layers = self.m // 2
        self.col_on = col_on
        self.loads, self.stores, self.stored = [], [], []
        self.row_on = row_on or bool(side)
        self.side = [job(self) for job in side]

    def layer_peer(self, step):
        return lax.rem(self.layer + step, self.layers) * 2 + self.core

    def greet(self):
        barrier = pltpu.get_barrier_semaphore()
        waits = 0
        if self.col_on:
            for step in range(1, self.n):
                pl.semaphore_signal(
                    barrier, inc=1, device_id={"col": lax.rem(self.me + step, self.n)},
                    device_id_type=MESH,
                )
            waits += self.n - 1
        if self.row_on:
            for step in range(1, self.layers):
                pl.semaphore_signal(
                    barrier, inc=1, device_id={"row": self.layer_peer(step)}, device_id_type=MESH
                )
            pl.semaphore_signal(
                barrier, inc=1, device_id={"row": self.partner}, device_id_type=MESH
            )
            waits += self.layers
        pl.semaphore_wait(barrier, waits)

    def remote(self, source, target, axis, peer):
        slot = self.used
        self.used += 1
        return pltpu.make_async_remote_copy(
            src_ref=source, dst_ref=target, send_sem=self.send_sem.at[slot],
            recv_sem=self.recv_sem.at[slot], device_id={axis: peer}, device_id_type=MESH,
        )

    def local(self, source, target):
        slot = self.used_local
        self.used_local += 1
        return pltpu.make_async_copy(source, target, self.local_sem.at[slot])

    def to_all(self, source_of, target):
        copies = [
            self.remote(source_of(lax.rem(self.me + step, self.n)), target, "col",
                        lax.rem(self.me + step, self.n))
            for step in range(1, self.n)
        ]
        for copy in copies:
            copy.start()
        return copies

    def loaded(self):
        for copy in self.loads:
            copy.wait()

    def store(self, copies):
        for copy in copies:
            copy.start()
        self.stored += copies

    def flush(self):
        self.store(self.stores)

    def settle(self):
        for copy in self.stored:
            copy.wait()

    def begin(self):
        for job in self.side:
            job.begin()

    def early(self):
        for job in self.side:
            job.early()

    def middle(self):
        for job in self.side:
            job.middle()

    def end(self):
        for job in self.side:
            job.end()

    def peers(self):
        if self.n == 4:
            across = self.me + 1 - 2 * lax.rem(self.me, 2)
            along = lax.rem(self.me + 2, 4)
            return [(across, 0), (along, 1), (3 - self.me, 2)]
        return [
            (lax.rem(self.me + self.n - step, self.n), self.n - step - 1)
            for step in range(1, self.n)
        ]


class Spread:
    def __init__(self, wire, ref, count):
        self.wire, self.ref, self.count = wire, ref, count
        me = wire.me
        if wire.n != 4:
            self.copies = [
                wire.remote(self.part(me), self.part(me), "col", lax.rem(me + step, wire.n))
                for step in range(1, wire.n)
            ]
            return
        (across, _), (along, _), (far, _) = wire.peers()
        self.across = [wire.remote(self.part(me, q), self.part(me, q), "col", across) for q in range(4)]
        self.along = [wire.remote(self.part(me, q), self.part(me, q), "col", along) for q in range(4)]
        self.onward = [
            wire.remote(self.part(across, q), self.part(across, q), "col", along) for q in (0, 1)
        ] + [wire.remote(self.part(along, q), self.part(along, q), "col", across) for q in (2, 3)]

    def part(self, chunk, quarter=None):
        if quarter is None:
            return self.ref.at[tile(chunk, self.count)]
        size = self.count // 4
        return self.ref.at[tile(chunk * 4 + quarter, size)]

    def start(self):
        if self.wire.n != 4:
            for copy in self.copies:
                copy.start()
            return
        for first, second in ((0, 2), (1, 3), (2, 0), (3, 1)):
            self.across[first].start()
            self.along[second].start()

    def relay(self):
        if self.wire.n != 4:
            return
        for turn in range(2):
            self.relay_turn(turn)

    def relay_turn(self, turn):
        self.across[turn].wait_recv()
        self.onward[turn].start()
        self.along[2 + turn].wait_recv()
        self.onward[2 + turn].start()

    def wait_place(self, place):
        for copy in (self.across[2:], self.along[:2], self.onward)[place - 1]:
            copy.wait_recv()

    def arrivals(self, relay=True):
        wire = self.wire
        yield wire.me, None
        if wire.n != 4:
            for step, (peer, slot) in zip(range(1, wire.n), wire.peers()):
                self.copies[step - 1].wait_recv()
                yield peer, slot
            return
        if relay:
            self.relay()
        for place, (peer, slot) in enumerate(wire.peers()):
            self.wait_place(place + 1)
            yield peer, slot

    def finish(self):
        copies = self.copies if self.wire.n != 4 else self.across + self.along + self.onward
        for copy in copies:
            copy.wait_send()


class Collect:
    def __init__(self, wire, part, got):
        self.wire, self.part, self.got = wire, part, got
        self.relayed = wire.n == 4
        self.count = part.shape[1]
        if not self.relayed:
            self.copies = {
                slot: wire.remote(part.at[slot], got.at[slot], "col", owner)
                for owner, slot in wire.peers()
            }
            return
        (across, _), (along, _), _ = wire.peers()
        half = self.count // 2
        first, second = pl.ds(0, half), pl.ds(half, half)
        places = [got.at[place // 2, (first, second)[place % 2]] for place in range(6)]
        self.far = [
            wire.remote(part.at[2, first], places[0], "col", across),
            wire.remote(part.at[2, second], places[1], "col", along),
        ]
        self.direct = {
            0: wire.remote(part.at[0, first], places[2], "col", across),
            1: wire.remote(part.at[1, second], places[4], "col", along),
        }
        self.onward = [
            wire.remote(part.at[0, second], places[3], "col", across),
            wire.remote(part.at[1, first], places[5], "col", along),
        ]

    def send(self, slot):
        if not self.relayed:
            self.copies[slot].start()
        elif slot == 2:
            for copy in self.far:
                copy.start()
        else:
            self.direct[slot].start()

    def combine(self):
        if not self.relayed:
            return
        half = self.count // 2
        for copy, slot, at, onward in (
            (self.far[1], 0, half, self.onward[0]), (self.far[0], 1, 0, self.onward[1])
        ):
            copy.wait_recv()
            place = 1 - slot

            def add(rows, index):
                mine = pl.ds(pl.multiple_of(at + index * 32, 32), 32)
                came = pl.ds(pl.multiple_of((half if place else 0) + index * 32, 32), 32)
                self.part[slot, mine] = (
                    self.part[slot, mine].astype(F32) + self.got[0, came].astype(F32)
                ).astype(BF16)

            row_loop(half, add)
            onward.start()

    def wait(self):
        if not self.relayed:
            for copy in self.copies.values():
                copy.wait()
            return
        for copy in self.far:
            copy.wait_send()
        for copy in list(self.direct.values()) + self.onward:
            copy.wait()

    def sum_loop(self, body):
        part, got, last = self.part, self.got, self.wire.n - 1
        if not self.relayed:
            def step(rows, index):
                total = part[last, rows].astype(F32)
                for slot in range(last):
                    total = total + got[slot, rows].astype(F32)
                body(rows, total)

            row_loop(self.count, step)
            return
        half = self.count // 2
        for at, sources in ((0, ((1, 0), (2, half))), (half, ((1, half), (2, 0)))):
            def step(rows, index, at=at, sources=sources):
                mine = pl.ds(pl.multiple_of(at + index * 32, 32), 32)
                total = part[last, mine].astype(F32)
                for slot, start in sources:
                    total = total + got[
                        slot, pl.ds(pl.multiple_of(start + index * 32, 32), 32)
                    ].astype(F32)
                body(mine, total)

            row_loop(half, step)


class RowChain:
    def __init__(self, shard, full, wire):
        self.wire, self.shard, self.full = wire, shard, full
        self.count = shard.shape[0]
        self.steps = wire.layers - 1
        self.base = wire.used
        wire.used += 4 * self.steps
        mine = full.at[tile(wire.row, self.count)]
        self.own = [wire.local(shard, mine), wire.remote(shard, mine, "row", wire.partner)]

    def block(self, layer):
        return self.full.at[tile(layer * 2 + self.wire.core, self.count)]

    def copy(self, kind, step, layer, peer):
        slot = self.base + kind * self.steps + step
        wire = self.wire
        source = self.shard if kind < 2 and step == 0 else self.block(layer)
        return pltpu.make_async_remote_copy(
            src_ref=source, dst_ref=self.block(layer), send_sem=wire.send_sem.at[slot],
            recv_sem=wire.recv_sem.at[slot], device_id={"row": peer}, device_id_type=MESH,
        )

    def up(self, step):
        wire = self.wire
        return self.copy(0, step, wire.layer - step, wire.row + 2)

    def down(self, step):
        wire = self.wire
        return self.copy(1, step, wire.layer + step, wire.row - 2)

    def begin(self):
        wire = self.wire
        pl.when(wire.layer + 1 < wire.layers)(lambda: self.up(0).start())
        pl.when(wire.layer > 0)(lambda: self.down(0).start())
        for copy in self.own:
            copy.start()

    def advance(self, step):
        wire = self.wire

        @pl.when(wire.layer - 1 - step >= 0)
        def _():
            self.copy(0, step, wire.layer - 1 - step, wire.row).wait_recv()
            if step + 1 < self.steps:
                pl.when(wire.layer + 1 < wire.layers)(lambda: self.up(step + 1).start())
            self.copy(2, step, wire.layer - 1 - step, wire.partner).start()

        @pl.when(wire.layer + 1 + step < wire.layers)
        def _():
            self.copy(1, step, wire.layer + 1 + step, wire.row).wait_recv()
            if step + 1 < self.steps:
                pl.when(wire.layer > 0)(lambda: self.down(step + 1).start())
            self.copy(3, step, wire.layer + 1 + step, wire.partner).start()

    def end(self):
        wire = self.wire
        for step in range(self.steps):
            pl.when((wire.layer + 1 < wire.layers) & (wire.layer - step >= 0))(
                lambda step=step: self.up(step).wait_send()
            )
            pl.when((wire.layer > 0) & (wire.layer + step < wire.layers))(
                lambda step=step: self.down(step).wait_send()
            )
            pl.when(wire.layer - 1 - step >= 0)(
                lambda step=step: self.copy(2, step, wire.layer - 1 - step, wire.partner).wait()
            )
            pl.when(wire.layer + 1 + step < wire.layers)(
                lambda step=step: self.copy(3, step, wire.layer + 1 + step, wire.partner).wait()
            )
        for copy in self.own:
            copy.wait()


class RowGather:
    def __init__(self, shard, full, wire):
        self.wire = wire
        count = shard.shape[0]
        mine = full.at[tile(wire.row, count)]
        self.first = [wire.local(shard, mine), wire.remote(shard, mine, "row", wire.partner)]
        self.along = [
            wire.remote(shard, mine, "row", wire.layer_peer(step))
            for step in range(1, wire.layers)
        ]
        self.onward = []
        for step in range(1, wire.layers):
            block = full.at[tile(wire.layer_peer(wire.layers - step), count)]
            self.onward.append(wire.remote(block, block, "row", wire.partner))

    def begin(self):
        for copy in self.along + self.first:
            copy.start()

    def early(self):
        pass

    def middle(self):
        for copy, onward in zip(self.along, self.onward):
            copy.wait_recv()
            onward.start()

    def end(self):
        for copy in self.along:
            copy.wait_send()
        for copy in self.first:
            copy.wait()
        for copy in self.onward:
            copy.wait()


class RowReduce:
    def __init__(self, grads, pieces, outs, held, pair, got, total, *rest, load=True):
        *parts, wire = rest
        self.wire, self.out, self.grads = wire, total, grads
        self.pieces = pieces
        self.parts = parts or [total]
        self.keep = [wire.local(part, out) for part, out in zip(self.parts, outs)]
        self.held, self.pair, self.got = held, pair, got
        self.count = held.shape[1]
        self.load = []
        if load:
            self.load = [
                wire.local(grads.at[tile(layer * 2 + wire.core, self.count)], held.at[layer])
                for layer in range(wire.layers)
            ]
        self.base = wire.used
        wire.used += 2 * wire.layers

    def layer_of(self, step):
        return lax.rem(self.wire.layer + 1 + step, self.wire.layers)

    def between(self, source, target, slot, peer):
        wire = self.wire
        return pltpu.make_async_remote_copy(
            src_ref=source, dst_ref=target, send_sem=wire.send_sem.at[self.base + slot],
            recv_sem=wire.recv_sem.at[self.base + slot], device_id={"row": peer}, device_id_type=MESH,
        )

    def swap(self, step):
        layer = self.layer_of(step)
        block = layer * 2 + 1 - self.wire.core
        return self.between(self.grads.at[tile(block, self.count)], self.pair.at[layer], step,
                            self.wire.partner)

    def along(self, step):
        layer = self.layer_of(step)
        return self.between(self.held.at[layer], self.got.at[step], self.wire.layers + step,
                            layer * 2 + self.wire.core)

    def begin_step(self, step):
        self.swap(step).start()

    def early_step(self, step):
        self.swap(step).wait()
        layer = self.layer_of(step)
        size = min(32, self.count)

        def add(rows, index):
            if self.load:
                mine = self.held[layer, rows]
            else:
                at = (layer * 2 + self.wire.core) * self.count + index * size
                mine = self.grads[pl.ds(pl.multiple_of(at, size), size)]
            self.held[layer, rows] = (
                mine.astype(F32) + self.pair[layer, rows].astype(F32)
            ).astype(BF16)

        row_loop(self.count, add)
        pl.when(step < self.wire.layers - 1)(lambda: self.along(step).start())

    def begin(self):
        for step in range(self.wire.layers):
            self.begin_step(step)
        for copy in self.load:
            copy.start()

    def early(self):
        for copy in self.load:
            copy.wait()

        def one(step, carry):
            self.early_step(step)
            return carry

        lax.fori_loop(0, self.wire.layers, one, 0)

    def middle(self):
        pass

    def end(self):
        for step in range(self.wire.layers - 1):
            self.along(step).wait()

        def add(rows, index):
            total = self.held[self.wire.layer, rows].astype(F32)
            for step in range(self.wire.layers - 1):
                total = total + self.got[step, rows].astype(F32)
            self.out[rows] = total

        row_loop(self.count, add)
        if len(self.parts) > 1 or self.pieces[0][1]:
            at = 0
            for part, (width, flip) in zip(self.parts, self.pieces):
                piece = self.out[:, at:at + width]
                part[...] = piece.T if flip else piece
                at += width
        self.wire.store(self.keep)


def piece_shapes(count, pieces):
    return [(width, count) if flip else (count, width) for width, flip in pieces]


def reduce_scratch(layers, count, width, pieces):
    apart = len(pieces) > 1 or pieces[0][1]
    parts = [pltpu.VMEM(shape, F32) for shape in piece_shapes(count, pieces)] if apart else []
    return parts_last(layers, count, width) + parts


def parts_last(layers, count, width):
    return [
        pltpu.VMEM((layers, count, width), BF16),
        pltpu.VMEM((layers, count, width), BF16),
        pltpu.VMEM((max(1, layers - 1), count, width), BF16),
        pltpu.VMEM((count, width), F32),
    ]


class SumItem:
    def __init__(self, kind, source, out, got, packed, got_row, wire):
        self.wire, self.kind, self.source, self.out = wire, kind, source, out
        self.got, self.packed, self.got_row = got, packed, got_row
        self.col = []
        if kind != "own":
            for step in range(1, wire.n):
                peer = lax.rem(wire.me + step, wire.n)
                piece = source.at[peer] if kind == "piece" else source
                self.col.append(wire.remote(piece, got.at[step - 1], "col", peer))
        self.swap = wire.remote(packed.at[0], got_row.at[0], "row", wire.partner)
        self.along = [
            wire.remote(packed.at[1], got_row.at[step], "row", wire.layer_peer(step))
            for step in range(1, wire.layers)
        ]

    def begin(self):
        for copy in self.col:
            copy.start()

    def early(self):
        for copy in self.col:
            copy.wait()
        total = self.source[self.wire.me] if self.kind == "piece" else self.source[...]
        if self.kind != "own":
            for step in range(self.wire.n - 1):
                total = total + self.got[step]
        self.packed[0] = total
        self.swap.start()

    def middle(self):
        self.swap.wait()
        self.packed[1] = self.packed[0] + self.got_row[0]
        for copy in self.along:
            copy.start()

    def end(self):
        for copy in self.along:
            copy.wait()
        total = self.packed[1]
        for step in range(1, self.wire.layers):
            total = total + self.got_row[step]
        self.out[...] = total


def sum_scratch(n, layers, shape):
    return [
        pltpu.VMEM(shape, F32),
        pltpu.VMEM((n - 1,) + shape, F32),
        pltpu.VMEM((2,) + shape, F32),
        pltpu.VMEM((layers,) + shape, F32),
    ]


def join(pieces, target):
    at = 0
    for ref, flip in pieces:
        width = ref.shape[0] if flip else ref.shape[1]
        target[:, at:at + width] = ref[...].T if flip else ref[...]
        at += width


def joined_shape(pieces):
    rows = {array.shape[1] if flip else array.shape[0] for array, flip in pieces}
    return rows.pop(), sum(array.shape[0] if flip else array.shape[1] for array, flip in pieces)


def row_loop(count, body):
    size = min(32, count)

    def step(index, carry):
        body(tile(index, size), index)
        return carry

    lax.fori_loop(0, count // size, step, 0)


def block_loop(extent, body):
    size = min(256, extent)

    def step(index, carry):
        body(tile(index, size), index)
        return carry

    lax.fori_loop(0, extent // size, step, 0)


def fold8(values):
    return jnp.sum(values.reshape(values.shape[0] // 8, 8, values.shape[1]), axis=0)


def normalize(values):
    average = jnp.mean(values, axis=1, keepdims=True)
    centered = values - average
    inverse = lax.rsqrt(jnp.mean(centered * centered, axis=1, keepdims=True) + EPSILON)
    return centered * inverse, inverse


def norm_back(grad_in, normed, inverse, gains):
    scaled = grad_in * gains
    first = jnp.mean(scaled, axis=1, keepdims=True)
    second = jnp.mean(scaled * normed, axis=1, keepdims=True)
    return inverse * (scaled - first - normed * second)


def comm_call(name, collective_id, sizes, main, ins, outs, scratch, gathers=(), reduces=(), cost=10**9,
              col_on=True, more_slots=0, row_on=False):
    n, m = sizes
    layers = m // 2
    gather_pieces = [piece for pieces in gathers for piece in pieces]
    in_arrays = [item[0] for item in ins] + [array for array, _ in gather_pieces]
    in_arrays += [grads for grads, _ in reduces]
    in_specs = [hbm() if item[1] == "load" else item[1] for item in ins]
    in_specs += [vmem()] * len(gather_pieces) + [hbm()] * len(reduces)
    out_shapes = [jax.ShapeDtypeStruct(item[0], item[1]) for item in outs]
    out_specs = [hbm() if item[2] == "store" else item[2] for item in outs]
    copied = [pltpu.VMEM(item[0].shape, item[0].dtype) for item in ins if item[1] == "load"]
    copied += [pltpu.VMEM(item[0], item[1]) for item in outs if item[2] == "store"]
    side_scratch = []
    for pieces in gathers:
        rows, width = joined_shape(pieces)
        out_shapes.append(jax.ShapeDtypeStruct((m * rows, width), BF16))
        out_specs.append(hbm())
        side_scratch.append(pltpu.VMEM((rows, width), BF16))
    reduce_counts = []
    for grads, pieces in reduces:
        count, width = grads.shape[0] // m, grads.shape[1]
        for shape in piece_shapes(count, pieces):
            out_shapes.append(jax.ShapeDtypeStruct(shape, F32))
            out_specs.append(hbm())
        made = reduce_scratch(layers, count, width, pieces)
        reduce_counts.append(len(made))
        side_scratch += made
    every_scratch = copied + list(scratch) + side_scratch
    held = sum(padded_bytes(item.shape, item.dtype) for item in every_scratch)
    remote_slots = 8 * n + 16 + len(gathers) * 2 * layers + len(reduces) * 2 * layers + more_slots
    local_slots = 12 + len(copied) + len(gathers) + len(reduces) * (layers + 4) + more_slots

    def kernel(*refs):
        at = 0

        def take(count):
            nonlocal at
            at += count
            return refs[at - count:at]

        main_ins = list(take(len(ins)))
        gather_ins = [
            [(ref, flip) for ref, (_, flip) in zip(take(len(pieces)), pieces)] for pieces in gathers
        ]
        reduce_ins = take(len(reduces))
        main_outs = list(take(len(outs)))
        gather_outs = take(len(gathers))
        reduce_outs = [take(len(pieces)) for _, pieces in reduces]
        loads, stores = [], []
        for place, item in enumerate(ins):
            if item[1] == "load":
                (held_ref,) = take(1)
                loads.append((main_ins[place], held_ref))
                main_ins[place] = held_ref
        for place, item in enumerate(outs):
            if item[2] == "store":
                (held_ref,) = take(1)
                stores.append((held_ref, main_outs[place]))
                main_outs[place] = held_ref
        main_scratch = take(len(scratch))
        side = []
        for pieces, full in zip(gather_ins, gather_outs):
            (shard,) = take(1)
            join(pieces, shard)
            side.append(functools.partial(RowGather, shard, full))
        for grads, out, (_, pieces), size in zip(reduce_ins, reduce_outs, reduces, reduce_counts):
            side.append(functools.partial(RowReduce, grads, pieces, out, *take(size)))
        send_sem, recv_sem, local_sem = take(3)
        wire = Wire(sizes, send_sem, recv_sem, local_sem, side, col_on, row_on)
        wire.loads = [wire.local(*pair) for pair in loads]
        wire.stores = [wire.local(*pair) for pair in stores]
        for copy in wire.loads:
            copy.start()
        main(wire, main_ins, main_outs, main_scratch)
        wire.settle()

    return pl.pallas_call(
        kernel,
        name=name,
        out_shape=tuple(out_shapes),
        in_specs=in_specs,
        out_specs=tuple(out_specs),
        scratch_shapes=every_scratch + [
            pltpu.SemaphoreType.DMA((remote_slots,)),
            pltpu.SemaphoreType.DMA((remote_slots,)),
            pltpu.SemaphoreType.DMA((local_slots,)),
        ],
        compiler_params=comm_params(collective_id, held),
        cost_estimate=pl.CostEstimate(flops=cost, bytes_accessed=10**8, transcendentals=0),
    )(*in_arrays)


def norm_rows(wire, count, source, gains, rows_ref):
    base = wire.me * count

    def work(rows, index):
        normed, _ = normalize(source[rows])
        size = min(32, count)
        rows_ref[pl.ds(pl.multiple_of(base + index * size, size), size)] = (normed * gains).astype(BF16)

    row_loop(count, work)


def cast_rows(wire, count, source, factor, rows_ref):
    base = wire.me * count

    def work(rows, index):
        size = min(32, count)
        rows_ref[pl.ds(pl.multiple_of(base + index * size, size), size)] = (
            factor * source[rows]
        ).astype(BF16)

    row_loop(count, work)


def keep_rows(limit, start, rows):
    place = lax.broadcasted_iota(jnp.int32, (rows, 1), 0) + start
    return jnp.where(place < limit, 1.0, 0.0)


def residual(collect, factor, resid, limit, after_ref, squares_ref):
    squares_ref[...] = jnp.zeros_like(squares_ref)
    base = collect.wire.me * collect.count

    def work(rows, branch):
        after = resid[rows] + factor * branch
        after_ref[rows] = after
        keep = keep_rows(limit, base + rows.start, branch.shape[0])
        squares_ref[0:8] += fold8(branch * branch * keep)
        squares_ref[8:16] += fold8(after * after * keep)

    collect.sum_loop(work)


def residual_back(collect, grad_ref, resid, gains, new_grad_ref, gain_grad_ref):
    gain_grad_ref[...] = jnp.zeros_like(gain_grad_ref)

    def work(rows, rows_grad):
        normed, inverse = normalize(resid[rows])
        new_grad_ref[rows] = grad_ref[rows] + norm_back(rows_grad, normed, inverse, gains)
        gain_grad_ref[...] += fold8(rows_grad * normed)

    collect.sum_loop(work)


def split_pieces(wire, count, source, pieces):
    width = pieces.shape[2]

    def split(rows, index):
        result = source[rows].astype(BF16)
        for part in range(wire.n):
            pieces[part, rows] = result[:, part * width:(part + 1) * width]

    row_loop(count, split)


def send_pieces(wire, count, source, pieces, out_ref):
    split_pieces(wire, count, source, pieces)
    mine = out_ref.at[tile(wire.me, count)]
    copies = wire.to_all(lambda peer: pieces.at[peer], mine)
    here = wire.local(pieces.at[wire.me], mine)
    here.start()
    return copies + [here]


def flipped(wire, place):
    flip_across, flip_along = lax.rem(place, 2), place // 2
    across_bit, along_bit = lax.rem(wire.me, 2), wire.me // 2
    return (
        across_bit + flip_across - 2 * across_bit * flip_across
        + 2 * (along_bit + flip_along - 2 * along_bit * flip_along)
    )


def send_shares(wire, chunks, collect, share, last=None):
    part = collect.part
    if wire.n == 4:
        def turn(step, carry):
            left = 3 - step
            share(flipped(wire, left), part.at[lax.rem(left + 3, 4)])
            for place in range(3):
                pl.when(step == place)(lambda place=place: collect.send(2 - place))
            if last is not None:
                pl.when(step == 2)(last)
            return carry

        lax.fori_loop(0, 4, turn, 0)
    else:
        for chunk, slot in reversed(chunks):
            share(chunk, part.at[wire.n - 1 if slot is None else slot])
            if slot is not None:
                collect.send(slot)
        if last is not None:
            last()


def feed_forward_first(count, chunk, rows_ref, up, pre_ref, act):
    rows = tile(chunk, count)
    left = rows_ref[rows]

    def first(cols, index):
        pre = matmul(left, up[:, cols])
        pre_ref[rows, cols] = pre.astype(BF16)
        act[:, cols] = (pre * jax.nn.sigmoid(pre)).astype(BF16)

    block_loop(up.shape[1], first)


def feed_forward_second(act, down_t, target):
    hidden = act[...]

    def second(cols, index):
        target[:, cols] = matmul_nt(hidden, down_t[cols]).astype(BF16)

    block_loop(down_t.shape[0], second)


def feed_forward_main(count, gain_row, factor, enter, turn, wire, ins, outs, scratch):
    ins, outs, scratch = list(ins), list(outs), list(scratch)
    if enter:
        limit_ref, tokens_ref, cot_in = ins[:3]
        gain_ins = ins[3:8]
        up_shard, down_ref = ins[8:10]
        next_pieces = [(ref, flip) for ref, flip in zip(ins[10:], enter)]
        ins = []
        resid, cot_out, gains_ref, up, down_t, next_full = outs[:6]
        outs = outs[6:]
        arrived, arrived_cot, arrived_gain, gain_in, down_shard, next_shard = scratch[:6]
        scratch = scratch[6:]
    else:
        limit_ref, resid, gains_ref = ins[:3]
        ins = ins[3:]
    if enter:
        for place, ref in enumerate(gain_ins):
            gain_in[place:place + 1] = ref[...]
        gain_in[len(gain_ins):] = jnp.zeros((8 - len(gain_ins), gain_in.shape[1]), F32)
        join([(down_ref, True)], down_shard)
        join(next_pieces, next_shard)
    else:
        up, down_t = ins[:2]
        ins = ins[2:]
    if turn:
        (cot_ref,) = ins
        grad_ref, gain_grad_ref, out_ref = outs[:3]
        outs = outs[3:]
        pieces, after_ref = scratch[:2]
        scratch = scratch[2:]
    else:
        after_ref = outs.pop(0)
    squares_ref, rows_ref, pre_ref = outs
    act, part, got = scratch
    wire.greet()
    wire.begin()
    if enter:
        up_job = RowChain(up_shard, up, wire)
        down_job = RowChain(down_shard, down_t, wire)
        next_job = RowChain(next_shard, next_full, wire)
        up_job.begin()
        width = arrived_gain.shape[2]
        turned = tokens_ref.shape[0] == width

        def share(ref, peer):
            return ref.at[:, tile(peer, count)] if turned else ref.at[tile(peer, count)]

        def settle(came, target):
            for piece in range(wire.n):
                cols = slice(piece * width, (piece + 1) * width)
                if turned:
                    target[:, cols] = came[piece].astype(F32).T
                else:
                    target[:, cols] = came[piece].astype(F32)

        mine = [
            wire.local(share(tokens_ref, wire.me), arrived.at[wire.me]),
            wire.local(gain_in, arrived_gain.at[wire.me]),
            wire.local(share(cot_in, wire.me), arrived_cot.at[wire.me]),
        ]
        copies = wire.to_all(lambda peer: share(tokens_ref, peer), arrived.at[wire.me])
        copies += wire.to_all(lambda peer: gain_in, arrived_gain.at[wire.me])
        for copy in mine:
            copy.start()
        for copy in mine + copies:
            copy.wait()
        for piece in range(wire.n):
            gains_ref[:, piece * width:(piece + 1) * width] = arrived_gain[piece]

        settle(arrived, resid)
    gains = gains_ref[gain_row:gain_row + 1]
    norm_rows(wire, count, resid, gains, rows_ref)
    spread = Spread(wire, rows_ref, count)
    spread.start()
    wire.loaded()
    collect = Collect(wire, part, got)
    wire.early()
    if enter:
        up_job.advance(0)
        spread.relay()
        cot_copies = wire.to_all(lambda peer: share(cot_in, peer), arrived_cot.at[wire.me])
        for step in range(1, up_job.steps):
            up_job.advance(step)
        down_job.begin()
        up_job.end()
        chunks = []
        for chunk, slot in spread.arrivals(relay=False):
            chunks.append((chunk, slot))
            feed_forward_first(count, chunk, rows_ref, up, pre_ref, act.at[len(chunks) - 1])
            if len(chunks) - 1 < down_job.steps:
                down_job.advance(len(chunks) - 1)
        for copy in cot_copies:
            copy.wait()

        settle(arrived_cot, cot_out)
        next_job.begin()
        down_job.end()
        for place, (chunk, slot) in reversed(list(enumerate(chunks))):
            target = part.at[wire.n - 1 if slot is None else slot]
            feed_forward_second(act.at[place], down_t, target)
            if slot is not None:
                collect.send(slot)
            if len(chunks) - 1 - place == 2:
                next_job.advance(0)
        next_job.advance(1)
        collect.combine()
        for step in range(2, next_job.steps):
            next_job.advance(step)
    else:
        for chunk, slot in spread.arrivals():
            target = part.at[wire.n - 1 if slot is None else slot]
            feed_forward_first(count, chunk, rows_ref, up, pre_ref, act.at[0])
            feed_forward_second(act.at[0], down_t, target)
            if slot is not None:
                collect.send(slot)
        collect.combine()
    wire.middle()
    wire.flush()
    collect.wait()
    residual(collect, factor, resid, limit_ref[0], after_ref, squares_ref)
    if turn:
        final_gains = gains_ref[gain_row + 1:gain_row + 2]
        gain_grad_ref[...] = jnp.zeros_like(gain_grad_ref)

        def final(rows, index):
            normed, inverse = normalize(after_ref[rows])
            cot = cot_ref[rows]
            grad_ref[rows] = norm_back(cot, normed, inverse, final_gains)
            gain_grad_ref[...] += fold8(cot * normed)
            after_ref[rows] = normed * final_gains

        row_loop(count, final)
        split_pieces(wire, count, after_ref, pieces)
        wire.store([wire.local(pieces, out_ref)])
    spread.finish()
    if enter:
        next_job.end()
    wire.end()


def feed_forward(sizes, name, collective_id, gain_row, up, down_t, limit, resid=None, gains=None,
                 enter=None, turn=None, **side):
    n, m = sizes
    hidden = up.shape[1]
    full = up.shape[0] * (m if enter else 1)
    next_pieces = None
    if enter:
        tokens, cotangent, gain_parts, next_pieces = enter
        turned = tokens.shape[0] * n == full
        width, length = tokens.shape if turned else tokens.shape[::-1]
        count = length // n
        came = (n, width, count) if turned else (n, count, width)
        ins = [(limit, smem()), (tokens, vmem()), (cotangent, vmem())]
        ins += [(part, vmem()) for part in gain_parts] + [(up, vmem()), (down_t, vmem())]
        ins += [(array, vmem()) for array, _ in next_pieces]
        down_shape, next_shape = (full // m, hidden), joined_shape(next_pieces)
        outs = [((count, full), F32, "store"), ((count, full), F32, "store"), ((8, full), F32, vmem())]
        scratch = [
            pltpu.VMEM(came, BF16),
            pltpu.VMEM(came, BF16),
            pltpu.VMEM((n, 8, width), F32),
            pltpu.VMEM((8, width), F32),
            pltpu.VMEM(down_shape, BF16),
            pltpu.VMEM(next_shape, BF16),
        ]
        for shape, spec in ((down_shape, "store"), (down_shape, "store"), (next_shape, hbm())):
            outs.append(((m * shape[0], shape[1]), BF16, spec))
        side = dict(side, more_slots=6 * m, row_on=True)
    else:
        count = resid.shape[0]
        ins = [(limit, smem()), (resid, vmem()), (gains, vmem())]
        outs, scratch = [], []
        ins += [(up, "load"), (down_t, "load")]
    if turn is not None:
        ins.append((turn, "load"))
        outs += [
            ((count, full), F32, vmem()),
            ((8, full), F32, vmem()),
            ((n, count, full // n), BF16, hbm()),
        ]
        scratch.append(pltpu.VMEM((n, count, full // n), BF16))
    if turn is None:
        outs.append(((count, full), F32, vmem()))
    else:
        scratch.append(pltpu.VMEM((count, full), F32))
    outs += [
        ((16, full), F32, vmem()),
        ((n * count, full), BF16, "store"),
        ((n * count, hidden), BF16, "store"),
    ]
    scratch += [
        pltpu.VMEM((n if enter else 1, count, hidden), BF16),
        pltpu.VMEM((n, count, full), BF16),
        pltpu.VMEM((n - 1, count, full), BF16),
    ]
    return comm_call(
        name, collective_id, sizes,
        functools.partial(
            feed_forward_main, count, gain_row, 0.5, enter and [flip for _, flip in next_pieces],
            turn is not None,
        ),
        ins, outs, scratch, **side,
    )


def lane_sum(values):
    total = values[:, 0:BLOCK]
    for at in range(BLOCK, values.shape[1], BLOCK):
        total = total + values[:, at:at + BLOCK]
    return total


def feed_forward_back_main(count, gain_row, leave, wire, ins, outs, scratch):
    grad_ref, resid, gains_ref, up, down_t, rows_ref, pre_ref = ins[:7]
    ins = ins[7:]
    grads, pre_grad, act, part, got = scratch[:5]
    scratch = list(scratch[5:])
    hidden = up.shape[1]
    full = up.shape[0]

    def take(size):
        taken, scratch[:size] = scratch[:size], []
        return taken

    if leave:
        up_width, down_pieces, reduce_sizes = leave
        limit_ref = ins[0]
        gain_parts, squares, table_part, tap_part, depth_part = ins[1:5], ins[5:9], *ins[9:12]
        gain_outs, table_out, rms_out, tap_out, depth_out = outs[:5], *outs[5:9]
        up_out, down_out, last_ref = outs[9:12]
        gain_grad_ref, up_grad_ref, down_grad_ref, new_grad_ref, pieces = take(5)
        width = pieces.shape[2]
        up_job = RowReduce(up_grad_ref, [(hidden, False)], [up_out], *take(reduce_sizes[0]), wire,
                           load=False)
        down_job = RowReduce(down_grad_ref, [(hidden, True)], [down_out], *take(reduce_sizes[1]), wire,
                             load=False)
        gain_pieces, square_parts, first_pieces = take(3)
        items = [
            SumItem(kind, source, *take(4), wire)
            for kind, source in (
                ("piece", gain_pieces), ("all", table_part), ("all", square_parts),
                ("own", tap_part), ("own", depth_part),
            )
        ]
        gain_item = SumItem("piece", first_pieces, *take(4), wire)
    else:
        gain_grad_ref, up_grad_ref, down_grad_ref, last_ref = outs
        new_grad_ref = last_ref
        items = []
        down_job = up_job = None
    gains = gains_ref[gain_row:gain_row + 1]
    wire.greet()
    wire.begin()
    cast_rows(wire, count, grad_ref, 0.5, grads)
    spread = Spread(wire, grads, count)
    spread.start()
    if leave:
        gain_pieces[...] = jnp.zeros_like(gain_pieces)
        square_parts[...] = jnp.zeros_like(square_parts)
        for place, ref in enumerate(gain_parts):
            row = jnp.sum(ref[...], axis=0, keepdims=True)
            for piece in range(wire.n):
                gain_pieces[piece, place:place + 1] = row[:, piece * width:(piece + 1) * width]
        for place, ref in enumerate(squares):
            for at in (0, 1):
                rows = ref[at * 8:(at + 1) * 8]
                square_parts[at * 4 + place:at * 4 + place + 1] = lane_sum(
                    jnp.sum(rows, axis=0, keepdims=True)
                )
        lane = lax.broadcasted_iota(jnp.int32, (1, BLOCK), 1)
        once = jnp.where(wire.me == 0, limit_ref[0], 0)
        square_parts[8:9] = jnp.where(lane == 0, once, 0).astype(F32)
        for item in items:
            item.begin()
    wire.loaded()
    collect = Collect(wire, part, got)
    def first_leg(chunk):
        rows = tile(chunk, count)
        left = grads[rows]

        def first(cols, index):
            act_grad = matmul(left, down_t[:, cols])
            pre = pre_ref[rows, cols].astype(F32)
            sig = jax.nn.sigmoid(pre)
            act[rows, cols] = (pre * sig).astype(BF16)
            pre_grad[rows, cols] = (act_grad * (sig + pre * sig * (1.0 - sig))).astype(BF16)

        block_loop(hidden, first)

    def second_leg(chunk, slot):
        target = part.at[wire.n - 1 if slot is None else slot]
        through = pre_grad[tile(chunk, count)]

        def second(cols, index):
            target[:, cols] = matmul_nt(through, up[cols]).astype(BF16)

        block_loop(full, second)
        if slot is not None:
            collect.send(slot)

    def weight_rows(left_ref, right_ref, out, rows):
        left = left_ref[:, rows]

        def piece(cols, index):
            out[rows, cols] = matmul_tn(left, right_ref[:, cols]).astype(BF16)

        block_loop(hidden, piece)

    def weight_grad(left_ref, right_ref, out, job=None):
        if job is None:
            block_loop(full, lambda rows, index: weight_rows(left_ref, right_ref, out, rows))
            return

        def layer(step, carry):
            weight_rows(left_ref, right_ref, out, tile(job.layer_of(step), 2 * job.count))
            job.begin_step(step)
            pl.when(step > 0)(lambda: job.early_step(step - 1))
            return carry

        lax.fori_loop(0, wire.layers, layer, 0)
        job.early_step(wire.layers - 1)

    late_leg = None
    for place, (chunk, slot) in enumerate(spread.arrivals()):
        if leave and place == wire.n - 1:
            late_leg = (chunk, slot)
        else:
            first_leg(chunk)
            second_leg(chunk, slot)
        if leave and place == wire.n - 2:
            rows = tile(wire.peers()[-1][0], count)

            def activate(cols, index):
                pre = pre_ref[rows, cols].astype(F32)
                act[rows, cols] = (pre * jax.nn.sigmoid(pre)).astype(BF16)

            block_loop(hidden, activate)
        if slot is None:
            wire.early()
            for item in items:
                item.early()
        elif slot == 0:
            for item in items:
                item.middle()
    wire.middle()
    weight_grad(grads, act, down_grad_ref, down_job)
    if leave:
        first_leg(late_leg[0])
        second_leg(*late_leg)
        weight_grad(rows_ref, pre_grad, up_grad_ref, up_job)
        collect.combine()
    else:
        collect.combine()
        weight_grad(rows_ref, pre_grad, up_grad_ref)
    wire.flush()
    collect.wait()
    residual_back(collect, grad_ref, resid, gains, new_grad_ref, gain_grad_ref)
    if leave:
        for piece in range(wire.n):
            first_pieces[piece] = gain_grad_ref[:, piece * width:(piece + 1) * width]
        gain_item.begin()
        late = send_pieces(wire, count, new_grad_ref, pieces, last_ref)
        gain_item.early()
        for item in items:
            item.end()
        gain_item.middle()
        totals = [item.out for item in items]
        for place, ref in enumerate(gain_outs[1:]):
            ref[...] = totals[0][place:place + 1]
        table = totals[1][...]
        for at in range(HEAD_DIM, table.shape[1], HEAD_DIM):
            table = table[:, 0:HEAD_DIM] + table[:, at:at + HEAD_DIM]
        table_out[...] = table[0:LEFT + RIGHT + 1]
        sums = jnp.sum(totals[2][...], axis=1, keepdims=True)
        rms_out[...] = jnp.broadcast_to(jnp.sqrt(sums[0:8] / (sums[8:9] * full)), rms_out.shape)
        tap_out[...] = totals[3][0:tap_out.shape[0]]
        depth_out[...] = jnp.sum(totals[4][...], axis=0, keepdims=True)
        for copy in late:
            copy.wait()
        wire.end()
        down_job.end()
        gain_item.end()
        gain_outs[0][...] = jnp.sum(gain_item.out[...], axis=0, keepdims=True)
        up_job.end()
    spread.finish()
    if not leave:
        wire.end()


def feed_forward_back(sizes, name, collective_id, gain_row, grad, resid, gains, up, down_t, rows, pre,
                      leave=None, taps=0, **side):
    n, m = sizes
    full, hidden = up.shape
    count = resid.shape[0]
    width = full // n
    ins = [(grad, vmem()), (resid, "load"), (gains, vmem())]
    ins += [(item, "load") for item in (up, down_t, rows, pre)]
    scratch = [
        pltpu.VMEM((n * count, full), BF16),
        pltpu.VMEM((n * count, hidden), BF16),
        pltpu.VMEM((n * count, hidden), BF16),
        pltpu.VMEM((n, count, full), BF16),
        pltpu.VMEM((n - 1, count, full), BF16),
    ]
    extra = None
    if leave:
        limit, gain_parts, squares, table_part, tap_part, depth_part = leave
        layers = m // 2
        ins.append((limit, smem()))
        ins += [(item, vmem()) for item in (*gain_parts, *squares, table_part, tap_part, depth_part)]
        outs = [((1, width), F32, vmem())] * 5
        outs += [
            ((LEFT + RIGHT + 1, HEAD_DIM), F32, vmem()),
            ((8, BLOCK), F32, vmem()),
            ((taps, width), F32, vmem()),
            ((1, width), F32, vmem()),
            ((full // m, hidden), F32, hbm()),
            ((hidden, full // m), F32, hbm()),
            ((n * count, width), BF16, hbm()),
        ]
        scratch += [
            pltpu.VMEM((8, full), F32),
            pltpu.VMEM((full, hidden), BF16),
            pltpu.VMEM((full, hidden), BF16),
            pltpu.VMEM((count, full), F32),
            pltpu.VMEM((n, count, width), BF16),
        ]
        reduces = [
            reduce_scratch(layers, full // m, hidden, [(hidden, flip)]) for flip in (False, True)
        ]
        scratch += reduces[0] + reduces[1]
        extra = (hidden, None, [len(made) for made in reduces])
        scratch += [
            pltpu.VMEM((n, 8, width), F32), pltpu.VMEM((16, BLOCK), F32), pltpu.VMEM((n, 8, width), F32)
        ]
        for shape in ((8, width), table_part.shape, (16, BLOCK), tap_part.shape, depth_part.shape,
                      (8, width)):
            scratch += sum_scratch(n, layers, shape)
        side = dict(side, more_slots=16 * m + 8 * n, row_on=True)
    else:
        outs = [
            ((8, full), F32, vmem()),
            ((full, hidden), BF16, "store"),
            ((full, hidden), BF16, "store"),
            ((count, full), F32, vmem()),
        ]
    return comm_call(
        name, collective_id, sizes,
        functools.partial(feed_forward_back_main, count, gain_row, extra),
        ins, outs, scratch, **side,
    )


def slot_rows(axis):
    slots = lax.broadcasted_iota(jnp.int32, (LEFT + RIGHT + 8, SPAN), axis)
    signed = jnp.where(slots < SPAN - BLOCK + 1, slots, slots - SPAN)
    return jnp.clip(signed - (BLOCK - LEFT), 0, LEFT + RIGHT)


def extend_table(table, copies):
    slots = jnp.arange(SPAN)
    signed = jnp.where(slots < SPAN - BLOCK + 1, slots, slots - SPAN)
    row_of = jnp.clip(signed - (BLOCK - LEFT), 0, LEFT + RIGHT)
    chosen = (row_of[:, None] == jnp.arange(LEFT + RIGHT + 1)[None, :]).astype(table.dtype)
    return jnp.tile(matmul(chosen, table).astype(table.dtype), (1, copies))


def fill_far(far_ref, table_ref, limit):
    blocks, length, _ = far_ref.shape
    lane = lax.broadcasted_iota(jnp.int32, (1, BLOCK), 1)

    def row(at, mark):
        ends = table_ref[at:at + 1].astype(F32)
        if ends.shape[1] < BLOCK:
            ends = jnp.concatenate([ends, jnp.zeros((1, BLOCK - ends.shape[1]), F32)], axis=1)
        return jnp.where(lane < HEAD_DIM, ends, jnp.where(lane == mark, 1.0, 0.0))

    first = row(0, HEAD_DIM + 1)
    last = row(SPAN - 2 * BLOCK, HEAD_DIM + 2)

    def block(step, carry):
        index, piece = step // (length // BLOCK), lax.rem(step, length // BLOCK)
        at = index * BLOCK
        column = lax.broadcasted_iota(jnp.int32, (BLOCK, 1), 0) + piece * BLOCK
        place = column + at - BLOCK
        key = jnp.where(place < 0, place + length, jnp.where(place >= length, place - length, place))
        near = (column < WINDOW) & (place >= 0) & (place < length)
        left = jnp.where(near | (key >= at), 0.0, 1.0)
        right = jnp.where(near | (key < at), 0.0, 1.0)
        bias = jnp.where(key < limit, 0.0, NEG_FILL)
        terms = left * first + right * last + jnp.where(lane == HEAD_DIM, bias, 0.0)
        far_ref[index, tile(piece, BLOCK)] = terms.astype(BF16)
        return carry

    lax.fori_loop(0, blocks * (length // BLOCK), block, 0)


def duplicate(qkv_ref, width, group, keys, values):
    length = qkv_ref.shape[0]
    for part in range(width // group):
        base = part * group
        for copy in range(2):
            place = slice(copy * length, (copy + 1) * length)
            keys[part, place] = qkv_ref[:, width + base:width + base + group]
            values[part, place] = qkv_ref[:, 2 * width + base:2 * width + base + group]


def by_head(values, group):
    if group == HEAD_DIM:
        return values
    lane = lax.broadcasted_iota(jnp.int32, (BLOCK, group), 1)
    zero = jnp.zeros_like(values)
    return jnp.concatenate(
        [
            jnp.where((lane >= at) & (lane < at + HEAD_DIM), values, zero)
            for at in range(0, group, HEAD_DIM)
        ],
        axis=0,
    )


def own_lanes(values, group):
    if group == HEAD_DIM:
        return values
    lane = lax.broadcasted_iota(jnp.int32, (BLOCK, group), 1)
    return jnp.where(lane < HEAD_DIM, values[0:BLOCK], values[BLOCK:2 * BLOCK])


def far_queries(values, group):
    wide = values.astype(F32)
    if group == HEAD_DIM:
        lane = lax.broadcasted_iota(jnp.int32, (BLOCK, BLOCK - HEAD_DIM), 1)
        return jnp.concatenate([wide, jnp.where(lane == 0, 1.0, 0.0)], axis=1).astype(BF16)
    lane = lax.broadcasted_iota(jnp.int32, (BLOCK, BLOCK), 1)
    rest = jnp.where(lane == HEAD_DIM, 1.0, 0.0)
    return jnp.concatenate(
        [
            jnp.where(lane < HEAD_DIM, wide, rest),
            jnp.where(lane < HEAD_DIM, pltpu.roll(wide, HEAD_DIM, 1), rest),
        ],
        axis=0,
    ).astype(BF16)


def near_mask(at, length):
    place = lax.broadcasted_iota(jnp.int32, (1, WINDOW), 1) + (at - BLOCK)
    return (place >= 0) & (place < length)


def near_terms(query, table, at, length):
    terms = matmul_nt(query, table)
    halves = [
        pltpu.roll(terms[start:start + BLOCK], 0, 1, stride=1, stride_axis=0)[:, :WINDOW]
        for start in range(0, query.shape[0], BLOCK)
    ]
    return jnp.where(near_mask(at, length), jnp.concatenate(halves, axis=0), 0.0)


def attend_blocks(first, blocks, width, group, qkv_ref, table_ref, far_ref, keys, values, context_ref,
                  log_ref, weights):
    length = qkv_ref.shape[0]
    heads = group // HEAD_DIM
    parts = width // group
    scale = 1.0 / math.sqrt(HEAD_DIM)

    def block(step, carry):
        index, part = first + step // parts, lax.rem(step, parts)
        at = pl.multiple_of(index * BLOCK, BLOCK)
        rows = pl.ds(at, BLOCK)
        cols = tile(part, group) if parts > 1 else slice(0, group)
        window = pl.ds(pl.multiple_of(lax.rem(at + length - BLOCK, length), BLOCK), length)
        query_rows = qkv_ref[rows, cols] * jnp.asarray(scale, BF16)
        query = by_head(query_rows, group)
        extra = far_queries(query_rows, group)
        if group == 2 * HEAD_DIM:
            scores = matmul_nt(
                jnp.concatenate([query, extra], axis=1),
                jnp.concatenate([keys[part, window], far_ref[index]], axis=1),
            )
        else:
            scores = matmul_nt(query, keys[part, window]) + matmul_nt(extra, far_ref[index])
        near = near_terms(query, table_ref[...], at, length)
        size = 32
        peaks, totals = [], []
        for start in range(0, heads * BLOCK, size):
            some = slice(start, start + size)
            first_part = scores[some, :WINDOW] + near[some]
            last_part = scores[some, WINDOW:]
            peak = jnp.maximum(
                jnp.max(first_part, axis=1, keepdims=True), jnp.max(last_part, axis=1, keepdims=True)
            )
            first_part = jnp.exp(first_part - peak)
            last_part = jnp.exp(last_part - peak)
            weights[some, :WINDOW] = first_part.astype(BF16)
            weights[some, WINDOW:] = last_part.astype(BF16)
            peaks.append(peak)
            totals.append(
                jnp.sum(first_part, axis=1, keepdims=True) + jnp.sum(last_part, axis=1, keepdims=True)
            )
        total = jnp.concatenate(totals, axis=0)
        mixed = matmul(weights[...], values[part, window]) * (1.0 / total)
        context_ref[rows, cols] = own_lanes(mixed, group).astype(BF16)
        log = jnp.concatenate(peaks, axis=0) + jnp.log(total)
        lane = lax.broadcasted_iota(jnp.int32, (BLOCK, BLOCK), 1)
        square = jnp.where(lane == 0, log[0:BLOCK], 0.0)
        for head in range(1, heads):
            square = jnp.where(lane == head, log[head * BLOCK:(head + 1) * BLOCK], square)
        log_ref[part, :, rows] = square.T[0:8]
        return carry

    lax.fori_loop(0, blocks * parts, block, 0)


def attend_back_core(width, group, qkv_ref, table_ref, far_ref, log_ref, grad_ref, out_ref,
                     table_grad_ref, keys, values, key_grad, value_grad, slot_grad, end_grad, probs,
                     prob_grads, back, blocks_in_turn):
    length = qkv_ref.shape[0]
    heads = group // HEAD_DIM
    parts = width // group
    scale = 1.0 / math.sqrt(HEAD_DIM)
    duplicate(qkv_ref, width, group, keys, values)
    slot_grad[...] = jnp.zeros_like(slot_grad)
    end_grad[...] = jnp.zeros_like(end_grad)
    key_grad[...] = jnp.zeros_like(key_grad)
    value_grad[...] = jnp.zeros_like(value_grad)
    down = lax.broadcasted_iota(jnp.int32, (BLOCK, BLOCK), 0)
    across = lax.broadcasted_iota(jnp.int32, (BLOCK, BLOCK), 1)
    reverse = jnp.where(down + across == BLOCK - 1, 1.0, 0.0).astype(BF16)

    def flip(values_in):
        return jnp.concatenate(
            [
                matmul(reverse, values_in[start:start + BLOCK])
                for start in range(0, heads * BLOCK, BLOCK)
            ],
            axis=0,
        )

    def block(index, part):
        at = pl.multiple_of(index * BLOCK, BLOCK)
        rows = pl.ds(at, BLOCK)
        cols = tile(part, group) if parts > 1 else slice(0, group)
        window = pl.ds(pl.multiple_of(lax.rem(at + length - BLOCK, length), BLOCK), length)
        key_rows = keys[part, window]
        far_rows = far_ref[index]
        query_rows = qkv_ref[rows, cols] * jnp.asarray(scale, BF16)
        query = by_head(query_rows, group)
        extra = far_queries(query_rows, group)
        grad = by_head(grad_ref[rows, cols], group)
        query_wide = [query, extra]
        if group == 2 * HEAD_DIM:
            query_wide = [jnp.concatenate(query_wide, axis=1)]
            key_wide = [jnp.concatenate([key_rows, far_rows], axis=1)]
        else:
            key_wide = [key_rows, far_rows]
        near = near_terms(query, table_ref[...], at, length)
        log = jnp.concatenate([log_ref[part, head:head + 1, rows] for head in range(heads)], axis=1)
        value_rows = values[part, window]
        row_dot = jnp.zeros((8, heads * BLOCK), F32)
        for start in range(0, length, BLOCK):
            some = slice(start, start + BLOCK)
            scores = sum(
                matmul_nt(left[some], right) for left, right in zip(key_wide, query_wide)
            )
            if start < WINDOW:
                scores = scores + near[:, some].T
            prob = jnp.exp(scores - log)
            prob_grad = matmul_nt(value_rows[some], grad)
            row_dot = row_dot + fold8(prob * prob_grad)
            probs[some] = prob
            prob_grads[some] = prob_grad
        row_dot = jnp.sum(row_dot, axis=0, keepdims=True)
        for start in range(0, length, BLOCK):
            some = slice(start, start + BLOCK)
            there = pl.ds(pl.multiple_of(window.start + start, BLOCK), BLOCK)
            prob = probs[some]
            score_grad = (prob * (prob_grads[some] - row_dot)).astype(BF16)
            value_grad[part, there] += matmul(prob.astype(BF16), grad)
            key_grad[part, there] += matmul(score_grad, query)
            back[:, some] = score_grad.T
        turned_back = back[...]
        if group == 2 * HEAD_DIM:
            both = matmul(turned_back, key_wide[0])
            direct, ends = both[:, :group], both[:, group:]
        else:
            direct, ends = matmul(turned_back, key_rows), matmul(turned_back, far_rows)
        left_sum, right_sum = ends[:, HEAD_DIM + 1:HEAD_DIM + 2], ends[:, HEAD_DIM + 2:HEAD_DIM + 3]
        query_full = query.astype(F32)
        end_grad[0:8] += fold8(left_sum * query_full)
        end_grad[8:16] += fold8(right_sum * query_full)
        near_grad = jnp.where(
            near_mask(at, length), turned_back[:, :WINDOW], jnp.asarray(0.0, BF16)
        )
        flipped = flip(near_grad)
        skewed = []
        for start in range(0, heads * BLOCK, BLOCK):
            padded = jnp.concatenate(
                [flipped[start:start + BLOCK], jnp.zeros((BLOCK, SPAN - WINDOW), F32)], axis=1
            )
            skewed.append(pltpu.roll(padded, SPAN - (BLOCK - 1), 1, stride=1, stride_axis=0))
        straight = jnp.concatenate(skewed, axis=0).astype(BF16)
        term = matmul(straight, table_ref[...])
        high = term.astype(BF16)
        low = (term - high.astype(F32)).astype(BF16)
        direct = direct + flip(high) + flip(low)
        result = own_lanes(direct, group)
        if heads == 1:
            result = result + ends[:, :HEAD_DIM]
        else:
            lane = lax.broadcasted_iota(jnp.int32, (BLOCK, BLOCK), 1)
            result = result + jnp.where(
                lane < HEAD_DIM, ends[0:BLOCK], pltpu.roll(ends[BLOCK:2 * BLOCK], HEAD_DIM, 1)
            )
        out_ref[rows, cols] = (result * scale).astype(BF16)
        slot_grad[...] += matmul_tn(flip(query).astype(BF16), straight)

    blocks_in_turn(block, parts)
    for part in range(parts):
        base = width + part * group
        out_ref[:, base:base + group] = (
            key_grad[part, 0:length] + key_grad[part, length:2 * length]
        ).astype(BF16)
        out_ref[:, width + base:width + base + group] = (
            value_grad[part, 0:length] + value_grad[part, length:2 * length]
        ).astype(BF16)
    chosen = jnp.where(
        slot_rows(1) == lax.broadcasted_iota(jnp.int32, (LEFT + RIGHT + 8, SPAN), 0), 1.0, 0.0
    )
    table_grad_ref[...] = lax.dot_general(
        chosen, slot_grad[...], (((1,), (1,)), ((), ())), precision=lax.Precision.HIGHEST,
        preferred_element_type=F32,
    )
    table_grad_ref[0:1] += jnp.sum(end_grad[0:8], axis=0, keepdims=True)
    table_grad_ref[LEFT + RIGHT:LEFT + RIGHT + 1] += jnp.sum(end_grad[8:16], axis=0, keepdims=True)


def attention_main(count, gain_row, wire, ins, outs, scratch):
    limit_ref, resid, gains_ref, weights, table_ref = ins
    after_ref, squares_ref, rows_ref, qkv_ref, context_ref, log_ref = outs
    far_ref, keys, values, weights_ref, part, got = scratch
    width = context_ref.shape[1]
    group = keys.shape[2]
    wire.greet()
    wire.begin()
    norm_rows(wire, count, resid, gains_ref[gain_row:gain_row + 1], rows_ref)
    spread = Spread(wire, rows_ref, count)
    spread.start()
    wire.loaded()
    collect = Collect(wire, part, got)
    spread.relay()
    wire.early()
    fill_far(far_ref, table_ref, limit_ref[0])
    chunks = []
    for chunk, slot in spread.arrivals(relay=False):
        chunks.append((chunk, slot))
        rows = tile(chunk, count)
        left = rows_ref[rows]

        def project(cols, index):
            qkv_ref[rows, cols] = matmul(left, weights[:, cols]).astype(BF16)

        block_loop(3 * width, project)
    duplicate(qkv_ref, width, group, keys, values)
    wire.side[0].middle()
    size = max(count, BLOCK)

    def share(chunk, target):
        attend_blocks(chunk * count // BLOCK, size // BLOCK, width, group, qkv_ref, table_ref, far_ref,
                      keys, values, context_ref, log_ref, weights_ref)
        left = context_ref[tile(chunk, count)]

        def leave(cols, index):
            target[:, cols] = matmul_nt(left, weights[cols, 3 * width:]).astype(BF16)

        block_loop(weights.shape[0], leave)

    def last():
        collect.combine()
        wire.side[1].middle()

    send_shares(wire, chunks, collect, share, last)
    wire.flush()
    collect.wait()
    residual(collect, 1.0, resid, limit_ref[0], after_ref, squares_ref)
    spread.finish()
    wire.end()


def attention(sizes, name, collective_id, gain_row, limit, resid, gains, weights, table, **side):
    n, m = sizes
    count, full = resid.shape
    length, width = n * count, weights.shape[1] // 4
    group = min(2 * HEAD_DIM, width)
    return comm_call(
        name, collective_id, sizes, functools.partial(attention_main, count, gain_row),
        [(limit, smem()), (resid, vmem()), (gains, vmem()), (weights, "load"), (table, "load")],
        [
            ((count, full), F32, vmem()),
            ((16, full), F32, vmem()),
            ((length, full), BF16, "store"),
            ((length, 3 * width), BF16, "store"),
            ((length, width), BF16, "store"),
            ((width // group, 8, length), F32, "store"),
        ],
        [
            pltpu.VMEM((length // BLOCK, length, BLOCK), BF16),
            pltpu.VMEM((width // group, 2 * length, group), BF16),
            pltpu.VMEM((width // group, 2 * length, group), BF16),
            pltpu.VMEM((group // HEAD_DIM * BLOCK, length), BF16),
            pltpu.VMEM((n, count, full), BF16),
            pltpu.VMEM((n - 1, count, full), BF16),
        ],
        cost=20 * 10**9, **side,
    )


def attention_back_main(count, gain_row, wire, ins, outs, scratch):
    (limit_ref, grad_ref, resid, gains_ref, weights, table_ref, rows_ref, qkv_ref, context_ref,
     log_ref, pieces) = ins
    gain_grad_ref, wide_ref, table_grad_ref, new_grad_ref, result_ref = outs
    (far_ref, grads, context_grad, qkv_grad, keys, values, key_grad, value_grad, slot_grad, end_grad,
     probs, prob_grads, back, part, got, came) = scratch
    width = context_ref.shape[1]
    group = keys.shape[2]
    wire.greet()
    wire.begin()
    cast_rows(wire, count, grad_ref, 1.0, grads)
    spread = Spread(wire, grads, count)
    spread.start()
    wire.loaded()
    collect = Collect(wire, part, got)
    fill_far(far_ref, table_ref, limit_ref[0])
    chunks = []
    per_chunk = max(count, BLOCK) // BLOCK

    mine = came.at[tile(wire.me, count)]
    output_copies = [
        wire.remote(pieces.at[lax.rem(wire.me + step, wire.n)], mine, "col",
                    lax.rem(wire.me + step, wire.n))
        for step in range(1, wire.n)
    ]
    output_copies.append(wire.local(pieces.at[wire.me], mine))

    def send_output():
        for copy in output_copies:
            copy.start()

    def down_gradient(chunk):
        rows = tile(chunk, count)
        context_grad[rows] = matmul(grads[rows], weights[:, 3 * width:]).astype(BF16)

    def in_turn(block, parts):
        if wire.n == 4:
            def turn(place, carry):
                pl.when(place == 1)(wire.early)
                for at in (1, 2, 3):
                    pl.when(place == at)(lambda at=at: spread.wait_place(at))
                pl.when(place == 3)(send_output)
                chunk = flipped(wire, place)
                down_gradient(chunk)

                def one(step, carry):
                    block(chunk * per_chunk + step // parts, lax.rem(step, parts))
                    final = per_chunk * parts - 1
                    for turn_of, after in ((0, min(1, final)), (1, final)):
                        pl.when((place == 0) & (step == after))(
                            lambda turn_of=turn_of: spread.relay_turn(turn_of)
                        )
                    return carry

                lax.fori_loop(0, per_chunk * parts, one, 0)
                return carry

            lax.fori_loop(0, 4, turn, 0)
            return
        wire.early()
        for chunk, slot in spread.arrivals():
            chunks.append((chunk, slot))
            down_gradient(chunk)
        send_output()

        def one(step, carry):
            block(step // parts, lax.rem(step, parts))
            return carry

        lax.fori_loop(0, wire.n * count // BLOCK * parts, one, 0)

    attend_back_core(width, group, qkv_ref, table_ref, far_ref, log_ref, context_grad, qkv_grad,
                     table_grad_ref, keys, values, key_grad, value_grad, slot_grad, end_grad, probs,
                     prob_grads, back, in_turn)
    wire.middle()

    def share(chunk, target):
        left = qkv_grad[tile(chunk, count)]

        def back(cols, index):
            target[:, cols] = matmul_nt(left, weights[cols, :3 * width]).astype(BF16)

        block_loop(weights.shape[0], back)

    send_shares(wire, chunks, collect, share)
    collect.combine()
    for copy in output_copies:
        copy.wait()
    result_ref[...] = came[...].T

    def weight_grads(rows, index):
        wide_ref[rows, :3 * width] = matmul_tn(rows_ref[:, rows], qkv_grad[...]).astype(BF16)
        wide_ref[rows, 3 * width:] = matmul_tn(grads[:, rows], context_ref[...]).astype(BF16)

    block_loop(weights.shape[0], weight_grads)
    wire.flush()
    wire.end()
    collect.wait()
    residual_back(collect, grad_ref, resid, gains_ref[gain_row:gain_row + 1], new_grad_ref,
                  gain_grad_ref)
    spread.finish()


def attention_back(sizes, name, collective_id, gain_row, limit, grad, resid, gains, weights, table, rows,
                   qkv, context, log_total, pieces, **side):
    n, m = sizes
    count, full = resid.shape
    length, width = context.shape
    group = min(2 * HEAD_DIM, width)
    return comm_call(
        name, collective_id, sizes, functools.partial(attention_back_main, count, gain_row),
        [(limit, smem()), (grad, vmem()), (resid, "load"), (gains, vmem())]
        + [(item, "load") for item in (weights, table, rows, qkv, context, log_total, pieces)],
        [
            ((8, full), F32, vmem()),
            ((full, 4 * width), BF16, "store"),
            ((LEFT + RIGHT + 8, group), F32, vmem()),
            ((count, full), F32, vmem()),
            ((width, length), BF16, "store"),
        ],
        [
            pltpu.VMEM((length // BLOCK, length, BLOCK), BF16),
            pltpu.VMEM((length, full), BF16),
            pltpu.VMEM((length, width), BF16),
            pltpu.VMEM((length, 3 * width), BF16),
            pltpu.VMEM((width // group, 2 * length, group), BF16),
            pltpu.VMEM((width // group, 2 * length, group), BF16),
            pltpu.VMEM((width // group, 2 * length, group), F32),
            pltpu.VMEM((width // group, 2 * length, group), F32),
            pltpu.VMEM((group, SPAN), F32),
            pltpu.VMEM((16, group), F32),
            pltpu.VMEM((length, group // HEAD_DIM * BLOCK), F32),
            pltpu.VMEM((length, group // HEAD_DIM * BLOCK), F32),
            pltpu.VMEM((group // HEAD_DIM * BLOCK, length), BF16),
            pltpu.VMEM((n, count, full), BF16),
            pltpu.VMEM((n - 1, count, full), BF16),
            pltpu.VMEM((length, width), BF16),
        ],
        cost=50 * 10**9, **side,
    )


PAD = 32
ROWS = 64


def shifted_sets(held, low, high, size):
    for residue in range(8):
        shifts = [shift for shift in range(low, high + 1) if shift % 8 == residue]
        if shifts:
            extent = shifts[-1] - residue + size
            moved = held[residue:residue + extent]
            for shift in shifts:
                yield shift, moved[shift - residue:shift - residue + size]


def stat_rows(blocks, first, second, stats_ref):
    lane = lax.broadcasted_iota(jnp.int32, (BLOCK, BLOCK), 1)
    both = jnp.where(lane == 0, first, jnp.where(lane == 1, second, 0.0))
    stats_ref[:, blocks] = both.T[0:8]


def stat_columns(stats):
    both = jnp.concatenate([stats, jnp.zeros((BLOCK - 8, stats.shape[1]), F32)], axis=0).T
    return both[:, 0:1], both[:, 1:2]


class Stats:
    def __init__(self, wire, mine, got):
        self.wire, self.mine, self.got = wire, mine, got
        self.copies = [
            wire.remote(mine, got.at[step - 1], "col", lax.rem(wire.me + step, wire.n))
            for step in range(1, wire.n)
        ]

    def total(self):
        for copy in self.copies:
            copy.start()
        for copy in self.copies:
            copy.wait()
        total = self.mine[...]
        for step in range(self.wire.n - 1):
            total = total + self.got[step]
        return total


def token_blocks(length, body):
    def step(index, carry):
        body(tile(index, BLOCK), index)
        return carry

    lax.fori_loop(0, length // BLOCK, step, 0)


def convolution_main(count, gain_row, taps, wire, ins, outs, scratch):
    limit_ref, resid, gains_ref, weights, taps_ref, depth_ref = ins
    after_ref, squares_ref, rows_ref, pre_ref, mixed_ref, stats_ref = outs
    kernel_ref, padded, stats_mine, stats_got, act, part, got = scratch
    length, width = mixed_ref.shape
    full = gains_ref.shape[1]
    wire.greet()
    wire.begin()
    norm_rows(wire, count, resid, gains_ref[gain_row:gain_row + 1], rows_ref)
    spread = Spread(wire, rows_ref, count)
    spread.start()
    wire.loaded()
    collect = Collect(wire, part, got)
    stats = Stats(wire, stats_mine, stats_got)
    padded[0:PAD] = jnp.zeros((PAD, width), F32)
    kernel_ref[0:taps] = taps_ref[...].astype(F32)
    spread.relay()
    wire.early()
    chunks = []
    for chunk, slot in spread.arrivals(relay=False):
        chunks.append((chunk, slot))
        rows = tile(chunk, count)
        left = rows_ref[rows]
        value_pre = matmul(left, weights[:, 0:width])
        gate_pre = matmul(left, weights[:, width:2 * width])
        pre_ref[rows, 0:width] = value_pre.astype(BF16)
        pre_ref[rows, width:2 * width] = gate_pre.astype(BF16)
        at = pl.multiple_of(chunk * count + PAD, PAD)
        keep = keep_rows(limit_ref[0], chunk * count, count)
        padded[pl.ds(at, count)] = value_pre * jax.nn.sigmoid(gate_pre) * keep

    def mix(index, carry):
        held = padded[pl.ds(pl.multiple_of(index * ROWS, ROWS), ROWS + PAD)]
        total = jnp.zeros((ROWS, width), F32)
        for shift, moved in shifted_sets(held, PAD - taps + 1, PAD, ROWS):
            tap = shift - (PAD - taps + 1)
            total = total + moved * kernel_ref[tap:tap + 1]
        mixed_ref[tile(index, ROWS)] = total
        return carry

    lax.fori_loop(0, length // ROWS, mix, 0)

    def sums(rows, index):
        mixed = mixed_ref[rows]
        stat_rows(rows, jnp.sum(mixed, axis=1, keepdims=True),
                  jnp.sum(mixed * mixed, axis=1, keepdims=True), stats_mine)

    token_blocks(length, sums)
    total = stats.total() * (1.0 / full)
    inverse = lax.rsqrt(total[1:2] - total[0:1] * total[0:1] + EPSILON)
    stats_ref[...] = jnp.concatenate([total[0:1], inverse, total[2:]], axis=0)

    def share(chunk, target):
        def activate(index, carry):
            rows = tile(chunk * count // BLOCK + index, BLOCK)
            mean, scale = stat_columns(stats_ref[:, rows])
            scaled = (mixed_ref[rows] - mean) * scale * depth_ref[...]
            act[tile(index, BLOCK)] = (scaled * jax.nn.sigmoid(scaled)).astype(BF16)
            return carry

        lax.fori_loop(0, -(-count // BLOCK), activate, 0)
        if count % BLOCK:
            at = lax.rem(chunk * count, BLOCK)
            left = act[pl.ds(pl.multiple_of(at, count), count)]
        else:
            left = act[...]

        def leave(cols, index):
            target[:, cols] = matmul_nt(left, weights[cols, 2 * width:]).astype(BF16)

        block_loop(weights.shape[0], leave)

    send_shares(wire, chunks, collect, share, collect.combine)
    wire.middle()
    wire.flush()
    collect.wait()
    residual(collect, 1.0, resid, limit_ref[0], after_ref, squares_ref)
    spread.finish()
    wire.end()


def convolution(sizes, name, collective_id, gain_row, limit, resid, gains, weights, kernel, depth_gain,
                **side):
    n, m = sizes
    count, full = resid.shape
    length, width = n * count, weights.shape[1] // 3
    return comm_call(
        name, collective_id, sizes,
        functools.partial(convolution_main, count, gain_row, kernel.shape[0]),
        [(limit, smem()), (resid, vmem()), (gains, vmem()), (weights, "load"), (kernel, vmem()),
         (depth_gain, vmem())],
        [
            ((count, full), F32, vmem()),
            ((16, full), F32, vmem()),
            ((length, full), BF16, "store"),
            ((length, 2 * width), BF16, "store"),
            ((length, width), F32, "store"),
            ((8, length), F32, "store"),
        ],
        [
            pltpu.VMEM((PAD, width), F32),
            pltpu.VMEM((length + PAD, width), F32),
            pltpu.VMEM((8, length), F32),
            pltpu.VMEM((n - 1, 8, length), F32),
            pltpu.VMEM((max(count, BLOCK), width), BF16),
            pltpu.VMEM((n, count, full), BF16),
            pltpu.VMEM((n - 1, count, full), BF16),
        ],
        cost=15 * 10**9, **side,
    )


def convolution_back_main(count, gain_row, taps, wire, ins, outs, scratch):
    (limit_ref, grad_ref, resid, gains_ref, weights, taps_ref, depth_ref, rows_ref, pre_ref, mixed_ref,
     stats_ref) = ins
    gain_grad_ref, wide_ref, kernel_grad_ref, depth_grad_ref, new_grad_ref = outs
    (kernel_ref, grads, padded, padded_grad, stats_mine, stats_got, sums_ref, act, pre_grad, part, got) = scratch
    length, width = mixed_ref.shape
    full = gains_ref.shape[1]
    wire.greet()
    wire.begin()
    cast_rows(wire, count, grad_ref, 1.0, grads)
    spread = Spread(wire, grads, count)
    spread.start()
    wire.loaded()
    collect = Collect(wire, part, got)
    stats = Stats(wire, stats_mine, stats_got)
    padded[0:PAD] = jnp.zeros((PAD, width), F32)
    padded_grad[length:] = jnp.zeros((PAD, width), F32)
    sums_ref[...] = jnp.zeros_like(sums_ref)
    depth_grad_ref[...] = jnp.zeros_like(depth_grad_ref)
    kernel_ref[0:taps] = taps_ref[...].astype(F32)
    kernel_grad_ref[...] = jnp.zeros_like(kernel_grad_ref)
    spread.relay()

    def regate(rows, index):
        value_pre = pre_ref[rows, 0:width].astype(F32)
        gate_pre = pre_ref[rows, width:2 * width].astype(F32)
        at = pl.multiple_of(index * BLOCK + PAD, PAD)
        keep = keep_rows(limit_ref[0], index * BLOCK, BLOCK)
        padded[pl.ds(at, BLOCK)] = value_pre * jax.nn.sigmoid(gate_pre) * keep

    token_blocks(length, regate)
    wire.early()
    def first(rows, index):
        mean, scale = stat_columns(stats_ref[:, rows])
        normed = (mixed_ref[rows] - mean) * scale
        scaled = normed * depth_ref[...]
        sig = jax.nn.sigmoid(scaled)
        act[rows] = (scaled * sig).astype(BF16)
        scaled_grad = padded_grad[rows] * (sig + scaled * sig * (1.0 - sig))
        depth_grad_ref[...] += fold8(scaled_grad * normed)
        weighted = scaled_grad * depth_ref[...]
        padded_grad[rows] = weighted
        stat_rows(rows, jnp.sum(weighted, axis=1, keepdims=True),
                  jnp.sum(weighted * normed, axis=1, keepdims=True), stats_mine)

    chunks = []
    for chunk, slot in spread.arrivals(relay=False):
        chunks.append((chunk, slot))
        rows = tile(chunk, count)
        padded_grad[rows] = matmul(grads[rows], weights[:, 2 * width:])
        if count % BLOCK == 0:
            def some(index, carry):
                first(tile(chunk * (count // BLOCK) + index, BLOCK), index)
                return carry

            lax.fori_loop(0, count // BLOCK, some, 0)
    wire.middle()
    if count % BLOCK:
        token_blocks(length, first)
    total = stats.total() * (1.0 / full)
    stats_mine[...] = total

    def second(rows, index):
        mean, scale = stat_columns(stats_ref[:, rows])
        normed = (mixed_ref[rows] - mean) * scale
        one, two = stat_columns(stats_mine[:, rows])
        padded_grad[rows] = scale * (padded_grad[rows] - one - normed * two)

    token_blocks(length, second)

    def share(chunk, target):
        def unmix(index, carry):
            start = chunk * count + index * ROWS
            rows = pl.ds(pl.multiple_of(start, ROWS), ROWS)
            ahead = padded_grad[pl.ds(pl.multiple_of(start, ROWS), ROWS + PAD)]
            total = jnp.zeros((ROWS, width), F32)
            for shift, moved in shifted_sets(ahead, 0, taps - 1, ROWS):
                tap = taps - 1 - shift
                total = total + moved * kernel_ref[tap:tap + 1]
            gate = jax.nn.sigmoid(pre_ref[rows, width:2 * width].astype(F32))
            through = total * keep_rows(limit_ref[0], start, ROWS) * gate
            pre_grad[rows, 0:width] = through.astype(BF16)
            pre_grad[rows, width:2 * width] = (
                through * pre_ref[rows, 0:width].astype(F32) * (1.0 - gate)
            ).astype(BF16)
            return carry

        lax.fori_loop(0, count // ROWS, unmix, 0)
        left = pre_grad[tile(chunk, count)]

        def back(cols, index):
            target[:, cols] = matmul_nt(left, weights[cols, :2 * width]).astype(BF16)

        block_loop(weights.shape[0], back)

    send_shares(wire, chunks, collect, share)
    collect.combine()

    def tap_grads(index, carry):
        here = padded_grad[tile(index, ROWS)]
        around = pl.ds(pl.multiple_of(index * ROWS, ROWS), ROWS + PAD)
        for shift, moved in shifted_sets(padded[around], PAD - taps + 1, PAD, ROWS):
            tap = shift - (PAD - taps + 1)
            sums_ref[tap * 8:(tap + 1) * 8] += fold8(here * moved)
        return carry

    lax.fori_loop(0, length // ROWS, tap_grads, 0)
    for tap in range(taps):
        kernel_grad_ref[tap:tap + 1] = jnp.sum(sums_ref[tap * 8:(tap + 1) * 8], axis=0, keepdims=True)

    def weight_grads(rows, index):
        wide_ref[rows, :2 * width] = matmul_tn(rows_ref[:, rows], pre_grad[...]).astype(BF16)
        wide_ref[rows, 2 * width:] = matmul_tn(grads[:, rows], act[...]).astype(BF16)

    block_loop(weights.shape[0], weight_grads)
    wire.flush()
    wire.end()
    collect.wait()
    residual_back(collect, grad_ref, resid, gains_ref[gain_row:gain_row + 1], new_grad_ref,
                  gain_grad_ref)
    spread.finish()


def convolution_back(sizes, name, collective_id, gain_row, limit, grad, resid, gains, weights, kernel,
                     depth_gain, rows, pre, mixed, stats, **side):
    n, m = sizes
    count, full = resid.shape
    length, width = mixed.shape
    taps = kernel.shape[0]
    return comm_call(
        name, collective_id, sizes,
        functools.partial(convolution_back_main, count, gain_row, taps),
        [(limit, smem()), (grad, vmem()), (resid, "load"), (gains, vmem()), (weights, "load"),
         (kernel, vmem()), (depth_gain, vmem())]
        + [(item, "load") for item in (rows, pre, mixed, stats)],
        [
            ((8, full), F32, vmem()),
            ((full, 3 * width), BF16, "store"),
            ((PAD, width), F32, vmem()),
            ((8, width), F32, vmem()),
            ((count, full), F32, vmem()),
        ],
        [
            pltpu.VMEM((PAD, width), F32),
            pltpu.VMEM((length, full), BF16),
            pltpu.VMEM((length + PAD, width), F32),
            pltpu.VMEM((length + PAD, width), F32),
            pltpu.VMEM((8, length), F32),
            pltpu.VMEM((n - 1, 8, length), F32),
            pltpu.VMEM((8 * taps, width), F32),
            pltpu.VMEM((length, width), BF16),
            pltpu.VMEM((length, 2 * width), BF16),
            pltpu.VMEM((n, count, full), BF16),
            pltpu.VMEM((n - 1, count, full), BF16),
        ],
        cost=20 * 10**9, **side,
    )


def results_kernel(*refs):
    sources, targets = refs[:len(refs) // 2], refs[len(refs) // 2:]
    for source, target in zip(sources, targets):
        if target.shape[0] == 1 and source.shape[0] == 8:
            target[...] = source[...].T[0:1]
        elif source.shape != target.shape:
            target[...] = source[...].astype(target.dtype).T
        else:
            target[...] = source[...]


def results(arrays, shapes):
    return pl.pallas_call(
        results_kernel,
        name="results",
        out_shape=tuple(shapes),
        in_specs=[vmem()] * len(arrays),
        out_specs=tuple(vmem() for _ in arrays),
        compiler_params=pltpu.CompilerParams(vmem_limit_bytes=VMEM_LIMIT),
    )(*arrays)


def body(
    layer_input,
    clip_lengths,
    first_gain,
    first_up,
    first_down,
    attend_gain,
    query_weight,
    key_weight,
    value_weight,
    output_weight,
    distance_table,
    conv_gain,
    pointwise_value,
    pointwise_gate,
    depthwise_kernel,
    depthwise_gain,
    pointwise_out,
    second_gain,
    second_up,
    second_down,
    final_gain,
    output_cotangent,
):
    n = lax.axis_size("col")
    me = lax.axis_index("col")
    width, length = layer_input.shape
    full = n * width
    count = length // n

    sizes = (n, lax.axis_size("row"))
    group = min(2 * HEAD_DIM, width)
    table_wide = extend_table(distance_table, group // HEAD_DIM)
    limit = clip_lengths
    tap_count = depthwise_kernel.shape[0]
    gain_parts = [
        gain[None] for gain in (first_gain, attend_gain, conv_gain, second_gain, final_gain)
    ]
    attend_pieces = [
        (query_weight, False), (key_weight, False), (value_weight, False), (output_weight, True)
    ]
    conv_pieces = [(pointwise_value, False), (pointwise_gate, False), (pointwise_out, True)]
    hidden = first_up.shape[1]
    tokens_in = (layer_input, output_cotangent)
    if count % BLOCK:
        tokens_in = (layer_input.T, output_cotangent.T)

    (start, cot, gains, up_first, down_first, attend_weights, after_first, squares_first, rows_first,
     pre_first) = feed_forward(
        sizes, "first", 1, 0, first_up, first_down, limit,
        enter=(*tokens_in, gain_parts, attend_pieces),
    )
    (after_attend, squares_attend, rows_attend, qkv, context, log_total, conv_weights,
     up_second) = attention(
        sizes, "attend", 2, 1, limit, after_first, gains, attend_weights, table_wide,
        gathers=[conv_pieces, [(second_up, False)]],
    )
    depth_row = depthwise_gain[None]
    (after_conv, squares_conv, rows_conv, conv_pre, mixed, stats, down_second) = convolution(
        sizes, "convolve", 3, 2, limit, after_attend, gains, conv_weights, depthwise_kernel, depth_row,
        gathers=[[(second_down, True)]],
    )
    (grad_second, final_part, out_tokens, squares_second, rows_second, pre_second) = feed_forward(
        sizes, "second", 4, 3, up_second, down_second, limit, resid=after_conv, gains=gains, turn=cot
    )

    second_part, second_up_wide, second_down_wide, grad_conv = feed_forward_back(
        sizes, "second_back", 5, 3, grad_second, after_conv, gains, up_second, down_second,
        rows_second, pre_second,
    )
    conv_part, conv_wide, kernel_part, depth_part, grad_attend, second_up_grad = convolution_back(
        sizes, "convolve_back", 6, 2, limit, grad_conv, after_attend, gains, conv_weights,
        depthwise_kernel, depth_row, rows_conv, conv_pre, mixed, stats,
        reduces=[(second_up_wide, [(hidden, False)])],
    )
    (attend_part, attend_wide, table_part, grad_first, layer_output, second_down_grad, value_grad, gate_grad,
     out_grad) = attention_back(
        sizes, "attend_back", 7, 1, limit, grad_attend, after_first, gains, attend_weights,
        table_wide, rows_attend, qkv, context, log_total, out_tokens,
        reduces=[
            (second_down_wide, [(hidden, True)]),
            (conv_wide, [(width, False), (width, False), (width, True)]),
        ],
    )
    (first_sum, attend_sum, conv_sum, second_sum, final_sum, table_sum, masked_rms, kernel_sum,
     depth_sum, first_up_grad, first_down_grad, grad_tokens, query_grad, key_grad, attend_value_grad,
     output_grad) = feed_forward_back(
        sizes, "first_back", 0, 0, grad_first, start, gains, up_first, down_first, rows_first,
        pre_first, taps=tap_count,
        leave=(
            limit, (attend_part, conv_part, second_part, final_part),
            (squares_first, squares_attend, squares_conv, squares_second), table_part, kernel_part,
            depth_part,
        ),
        reduces=[(attend_wide, [(width, False), (width, False), (width, False), (width, True)])],
    )

    arrays = [
        layer_output, grad_tokens, first_sum, first_up_grad, first_down_grad, attend_sum, query_grad,
        key_grad, attend_value_grad, output_grad, table_sum, conv_sum, value_grad, gate_grad, kernel_sum,
        depth_sum, out_grad, second_sum, second_up_grad, second_down_grad, final_sum, masked_rms,
    ]
    shapes = [jax.ShapeDtypeStruct(array.shape, array.dtype) for array in arrays]
    shapes[1] = jax.ShapeDtypeStruct(grad_tokens.shape[::-1], F32)
    shapes[-1] = jax.ShapeDtypeStruct((1, 8), F32)
    arrays = results(arrays, shapes)
    return tuple(array[0] if array.shape[0] == 1 else array for array in arrays)


def solution(mesh):
    in_specs = (
        P("col", "row"),
        P("row"),
        P("col"),
        P("row", "col"),
        P("col", "row"),
        P("col"),
        P("row", "col"),
        P("row", "col"),
        P("row", "col"),
        P("col", "row"),
        P(),
        P("col"),
        P("row", "col"),
        P("row", "col"),
        P(None, "col"),
        P("col"),
        P("col", "row"),
        P("col"),
        P("row", "col"),
        P("col", "row"),
        P("col"),
        P("col", "row"),
    )
    out_specs = (
        P("col", "row"),
        P("col", "row"),
        P("col"),
        P("row", "col"),
        P("col", "row"),
        P("col"),
        P("row", "col"),
        P("row", "col"),
        P("row", "col"),
        P("col", "row"),
        P(),
        P("col"),
        P("row", "col"),
        P("row", "col"),
        P(None, "col"),
        P("col"),
        P("col", "row"),
        P("col"),
        P("row", "col"),
        P("col", "row"),
        P("col"),
        P(),
    )
    return jax.shard_map(body, mesh=mesh, in_specs=in_specs, out_specs=out_specs, check_vma=False)
```
